32 devices in a mesh: grp: 2 (over y), seg: 4 (over z), tm: 2 (over x), rep: 2 (over core).
Axes of the slice: x: 2, y: 2, z: 4, core: 2. Of those that a mesh axis runs over, the one named last changes fastest.
Arguments:
- series: bfloat16 [3072, 2, 16, 128], P(('grp', 'seg'), 'rep', 'tm'), parts along dimension 0, may hold values from -6 to 6
- cotangent: bfloat16 [3072, 2, 16, 128], P(('grp', 'seg'), 'rep', 'tm'), parts along dimension 0, may hold values from -6 to 6
- w_filter: bfloat16 [2, 128, 128], replicated, may hold values from -0.375 to 0.375
- w_gate: bfloat16 [2, 128, 128], replicated, may hold values from -0.375 to 0.375
- b_filter: float32 [128], replicated, may hold values from -3 to 3
- b_gate: float32 [128], replicated, may hold values from -3 to 3
- w_diff: bfloat16 [3, 128, 128], replicated, may hold values from -0.5 to 0.5
- b_diff: float32 [128], replicated, may hold values from -3 to 3
- tile_row: int32 [8, 9], P(('grp', 'seg')), parts along dimension 0, may hold values from 0 to 2, as said below
- tile_col: int32 [8, 9], P(('grp', 'seg')), parts along dimension 0, may hold values from 0 to 5, as said below
- tile_val: bfloat16 [8, 9, 128, 128], P(('grp', 'seg')), parts along dimension 0, may hold values from -0.5 to 0.5
- send_nodes: int32 [8, 3, 128], P(('grp', 'seg')), parts along dimension 0, may hold values from 0 to 383
- send_count: int32 [8, 3], P(('grp', 'seg')), parts along dimension 0, may hold values from 0 to 128, as said below
Outputs:
- output: bfloat16 [3072, 2, 16, 128], P(('grp', 'seg'), 'rep', 'tm'), parts along dimension 0
- grad_series: bfloat16 [3072, 2, 16, 128], P(('grp', 'seg'), 'rep', 'tm'), parts along dimension 0
- grad_w_filter: float32 [4, 128, 128], P('grp'), parts along dimension 0
- grad_w_gate: float32 [4, 128, 128], P('grp'), parts along dimension 0
- grad_b_filter: float32 [256], P('grp'), parts along dimension 0
- grad_b_gate: float32 [256], P('grp'), parts along dimension 0
- grad_w_diff: float32 [6, 128, 128], P('grp'), parts along dimension 0
- grad_b_diff: float32 [256], P('grp'), parts along dimension 0
The draws below stay inside these ranges and needn't reach their ends.
There are 2 independent parts, one for each index of `grp`. The reference program is written for one: setup_inputs(seed, part) draws one part's arguments, and reference() takes and returns one part's arrays. A program takes and returns all parts, laid end to end along the dimension named above; an argument that names none is the same for every part. Nothing has to cross between parts.
Inputs may be any that keep to these rules, and one draw needn't show every extreme that they name: The first 3 tiles of each partition have tile_row 0, 1, ..., 2 in order. The first 3 tiles of each partition have tile_col 0, ..., 2 and the next 3 have tile_col 3, ..., 5, in order. `send_count`: list j of partition q is read by partition (q - d_j) mod 4; list 0 of every partition has 128 live entries.
All inputs are finite; a program needn't handle non-finite values.
Results may differ from the reference program's by a relative error of at most 0.0062.
Values may be sent and summed in bfloat16 or wider, within the bound.
A program may use at most 128 MiB of HBM per device.

```python
import math
import jax
import jax.numpy as jnp
from jax import lax

C = 128
TILE = 128
DILATION_FRAMES = 8
NODE_DEV = 384
NBR = 3
CAPN = 128
NB = 3
HALO = 384
HB = 3
NT = 9
NODES = 1536
WINDOW_FRAMES = 16
BATCH = 2
ROWS = 49152
N_SEG = 4


def draw_tile_row(key, part):
    diagonal = jnp.broadcast_to(jnp.arange(NB, dtype=jnp.int32)[None, :], (N_SEG, NB))
    extra_rows = jax.random.randint(key, (N_SEG, NT - NB), 0, NB, dtype=jnp.int32)
    return jnp.concatenate([diagonal, extra_rows], axis=1).astype(jnp.int32)


def draw_tile_col(key, part):
    diagonal = jnp.broadcast_to(jnp.arange(NB, dtype=jnp.int32)[None, :], (N_SEG, NB))
    boundary = jnp.broadcast_to(NB + jnp.arange(HB, dtype=jnp.int32)[None, :], (N_SEG, HB))
    extra_cols = jax.random.randint(key, (N_SEG, NT - NB - HB), 0, NB + HB, dtype=jnp.int32)
    return jnp.concatenate([diagonal, boundary, extra_cols], axis=1).astype(jnp.int32)


def draw_send_count(key, part):
    counts = jax.random.randint(key, (N_SEG, NBR), 0, CAPN + 1, dtype=jnp.int32)
    col_ids = lax.broadcasted_iota(jnp.int32, (N_SEG, NBR), 1)
    counts = jnp.where(col_ids == 0, CAPN, counts)
    return counts.astype(jnp.int32)


def plant(result, rng, low, top_value):
    dims = result.shape
    index_at = [jax.random.randint(jax.random.fold_in(rng, axis), (), 0, dims[axis]) for axis in range(len(dims))]
    result = result.at[tuple(index_at)].set(low)
    longest = dims.index(max(dims))
    index_at[longest] = (index_at[longest] + 1) % dims[longest]
    return result.at[tuple(index_at)].set(top_value)


def block_scale(stream_key, shape, cuts, low, high):
    factor_of, own = 1.0, jax.random.fold_in(stream_key, 6)
    for dim, parts in cuts:
        steps = jnp.exp(jax.random.uniform(jax.random.fold_in(own, dim), (parts,), jnp.float32, low / len(cuts), high / len(cuts)))
        factor_of = factor_of * jnp.repeat(steps, shape[dim] // parts).reshape([-1 if axis == dim else 1 for axis in range(len(shape))])
    return factor_of


def gaussian(stream_key, shape, scale, most, cuts=(), kind=jnp.bfloat16):
    factor_of = block_scale(stream_key, shape, cuts, -0.22, 0.18) if cuts else 1.0
    drawn = jax.random.normal(stream_key, shape, jnp.float32) * scale * factor_of
    return jnp.minimum(jnp.maximum(drawn, -most), most).astype(kind)


def setup_inputs(seed: int = 0, part: int = 0) -> dict:
    key_of = jax.random.split(jax.random.key(seed), 14)
    own_keys = jax.random.split(jax.random.fold_in(key_of[13], part), 14)
    series = gaussian(own_keys[0], (NODES, BATCH, WINDOW_FRAMES, C), 1.0, 6.0, ((0, 4), (1, 2), (2, 2)))
    cotangent = gaussian(own_keys[1], (NODES, BATCH, WINDOW_FRAMES, C), 1.0, 6.0, ((0, 4), (1, 2), (2, 2)))
    w_filter = gaussian(key_of[2], (2, C, C), (2 * C) ** -0.5, 0.375)
    w_gate = gaussian(key_of[3], (2, C, C), (2 * C) ** -0.5, 0.375)
    b_filter = gaussian(key_of[4], (C,), 0.5, 3.0, (), jnp.float32)
    b_gate = gaussian(key_of[5], (C,), 0.5, 3.0, (), jnp.float32)
    w_diff = gaussian(key_of[6], (3, C, C), C ** -0.5, 0.5)
    b_diff = gaussian(key_of[7], (C,), 0.5, 3.0, (), jnp.float32)
    tile_row = draw_tile_row(jax.random.fold_in(jax.random.fold_in(key_of[13], part), 71), part)
    tile_col = draw_tile_col(jax.random.fold_in(jax.random.fold_in(key_of[13], part), 71), part)
    tile_val = gaussian(own_keys[10], (N_SEG, NT, TILE, TILE), TILE ** -0.5, 0.5, ((0, 4),))
    send_nodes = plant(jax.random.randint(own_keys[11], (N_SEG, NBR, CAPN), 0, NODE_DEV), jax.random.fold_in(own_keys[11], 1), 0, NODE_DEV - 1).astype(jnp.int32)
    send_count = draw_send_count(jax.random.fold_in(jax.random.fold_in(key_of[13], part), 71), part)
    return {"series": series, "cotangent": cotangent, "w_filter": w_filter, "w_gate": w_gate, "b_filter": b_filter, "b_gate": b_gate, "w_diff": w_diff, "b_diff": b_diff, "tile_row": tile_row, "tile_col": tile_col, "tile_val": tile_val, "send_nodes": send_nodes, "send_count": send_count}


neighbour_steps = (1, -1, 2)

def linear_map(inputs, weight):
    return jnp.dot(inputs, weight, preferred_element_type=jnp.float32)

def linear_back(inputs, weight):
    return lax.dot_general(inputs, weight, (((1,), (1,)), ((), ())), preferred_element_type=jnp.float32)

def outer_sum(left_rows, right_rows):
    return lax.dot_general(left_rows, right_rows, (((0,), (0,)), ((), ())), preferred_element_type=jnp.float32)

def pre_acts(prior_frames, current, w_filter, w_gate, b_filter, b_gate):
    channels = current.shape[-1]
    prev_rows = prior_frames.reshape(-1, channels)
    curr_rows = current.reshape(-1, channels)
    filter_pre = linear_map(prev_rows, w_filter[0]) + linear_map(curr_rows, w_filter[1]) + b_filter
    gate_pre = linear_map(prev_rows, w_gate[0]) + linear_map(curr_rows, w_gate[1]) + b_gate
    return (filter_pre, gate_pre)

def gated_units(filter_pre, gate_pre):
    return (jnp.tanh(filter_pre) * jax.nn.sigmoid(gate_pre)).astype(jnp.bfloat16)

def spread_tiles(source, row_list, col_list, tile_values, out_rows):
    tile_side = tile_values.shape[1]
    row_width = source.shape[1]

    def add_tile(tile_index, running):
        source_piece = lax.dynamic_slice_in_dim(source, col_list[tile_index] * tile_side, tile_side, 0)
        product = jnp.dot(tile_values[tile_index], source_piece, preferred_element_type=jnp.float32)
        row_start = row_list[tile_index] * tile_side
        current = lax.dynamic_slice_in_dim(running, row_start, tile_side, 0)
        return lax.dynamic_update_slice_in_dim(running, current + product, row_start, 0)
    return lax.fori_loop(0, tile_values.shape[0], add_tile, jnp.zeros((out_rows, row_width), jnp.float32))

def gather_tiles(cotan, row_list, col_list, tile_values, out_rows):
    tile_side = tile_values.shape[1]
    row_width = cotan.shape[1]

    def add_tile(tile_index, running):
        source_piece = lax.dynamic_slice_in_dim(cotan, row_list[tile_index] * tile_side, tile_side, 0)
        product = outer_sum(tile_values[tile_index], source_piece)
        row_start = col_list[tile_index] * tile_side
        current = lax.dynamic_slice_in_dim(running, row_start, tile_side, 0)
        return lax.dynamic_update_slice_in_dim(running, current + product, row_start, 0)
    return lax.fori_loop(0, tile_values.shape[0], add_tile, jnp.zeros((out_rows, row_width), jnp.float32))

def reference(series, cotangent, w_filter, w_gate, b_filter, b_gate, w_diff, b_diff, tile_row, tile_col, tile_val, send_nodes, send_count):
    row_width = BATCH * WINDOW_FRAMES * C
    prior_frames = jnp.pad(series, ((0, 0), (0, 0), (DILATION_FRAMES, 0), (0, 0)))[:, :, :WINDOW_FRAMES]
    filter_pre, gate_pre = pre_acts(prior_frames, series, w_filter, w_gate, b_filter, b_gate)
    hidden = gated_units(filter_pre, gate_pre)
    live_slots = jnp.arange(CAPN, dtype=jnp.int32)[None, None, :] < send_count[:, :, None]
    owners = jnp.arange(N_SEG, dtype=jnp.int32)

    def forward_op(field):
        blocks = field.reshape(N_SEG, NODE_DEV, row_width)

        def one_part(part_id):
            pieces = [blocks[part_id]]
            for neighbour, offset in enumerate(neighbour_steps):
                owner = ((part_id + offset) % N_SEG).astype(jnp.int32)
                picked = blocks[owner][send_nodes[owner, neighbour]]
                picked = jnp.where(live_slots[owner, neighbour][:, None], picked, jnp.zeros((), field.dtype))
                pieces.append(picked)
            source = jnp.concatenate(pieces, axis=0)
            return spread_tiles(source, tile_row[part_id], tile_col[part_id], tile_val[part_id], NODE_DEV)
        return lax.map(one_part, owners).reshape(NODES, row_width)

    def backward_op(cotan):
        blocks = cotan.reshape(N_SEG, NODE_DEV, row_width)

        def one_part(part_id):
            summed = gather_tiles(blocks[part_id], tile_row[part_id], tile_col[part_id], tile_val[part_id], NODE_DEV + HALO)
            return (summed[:NODE_DEV], summed[NODE_DEV:].astype(jnp.bfloat16))
        local_part, halo_part = lax.map(one_part, owners)
        halo_part = halo_part.reshape(N_SEG, NBR, CAPN, row_width)

        def one_owner(owner_id):
            total = jnp.zeros((NODE_DEV, row_width), jnp.float32)
            for neighbour, offset in enumerate(neighbour_steps):
                reader = ((owner_id - offset) % N_SEG).astype(jnp.int32)
                incoming = halo_part[reader, neighbour].astype(jnp.float32)
                incoming = incoming * live_slots[owner_id, neighbour][:, None].astype(jnp.float32)
                total = total.at[send_nodes[owner_id, neighbour]].add(incoming)
            return total
        scattered = lax.map(one_owner, owners)
        return (local_part + scattered).reshape(NODES, row_width)
    hop_one = forward_op(hidden.reshape(NODES, row_width)).astype(jnp.bfloat16)
    hop_two = forward_op(hop_one).astype(jnp.bfloat16)
    one_rows = hop_one.reshape(-1, C)
    two_rows = hop_two.reshape(-1, C)
    diffusion_out = linear_map(hidden, w_diff[0]) + linear_map(one_rows, w_diff[1]) + linear_map(two_rows, w_diff[2]) + b_diff
    output = (series.reshape(-1, C).astype(jnp.float32) + diffusion_out).astype(jnp.bfloat16).reshape(series.shape)
    grad_scale = 1.0 / math.sqrt(ROWS)
    grad_rows = cotangent.reshape(-1, C)
    grad_b_diff = lax.optimization_barrier(jnp.sum(grad_rows.astype(jnp.float32), axis=0)) * grad_scale
    grad_w_diff = jnp.stack([outer_sum(hidden, grad_rows), outer_sum(one_rows, grad_rows), outer_sum(two_rows, grad_rows)]) * grad_scale
    up_two = linear_back(grad_rows, w_diff[2]).astype(jnp.bfloat16)
    up_one = (linear_back(grad_rows, w_diff[1]) + backward_op(up_two.reshape(NODES, row_width)).reshape(-1, C)).astype(jnp.bfloat16)
    grad_hidden = linear_back(grad_rows, w_diff[0]) + backward_op(up_one.reshape(NODES, row_width)).reshape(-1, C)
    act_filter = jnp.tanh(filter_pre)
    act_gate = jax.nn.sigmoid(gate_pre)
    grad_filter = (grad_hidden * act_gate * (1.0 - act_filter * act_filter)).astype(jnp.bfloat16)
    grad_gate = (grad_hidden * act_filter * (act_gate * (1.0 - act_gate))).astype(jnp.bfloat16)
    prev_rows = prior_frames.reshape(-1, C)
    curr_rows = series.reshape(-1, C)
    grad_w_filter = jnp.stack([outer_sum(prev_rows, grad_filter), outer_sum(curr_rows, grad_filter)]) * grad_scale
    grad_b_filter = lax.optimization_barrier(jnp.sum(grad_filter.astype(jnp.float32), axis=0)) * grad_scale
    grad_w_gate = jnp.stack([outer_sum(prev_rows, grad_gate), outer_sum(curr_rows, grad_gate)]) * grad_scale
    grad_b_gate = lax.optimization_barrier(jnp.sum(grad_gate.astype(jnp.float32), axis=0)) * grad_scale
    lagged_series = (linear_back(grad_filter, w_filter[0]) + linear_back(grad_gate, w_gate[0])).astype(jnp.bfloat16)
    lagged_series = lagged_series.reshape(series.shape)
    forward_moved = jnp.pad(lagged_series, ((0, 0), (0, 0), (0, DILATION_FRAMES), (0, 0)))[:, :, DILATION_FRAMES:]
    grad_series = (grad_rows.astype(jnp.float32) + linear_back(grad_filter, w_filter[1]) + linear_back(grad_gate, w_gate[1]) + forward_moved.reshape(-1, C).astype(jnp.float32)).astype(jnp.bfloat16).reshape(series.shape)
    return (output, grad_series, grad_w_filter, grad_w_gate, grad_b_filter, grad_b_gate, grad_w_diff, grad_b_diff)
```

```python
import functools
import math

import jax
import jax.numpy as jnp
from jax import lax
from jax.experimental import pallas as pl
from jax.experimental.pallas import tpu as pltpu
from jax.sharding import PartitionSpec as P

DILATION_FRAMES = 8
STEPS = (1, -1, 2)
MESH = pl.DeviceIdType.MESH
WIDE = 256
BF = jnp.bfloat16
F32 = jnp.float32


def mm(a, b):
    return lax.dot_general(a, b, (((1,), (0,)), ((), ())), preferred_element_type=F32)


def mm_nt(a, b):
    return lax.dot_general(a, b, (((1,), (1,)), ((), ())), preferred_element_type=F32)


def mm_tn(a, b):
    return lax.dot_general(a, b, (((0,), (0,)), ((), ())), preferred_element_type=F32)


def halo_kernel(
    seg_n, tm_n, scale,
    ser3, cot3, wf, wg, bf, bg, wd, bd, trow, tcol, tval, snodes, scount,
    out3, gs3, fin1, fin2,
    big, big_g, ser, cot, prev, ops_f, ops_b, pick, give, wblk,
    acc, act_f, act_g, hid, hop1, delayed_out, delayed_in,
    snd, rcv, wacc, dacc, bacc, cacc,
    red1, red2, rb1, rc1, sb1, rb2, rc2, sb2,
    tm_s, tm_r, ex_s, ex_r, dl_s, dl_r, ar_s, ar_r,
):
    p = lax.axis_index("seg")
    t = lax.axis_index("tm")
    rep = lax.axis_index("rep")
    chunks, nodes, _ = ser.shape
    doublings = seg_n.bit_length() - 1
    cap = 128
    ch = 128

    barrier = pltpu.get_barrier_semaphore()
    for k in range(1, seg_n):
        pl.semaphore_signal(barrier, inc=1, device_id={"seg": lax.rem(p + k, seg_n)}, device_id_type=MESH)
    crew = 2 * tm_n
    me = t * 2 + rep

    def crew_device(i):
        return {"tm": lax.div(i, 2), "rep": lax.rem(i, 2)}

    for k in range(1, crew):
        pl.semaphore_signal(barrier, inc=1, device_id=crew_device(lax.rem(me + k, crew)), device_id_type=MESH)
    pl.semaphore_wait(barrier, seg_n - 1 + crew - 1)

    def series_copy(c):
        return pltpu.make_async_remote_copy(
            src_ref=ser.at[c], dst_ref=prev.at[c], send_sem=tm_s.at[c], recv_sem=tm_r.at[c],
            device_id={"tm": lax.rem(t + 1, tm_n)}, device_id_type=MESH)

    def delayed_copy(c):
        return pltpu.make_async_remote_copy(
            src_ref=delayed_out.at[c], dst_ref=delayed_in.at[c], send_sem=dl_s.at[c], recv_sem=dl_r.at[c],
            device_id={"tm": lax.rem(t + tm_n - 1, tm_n)}, device_id_type=MESH)

    def halo_copy(e, c, j):
        step = STEPS[j] if e % 2 == 0 else -STEPS[j]
        return pltpu.make_async_remote_copy(
            src_ref=snd.at[e, c, j], dst_ref=rcv.at[e, c, j],
            send_sem=ex_s.at[e, c, j], recv_sem=ex_r.at[e, c, j],
            device_id={"seg": lax.rem(p + step + seg_n, seg_n)}, device_id_type=MESH)

    def side_by_side(src, dst):
        big[...] = src[...].astype(F32)
        for c in range(chunks):
            dst[c] = jnp.concatenate([big[:, 2 * c, :], big[:, 2 * c + 1, :]], axis=1).astype(BF)

    side_by_side(cot3, cot)

    rows_n, cols_n, tiles_n = nodes // 128, nodes // 128 + 3, tval.shape[0]
    for r in range(rows_n):
        for c in range(cols_n):
            total = jnp.zeros((128, 128), F32)
            for k in range(tiles_n):
                if k < rows_n and (r != k or c != k):
                    continue
                if rows_n <= k < cols_n and c != k:
                    continue
                hit = jnp.where(trow[0, k] == r, 1.0, 0.0) * jnp.where(tcol[0, k] == c, 1.0, 0.0)
                total = total + hit * tval[k].astype(F32)
            ops_f[r * 128:(r + 1) * 128, c * 128:(c + 1) * 128] = total.astype(BF)
            ops_b[c * 128:(c + 1) * 128, r * 128:(r + 1) * 128] = total.T.astype(BF)
    wblk[4:7] = jnp.zeros((3, WIDE, WIDE), BF)
    for i in range(2):
        lo, hi = i * ch, (i + 1) * ch
        for k in range(3):
            wblk[4 + k, lo:hi, lo:hi] = wd[k]

    def put(e, c, rows):
        for j in range(3):
            snd[e, c, j] = rows[j * cap:(j + 1) * cap]
            halo_copy(e, c, j).start()

    def back_one(c, _):
        g = cot[c]
        up = mm_nt(g, wblk[6]).astype(BF)
        put(0, c, mm(ops_b[nodes:, :], up).astype(BF))
        acc[c] = mm(ops_b[:nodes, :], up) + mm_nt(g, wblk[5])
        return 0

    lax.fori_loop(0, chunks, back_one, 0)

    side_by_side(ser3, ser)

    @pl.when(t < tm_n - 1)
    def _():
        for c in range(chunks):
            series_copy(c).start()

    @pl.when(t == 0)
    def _():
        prev[...] = jnp.zeros_like(prev)

    @pl.when(t == tm_n - 1)
    def _():
        delayed_in[...] = jnp.zeros_like(delayed_in)

    wblk[0:4] = jnp.zeros((4, WIDE, WIDE), BF)
    for i in range(2):
        lo, hi = i * ch, (i + 1) * ch
        for k in range(2):
            wblk[k, lo:hi, lo:hi] = wf[k]
            wblk[2 + k, lo:hi, lo:hi] = wg[k]

    node_ids = lax.broadcasted_iota(jnp.int32, (nodes, cap), 0)
    slot_ids = lax.broadcasted_iota(jnp.int32, (nodes, cap), 1)
    for j in range(3):
        here = jnp.where(node_ids == snodes[j:j + 1, :], 1.0, 0.0)
        live = jnp.where(slot_ids < scount[0, j], 1.0, 0.0)
        hot = here * live
        give[:, j * cap:(j + 1) * cap] = hot.astype(BF)
        pick[j * cap:(j + 1) * cap, :] = hot.T.astype(BF)
    wacc[...] = jnp.zeros_like(wacc)
    dacc[...] = jnp.zeros_like(dacc)
    bacc[...] = jnp.zeros_like(bacc)
    cacc[...] = jnp.zeros_like(cacc)
    red1[...] = jnp.zeros_like(red1)
    red2[...] = jnp.zeros_like(red2)
    ones = jnp.ones((8, nodes), BF)

    def arrived(e, c):
        for j in range(3):
            halo_copy(e, c, j).wait_recv()
        return rcv[e, c].reshape(3 * cap, WIDE)

    def back_two(c, _):
        got = arrived(0, c)
        up = (acc[c] + mm(give[...], got)).astype(BF)
        put(2, c, mm(ops_b[nodes:, :], up).astype(BF))
        acc[c] = mm(ops_b[:nodes, :], up) + mm_nt(cot[c], wblk[4])
        return 0

    lax.fori_loop(0, chunks, back_two, 0)

    bf2 = jnp.concatenate([bf[...], bf[...]], axis=1)
    bg2 = jnp.concatenate([bg[...], bg[...]], axis=1)
    bd2 = jnp.concatenate([bd[...], bd[...]], axis=1)

    def fore_one(c, _):
        @pl.when(t > 0)
        def _():
            series_copy(c).wait_recv()

        before, now = prev[c], ser[c]
        a = jnp.tanh(mm(before, wblk[0]) + mm(now, wblk[1]) + bf2)
        act_f[c] = a
        s = jax.nn.sigmoid(mm(before, wblk[2]) + mm(now, wblk[3]) + bg2)
        act_g[c] = s
        h = (a * s).astype(BF)
        hid[c] = h
        put(1, c, mm(pick[...], h).astype(BF))
        return 0

    lax.fori_loop(0, chunks, fore_one, 0)

    def back_three(c, _):
        got = arrived(2, c)
        gh = acc[c] + mm(give[...], got)
        a, s = act_f[c], act_g[c]
        gf = (gh * s * (1.0 - a * a)).astype(BF)
        gg = (gh * a * (s * (1.0 - s))).astype(BF)
        delayed_out[c] = (mm_nt(gf, wblk[0]) + mm_nt(gg, wblk[2])).astype(BF)

        @pl.when(t > 0)
        def _():
            delayed_copy(c).start()

        g = cot[c]
        acc[c] = g.astype(F32) + mm_nt(gf, wblk[1]) + mm_nt(gg, wblk[3])
        before, now, h = prev[c], ser[c], hid[c]
        for i in range(2):
            lo, hi = i * ch, (i + 1) * ch
            right = jnp.concatenate([gf[:, lo:hi], gg[:, lo:hi]], axis=1)
            left = jnp.concatenate([before[:, lo:hi], now[:, lo:hi]], axis=1)
            wacc[...] += mm_tn(left, right)
            dacc[...] += mm_tn(h[:, lo:hi], g[:, lo:hi])
            bacc[...] += mm(ones, right)
            cacc[...] += mm(ones, g[:, lo:hi])
        return 0

    lax.fori_loop(0, chunks, back_three, 0)

    red1[0:256, :] = wacc[:, 0:128]
    red1[256:512, :] = wacc[:, 128:256]
    red1[512:640, :] = dacc[...]
    rid = lax.broadcasted_iota(jnp.int32, (8, 128), 0)
    red1[640:648, :] = jnp.where(
        rid == 0, bacc[:, 0:128], jnp.where(rid == 1, bacc[:, 128:256], cacc[...]))

    def all_sum(base, direct, red, rb, rc, sb, fin):
        part = red.shape[0] // crew

        def copy(src, dst, at, device):
            made = pltpu.make_async_remote_copy(
                src_ref=src, dst_ref=dst, send_sem=ar_s.at[at], recv_sem=ar_r.at[at],
                device_id=device, device_id_type=MESH)
            made.start()
            return made

        def rows(i):
            return pl.ds(pl.multiple_of(i * part, 8), part)

        sends = []
        for k in range(1, crew):
            o = lax.rem(me + k, crew)
            sends.append(copy(red.at[rows(o)], rb.at[k - 1], base + k, crew_device(o)))
        yield
        s = red[rows(me), :]
        for k in range(1, crew):
            sends[k - 1].wait()
            s = s + rb[k - 1]
        at = base + crew
        if direct:
            sb[0] = s
            rc[p] = s
            sends = [
                copy(sb.at[0], rc.at[p], at + k, {"seg": lax.rem(p + k, seg_n)})
                for k in range(1, seg_n)]
            yield
            for one in sends:
                one.wait()
            s = rc[0]
            for k in range(1, seg_n):
                s = s + rc[k]
        else:
            bit = 1
            for k in range(doublings):
                sb[k] = s
                mate = p + (1 - 2 * lax.rem(lax.div(p, bit), 2)) * bit
                one = copy(sb.at[k], rc.at[k], at + k, {"seg": mate})
                yield
                one.wait()
                s = s + rc[k]
                bit *= 2
        fin[rows(me), :] = s * scale
        at = at + seg_n
        sends = [
            copy(fin.at[rows(me)], fin.at[rows(me)], at + k, crew_device(lax.rem(me + k, crew)))
            for k in range(1, crew)]
        yield
        for one in sends:
            one.wait()
        yield

    first = all_sum(0, False, red1, rb1, rc1, sb1, fin1)
    next(first)
    def fore_two(c, _):
        got = arrived(1, c)
        h = (mm(ops_f[:, :nodes], hid[c]) + mm(ops_f[:, nodes:], got)).astype(BF)
        hop1[c] = h
        put(3, c, mm(pick[...], h).astype(BF))
        return 0

    for c in range(chunks):
        fore_two(c, 0)
        if c in (0, 1):
            next(first)

    for c in range(chunks):
        if c >= 2:
            next(first, None)
        got = arrived(3, c)
        h, h1, g = hid[c], hop1[c], cot[c]
        h2 = (mm(ops_f[:, :nodes], h1) + mm(ops_f[:, nodes:], got)).astype(BF)
        total = mm(h, wblk[4]) + mm(h1, wblk[5]) + mm(h2, wblk[6]) + bd2
        total = ser[c].astype(F32) + total
        for i in range(2):
            lo, hi = i * ch, (i + 1) * ch
            both = jnp.concatenate([h1[:, lo:hi], h2[:, lo:hi]], axis=1)
            red2[...] += mm_tn(both, g[:, lo:hi])
            big[:, 2 * c + i, :] = total[:, lo:hi]
    second = all_sum(2 * crew + seg_n, True, red2, rb2, rc2, sb2, fin2)
    next(second)
    out3[...] = big[...].astype(BF)
    next(second)
    for c in range(chunks):
        @pl.when(t < tm_n - 1)
        def _():
            delayed_copy(c).wait_recv()

        total = acc[c] + delayed_in[c].astype(F32)
        for i in range(2):
            big_g[:, 2 * c + i, :] = total[:, i * ch:(i + 1) * ch]
    next(second)
    gs3[...] = big_g[...].astype(BF)
    for _ in first:
        pass
    for _ in second:
        pass

    def drain(c, _):
        @pl.when(t < tm_n - 1)
        def _():
            series_copy(c).wait_send()

        @pl.when(t > 0)
        def _():
            delayed_copy(c).wait_send()

        for e in range(4):
            for j in range(3):
                halo_copy(e, c, j).wait_send()
        return 0

    lax.fori_loop(0, chunks, drain, 0)


def halo_plan(mesh, series, cotangent, w_filter, w_gate, b_filter, b_gate, w_diff, b_diff,
              tile_row, tile_col, tile_val, send_nodes, send_count):
    nodes, batch, frames, channels = series.shape
    seg_n, tm_n, rep_n = mesh.shape["seg"], mesh.shape["tm"], mesh.shape["rep"]
    chunks = batch * frames * channels // WIDE
    scale = 1.0 / math.sqrt(nodes * batch * frames * seg_n * tm_n * rep_n)
    unit = 16 * tm_n
    r1 = -(-648 // unit) * unit
    r2 = -(-256 // unit) * unit

    doublings = seg_n.bit_length() - 1
    vmem = pl.BlockSpec(memory_space=pltpu.VMEM)
    smem = pl.BlockSpec(memory_space=pltpu.SMEM)
    field = (chunks, nodes, WIDE)

    def sums(r):
        crew = 2 * tm_n
        q = r // crew
        return [
            pltpu.VMEM((crew - 1, q, 128), F32),
            pltpu.VMEM((seg_n, q, 128), F32),
            pltpu.VMEM((doublings, q, 128), F32),
        ]

    n_ar = 2 * (4 * tm_n + seg_n)
    raw = (nodes, batch * frames, channels)
    halo = (4, chunks, 3, 128, WIDE)
    out, gs, fin1, fin2 = pl.pallas_call(
        functools.partial(halo_kernel, seg_n, tm_n, scale),
        out_shape=(
            jax.ShapeDtypeStruct(raw, BF),
            jax.ShapeDtypeStruct(raw, BF),
            jax.ShapeDtypeStruct((r1, 128), F32),
            jax.ShapeDtypeStruct((r2, 128), F32),
        ),
        in_specs=[vmem] * 8 + [smem, smem, vmem, vmem, smem],
        out_specs=(vmem,) * 4,
        scratch_shapes=[
            pltpu.VMEM(raw, F32),
            pltpu.VMEM(raw, F32),
            pltpu.VMEM(field, BF),
            pltpu.VMEM(field, BF),
            pltpu.VMEM(field, BF),
            pltpu.VMEM((nodes, nodes + 384), BF),
            pltpu.VMEM((nodes + 384, nodes), BF),
            pltpu.VMEM((384, nodes), BF),
            pltpu.VMEM((nodes, 384), BF),
            pltpu.VMEM((7, WIDE, WIDE), BF),
            pltpu.VMEM(field, F32),
            pltpu.VMEM(field, F32),
            pltpu.VMEM(field, F32),
            pltpu.VMEM(field, BF),
            pltpu.VMEM(field, BF),
            pltpu.VMEM(field, BF),
            pltpu.VMEM(field, BF),
            pltpu.VMEM(halo, BF),
            pltpu.VMEM(halo, BF),
            pltpu.VMEM((256, 256), F32),
            pltpu.VMEM((128, 128), F32),
            pltpu.VMEM((8, 256), F32),
            pltpu.VMEM((8, 128), F32),
            pltpu.VMEM((r1, 128), F32),
            pltpu.VMEM((r2, 128), F32),
            *sums(r1),
            *sums(r2),
            pltpu.SemaphoreType.DMA((chunks,)),
            pltpu.SemaphoreType.DMA((chunks,)),
            pltpu.SemaphoreType.DMA((4, chunks, 3)),
            pltpu.SemaphoreType.DMA((4, chunks, 3)),
            pltpu.SemaphoreType.DMA((chunks,)),
            pltpu.SemaphoreType.DMA((chunks,)),
            pltpu.SemaphoreType.DMA((n_ar,)),
            pltpu.SemaphoreType.DMA((n_ar,)),
        ],
        compiler_params=pltpu.CompilerParams(
            collective_id=0, has_side_effects=True, vmem_limit_bytes=56 << 20),
    )(
        series.reshape(raw), cotangent.reshape(raw), w_filter, w_gate,
        b_filter.reshape(1, -1), b_gate.reshape(1, -1), w_diff, b_diff.reshape(1, -1),
        tile_row, tile_col, tile_val[0], send_nodes[0], send_count,
    )
    return (
        out.reshape(series.shape),
        gs.reshape(series.shape),
        fin1[0:256].reshape(2, 128, 128),
        fin1[256:512].reshape(2, 128, 128),
        fin1[640],
        fin1[641],
        jnp.concatenate([fin1[512:640], fin2[:256]], axis=0).reshape(3, 128, 128),
        fin1[642],
    )


def gather_kernel(
    seg_n, tm_n, scale,
    ser3, cot3, wf, wg, bf, bg, wd, bd, trow, tcol, tval, snodes, scount,
    out3, gs3, fin,
    big, big_g, stage_s, stage_c, ser, cot, tiles, meta,
    opf, opb, oph, pick, wc, wct, wdt,
    act_f, act_g, src0, src1, hop2, sb0, sb1, acc,
    out_b, gs_b, out_r, gs_r,
    red, rbuf0, rbuf1, rz,
    tz_s, tz_r, mz_s, mz_r, tx_s, tx_r, tc_s, tc_r,
    se_s, se_r, co_s, co_r, ou_s, ou_r, gr_s, gr_r, ar_s, ar_r,
):
    p = lax.axis_index("seg")
    t = lax.axis_index("tm")
    rep = lax.axis_index("rep")
    nodes, frames, ch = ser3.shape
    mine = p * tm_n + t
    crew = 2 * tm_n
    quarter = tiles.shape[1] // crew

    def rc(src, dst, ss, rs, dev):
        return pltpu.make_async_remote_copy(
            src_ref=src, dst_ref=dst, send_sem=ss, recv_sem=rs, device_id=dev, device_id_type=MESH)

    def seg_at(k):
        return lax.rem(p + k, seg_n)

    others = [(k, m) for k in range(seg_n) for m in range(tm_n) if (k, m) != (0, 0)]
    others.sort(key=lambda o: (abs(o[0] - seg_n // 2), o[1]))

    def peer(k, m):
        return seg_at(k), lax.rem(t + m, tm_n)

    def rows_of(q):
        return pl.ds(pl.multiple_of(q * nodes, 128), nodes)

    def piece(c):
        return pl.ds(pl.multiple_of(c * quarter, 16), quarter)

    core = {"rep": 1 - rep}
    across = {"tm": 1 - t}

    barrier = pltpu.get_barrier_semaphore()
    for k, m in others:
        q, tt = peer(k, m)
        pl.semaphore_signal(barrier, inc=1, device_id={"seg": q, "tm": tt}, device_id_type=MESH)
    pl.semaphore_signal(barrier, inc=1, device_id=core, device_id_type=MESH)

    def frame_major(source, wide, stage, whole):
        wide[...] = source[...].astype(F32)
        for f in range(frames):
            stage[f] = wide[:, f, :].astype(BF)
        whole[t, rows_of(p), :] = stage[mine]

    tiles[p] = tval[...]
    meta[p] = jnp.zeros_like(meta[p])
    meta[p, 0:3, :] = snodes[...]
    meta[p, 3:4, 0:trow.shape[1]] = trow[...]
    meta[p, 4:5, 0:tcol.shape[1]] = tcol[...]
    meta[p, 5:6, 0:scount.shape[1]] = scount[...]
    frame_major(ser3, big, stage_s, ser)
    pl.semaphore_wait(barrier, len(others) + 1)

    c_me = t * 2 + rep

    def tile_z(at, k_sem, dev):
        return rc(tiles.at[at, piece(c_me)], tiles.at[at, piece(c_me)], tz_s.at[k_sem], tz_r.at[at], dev)

    def meta_z(at, k_sem, dev):
        return rc(meta.at[at], meta.at[at], mz_s.at[k_sem], mz_r.at[at], dev)

    def field_in(stage, whole, ss, rs, k, m):
        q, tt = peer(k, m)
        f = q * tm_n + tt
        return rc(stage.at[f], whole.at[t, rows_of(p)], ss.at[f], rs.at[mine], {"seg": q, "tm": tt})

    def field_got(stage, whole, ss, rs, k, m):
        q, tt = peer(k, m)
        f = q * tm_n + tt
        return rc(stage.at[f], whole.at[tt, rows_of(q)], ss.at[f], rs.at[f], {"seg": q, "tm": tt})

    far_first = sorted(range(1, seg_n), key=lambda k: abs(k - seg_n // 2))
    for k in far_first:
        meta_z(p, k, {"seg": seg_at(k)}).start()
        tile_z(p, k, {"seg": seg_at(k)}).start()
    for k, m in others:
        field_in(stage_s, ser, se_s, se_r, k, m).start()

    frame_major(cot3, big_g, stage_c, cot)

    for i in range(2):
        wc[i * ch:(i + 1) * ch, 0:ch] = wf[i]
        wc[i * ch:(i + 1) * ch, ch:2 * ch] = wg[i]
    wct[...] = wc[...].astype(F32).T.astype(BF)
    for i in range(3):
        wdt[i] = wd[i].astype(F32).T.astype(BF)
    bias = jnp.concatenate([bf[...], bg[...]], axis=1)
    red[...] = jnp.zeros_like(red)

    def tile_x(q, c):
        return rc(tiles.at[q, piece(c)], tiles.at[q, piece(c)], tx_s.at[q], tx_r.at[q], across)

    def tile_c(q, c, i):
        return rc(tiles.at[q, piece(c)], tiles.at[q, piece(c)], tc_s.at[q, i], tc_r.at[q, i], core)

    c_across = (1 - t) * 2 + rep
    for k in far_first:
        tile_z(seg_at(k), 0, {"seg": seg_at(k)}).wait_recv()
        tile_x(seg_at(k), c_me).start()
    for k in far_first:
        tile_x(seg_at(k), c_across).wait_recv()
        tile_c(seg_at(k), c_me, 0).start()
        tile_c(seg_at(k), c_across, 1).start()
    for k in far_first:
        tile_c(seg_at(k), t * 2 + (1 - rep), 0).wait_recv()
        tile_c(seg_at(k), (1 - t) * 2 + (1 - rep), 1).wait_recv()
        meta_z(seg_at(k), 0, {"seg": seg_at(k)}).wait_recv()

    rows_n = nodes // 128
    cols_n = rows_n + 3
    tiles_n = tiles.shape[1] // 128
    halo = 3 * 128
    lane_ids = lax.broadcasted_iota(jnp.int32, (128, nodes), 1)
    sub_ids = lax.broadcasted_iota(jnp.int32, (nodes, 128), 0)
    slot_lane = lax.broadcasted_iota(jnp.int32, (1, 128), 1)
    slot_sub = lax.broadcasted_iota(jnp.int32, (128, 1), 0)

    def build(q, _):
        info = meta[q]
        tr, tc = info[3:4, :], info[4:5, :]
        t_all = [tiles[q, k * 128:(k + 1) * 128, :].astype(F32) for k in range(tiles_n)]
        for r in range(rows_n):
            for c in range(cols_n):
                hits = jnp.where((tr == r) & (tc == c), 1.0, 0.0)
                total = jnp.zeros((128, 128), F32)
                for k in range(tiles_n):
                    if k < rows_n and (r != k or c != k):
                        continue
                    if rows_n <= k < cols_n and c != k:
                        continue
                    total = total + hits[:, k:k + 1] * t_all[k]
                flipped = total.T.astype(BF)
                opf[q, r * 128:(r + 1) * 128, c * 128:(c + 1) * 128] = total.astype(BF)
                if c < rows_n:
                    opb[q, c * 128:(c + 1) * 128, r * 128:(r + 1) * 128] = flipped
                else:
                    oph[q, (c - rows_n) * 128:(c - rows_n + 1) * 128, r * 128:(r + 1) * 128] = flipped
        col = info.astype(F32).T.astype(jnp.int32)
        for j in range(3):
            count = info[5:6, j:j + 1]
            give = jnp.where((sub_ids == info[j:j + 1, :]) & (slot_lane < count), 1.0, 0.0)
            opb[q, :, nodes + j * 128:nodes + (j + 1) * 128] = give.astype(BF)
            take = jnp.where((lane_ids == col[:, j:j + 1]) & (slot_sub < count), 1.0, 0.0)
            pick[q, j * 128:(j + 1) * 128, :] = take.astype(BF)
        return 0

    lax.fori_loop(0, seg_n, build, 0)

    for k, m in others:
        field_in(stage_s, ser, se_s, se_r, k, m).wait_send()
        field_in(stage_c, cot, co_s, co_r, k, m).start()

    for k, m in others:
        field_got(stage_s, ser, se_s, se_r, k, m).wait_recv()

    def conv(q, _):
        for tt in range(tm_n):
            now = ser[tt, rows_of(q), :]
            if tt == 0:
                pre = mm(now, wc[ch:2 * ch, :]) + bias
            else:
                pre = mm(jnp.concatenate([ser[tt - 1, rows_of(q), :], now], axis=1), wc[...]) + bias
            a = jnp.tanh(pre[:, 0:ch])
            s = jax.nn.sigmoid(pre[:, ch:2 * ch])
            act_f[tt, rows_of(q), :] = a
            act_g[tt, rows_of(q), :] = s
            src0[q, 0:nodes, tt * ch:(tt + 1) * ch] = (a * s).astype(BF)
        return 0

    def send_slots(src):
        def one(q, _):
            got = mm(pick[q], src[q, 0:nodes, :]).astype(BF)
            for j in range(3):
                reader = lax.rem(q - STEPS[j] + seg_n, seg_n)
                src[reader, nodes + j * 128:nodes + (j + 1) * 128, :] = got[j * 128:(j + 1) * 128]
            return 0
        lax.fori_loop(0, seg_n, one, 0)

    def hop(src, dst):
        def one(q, _):
            dst[q, 0:nodes, :] = mm(opf[q], src[q]).astype(BF)
            return 0
        lax.fori_loop(0, seg_n, one, 0)

    def home(buf, got, ss, rs, q, tt):
        return rc(buf.at[tt, rows_of(q)], got.at[mine], ss.at[q * tm_n + tt], rs.at[mine], {"seg": q, "tm": tt})

    def arrived(buf, got, ss, rs, f):
        return rc(buf.at[f % tm_n, pl.ds(f // tm_n * nodes, nodes)], got.at[f], ss.at[f], rs.at[f],
                  {"seg": f // tm_n, "tm": f % tm_n})

    def send_home(buf, got, ss, rs, q, tt):
        here = (q == p) & (tt == t)

        @pl.when(jnp.logical_not(here))
        def _():
            home(buf, got, ss, rs, q, tt).start()

    lax.fori_loop(0, seg_n, conv, 0)
    send_slots(src0)
    hop(src0, src1)
    send_slots(src1)
    hop(src1, hop2)
    bias_d = bd[...]

    def put_out(q, _):
        for tt in range(tm_n):
            lo, hi = tt * ch, (tt + 1) * ch
            two = jnp.concatenate([src0[q, 0:nodes, lo:hi], src1[q, 0:nodes, lo:hi]], axis=1)
            total = mm(two, jnp.concatenate([wd[0], wd[1]], axis=0)) + mm(hop2[q, :, lo:hi], wd[2]) + bias_d
            out_b[tt, rows_of(q), :] = (ser[tt, rows_of(q), :].astype(F32) + total).astype(BF)
            send_home(out_b, out_r, ou_s, ou_r, q, tt)
        return 0

    lax.fori_loop(0, seg_n, put_out, 0)

    for k, m in others:
        field_got(stage_c, cot, co_s, co_r, k, m).wait_recv()

    def back(q, _):
        for tt in range(tm_n):
            lo, hi = tt * ch, (tt + 1) * ch
            g = cot[tt, rows_of(q), :]
            u = mm(g, jnp.concatenate([wdt[2], wdt[1]], axis=1))
            sb0[q, 0:nodes, lo:hi] = u[:, 0:ch].astype(BF)
            acc[q, :, lo:hi] = u[:, ch:2 * ch]
        return 0

    def send_back(sb):
        def one(q, _):
            got = mm(oph[q], sb[q, 0:nodes, :]).astype(BF)
            for j in range(3):
                owner = lax.rem(q + STEPS[j] + seg_n, seg_n)
                sb[owner, nodes + j * 128:nodes + (j + 1) * 128, :] = got[j * 128:(j + 1) * 128]
            return 0
        lax.fori_loop(0, seg_n, one, 0)

    lax.fori_loop(0, seg_n, back, 0)
    send_back(sb0)

    def back_mid(q, _):
        sb1[q, 0:nodes, :] = (acc[q] + mm(opb[q], sb0[q])).astype(BF)
        return 0

    lax.fori_loop(0, seg_n, back_mid, 0)
    send_back(sb1)

    def back_last(q, _):
        gh_all = mm(opb[q], sb1[q])
        later = None
        for tt in reversed(range(tm_n)):
            lo, hi = tt * ch, (tt + 1) * ch
            g = cot[tt, rows_of(q), :]
            gh = gh_all[:, lo:hi] + mm(g, wdt[0])
            a, s = act_f[tt, rows_of(q), :], act_g[tt, rows_of(q), :]
            gf = (gh * s * (1.0 - a * a)).astype(BF)
            gg = (gh * a * (s * (1.0 - s))).astype(BF)
            both = jnp.concatenate([gf, gg], axis=1)
            now = ser[tt, rows_of(q), :]
            if tt == 0:
                total = mm(both, wct[:, ch:2 * ch])
                part = mm_tn(now, both)
                red[ch:2 * ch, :] += part[:, 0:ch]
                red[3 * ch:4 * ch, :] += part[:, ch:2 * ch]
            else:
                r = mm(both, wct[...])
                total = r[:, ch:2 * ch]
                part = mm_tn(jnp.concatenate([ser[tt - 1, rows_of(q), :], now], axis=1), both)
                red[0:2 * ch, :] += part[:, 0:ch]
                red[2 * ch:4 * ch, :] += part[:, ch:2 * ch]
            total = g.astype(F32) + total
            if later is not None:
                total = total + later.astype(F32)
            if tt > 0:
                later = r[:, 0:ch].astype(BF)
            gs_b[tt, rows_of(q), :] = total.astype(BF)
            send_home(gs_b, gs_r, gr_s, gr_r, q, tt)
            hops = jnp.concatenate(
                [src0[q, 0:nodes, lo:hi], src1[q, 0:nodes, lo:hi], hop2[q, :, lo:hi]], axis=1)
            red[4 * ch:7 * ch, :] += mm_tn(hops, g)
            base = 7 * ch
            red[base:base + 1, :] += jnp.sum(gf.astype(F32), axis=0, keepdims=True)
            red[base + 1:base + 2, :] += jnp.sum(gg.astype(F32), axis=0, keepdims=True)
            red[base + 2:base + 3, :] += jnp.sum(g.astype(F32), axis=0, keepdims=True)
        return 0

    lax.fori_loop(0, seg_n, back_last, 0)

    total_rows = red.shape[0]
    half = total_rows // 2
    fourth = half // tm_n
    small = fourth // seg_n

    def span(start, size):
        return pl.ds(pl.multiple_of(start, 8), size)

    def go(src, dst, at, dev):
        made = rc(src, dst, ar_s.at[at], ar_r.at[at], dev)
        made.start()
        return made

    one = go(red.at[span((1 - rep) * half, half)], rbuf0, 0, core)
    out_b_own = out_b[t, rows_of(p), :]
    out_r[mine] = out_b_own
    gs_r[mine] = gs_b[t, rows_of(p), :]
    one.wait()
    red[span(rep * half, half), :] += rbuf0[...]
    two = go(red.at[span(rep * half + (1 - t) * fourth, fourth)], rbuf1, 1, across)

    def node_major(got, wide, dest, buf, ss, rs):
        for f in range(frames):
            @pl.when(f != mine)
            def _():
                arrived(buf, got, ss, rs, f).wait_recv()

            wide[:, f, :] = got[f].astype(F32)
        dest[...] = wide[...].astype(BF)

    two.wait()
    at4 = rep * half + t * fourth
    red[span(at4, fourth), :] += rbuf1[...]
    zs = [go(red.at[span(at4 + seg_at(k) * small, small)], rz.at[k], 2 + k, {"seg": seg_at(k)})
          for k in range(1, seg_n)]
    node_major(out_r, big, out3, out_b, ou_s, ou_r)
    for one in zs:
        one.wait()
    total = red[span(at4 + p * small, small), :]
    for k in range(1, seg_n):
        total = total + rz[k]
    fin[span(at4 + p * small, small), :] = total * scale
    here = fin.at[span(at4 + p * small, small)]
    zs = [go(here, here, 2 + seg_n + k, {"seg": seg_at(k)}) for k in range(1, seg_n)]
    for one in zs:
        one.wait()
    here = fin.at[span(at4, fourth)]
    go(here, here, 2 + 2 * seg_n, across).wait()
    here = fin.at[span(rep * half, half)]
    go(here, here, 3 + 2 * seg_n, core).wait()
    node_major(gs_r, big_g, gs3, gs_b, gr_s, gr_r)

    for k in range(1, seg_n):
        tile_z(p, k, {"seg": seg_at(k)}).wait_send()
        meta_z(p, k, {"seg": seg_at(k)}).wait_send()
        q = seg_at(k)
        tile_x(q, c_me).wait_send()
        tile_c(q, c_me, 0).wait_send()
        tile_c(q, c_across, 1).wait_send()
    for k, m in others:
        q, tt = peer(k, m)
        field_in(stage_c, cot, co_s, co_r, k, m).wait_send()
        home(out_b, out_r, ou_s, ou_r, q, tt).wait_send()
        home(gs_b, gs_r, gr_s, gr_r, q, tt).wait_send()


def finish_kernel(out_i, gs_i, fin, out_o, gs_o, o_wf, o_wg, o_bf, o_bg, o_wd, o_bd, sems):
    one = pltpu.make_async_copy(out_i, out_o, sems.at[0])
    two = pltpu.make_async_copy(gs_i, gs_o, sems.at[1])
    one.start()
    two.start()
    ch = o_wf.shape[1]
    for i in range(2):
        o_wf[i] = fin[i * ch:(i + 1) * ch, :]
        o_wg[i] = fin[(2 + i) * ch:(3 + i) * ch, :]
    for i in range(3):
        o_wd[i] = fin[(4 + i) * ch:(5 + i) * ch, :]
    o_bf[...] = fin[7 * ch:7 * ch + 1, :]
    o_bg[...] = fin[7 * ch + 1:7 * ch + 2, :]
    o_bd[...] = fin[7 * ch + 2:7 * ch + 3, :]
    one.wait()
    two.wait()


def gather_plan(mesh, series, cotangent, w_filter, w_gate, b_filter, b_gate, w_diff, b_diff,
                tile_row, tile_col, tile_val, send_nodes, send_count):
    nodes, batch, frames, ch = series.shape
    seg_n, tm_n, rep_n = mesh.shape["seg"], mesh.shape["tm"], mesh.shape["rep"]
    scale = 1.0 / math.sqrt(nodes * batch * frames * seg_n * tm_n * rep_n)
    unit = 8 * 2 * tm_n * seg_n
    total_rows = -(-(7 * ch + 8) // unit) * unit
    vmem = pl.BlockSpec(memory_space=pltpu.VMEM)
    anyw = pl.BlockSpec(memory_space=pl.ANY)
    raw = (nodes, batch * frames, ch)
    tall = (frames, nodes, ch)
    everyone = (tm_n, seg_n * nodes, ch)
    wide = tm_n * ch
    tile_rows = tile_val.shape[1] * 128
    halo = 3 * 128
    dma = pltpu.SemaphoreType.DMA
    half = total_rows // 2
    fourth = half // tm_n
    small = fourth // seg_n
    out, gs, fin = pl.pallas_call(
        functools.partial(gather_kernel, seg_n, tm_n, scale),
        out_shape=(
            jax.ShapeDtypeStruct(raw, BF),
            jax.ShapeDtypeStruct(raw, BF),
            jax.ShapeDtypeStruct((total_rows, ch), F32),
        ),
        in_specs=[vmem] * 13,
        out_specs=(vmem,) * 3,
        scratch_shapes=[
            pltpu.VMEM(raw, F32),
            pltpu.VMEM(raw, F32),
            pltpu.VMEM(tall, BF),
            pltpu.VMEM(tall, BF),
            pltpu.VMEM(everyone, BF),
            pltpu.VMEM(everyone, BF),
            pltpu.VMEM((seg_n, tile_rows, 128), BF),
            pltpu.VMEM((seg_n, 8, 128), jnp.int32),
            pltpu.VMEM((seg_n, nodes, nodes + halo), BF),
            pltpu.VMEM((seg_n, nodes, nodes + halo), BF),
            pltpu.VMEM((seg_n, halo, nodes), BF),
            pltpu.VMEM((seg_n, halo, nodes), BF),
            pltpu.VMEM((2 * ch, 2 * ch), BF),
            pltpu.VMEM((2 * ch, 2 * ch), BF),
            pltpu.VMEM((3, ch, ch), BF),
            pltpu.VMEM(everyone, F32),
            pltpu.VMEM(everyone, F32),
            pltpu.VMEM((seg_n, nodes + halo, wide), BF),
            pltpu.VMEM((seg_n, nodes + halo, wide), BF),
            pltpu.VMEM((seg_n, nodes, wide), BF),
            pltpu.VMEM((seg_n, nodes + halo, wide), BF),
            pltpu.VMEM((seg_n, nodes + halo, wide), BF),
            pltpu.VMEM((seg_n, nodes, wide), F32),
            pltpu.VMEM(everyone, BF),
            pltpu.VMEM(everyone, BF),
            pltpu.VMEM(tall, BF),
            pltpu.VMEM(tall, BF),
            pltpu.VMEM((total_rows, ch), F32),
            pltpu.VMEM((half, ch), F32),
            pltpu.VMEM((fourth, ch), F32),
            pltpu.VMEM((seg_n, small, ch), F32),
            dma((seg_n,)), dma((seg_n,)), dma((seg_n,)), dma((seg_n,)),
            dma((seg_n,)), dma((seg_n,)), dma((seg_n, 2)), dma((seg_n, 2)),
            dma((frames,)), dma((frames,)), dma((frames,)), dma((frames,)),
            dma((frames,)), dma((frames,)), dma((frames,)), dma((frames,)),
            dma((4 + 2 * seg_n,)), dma((4 + 2 * seg_n,)),
        ],
        compiler_params=pltpu.CompilerParams(
            collective_id=0, has_side_effects=True, vmem_limit_bytes=56 << 20),
    )(
        series.reshape(raw), cotangent.reshape(raw), w_filter, w_gate,
        b_filter.reshape(1, -1), b_gate.reshape(1, -1), w_diff, b_diff.reshape(1, -1),
        tile_row, tile_col, tile_val.reshape(tile_rows, 128), send_nodes[0], send_count,
    )
    vec = jax.ShapeDtypeStruct((1, ch), F32)
    out, gs, g_wf, g_wg, g_bf, g_bg, g_wd, g_bd = pl.pallas_call(
        finish_kernel,
        out_shape=(
            jax.ShapeDtypeStruct(raw, BF),
            jax.ShapeDtypeStruct(raw, BF),
            jax.ShapeDtypeStruct((2, ch, ch), F32),
            jax.ShapeDtypeStruct((2, ch, ch), F32),
            vec, vec,
            jax.ShapeDtypeStruct((3, ch, ch), F32),
            vec,
        ),
        in_specs=[anyw, anyw, vmem],
        out_specs=(anyw, anyw, vmem, vmem, vmem, vmem, vmem, vmem),
        scratch_shapes=[dma((2,))],
    )(out, gs, fin)
    return (
        out.reshape(series.shape), gs.reshape(series.shape), g_wf, g_wg,
        g_bf.reshape(-1), g_bg.reshape(-1), g_wd, g_bd.reshape(-1))


def on_device(mesh, series, *rest):
    nodes, batch, frames, ch = series.shape
    seg_n, tm_n = mesh.shape["seg"], mesh.shape["tm"]
    fits = tm_n == 2 and batch == 1 and frames == seg_n * tm_n and frames == DILATION_FRAMES
    plan = gather_plan if fits else halo_plan
    return plan(mesh, series, *rest)


def solution(mesh):
    field = P(("grp", "seg"), "rep", "tm", None)
    part = ("grp", "seg")
    in_specs = (
        field, field, P(), P(), P(), P(), P(), P(),
        P(part, None), P(part, None), P(part, None, None, None), P(part, None, None), P(part, None),
    )
    out_specs = (
        field, field, P("grp", None, None), P("grp", None, None), P("grp"), P("grp"),
        P("grp", None, None), P("grp"),
    )
    return jax.shard_map(
        functools.partial(on_device, mesh), mesh=mesh, in_specs=in_specs, out_specs=out_specs,
        check_vma=False)
```

```python
import functools
import math

import jax
import jax.numpy as jnp
from jax import lax
from jax.experimental import pallas as pl
from jax.experimental.pallas import tpu as pltpu
from jax.sharding import PartitionSpec as P

DILATION_FRAMES = 8
STEPS = (1, -1, 2)
MESH = pl.DeviceIdType.MESH
WIDE = 256
BF = jnp.bfloat16
F32 = jnp.float32


def mm(a, b):
    return lax.dot_general(a, b, (((1,), (0,)), ((), ())), preferred_element_type=F32)


def mm_nt(a, b):
    return lax.dot_general(a, b, (((1,), (1,)), ((), ())), preferred_element_type=F32)


def mm_tn(a, b):
    return lax.dot_general(a, b, (((0,), (0,)), ((), ())), preferred_element_type=F32)


def halo_kernel(
    seg_n, tm_n, scale,
    ser3, cot3, wf, wg, bf, bg, wd, bd, trow, tcol, tval, snodes, scount,
    out3, gs3, fin1, fin2,
    big, big_g, ser, cot, prev, ops_f, ops_b, pick, give, wblk,
    acc, act_f, act_g, hid, hop1, delayed_out, delayed_in,
    snd, rcv, wacc, dacc, bacc, cacc,
    red1, red2, rb1, rc1, sb1, rb2, rc2, sb2,
    tm_s, tm_r, ex_s, ex_r, dl_s, dl_r, ar_s, ar_r,
):
    p = lax.axis_index("seg")
    t = lax.axis_index("tm")
    rep = lax.axis_index("rep")
    chunks, nodes, _ = ser.shape
    doublings = seg_n.bit_length() - 1
    cap = 128
    ch = 128

    barrier = pltpu.get_barrier_semaphore()
    for k in range(1, seg_n):
        pl.semaphore_signal(barrier, inc=1, device_id={"seg": lax.rem(p + k, seg_n)}, device_id_type=MESH)
    crew = 2 * tm_n
    me = t * 2 + rep

    def crew_device(i):
        return {"tm": lax.div(i, 2), "rep": lax.rem(i, 2)}

    for k in range(1, crew):
        pl.semaphore_signal(barrier, inc=1, device_id=crew_device(lax.rem(me + k, crew)), device_id_type=MESH)
    pl.semaphore_wait(barrier, seg_n - 1 + crew - 1)

    def series_copy(c):
        return pltpu.make_async_remote_copy(
            src_ref=ser.at[c], dst_ref=prev.at[c], send_sem=tm_s.at[c], recv_sem=tm_r.at[c],
            device_id={"tm": lax.rem(t + 1, tm_n)}, device_id_type=MESH)

    def delayed_copy(c):
        return pltpu.make_async_remote_copy(
            src_ref=delayed_out.at[c], dst_ref=delayed_in.at[c], send_sem=dl_s.at[c], recv_sem=dl_r.at[c],
            device_id={"tm": lax.rem(t + tm_n - 1, tm_n)}, device_id_type=MESH)

    def halo_copy(e, c, j):
        step = STEPS[j] if e % 2 == 0 else -STEPS[j]
        return pltpu.make_async_remote_copy(
            src_ref=snd.at[e, c, j], dst_ref=rcv.at[e, c, j],
            send_sem=ex_s.at[e, c, j], recv_sem=ex_r.at[e, c, j],
            device_id={"seg": lax.rem(p + step + seg_n, seg_n)}, device_id_type=MESH)

    def side_by_side(src, dst):
        big[...] = src[...].astype(F32)
        for c in range(chunks):
            dst[c] = jnp.concatenate([big[:, 2 * c, :], big[:, 2 * c + 1, :]], axis=1).astype(BF)

    side_by_side(cot3, cot)

    rows_n, cols_n, tiles_n = nodes // 128, nodes // 128 + 3, tval.shape[0]
    for r in range(rows_n):
        for c in range(cols_n):
            total = jnp.zeros((128, 128), F32)
            for k in range(tiles_n):
                if k < rows_n and (r != k or c != k):
                    continue
                if rows_n <= k < cols_n and c != k:
                    continue
                hit = jnp.where(trow[0, k] == r, 1.0, 0.0) * jnp.where(tcol[0, k] == c, 1.0, 0.0)
                total = total + hit * tval[k].astype(F32)
            ops_f[r * 128:(r + 1) * 128, c * 128:(c + 1) * 128] = total.astype(BF)
            ops_b[c * 128:(c + 1) * 128, r * 128:(r + 1) * 128] = total.T.astype(BF)
    wblk[4:7] = jnp.zeros((3, WIDE, WIDE), BF)
    for i in range(2):
        lo, hi = i * ch, (i + 1) * ch
        for k in range(3):
            wblk[4 + k, lo:hi, lo:hi] = wd[k]

    def put(e, c, rows):
        for j in range(3):
            snd[e, c, j] = rows[j * cap:(j + 1) * cap]
            halo_copy(e, c, j).start()

    def back_one(c, _):
        g = cot[c]
        up = mm_nt(g, wblk[6]).astype(BF)
        put(0, c, mm(ops_b[nodes:, :], up).astype(BF))
        acc[c] = mm(ops_b[:nodes, :], up) + mm_nt(g, wblk[5])
        return 0

    lax.fori_loop(0, chunks, back_one, 0)

    side_by_side(ser3, ser)

    @pl.when(t < tm_n - 1)
    def _():
        for c in range(chunks):
            series_copy(c).start()

    @pl.when(t == 0)
    def _():
        prev[...] = jnp.zeros_like(prev)

    @pl.when(t == tm_n - 1)
    def _():
        delayed_in[...] = jnp.zeros_like(delayed_in)

    wblk[0:4] = jnp.zeros((4, WIDE, WIDE), BF)
    for i in range(2):
        lo, hi = i * ch, (i + 1) * ch
        for k in range(2):
            wblk[k, lo:hi, lo:hi] = wf[k]
            wblk[2 + k, lo:hi, lo:hi] = wg[k]

    node_ids = lax.broadcasted_iota(jnp.int32, (nodes, cap), 0)
    slot_ids = lax.broadcasted_iota(jnp.int32, (nodes, cap), 1)
    for j in range(3):
        here = jnp.where(node_ids == snodes[j:j + 1, :], 1.0, 0.0)
        live = jnp.where(slot_ids < scount[0, j], 1.0, 0.0)
        hot = here * live
        give[:, j * cap:(j + 1) * cap] = hot.astype(BF)
        pick[j * cap:(j + 1) * cap, :] = hot.T.astype(BF)
    wacc[...] = jnp.zeros_like(wacc)
    dacc[...] = jnp.zeros_like(dacc)
    bacc[...] = jnp.zeros_like(bacc)
    cacc[...] = jnp.zeros_like(cacc)
    red1[...] = jnp.zeros_like(red1)
    red2[...] = jnp.zeros_like(red2)
    ones = jnp.ones((8, nodes), BF)

    def arrived(e, c):
        for j in range(3):
            halo_copy(e, c, j).wait_recv()
        return rcv[e, c].reshape(3 * cap, WIDE)

    def back_two(c, _):
        got = arrived(0, c)
        up = (acc[c] + mm(give[...], got)).astype(BF)
        put(2, c, mm(ops_b[nodes:, :], up).astype(BF))
        acc[c] = mm(ops_b[:nodes, :], up) + mm_nt(cot[c], wblk[4])
        return 0

    lax.fori_loop(0, chunks, back_two, 0)

    bf2 = jnp.concatenate([bf[...], bf[...]], axis=1)
    bg2 = jnp.concatenate([bg[...], bg[...]], axis=1)
    bd2 = jnp.concatenate([bd[...], bd[...]], axis=1)

    def fore_one(c, _):
        @pl.when(t > 0)
        def _():
            series_copy(c).wait_recv()

        before, now = prev[c], ser[c]
        a = jnp.tanh(mm(before, wblk[0]) + mm(now, wblk[1]) + bf2)
        act_f[c] = a
        s = jax.nn.sigmoid(mm(before, wblk[2]) + mm(now, wblk[3]) + bg2)
        act_g[c] = s
        h = (a * s).astype(BF)
        hid[c] = h
        put(1, c, mm(pick[...], h).astype(BF))
        return 0

    lax.fori_loop(0, chunks, fore_one, 0)

    def back_three(c, _):
        got = arrived(2, c)
        gh = acc[c] + mm(give[...], got)
        a, s = act_f[c], act_g[c]
        gf = (gh * s * (1.0 - a * a)).astype(BF)
        gg = (gh * a * (s * (1.0 - s))).astype(BF)
        delayed_out[c] = (mm_nt(gf, wblk[0]) + mm_nt(gg, wblk[2])).astype(BF)

        @pl.when(t > 0)
        def _():
            delayed_copy(c).start()

        g = cot[c]
        acc[c] = g.astype(F32) + mm_nt(gf, wblk[1]) + mm_nt(gg, wblk[3])
        before, now, h = prev[c], ser[c], hid[c]
        for i in range(2):
            lo, hi = i * ch, (i + 1) * ch
            right = jnp.concatenate([gf[:, lo:hi], gg[:, lo:hi]], axis=1)
            left = jnp.concatenate([before[:, lo:hi], now[:, lo:hi]], axis=1)
            wacc[...] += mm_tn(left, right)
            dacc[...] += mm_tn(h[:, lo:hi], g[:, lo:hi])
            bacc[...] += mm(ones, right)
            cacc[...] += mm(ones, g[:, lo:hi])
        return 0

    lax.fori_loop(0, chunks, back_three, 0)

    red1[0:256, :] = wacc[:, 0:128]
    red1[256:512, :] = wacc[:, 128:256]
    red1[512:640, :] = dacc[...]
    rid = lax.broadcasted_iota(jnp.int32, (8, 128), 0)
    red1[640:648, :] = jnp.where(
        rid == 0, bacc[:, 0:128], jnp.where(rid == 1, bacc[:, 128:256], cacc[...]))

    def all_sum(base, direct, red, rb, rc, sb, fin):
        part = red.shape[0] // crew

        def copy(src, dst, at, device):
            made = pltpu.make_async_remote_copy(
                src_ref=src, dst_ref=dst, send_sem=ar_s.at[at], recv_sem=ar_r.at[at],
                device_id=device, device_id_type=MESH)
            made.start()
            return made

        def rows(i):
            return pl.ds(pl.multiple_of(i * part, 8), part)

        sends = []
        for k in range(1, crew):
            o = lax.rem(me + k, crew)
            sends.append(copy(red.at[rows(o)], rb.at[k - 1], base + k, crew_device(o)))
        yield
        s = red[rows(me), :]
        for k in range(1, crew):
            sends[k - 1].wait()
            s = s + rb[k - 1]
        at = base + crew
        if direct:
            sb[0] = s
            rc[p] = s
            sends = [
                copy(sb.at[0], rc.at[p], at + k, {"seg": lax.rem(p + k, seg_n)})
                for k in range(1, seg_n)]
            yield
            for one in sends:
                one.wait()
            s = rc[0]
            for k in range(1, seg_n):
                s = s + rc[k]
        else:
            bit = 1
            for k in range(doublings):
                sb[k] = s
                mate = p + (1 - 2 * lax.rem(lax.div(p, bit), 2)) * bit
                one = copy(sb.at[k], rc.at[k], at + k, {"seg": mate})
                yield
                one.wait()
                s = s + rc[k]
                bit *= 2
        fin[rows(me), :] = s * scale
        at = at + seg_n
        sends = [
            copy(fin.at[rows(me)], fin.at[rows(me)], at + k, crew_device(lax.rem(me + k, crew)))
            for k in range(1, crew)]
        yield
        for one in sends:
            one.wait()
        yield

    first = all_sum(0, False, red1, rb1, rc1, sb1, fin1)
    next(first)
    def fore_two(c, _):
        got = arrived(1, c)
        h = (mm(ops_f[:, :nodes], hid[c]) + mm(ops_f[:, nodes:], got)).astype(BF)
        hop1[c] = h
        put(3, c, mm(pick[...], h).astype(BF))
        return 0

    for c in range(chunks):
        fore_two(c, 0)
        if c in (0, 1):
            next(first)

    for c in range(chunks):
        if c >= 2:
            next(first, None)
        got = arrived(3, c)
        h, h1, g = hid[c], hop1[c], cot[c]
        h2 = (mm(ops_f[:, :nodes], h1) + mm(ops_f[:, nodes:], got)).astype(BF)
        total = mm(h, wblk[4]) + mm(h1, wblk[5]) + mm(h2, wblk[6]) + bd2
        total = ser[c].astype(F32) + total
        for i in range(2):
            lo, hi = i * ch, (i + 1) * ch
            both = jnp.concatenate([h1[:, lo:hi], h2[:, lo:hi]], axis=1)
            red2[...] += mm_tn(both, g[:, lo:hi])
            big[:, 2 * c + i, :] = total[:, lo:hi]
    second = all_sum(2 * crew + seg_n, True, red2, rb2, rc2, sb2, fin2)
    next(second)
    out3[...] = big[...].astype(BF)
    next(second)
    for c in range(chunks):
        @pl.when(t < tm_n - 1)
        def _():
            delayed_copy(c).wait_recv()

        total = acc[c] + delayed_in[c].astype(F32)
        for i in range(2):
            big_g[:, 2 * c + i, :] = total[:, i * ch:(i + 1) * ch]
    next(second)
    gs3[...] = big_g[...].astype(BF)
    for _ in first:
        pass
    for _ in second:
        pass

    def drain(c, _):
        @pl.when(t < tm_n - 1)
        def _():
            series_copy(c).wait_send()

        @pl.when(t > 0)
        def _():
            delayed_copy(c).wait_send()

        for e in range(4):
            for j in range(3):
                halo_copy(e, c, j).wait_send()
        return 0

    lax.fori_loop(0, chunks, drain, 0)


def halo_plan(mesh, series, cotangent, w_filter, w_gate, b_filter, b_gate, w_diff, b_diff,
              tile_row, tile_col, tile_val, send_nodes, send_count):
    nodes, batch, frames, channels = series.shape
    seg_n, tm_n, rep_n = mesh.shape["seg"], mesh.shape["tm"], mesh.shape["rep"]
    chunks = batch * frames * channels // WIDE
    scale = 1.0 / math.sqrt(nodes * batch * frames * seg_n * tm_n * rep_n)
    unit = 16 * tm_n
    r1 = -(-648 // unit) * unit
    r2 = -(-256 // unit) * unit

    doublings = seg_n.bit_length() - 1
    vmem = pl.BlockSpec(memory_space=pltpu.VMEM)
    smem = pl.BlockSpec(memory_space=pltpu.SMEM)
    field = (chunks, nodes, WIDE)

    def sums(r):
        crew = 2 * tm_n
        q = r // crew
        return [
            pltpu.VMEM((crew - 1, q, 128), F32),
            pltpu.VMEM((seg_n, q, 128), F32),
            pltpu.VMEM((doublings, q, 128), F32),
        ]

    n_ar = 2 * (4 * tm_n + seg_n)
    raw = (nodes, batch * frames, channels)
    halo = (4, chunks, 3, 128, WIDE)
    out, gs, fin1, fin2 = pl.pallas_call(
        functools.partial(halo_kernel, seg_n, tm_n, scale),
        out_shape=(
            jax.ShapeDtypeStruct(raw, BF),
            jax.ShapeDtypeStruct(raw, BF),
            jax.ShapeDtypeStruct((r1, 128), F32),
            jax.ShapeDtypeStruct((r2, 128), F32),
        ),
        in_specs=[vmem] * 8 + [smem, smem, vmem, vmem, smem],
        out_specs=(vmem,) * 4,
        scratch_shapes=[
            pltpu.VMEM(raw, F32),
            pltpu.VMEM(raw, F32),
            pltpu.VMEM(field, BF),
            pltpu.VMEM(field, BF),
            pltpu.VMEM(field, BF),
            pltpu.VMEM((nodes, nodes + 384), BF),
            pltpu.VMEM((nodes + 384, nodes), BF),
            pltpu.VMEM((384, nodes), BF),
            pltpu.VMEM((nodes, 384), BF),
            pltpu.VMEM((7, WIDE, WIDE), BF),
            pltpu.VMEM(field, F32),
            pltpu.VMEM(field, F32),
            pltpu.VMEM(field, F32),
            pltpu.VMEM(field, BF),
            pltpu.VMEM(field, BF),
            pltpu.VMEM(field, BF),
            pltpu.VMEM(field, BF),
            pltpu.VMEM(halo, BF),
            pltpu.VMEM(halo, BF),
            pltpu.VMEM((256, 256), F32),
            pltpu.VMEM((128, 128), F32),
            pltpu.VMEM((8, 256), F32),
            pltpu.VMEM((8, 128), F32),
            pltpu.VMEM((r1, 128), F32),
            pltpu.VMEM((r2, 128), F32),
            *sums(r1),
            *sums(r2),
            pltpu.SemaphoreType.DMA((chunks,)),
            pltpu.SemaphoreType.DMA((chunks,)),
            pltpu.SemaphoreType.DMA((4, chunks, 3)),
            pltpu.SemaphoreType.DMA((4, chunks, 3)),
            pltpu.SemaphoreType.DMA((chunks,)),
            pltpu.SemaphoreType.DMA((chunks,)),
            pltpu.SemaphoreType.DMA((n_ar,)),
            pltpu.SemaphoreType.DMA((n_ar,)),
        ],
        compiler_params=pltpu.CompilerParams(
            collective_id=0, has_side_effects=True, vmem_limit_bytes=56 << 20),
    )(
        series.reshape(raw), cotangent.reshape(raw), w_filter, w_gate,
        b_filter.reshape(1, -1), b_gate.reshape(1, -1), w_diff, b_diff.reshape(1, -1),
        tile_row, tile_col, tile_val[0], send_nodes[0], send_count,
    )
    return (
        out.reshape(series.shape),
        gs.reshape(series.shape),
        fin1[0:256].reshape(2, 128, 128),
        fin1[256:512].reshape(2, 128, 128),
        fin1[640],
        fin1[641],
        jnp.concatenate([fin1[512:640], fin2[:256]], axis=0).reshape(3, 128, 128),
        fin1[642],
    )


def gather_kernel(
    seg_n, tm_n, scale,
    ser3, cot3, wf, wg, bf, bg, wd, bd, trow, tcol, tval, snodes, scount,
    out3, gs3, fin,
    big, big_g, stage_s, stage_c, ser, cot, tiles, meta,
    opf, opb, oph, pick, wc, wct, wdt,
    act_f, act_g, src0, src1, hop2, sb0, sb1, acc,
    out_b, gs_b, out_r, gs_r,
    red, rbuf0, rbuf1, rz,
    tz_s, tz_r, mz_s, mz_r, tx_s, tx_r, tc_s, tc_r,
    se_s, se_r, co_s, co_r, ou_s, ou_r, gr_s, gr_r, ar_s, ar_r,
):
    p = lax.axis_index("seg")
    t = lax.axis_index("tm")
    rep = lax.axis_index("rep")
    nodes, frames, ch = ser3.shape
    mine = p * tm_n + t
    crew = 2 * tm_n
    quarter = tiles.shape[1] // crew

    def rc(src, dst, ss, rs, dev):
        return pltpu.make_async_remote_copy(
            src_ref=src, dst_ref=dst, send_sem=ss, recv_sem=rs, device_id=dev, device_id_type=MESH)

    def seg_at(k):
        return lax.rem(p + k, seg_n)

    others = [(k, m) for k in range(seg_n) for m in range(tm_n) if (k, m) != (0, 0)]
    others.sort(key=lambda o: (abs(o[0] - seg_n // 2), o[1]))

    def peer(k, m):
        return seg_at(k), lax.rem(t + m, tm_n)

    def rows_of(q):
        return pl.ds(pl.multiple_of(q * nodes, 128), nodes)

    def piece(c):
        return pl.ds(pl.multiple_of(c * quarter, 16), quarter)

    core = {"rep": 1 - rep}
    across = {"tm": 1 - t}

    barrier = pltpu.get_barrier_semaphore()
    for k, m in others:
        q, tt = peer(k, m)
        pl.semaphore_signal(barrier, inc=1, device_id={"seg": q, "tm": tt}, device_id_type=MESH)
    pl.semaphore_signal(barrier, inc=1, device_id=core, device_id_type=MESH)

    def frame_major(source, wide, stage, whole):
        wide[...] = source[...].astype(F32)
        for f in range(frames):
            stage[f] = wide[:, f, :].astype(BF)
        whole[t, rows_of(p), :] = stage[mine]

    tiles[p] = tval[...]
    meta[p] = jnp.zeros_like(meta[p])
    meta[p, 0:3, :] = snodes[...]
    meta[p, 3:4, 0:trow.shape[1]] = trow[...]
    meta[p, 4:5, 0:tcol.shape[1]] = tcol[...]
    meta[p, 5:6, 0:scount.shape[1]] = scount[...]
    frame_major(ser3, big, stage_s, ser)
    pl.semaphore_wait(barrier, len(others) + 1)

    c_me = t * 2 + rep

    def tile_z(at, k_sem, dev):
        return rc(tiles.at[at, piece(c_me)], tiles.at[at, piece(c_me)], tz_s.at[k_sem], tz_r.at[at], dev)

    def meta_z(at, k_sem, dev):
        return rc(meta.at[at], meta.at[at], mz_s.at[k_sem], mz_r.at[at], dev)

    def field_in(stage, whole, ss, rs, k, m):
        q, tt = peer(k, m)
        f = q * tm_n + tt
        return rc(stage.at[f], whole.at[t, rows_of(p)], ss.at[f], rs.at[mine], {"seg": q, "tm": tt})

    def field_got(stage, whole, ss, rs, k, m):
        q, tt = peer(k, m)
        f = q * tm_n + tt
        return rc(stage.at[f], whole.at[tt, rows_of(q)], ss.at[f], rs.at[f], {"seg": q, "tm": tt})

    far_first = sorted(range(1, seg_n), key=lambda k: abs(k - seg_n // 2))
    for k in far_first:
        meta_z(p, k, {"seg": seg_at(k)}).start()
        tile_z(p, k, {"seg": seg_at(k)}).start()
    for k, m in others:
        field_in(stage_s, ser, se_s, se_r, k, m).start()

    frame_major(cot3, big_g, stage_c, cot)

    for i in range(2):
        wc[i * ch:(i + 1) * ch, 0:ch] = wf[i]
        wc[i * ch:(i + 1) * ch, ch:2 * ch] = wg[i]
    wct[...] = wc[...].astype(F32).T.astype(BF)
    for i in range(3):
        wdt[i] = wd[i].astype(F32).T.astype(BF)
    bias = jnp.concatenate([bf[...], bg[...]], axis=1)
    red[...] = jnp.zeros_like(red)

    def tile_x(q, c):
        return rc(tiles.at[q, piece(c)], tiles.at[q, piece(c)], tx_s.at[q], tx_r.at[q], across)

    def tile_c(q, c, i):
        return rc(tiles.at[q, piece(c)], tiles.at[q, piece(c)], tc_s.at[q, i], tc_r.at[q, i], core)

    c_across = (1 - t) * 2 + rep
    for k in far_first:
        tile_z(seg_at(k), 0, {"seg": seg_at(k)}).wait_recv()
        tile_x(seg_at(k), c_me).start()
    for k in far_first:
        tile_x(seg_at(k), c_across).wait_recv()
        tile_c(seg_at(k), c_me, 0).start()
        tile_c(seg_at(k), c_across, 1).start()
    for k in far_first:
        tile_c(seg_at(k), t * 2 + (1 - rep), 0).wait_recv()
        tile_c(seg_at(k), (1 - t) * 2 + (1 - rep), 1).wait_recv()
        meta_z(seg_at(k), 0, {"seg": seg_at(k)}).wait_recv()

    rows_n = nodes // 128
    cols_n = rows_n + 3
    tiles_n = tiles.shape[1] // 128
    halo = 3 * 128
    lane_ids = lax.broadcasted_iota(jnp.int32, (128, nodes), 1)
    sub_ids = lax.broadcasted_iota(jnp.int32, (nodes, 128), 0)
    slot_lane = lax.broadcasted_iota(jnp.int32, (1, 128), 1)
    slot_sub = lax.broadcasted_iota(jnp.int32, (128, 1), 0)

    def build(q, _):
        info = meta[q]
        tr, tc = info[3:4, :], info[4:5, :]
        t_all = [tiles[q, k * 128:(k + 1) * 128, :].astype(F32) for k in range(tiles_n)]
        for r in range(rows_n):
            for c in range(cols_n):
                hits = jnp.where((tr == r) & (tc == c), 1.0, 0.0)
                total = jnp.zeros((128, 128), F32)
                for k in range(tiles_n):
                    if k < rows_n and (r != k or c != k):
                        continue
                    if rows_n <= k < cols_n and c != k:
                        continue
                    total = total + hits[:, k:k + 1] * t_all[k]
                flipped = total.T.astype(BF)
                opf[q, r * 128:(r + 1) * 128, c * 128:(c + 1) * 128] = total.astype(BF)
                if c < rows_n:
                    opb[q, c * 128:(c + 1) * 128, r * 128:(r + 1) * 128] = flipped
                else:
                    oph[q, (c - rows_n) * 128:(c - rows_n + 1) * 128, r * 128:(r + 1) * 128] = flipped
        col = info.astype(F32).T.astype(jnp.int32)
        for j in range(3):
            count = info[5:6, j:j + 1]
            give = jnp.where((sub_ids == info[j:j + 1, :]) & (slot_lane < count), 1.0, 0.0)
            opb[q, :, nodes + j * 128:nodes + (j + 1) * 128] = give.astype(BF)
            take = jnp.where((lane_ids == col[:, j:j + 1]) & (slot_sub < count), 1.0, 0.0)
            pick[q, j * 128:(j + 1) * 128, :] = take.astype(BF)
        return 0

    lax.fori_loop(0, seg_n, build, 0)

    for k, m in others:
        field_in(stage_s, ser, se_s, se_r, k, m).wait_send()
        field_in(stage_c, cot, co_s, co_r, k, m).start()

    for k, m in others:
        field_got(stage_s, ser, se_s, se_r, k, m).wait_recv()

    def conv(q, _):
        for tt in range(tm_n):
            now = ser[tt, rows_of(q), :]
            if tt == 0:
                pre = mm(now, wc[ch:2 * ch, :]) + bias
            else:
                pre = mm(jnp.concatenate([ser[tt - 1, rows_of(q), :], now], axis=1), wc[...]) + bias
            a = jnp.tanh(pre[:, 0:ch])
            s = jax.nn.sigmoid(pre[:, ch:2 * ch])
            act_f[tt, rows_of(q), :] = a
            act_g[tt, rows_of(q), :] = s
            src0[q, 0:nodes, tt * ch:(tt + 1) * ch] = (a * s).astype(BF)
        return 0

    def send_slots(src):
        def one(q, _):
            got = mm(pick[q], src[q, 0:nodes, :]).astype(BF)
            for j in range(3):
                reader = lax.rem(q - STEPS[j] + seg_n, seg_n)
                src[reader, nodes + j * 128:nodes + (j + 1) * 128, :] = got[j * 128:(j + 1) * 128]
            return 0
        lax.fori_loop(0, seg_n, one, 0)

    def hop(src, dst):
        def one(q, _):
            dst[q, 0:nodes, :] = mm(opf[q], src[q]).astype(BF)
            return 0
        lax.fori_loop(0, seg_n, one, 0)

    def home(buf, got, ss, rs, q, tt):
        return rc(buf.at[tt, rows_of(q)], got.at[mine], ss.at[q * tm_n + tt], rs.at[mine], {"seg": q, "tm": tt})

    def arrived(buf, got, ss, rs, f):
        return rc(buf.at[f % tm_n, pl.ds(f // tm_n * nodes, nodes)], got.at[f], ss.at[f], rs.at[f],
                  {"seg": f // tm_n, "tm": f % tm_n})

    def send_home(buf, got, ss, rs, q, tt):
        here = (q == p) & (tt == t)

        @pl.when(jnp.logical_not(here))
        def _():
            home(buf, got, ss, rs, q, tt).start()

    lax.fori_loop(0, seg_n, conv, 0)
    send_slots(src0)
    hop(src0, src1)
    send_slots(src1)
    hop(src1, hop2)
    bias_d = bd[...]

    def put_out(q, _):
        for tt in range(tm_n):
            lo, hi = tt * ch, (tt + 1) * ch
            two = jnp.concatenate([src0[q, 0:nodes, lo:hi], src1[q, 0:nodes, lo:hi]], axis=1)
            total = mm(two, jnp.concatenate([wd[0], wd[1]], axis=0)) + mm(hop2[q, :, lo:hi], wd[2]) + bias_d
            out_b[tt, rows_of(q), :] = (ser[tt, rows_of(q), :].astype(F32) + total).astype(BF)
            send_home(out_b, out_r, ou_s, ou_r, q, tt)
        return 0

    lax.fori_loop(0, seg_n, put_out, 0)

    for k, m in others:
        field_got(stage_c, cot, co_s, co_r, k, m).wait_recv()

    def back(q, _):
        for tt in range(tm_n):
            lo, hi = tt * ch, (tt + 1) * ch
            g = cot[tt, rows_of(q), :]
            u = mm(g, jnp.concatenate([wdt[2], wdt[1]], axis=1))
            sb0[q, 0:nodes, lo:hi] = u[:, 0:ch].astype(BF)
            acc[q, :, lo:hi] = u[:, ch:2 * ch]
        return 0

    def send_back(sb):
        def one(q, _):
            got = mm(oph[q], sb[q, 0:nodes, :]).astype(BF)
            for j in range(3):
                owner = lax.rem(q + STEPS[j] + seg_n, seg_n)
                sb[owner, nodes + j * 128:nodes + (j + 1) * 128, :] = got[j * 128:(j + 1) * 128]
            return 0
        lax.fori_loop(0, seg_n, one, 0)

    lax.fori_loop(0, seg_n, back, 0)
    send_back(sb0)

    def back_mid(q, _):
        sb1[q, 0:nodes, :] = (acc[q] + mm(opb[q], sb0[q])).astype(BF)
        return 0

    lax.fori_loop(0, seg_n, back_mid, 0)
    send_back(sb1)

    def back_last(q, _):
        gh_all = mm(opb[q], sb1[q])
        later = None
        for tt in reversed(range(tm_n)):
            lo, hi = tt * ch, (tt + 1) * ch
            g = cot[tt, rows_of(q), :]
            gh = gh_all[:, lo:hi] + mm(g, wdt[0])
            a, s = act_f[tt, rows_of(q), :], act_g[tt, rows_of(q), :]
            gf = (gh * s * (1.0 - a * a)).astype(BF)
            gg = (gh * a * (s * (1.0 - s))).astype(BF)
            both = jnp.concatenate([gf, gg], axis=1)
            now = ser[tt, rows_of(q), :]
            if tt == 0:
                total = mm(both, wct[:, ch:2 * ch])
                part = mm_tn(now, both)
                red[ch:2 * ch, :] += part[:, 0:ch]
                red[3 * ch:4 * ch, :] += part[:, ch:2 * ch]
            else:
                r = mm(both, wct[...])
                total = r[:, ch:2 * ch]
                part = mm_tn(jnp.concatenate([ser[tt - 1, rows_of(q), :], now], axis=1), both)
                red[0:2 * ch, :] += part[:, 0:ch]
                red[2 * ch:4 * ch, :] += part[:, ch:2 * ch]
            total = g.astype(F32) + total
            if later is not None:
                total = total + later.astype(F32)
            if tt > 0:
                later = r[:, 0:ch].astype(BF)
            gs_b[tt, rows_of(q), :] = total.astype(BF)
            send_home(gs_b, gs_r, gr_s, gr_r, q, tt)
            hops = jnp.concatenate(
                [src0[q, 0:nodes, lo:hi], src1[q, 0:nodes, lo:hi], hop2[q, :, lo:hi]], axis=1)
            red[4 * ch:7 * ch, :] += mm_tn(hops, g)
            base = 7 * ch
            red[base:base + 1, :] += jnp.sum(gf.astype(F32), axis=0, keepdims=True)
            red[base + 1:base + 2, :] += jnp.sum(gg.astype(F32), axis=0, keepdims=True)
            red[base + 2:base + 3, :] += jnp.sum(g.astype(F32), axis=0, keepdims=True)
        return 0

    lax.fori_loop(0, seg_n, back_last, 0)

    total_rows = red.shape[0]
    half = total_rows // 2
    fourth = half // tm_n
    small = fourth // seg_n

    def span(start, size):
        return pl.ds(pl.multiple_of(start, 8), size)

    def go(src, dst, at, dev):
        made = rc(src, dst, ar_s.at[at], ar_r.at[at], dev)
        made.start()
        return made

    one = go(red.at[span((1 - rep) * half, half)], rbuf0, 0, core)
    out_b_own = out_b[t, rows_of(p), :]
    out_r[mine] = out_b_own
    gs_r[mine] = gs_b[t, rows_of(p), :]
    one.wait()
    red[span(rep * half, half), :] += rbuf0[...]
    two = go(red.at[span(rep * half + (1 - t) * fourth, fourth)], rbuf1, 1, across)

    def node_major(got, wide, dest, buf, ss, rs):
        for f in range(frames):
            @pl.when(f != mine)
            def _():
                arrived(buf, got, ss, rs, f).wait_recv()

            wide[:, f, :] = got[f].astype(F32)
        dest[...] = wide[...].astype(BF)

    two.wait()
    at4 = rep * half + t * fourth
    red[span(at4, fourth), :] += rbuf1[...]
    zs = [go(red.at[span(at4 + seg_at(k) * small, small)], rz.at[k], 2 + k, {"seg": seg_at(k)})
          for k in range(1, seg_n)]
    node_major(out_r, big, out3, out_b, ou_s, ou_r)
    for one in zs:
        one.wait()
    total = red[span(at4 + p * small, small), :]
    for k in range(1, seg_n):
        total = total + rz[k]
    fin[span(at4 + p * small, small), :] = total * scale
    here = fin.at[span(at4 + p * small, small)]
    zs = [go(here, here, 2 + seg_n + k, {"seg": seg_at(k)}) for k in range(1, seg_n)]
    for one in zs:
        one.wait()
    here = fin.at[span(at4, fourth)]
    go(here, here, 2 + 2 * seg_n, across).wait()
    here = fin.at[span(rep * half, half)]
    go(here, here, 3 + 2 * seg_n, core).wait()
    node_major(gs_r, big_g, gs3, gs_b, gr_s, gr_r)

    for k in range(1, seg_n):
        tile_z(p, k, {"seg": seg_at(k)}).wait_send()
        meta_z(p, k, {"seg": seg_at(k)}).wait_send()
        q = seg_at(k)
        tile_x(q, c_me).wait_send()
        tile_c(q, c_me, 0).wait_send()
        tile_c(q, c_across, 1).wait_send()
    for k, m in others:
        q, tt = peer(k, m)
        field_in(stage_c, cot, co_s, co_r, k, m).wait_send()
        home(out_b, out_r, ou_s, ou_r, q, tt).wait_send()
        home(gs_b, gs_r, gr_s, gr_r, q, tt).wait_send()


def finish_kernel(out_i, gs_i, fin, out_o, gs_o, o_wf, o_wg, o_bf, o_bg, o_wd, o_bd, sems):
    one = pltpu.make_async_copy(out_i, out_o, sems.at[0])
    two = pltpu.make_async_copy(gs_i, gs_o, sems.at[1])
    one.start()
    two.start()
    ch = o_wf.shape[1]
    for i in range(2):
        o_wf[i] = fin[i * ch:(i + 1) * ch, :]
        o_wg[i] = fin[(2 + i) * ch:(3 + i) * ch, :]
    for i in range(3):
        o_wd[i] = fin[(4 + i) * ch:(5 + i) * ch, :]
    o_bf[...] = fin[7 * ch:7 * ch + 1, :]
    o_bg[...] = fin[7 * ch + 1:7 * ch + 2, :]
    o_bd[...] = fin[7 * ch + 2:7 * ch + 3, :]
    one.wait()
    two.wait()


def gather_plan(mesh, series, cotangent, w_filter, w_gate, b_filter, b_gate, w_diff, b_diff,
                tile_row, tile_col, tile_val, send_nodes, send_count):
    nodes, batch, frames, ch = series.shape
    seg_n, tm_n, rep_n = mesh.shape["seg"], mesh.shape["tm"], mesh.shape["rep"]
    scale = 1.0 / math.sqrt(nodes * batch * frames * seg_n * tm_n * rep_n)
    unit = 8 * 2 * tm_n * seg_n
    total_rows = -(-(7 * ch + 8) // unit) * unit
    vmem = pl.BlockSpec(memory_space=pltpu.VMEM)
    anyw = pl.BlockSpec(memory_space=pl.ANY)
    raw = (nodes, batch * frames, ch)
    tall = (frames, nodes, ch)
    everyone = (tm_n, seg_n * nodes, ch)
    wide = tm_n * ch
    tile_rows = tile_val.shape[1] * 128
    halo = 3 * 128
    dma = pltpu.SemaphoreType.DMA
    half = total_rows // 2
    fourth = half // tm_n
    small = fourth // seg_n
    out, gs, fin = pl.pallas_call(
        functools.partial(gather_kernel, seg_n, tm_n, scale),
        out_shape=(
            jax.ShapeDtypeStruct(raw, BF),
            jax.ShapeDtypeStruct(raw, BF),
            jax.ShapeDtypeStruct((total_rows, ch), F32),
        ),
        in_specs=[vmem] * 13,
        out_specs=(vmem,) * 3,
        scratch_shapes=[
            pltpu.VMEM(raw, F32),
            pltpu.VMEM(raw, F32),
            pltpu.VMEM(tall, BF),
            pltpu.VMEM(tall, BF),
            pltpu.VMEM(everyone, BF),
            pltpu.VMEM(everyone, BF),
            pltpu.VMEM((seg_n, tile_rows, 128), BF),
            pltpu.VMEM((seg_n, 8, 128), jnp.int32),
            pltpu.VMEM((seg_n, nodes, nodes + halo), BF),
            pltpu.VMEM((seg_n, nodes, nodes + halo), BF),
            pltpu.VMEM((seg_n, halo, nodes), BF),
            pltpu.VMEM((seg_n, halo, nodes), BF),
            pltpu.VMEM((2 * ch, 2 * ch), BF),
            pltpu.VMEM((2 * ch, 2 * ch), BF),
            pltpu.VMEM((3, ch, ch), BF),
            pltpu.VMEM(everyone, F32),
            pltpu.VMEM(everyone, F32),
            pltpu.VMEM((seg_n, nodes + halo, wide), BF),
            pltpu.VMEM((seg_n, nodes + halo, wide), BF),
            pltpu.VMEM((seg_n, nodes, wide), BF),
            pltpu.VMEM((seg_n, nodes + halo, wide), BF),
            pltpu.VMEM((seg_n, nodes + halo, wide), BF),
            pltpu.VMEM((seg_n, nodes, wide), F32),
            pltpu.VMEM(everyone, BF),
            pltpu.VMEM(everyone, BF),
            pltpu.VMEM(tall, BF),
            pltpu.VMEM(tall, BF),
            pltpu.VMEM((total_rows, ch), F32),
            pltpu.VMEM((half, ch), F32),
            pltpu.VMEM((fourth, ch), F32),
            pltpu.VMEM((seg_n, small, ch), F32),
            dma((seg_n,)), dma((seg_n,)), dma((seg_n,)), dma((seg_n,)),
            dma((seg_n,)), dma((seg_n,)), dma((seg_n, 2)), dma((seg_n, 2)),
            dma((frames,)), dma((frames,)), dma((frames,)), dma((frames,)),
            dma((frames,)), dma((frames,)), dma((frames,)), dma((frames,)),
            dma((4 + 2 * seg_n,)), dma((4 + 2 * seg_n,)),
        ],
        compiler_params=pltpu.CompilerParams(
            collective_id=0, has_side_effects=True, vmem_limit_bytes=56 << 20),
    )(
        series.reshape(raw), cotangent.reshape(raw), w_filter, w_gate,
        b_filter.reshape(1, -1), b_gate.reshape(1, -1), w_diff, b_diff.reshape(1, -1),
        tile_row, tile_col, tile_val.reshape(tile_rows, 128), send_nodes[0], send_count,
    )
    vec = jax.ShapeDtypeStruct((1, ch), F32)
    out, gs, g_wf, g_wg, g_bf, g_bg, g_wd, g_bd = pl.pallas_call(
        finish_kernel,
        out_shape=(
            jax.ShapeDtypeStruct(raw, BF),
            jax.ShapeDtypeStruct(raw, BF),
            jax.ShapeDtypeStruct((2, ch, ch), F32),
            jax.ShapeDtypeStruct((2, ch, ch), F32),
            vec, vec,
            jax.ShapeDtypeStruct((3, ch, ch), F32),
            vec,
        ),
        in_specs=[anyw, anyw, vmem],
        out_specs=(vmem,) * 8,
        scratch_shapes=[dma((2,))],
    )(out, gs, fin)
    return (
        out.reshape(series.shape), gs.reshape(series.shape), g_wf, g_wg,
        g_bf.reshape(-1), g_bg.reshape(-1), g_wd, g_bd.reshape(-1))


def on_device(mesh, series, *rest):
    nodes, batch, frames, ch = series.shape
    seg_n, tm_n = mesh.shape["seg"], mesh.shape["tm"]
    fits = tm_n == 2 and batch == 1 and frames == seg_n * tm_n and frames == DILATION_FRAMES
    plan = gather_plan if fits else halo_plan
    return plan(mesh, series, *rest)


def solution(mesh):
    field = P(("grp", "seg"), "rep", "tm", None)
    part = ("grp", "seg")
    in_specs = (
        field, field, P(), P(), P(), P(), P(), P(),
        P(part, None), P(part, None), P(part, None, None, None), P(part, None, None), P(part, None),
    )
    out_specs = (
        field, field, P("grp", None, None), P("grp", None, None), P("grp"), P("grp"),
        P("grp", None, None), P("grp"),
    )
    return jax.shard_map(
        functools.partial(on_device, mesh), mesh=mesh, in_specs=in_specs, out_specs=out_specs,
        check_vma=False)
```

```python
import functools
import math

import jax
import jax.numpy as jnp
from jax import lax
from jax.experimental import pallas as pl
from jax.experimental.pallas import tpu as pltpu
from jax.sharding import PartitionSpec as P

DILATION_FRAMES = 8
STEPS = (1, -1, 2)
MESH = pl.DeviceIdType.MESH
WIDE = 256
BF = jnp.bfloat16
F32 = jnp.float32


def mm(a, b):
    return lax.dot_general(a, b, (((1,), (0,)), ((), ())), preferred_element_type=F32)


def mm_nt(a, b):
    return lax.dot_general(a, b, (((1,), (1,)), ((), ())), preferred_element_type=F32)


def mm_tn(a, b):
    return lax.dot_general(a, b, (((0,), (0,)), ((), ())), preferred_element_type=F32)


def halo_kernel(
    seg_n, tm_n, scale,
    ser3, cot3, wf, wg, bf, bg, wd, bd, trow, tcol, tval, snodes, scount,
    out3, gs3, fin1, fin2,
    big, big_g, ser, cot, prev, ops_f, ops_b, pick, give, wblk,
    acc, act_f, act_g, hid, hop1, delayed_out, delayed_in,
    snd, rcv, wacc, dacc, bacc, cacc,
    red1, red2, rb1, rc1, sb1, rb2, rc2, sb2,
    tm_s, tm_r, ex_s, ex_r, dl_s, dl_r, ar_s, ar_r,
):
    p = lax.axis_index("seg")
    t = lax.axis_index("tm")
    rep = lax.axis_index("rep")
    chunks, nodes, _ = ser.shape
    doublings = seg_n.bit_length() - 1
    cap = 128
    ch = 128

    barrier = pltpu.get_barrier_semaphore()
    for k in range(1, seg_n):
        pl.semaphore_signal(barrier, inc=1, device_id={"seg": lax.rem(p + k, seg_n)}, device_id_type=MESH)
    crew = 2 * tm_n
    me = t * 2 + rep

    def crew_device(i):
        return {"tm": lax.div(i, 2), "rep": lax.rem(i, 2)}

    for k in range(1, crew):
        pl.semaphore_signal(barrier, inc=1, device_id=crew_device(lax.rem(me + k, crew)), device_id_type=MESH)
    pl.semaphore_wait(barrier, seg_n - 1 + crew - 1)

    def series_copy(c):
        return pltpu.make_async_remote_copy(
            src_ref=ser.at[c], dst_ref=prev.at[c], send_sem=tm_s.at[c], recv_sem=tm_r.at[c],
            device_id={"tm": lax.rem(t + 1, tm_n)}, device_id_type=MESH)

    def delayed_copy(c):
        return pltpu.make_async_remote_copy(
            src_ref=delayed_out.at[c], dst_ref=delayed_in.at[c], send_sem=dl_s.at[c], recv_sem=dl_r.at[c],
            device_id={"tm": lax.rem(t + tm_n - 1, tm_n)}, device_id_type=MESH)

    def halo_copy(e, c, j):
        step = STEPS[j] if e % 2 == 0 else -STEPS[j]
        return pltpu.make_async_remote_copy(
            src_ref=snd.at[e, c, j], dst_ref=rcv.at[e, c, j],
            send_sem=ex_s.at[e, c, j], recv_sem=ex_r.at[e, c, j],
            device_id={"seg": lax.rem(p + step + seg_n, seg_n)}, device_id_type=MESH)

    def side_by_side(src, dst):
        big[...] = src[...].astype(F32)
        for c in range(chunks):
            dst[c] = jnp.concatenate([big[:, 2 * c, :], big[:, 2 * c + 1, :]], axis=1).astype(BF)

    side_by_side(cot3, cot)

    rows_n, cols_n, tiles_n = nodes // 128, nodes // 128 + 3, tval.shape[0]
    for r in range(rows_n):
        for c in range(cols_n):
            total = jnp.zeros((128, 128), F32)
            for k in range(tiles_n):
                if k < rows_n and (r != k or c != k):
                    continue
                if rows_n <= k < cols_n and c != k:
                    continue
                hit = jnp.where(trow[0, k] == r, 1.0, 0.0) * jnp.where(tcol[0, k] == c, 1.0, 0.0)
                total = total + hit * tval[k].astype(F32)
            ops_f[r * 128:(r + 1) * 128, c * 128:(c + 1) * 128] = total.astype(BF)
            ops_b[c * 128:(c + 1) * 128, r * 128:(r + 1) * 128] = total.T.astype(BF)
    wblk[4:7] = jnp.zeros((3, WIDE, WIDE), BF)
    for i in range(2):
        lo, hi = i * ch, (i + 1) * ch
        for k in range(3):
            wblk[4 + k, lo:hi, lo:hi] = wd[k]

    def put(e, c, rows):
        for j in range(3):
            snd[e, c, j] = rows[j * cap:(j + 1) * cap]
            halo_copy(e, c, j).start()

    def back_one(c, _):
        g = cot[c]
        up = mm_nt(g, wblk[6]).astype(BF)
        put(0, c, mm(ops_b[nodes:, :], up).astype(BF))
        acc[c] = mm(ops_b[:nodes, :], up) + mm_nt(g, wblk[5])
        return 0

    lax.fori_loop(0, chunks, back_one, 0)

    side_by_side(ser3, ser)

    @pl.when(t < tm_n - 1)
    def _():
        for c in range(chunks):
            series_copy(c).start()

    @pl.when(t == 0)
    def _():
        prev[...] = jnp.zeros_like(prev)

    @pl.when(t == tm_n - 1)
    def _():
        delayed_in[...] = jnp.zeros_like(delayed_in)

    wblk[0:4] = jnp.zeros((4, WIDE, WIDE), BF)
    for i in range(2):
        lo, hi = i * ch, (i + 1) * ch
        for k in range(2):
            wblk[k, lo:hi, lo:hi] = wf[k]
            wblk[2 + k, lo:hi, lo:hi] = wg[k]

    node_ids = lax.broadcasted_iota(jnp.int32, (nodes, cap), 0)
    slot_ids = lax.broadcasted_iota(jnp.int32, (nodes, cap), 1)
    for j in range(3):
        here = jnp.where(node_ids == snodes[j:j + 1, :], 1.0, 0.0)
        live = jnp.where(slot_ids < scount[0, j], 1.0, 0.0)
        hot = here * live
        give[:, j * cap:(j + 1) * cap] = hot.astype(BF)
        pick[j * cap:(j + 1) * cap, :] = hot.T.astype(BF)
    wacc[...] = jnp.zeros_like(wacc)
    dacc[...] = jnp.zeros_like(dacc)
    bacc[...] = jnp.zeros_like(bacc)
    cacc[...] = jnp.zeros_like(cacc)
    red1[...] = jnp.zeros_like(red1)
    red2[...] = jnp.zeros_like(red2)
    ones = jnp.ones((8, nodes), BF)

    def arrived(e, c):
        for j in range(3):
            halo_copy(e, c, j).wait_recv()
        return rcv[e, c].reshape(3 * cap, WIDE)

    def back_two(c, _):
        got = arrived(0, c)
        up = (acc[c] + mm(give[...], got)).astype(BF)
        put(2, c, mm(ops_b[nodes:, :], up).astype(BF))
        acc[c] = mm(ops_b[:nodes, :], up) + mm_nt(cot[c], wblk[4])
        return 0

    lax.fori_loop(0, chunks, back_two, 0)

    bf2 = jnp.concatenate([bf[...], bf[...]], axis=1)
    bg2 = jnp.concatenate([bg[...], bg[...]], axis=1)
    bd2 = jnp.concatenate([bd[...], bd[...]], axis=1)

    def fore_one(c, _):
        @pl.when(t > 0)
        def _():
            series_copy(c).wait_recv()

        before, now = prev[c], ser[c]
        a = jnp.tanh(mm(before, wblk[0]) + mm(now, wblk[1]) + bf2)
        act_f[c] = a
        s = jax.nn.sigmoid(mm(before, wblk[2]) + mm(now, wblk[3]) + bg2)
        act_g[c] = s
        h = (a * s).astype(BF)
        hid[c] = h
        put(1, c, mm(pick[...], h).astype(BF))
        return 0

    lax.fori_loop(0, chunks, fore_one, 0)

    def back_three(c, _):
        got = arrived(2, c)
        gh = acc[c] + mm(give[...], got)
        a, s = act_f[c], act_g[c]
        gf = (gh * s * (1.0 - a * a)).astype(BF)
        gg = (gh * a * (s * (1.0 - s))).astype(BF)
        delayed_out[c] = (mm_nt(gf, wblk[0]) + mm_nt(gg, wblk[2])).astype(BF)

        @pl.when(t > 0)
        def _():
            delayed_copy(c).start()

        g = cot[c]
        acc[c] = g.astype(F32) + mm_nt(gf, wblk[1]) + mm_nt(gg, wblk[3])
        before, now, h = prev[c], ser[c], hid[c]
        for i in range(2):
            lo, hi = i * ch, (i + 1) * ch
            right = jnp.concatenate([gf[:, lo:hi], gg[:, lo:hi]], axis=1)
            left = jnp.concatenate([before[:, lo:hi], now[:, lo:hi]], axis=1)
            wacc[...] += mm_tn(left, right)
            dacc[...] += mm_tn(h[:, lo:hi], g[:, lo:hi])
            bacc[...] += mm(ones, right)
            cacc[...] += mm(ones, g[:, lo:hi])
        return 0

    lax.fori_loop(0, chunks, back_three, 0)

    red1[0:256, :] = wacc[:, 0:128]
    red1[256:512, :] = wacc[:, 128:256]
    red1[512:640, :] = dacc[...]
    rid = lax.broadcasted_iota(jnp.int32, (8, 128), 0)
    red1[640:648, :] = jnp.where(
        rid == 0, bacc[:, 0:128], jnp.where(rid == 1, bacc[:, 128:256], cacc[...]))

    def all_sum(base, direct, red, rb, rc, sb, fin):
        part = red.shape[0] // crew

        def copy(src, dst, at, device):
            made = pltpu.make_async_remote_copy(
                src_ref=src, dst_ref=dst, send_sem=ar_s.at[at], recv_sem=ar_r.at[at],
                device_id=device, device_id_type=MESH)
            made.start()
            return made

        def rows(i):
            return pl.ds(pl.multiple_of(i * part, 8), part)

        sends = []
        for k in range(1, crew):
            o = lax.rem(me + k, crew)
            sends.append(copy(red.at[rows(o)], rb.at[k - 1], base + k, crew_device(o)))
        yield
        s = red[rows(me), :]
        for k in range(1, crew):
            sends[k - 1].wait()
            s = s + rb[k - 1]
        at = base + crew
        if direct:
            sb[0] = s
            rc[p] = s
            sends = [
                copy(sb.at[0], rc.at[p], at + k, {"seg": lax.rem(p + k, seg_n)})
                for k in range(1, seg_n)]
            yield
            for one in sends:
                one.wait()
            s = rc[0]
            for k in range(1, seg_n):
                s = s + rc[k]
        else:
            bit = 1
            for k in range(doublings):
                sb[k] = s
                mate = p + (1 - 2 * lax.rem(lax.div(p, bit), 2)) * bit
                one = copy(sb.at[k], rc.at[k], at + k, {"seg": mate})
                yield
                one.wait()
                s = s + rc[k]
                bit *= 2
        fin[rows(me), :] = s * scale
        at = at + seg_n
        sends = [
            copy(fin.at[rows(me)], fin.at[rows(me)], at + k, crew_device(lax.rem(me + k, crew)))
            for k in range(1, crew)]
        yield
        for one in sends:
            one.wait()
        yield

    first = all_sum(0, False, red1, rb1, rc1, sb1, fin1)
    next(first)
    def fore_two(c, _):
        got = arrived(1, c)
        h = (mm(ops_f[:, :nodes], hid[c]) + mm(ops_f[:, nodes:], got)).astype(BF)
        hop1[c] = h
        put(3, c, mm(pick[...], h).astype(BF))
        return 0

    for c in range(chunks):
        fore_two(c, 0)
        if c in (0, 1):
            next(first)

    for c in range(chunks):
        if c >= 2:
            next(first, None)
        got = arrived(3, c)
        h, h1, g = hid[c], hop1[c], cot[c]
        h2 = (mm(ops_f[:, :nodes], h1) + mm(ops_f[:, nodes:], got)).astype(BF)
        total = mm(h, wblk[4]) + mm(h1, wblk[5]) + mm(h2, wblk[6]) + bd2
        total = ser[c].astype(F32) + total
        for i in range(2):
            lo, hi = i * ch, (i + 1) * ch
            both = jnp.concatenate([h1[:, lo:hi], h2[:, lo:hi]], axis=1)
            red2[...] += mm_tn(both, g[:, lo:hi])
            big[:, 2 * c + i, :] = total[:, lo:hi]
    second = all_sum(2 * crew + seg_n, True, red2, rb2, rc2, sb2, fin2)
    next(second)
    out3[...] = big[...].astype(BF)
    next(second)
    for c in range(chunks):
        @pl.when(t < tm_n - 1)
        def _():
            delayed_copy(c).wait_recv()

        total = acc[c] + delayed_in[c].astype(F32)
        for i in range(2):
            big_g[:, 2 * c + i, :] = total[:, i * ch:(i + 1) * ch]
    next(second)
    gs3[...] = big_g[...].astype(BF)
    for _ in first:
        pass
    for _ in second:
        pass

    def drain(c, _):
        @pl.when(t < tm_n - 1)
        def _():
            series_copy(c).wait_send()

        @pl.when(t > 0)
        def _():
            delayed_copy(c).wait_send()

        for e in range(4):
            for j in range(3):
                halo_copy(e, c, j).wait_send()
        return 0

    lax.fori_loop(0, chunks, drain, 0)


def halo_plan(mesh, series, cotangent, w_filter, w_gate, b_filter, b_gate, w_diff, b_diff,
              tile_row, tile_col, tile_val, send_nodes, send_count):
    nodes, batch, frames, channels = series.shape
    seg_n, tm_n, rep_n = mesh.shape["seg"], mesh.shape["tm"], mesh.shape["rep"]
    chunks = batch * frames * channels // WIDE
    scale = 1.0 / math.sqrt(nodes * batch * frames * seg_n * tm_n * rep_n)
    unit = 16 * tm_n
    r1 = -(-648 // unit) * unit
    r2 = -(-256 // unit) * unit

    doublings = seg_n.bit_length() - 1
    vmem = pl.BlockSpec(memory_space=pltpu.VMEM)
    smem = pl.BlockSpec(memory_space=pltpu.SMEM)
    field = (chunks, nodes, WIDE)

    def sums(r):
        crew = 2 * tm_n
        q = r // crew
        return [
            pltpu.VMEM((crew - 1, q, 128), F32),
            pltpu.VMEM((seg_n, q, 128), F32),
            pltpu.VMEM((doublings, q, 128), F32),
        ]

    n_ar = 2 * (4 * tm_n + seg_n)
    raw = (nodes, batch * frames, channels)
    halo = (4, chunks, 3, 128, WIDE)
    out, gs, fin1, fin2 = pl.pallas_call(
        functools.partial(halo_kernel, seg_n, tm_n, scale),
        out_shape=(
            jax.ShapeDtypeStruct(raw, BF),
            jax.ShapeDtypeStruct(raw, BF),
            jax.ShapeDtypeStruct((r1, 128), F32),
            jax.ShapeDtypeStruct((r2, 128), F32),
        ),
        in_specs=[vmem] * 8 + [smem, smem, vmem, vmem, smem],
        out_specs=(vmem,) * 4,
        scratch_shapes=[
            pltpu.VMEM(raw, F32),
            pltpu.VMEM(raw, F32),
            pltpu.VMEM(field, BF),
            pltpu.VMEM(field, BF),
            pltpu.VMEM(field, BF),
            pltpu.VMEM((nodes, nodes + 384), BF),
            pltpu.VMEM((nodes + 384, nodes), BF),
            pltpu.VMEM((384, nodes), BF),
            pltpu.VMEM((nodes, 384), BF),
            pltpu.VMEM((7, WIDE, WIDE), BF),
            pltpu.VMEM(field, F32),
            pltpu.VMEM(field, F32),
            pltpu.VMEM(field, F32),
            pltpu.VMEM(field, BF),
            pltpu.VMEM(field, BF),
            pltpu.VMEM(field, BF),
            pltpu.VMEM(field, BF),
            pltpu.VMEM(halo, BF),
            pltpu.VMEM(halo, BF),
            pltpu.VMEM((256, 256), F32),
            pltpu.VMEM((128, 128), F32),
            pltpu.VMEM((8, 256), F32),
            pltpu.VMEM((8, 128), F32),
            pltpu.VMEM((r1, 128), F32),
            pltpu.VMEM((r2, 128), F32),
            *sums(r1),
            *sums(r2),
            pltpu.SemaphoreType.DMA((chunks,)),
            pltpu.SemaphoreType.DMA((chunks,)),
            pltpu.SemaphoreType.DMA((4, chunks, 3)),
            pltpu.SemaphoreType.DMA((4, chunks, 3)),
            pltpu.SemaphoreType.DMA((chunks,)),
            pltpu.SemaphoreType.DMA((chunks,)),
            pltpu.SemaphoreType.DMA((n_ar,)),
            pltpu.SemaphoreType.DMA((n_ar,)),
        ],
        compiler_params=pltpu.CompilerParams(
            collective_id=0, has_side_effects=True, vmem_limit_bytes=56 << 20),
    )(
        series.reshape(raw), cotangent.reshape(raw), w_filter, w_gate,
        b_filter.reshape(1, -1), b_gate.reshape(1, -1), w_diff, b_diff.reshape(1, -1),
        tile_row, tile_col, tile_val[0], send_nodes[0], send_count,
    )
    return (
        out.reshape(series.shape),
        gs.reshape(series.shape),
        fin1[0:256].reshape(2, 128, 128),
        fin1[256:512].reshape(2, 128, 128),
        fin1[640],
        fin1[641],
        jnp.concatenate([fin1[512:640], fin2[:256]], axis=0).reshape(3, 128, 128),
        fin1[642],
    )


def gather_kernel(
    seg_n, tm_n, scale,
    ser3, cot3, wf, wg, bf, bg, wd, bd, trow, tcol, tval, snodes, scount,
    out3, gs3, fin,
    big, big_g, stage_s, stage_c, ser, cot, tiles, meta,
    opf, opb, oph, pick, wc, wct, wdt,
    act_f, act_g, src0, src1, hop2, sb0, sb1, acc,
    out_b, gs_b, out_r, gs_r, pair,
    red, rbuf0, rbuf1, rbuf2, rbuf3,
    tz_s, tz_r, mz_s, mz_r, tx_s, tx_r, tc_s, tc_r,
    se_s, se_r, co_s, co_r, ou_s, ou_r, gr_s, gr_r, ar_s, ar_r,
):
    p = lax.axis_index("seg")
    t = lax.axis_index("tm")
    rep = lax.axis_index("rep")
    nodes, frames, ch = ser3.shape
    mine = p * tm_n + t
    crew = 2 * tm_n
    quarter = tiles.shape[1] // crew

    def rc(src, dst, ss, rs, dev):
        return pltpu.make_async_remote_copy(
            src_ref=src, dst_ref=dst, send_sem=ss, recv_sem=rs, device_id=dev, device_id_type=MESH)

    low, high = lax.rem(p, 2), lax.div(p, 2)

    def flip(j):
        return lax.rem(high + j // 2, 2) * 2 + lax.rem(low + j % 2, 2)

    def peer(j, m):
        return flip(j), lax.rem(t + m, tm_n)

    others = [(2, 0), (3, 0), (2, 1), (3, 1), (1, 0), (1, 1), (0, 1)]

    def rows_of(q):
        return pl.ds(pl.multiple_of(q * nodes, 128), nodes)

    def piece(c):
        return pl.ds(pl.multiple_of(c * quarter, 16), quarter)

    core = {"rep": 1 - rep}
    across = {"tm": 1 - t}

    barrier = pltpu.get_barrier_semaphore()
    for j, m in others:
        q, tt = peer(j, m)
        pl.semaphore_signal(barrier, inc=1, device_id={"seg": q, "tm": tt}, device_id_type=MESH)
    pl.semaphore_signal(barrier, inc=1, device_id=core, device_id_type=MESH)

    meta[p] = jnp.zeros_like(meta[p])
    for j in range(3):
        meta[p, j:j + 1, :] = snodes[j]
    meta[p, 3:4, 0:trow.shape[1]] = trow[...]
    meta[p, 4:5, 0:tcol.shape[1]] = tcol[...]
    meta[p, 5:6, 0:scount.shape[1]] = scount[...]
    pl.semaphore_wait(barrier, len(others) + 1)

    c_me = t * 2 + rep
    c_across = (1 - t) * 2 + rep

    def tile_z(j):
        return rc(tval.at[piece(c_me)], tiles.at[p, piece(c_me)], tz_s.at[j], tz_r.at[j], {"seg": flip(j)})

    def tile_on():
        at = tiles.at[flip(2), piece(c_me)]
        return rc(at, at, tz_s.at[3], tz_r.at[3], {"seg": flip(1)})

    def meta_z(j):
        return rc(meta.at[p], meta.at[p], mz_s.at[j], mz_r.at[j], {"seg": flip(j)})

    def tile_x(j):
        at = tiles.at[flip(j), piece(c_me)]
        return rc(at, at, tx_s.at[j], tx_r.at[j], across)

    def tile_c(j, c, i):
        at = tiles.at[flip(j), piece(c)]
        return rc(at, at, tc_s.at[j, i], tc_r.at[j, i], core)

    def field_in(stage, whole, ss, rs, j, m):
        q, tt = peer(j, m)
        f = q * tm_n + tt
        return rc(stage.at[f], whole.at[t, rows_of(p)], ss.at[f], rs.at[mine], {"seg": q, "tm": tt})

    def field_got(stage, whole, ss, rs, j, m):
        q, tt = peer(j, m)
        f = q * tm_n + tt
        return rc(stage.at[f], whole.at[tt, rows_of(q)], ss.at[f], rs.at[f], {"seg": q, "tm": tt})

    def frame_major(source, wide, stage, whole):
        wide[...] = source[...].astype(F32)
        for f in range(frames):
            stage[f] = wide[:, f, :].astype(BF)
        whole[t, rows_of(p), :] = stage[mine]

    tile_z(2).start()
    tile_z(1).start()
    for j in (2, 3, 1):
        meta_z(j).start()
    frame_major(ser3, big, stage_s, ser)
    field_in(stage_s, ser, se_s, se_r, 2, 0).start()
    tiles[p] = tval[...]

    tile_z(2).wait_recv()
    tile_on().start()
    tile_x(2).start()
    tile_z(1).wait_recv()
    tile_x(1).start()
    field_in(stage_s, ser, se_s, se_r, 3, 0).start()
    tile_on().wait_recv()
    tile_x(3).start()
    for j, m in others[2:]:
        field_in(stage_s, ser, se_s, se_r, j, m).start()

    frame_major(cot3, big_g, stage_c, cot)
    for j, m in others:
        field_in(stage_c, cot, co_s, co_r, j, m).start()

    for j in (2, 1, 3):
        tile_x(j).wait_recv()
        tile_c(j, c_me, 0).start()
        tile_c(j, c_across, 1).start()

    for i in range(2):
        wc[i * ch:(i + 1) * ch, 0:ch] = wf[i]
        wc[i * ch:(i + 1) * ch, ch:2 * ch] = wg[i]
    wct[...] = wc[...].astype(F32).T.astype(BF)
    for i in range(3):
        wdt[i] = wd[i].astype(F32).T.astype(BF)
    bias = jnp.concatenate([bf[...], bg[...]], axis=1)
    red[...] = jnp.zeros_like(red)

    for j in (2, 1, 3):
        tile_c(j, c_me, 0).wait_recv()
        tile_c(j, c_across, 1).wait_recv()
        meta_z(j).wait_recv()

    rows_n = nodes // 128
    cols_n = rows_n + 3
    tiles_n = tiles.shape[1] // 128
    halo = 3 * 128
    lane_ids = lax.broadcasted_iota(jnp.int32, (128, nodes), 1)
    sub_ids = lax.broadcasted_iota(jnp.int32, (nodes, 128), 0)
    slot_lane = lax.broadcasted_iota(jnp.int32, (1, 128), 1)
    slot_sub = lax.broadcasted_iota(jnp.int32, (128, 1), 0)

    def build(q, _):
        info = meta[q]
        tr, tc = info[3:4, :], info[4:5, :]
        t_all = [tiles[q, k * 128:(k + 1) * 128, :].astype(F32) for k in range(tiles_n)]
        for r in range(rows_n):
            for c in range(cols_n):
                hits = jnp.where((tr == r) & (tc == c), 1.0, 0.0)
                total = jnp.zeros((128, 128), F32)
                for k in range(tiles_n):
                    if k < rows_n and (r != k or c != k):
                        continue
                    if rows_n <= k < cols_n and c != k:
                        continue
                    total = total + hits[:, k:k + 1] * t_all[k]
                flipped = total.T.astype(BF)
                opf[q, r * 128:(r + 1) * 128, c * 128:(c + 1) * 128] = total.astype(BF)
                if c < rows_n:
                    opb[q, c * 128:(c + 1) * 128, r * 128:(r + 1) * 128] = flipped
                else:
                    oph[q, (c - rows_n) * 128:(c - rows_n + 1) * 128, r * 128:(r + 1) * 128] = flipped
        col = info.astype(F32).T.astype(jnp.int32)
        for j in range(3):
            count = info[5:6, j:j + 1]
            give = jnp.where((sub_ids == info[j:j + 1, :]) & (slot_lane < count), 1.0, 0.0)
            opb[q, :, nodes + j * 128:nodes + (j + 1) * 128] = give.astype(BF)
            take = jnp.where((lane_ids == col[:, j:j + 1]) & (slot_sub < count), 1.0, 0.0)
            pick[q, j * 128:(j + 1) * 128, :] = take.astype(BF)
        return 0

    lax.fori_loop(0, seg_n, build, 0)

    for j, m in others:
        field_got(stage_s, ser, se_s, se_r, j, m).wait_recv()

    def conv(q, _):
        for tt in range(tm_n):
            now = ser[tt, rows_of(q), :]
            if tt == 0:
                pre = mm(now, wc[ch:2 * ch, :]) + bias
            else:
                pre = mm(jnp.concatenate([ser[tt - 1, rows_of(q), :], now], axis=1), wc[...]) + bias
            a = jnp.tanh(pre[:, 0:ch])
            s = jax.nn.sigmoid(pre[:, ch:2 * ch])
            act_f[tt, rows_of(q), :] = a
            act_g[tt, rows_of(q), :] = s
            src0[q, 0:nodes, tt * ch:(tt + 1) * ch] = (a * s).astype(BF)
        return 0

    def send_slots(src):
        def one(q, _):
            got = mm(pick[q], src[q, 0:nodes, :]).astype(BF)
            for j in range(3):
                reader = lax.rem(q - STEPS[j] + seg_n, seg_n)
                src[reader, nodes + j * 128:nodes + (j + 1) * 128, :] = got[j * 128:(j + 1) * 128]
            return 0
        lax.fori_loop(0, seg_n, one, 0)

    def hop(src, dst):
        def one(q, _):
            dst[q, 0:nodes, :] = mm(opf[q], src[q]).astype(BF)
            return 0
        lax.fori_loop(0, seg_n, one, 0)

    def home(buf, got, ss, rs, q, tt):
        return rc(buf.at[tt, rows_of(q)], got.at[mine], ss.at[q * tm_n + tt], rs.at[mine], {"seg": q, "tm": tt})

    def arrived(buf, got, ss, rs, f):
        return rc(buf.at[f % tm_n, pl.ds(f // tm_n * nodes, nodes)], got.at[f], ss.at[f], rs.at[f],
                  {"seg": f // tm_n, "tm": f % tm_n})

    def send_home(buf, got, ss, rs, q, tt):
        here = (q == p) & (tt == t)

        @pl.when(jnp.logical_not(here))
        def _():
            home(buf, got, ss, rs, q, tt).start()

    lax.fori_loop(0, seg_n, conv, 0)
    send_slots(src0)
    hop(src0, src1)
    send_slots(src1)
    hop(src1, hop2)
    bias_d = bd[...]

    def put_out(i, _):
        j = 2 + i - lax.div(i, 2) * (2 * i - 1)
        q = lax.rem(high + lax.div(j, 2), 2) * 2 + lax.rem(low + lax.rem(j, 2), 2)
        for tt in range(tm_n):
            lo, hi = tt * ch, (tt + 1) * ch
            two = jnp.concatenate([src0[q, 0:nodes, lo:hi], src1[q, 0:nodes, lo:hi]], axis=1)
            total = mm(two, jnp.concatenate([wd[0], wd[1]], axis=0)) + mm(hop2[q, :, lo:hi], wd[2]) + bias_d
            out_b[tt, rows_of(q), :] = (ser[tt, rows_of(q), :].astype(F32) + total).astype(BF)
            send_home(out_b, out_r, ou_s, ou_r, q, tt)
        return 0

    lax.fori_loop(0, seg_n, put_out, 0)

    for j, m in others:
        field_got(stage_c, cot, co_s, co_r, j, m).wait_recv()

    def back(q, _):
        for tt in range(tm_n):
            lo, hi = tt * ch, (tt + 1) * ch
            g = cot[tt, rows_of(q), :]
            u = mm(g, jnp.concatenate([wdt[2], wdt[1]], axis=1))
            sb0[q, 0:nodes, lo:hi] = u[:, 0:ch].astype(BF)
            acc[q, :, lo:hi] = u[:, ch:2 * ch]
        return 0

    def send_back(sb):
        def one(q, _):
            got = mm(oph[q], sb[q, 0:nodes, :]).astype(BF)
            for j in range(3):
                owner = lax.rem(q + STEPS[j] + seg_n, seg_n)
                sb[owner, nodes + j * 128:nodes + (j + 1) * 128, :] = got[j * 128:(j + 1) * 128]
            return 0
        lax.fori_loop(0, seg_n, one, 0)

    lax.fori_loop(0, seg_n, back, 0)
    send_back(sb0)

    def back_mid(q, _):
        sb1[q, 0:nodes, :] = (acc[q] + mm(opb[q], sb0[q])).astype(BF)
        return 0

    lax.fori_loop(0, seg_n, back_mid, 0)
    send_back(sb1)

    def back_last(q, _):
        gh_all = mm(opb[q], sb1[q])
        for tt in range(tm_n):
            lo, hi = tt * ch, (tt + 1) * ch
            g = cot[tt, rows_of(q), :]
            gh = gh_all[:, lo:hi] + mm(g, wdt[0])
            a, s = act_f[tt, rows_of(q), :], act_g[tt, rows_of(q), :]
            gf = (gh * s * (1.0 - a * a)).astype(BF)
            gg = (gh * a * (s * (1.0 - s))).astype(BF)
            both = jnp.concatenate([gf, gg], axis=1)
            pair[tt, rows_of(q), :] = both
            now = ser[tt, rows_of(q), :]
            if tt == 0:
                part = mm_tn(now, both)
                red[ch:2 * ch, :] += part[:, 0:ch]
                red[3 * ch:4 * ch, :] += part[:, ch:2 * ch]
            else:
                part = mm_tn(jnp.concatenate([ser[tt - 1, rows_of(q), :], now], axis=1), both)
                red[0:2 * ch, :] += part[:, 0:ch]
                red[2 * ch:4 * ch, :] += part[:, ch:2 * ch]
            hops = jnp.concatenate(
                [src0[q, 0:nodes, lo:hi], src1[q, 0:nodes, lo:hi], hop2[q, :, lo:hi]], axis=1)
            red[4 * ch:7 * ch, :] += mm_tn(hops, g)
            base = 7 * ch
            red[base:base + 1, :] += jnp.sum(gf.astype(F32), axis=0, keepdims=True)
            red[base + 1:base + 2, :] += jnp.sum(gg.astype(F32), axis=0, keepdims=True)
            red[base + 2:base + 3, :] += jnp.sum(g.astype(F32), axis=0, keepdims=True)
        return 0

    lax.fori_loop(0, seg_n, back_last, 0)

    half = red.shape[0] // 2
    fourth, eighth, last = half // 2, half // 4, half // 8

    def span(start, size):
        return pl.ds(pl.multiple_of(start, 8), size)

    def go(src, dst, at, dev):
        made = rc(src, dst, ar_s.at[at], ar_r.at[at], dev)
        made.start()
        return made

    def gs_go(j, m):
        q, tt = peer(j, m)
        home(gs_b, gs_r, gr_s, gr_r, q, tt).start()

    at_core = rep * half
    at_x = at_core + t * fourth
    at_one = at_x + low * eighth
    at_two = at_one + high * last
    step = go(red.at[span((1 - rep) * half, half)], rbuf0, 0, core)

    def put_gs(q, _):
        later = None
        for tt in reversed(range(tm_n)):
            both = pair[tt, rows_of(q), :]
            if tt == 0:
                total = mm(both, wct[:, ch:2 * ch])
            else:
                r = mm(both, wct[...])
                total = r[:, ch:2 * ch]
            total = cot[tt, rows_of(q), :].astype(F32) + total
            if later is not None:
                total = total + later.astype(F32)
            if tt > 0:
                later = r[:, 0:ch].astype(BF)
            gs_b[tt, rows_of(q), :] = total.astype(BF)
        return 0

    lax.fori_loop(0, seg_n, put_gs, 0)
    step.wait()
    red[span(at_core, half), :] += rbuf0[...]
    step = go(red.at[span(at_core + (1 - t) * fourth, fourth)], rbuf1, 1, across)
    gs_go(0, 1)
    out_r[mine] = out_b[t, rows_of(p), :]
    gs_r[mine] = gs_b[t, rows_of(p), :]

    def node_major(got, wide, dest, buf, ss, rs):
        for f in range(frames):
            @pl.when(f != mine)
            def _():
                arrived(buf, got, ss, rs, f).wait_recv()

            wide[:, f, :] = got[f].astype(F32)
        dest[...] = wide[...].astype(BF)

    step.wait()
    red[span(at_x, fourth), :] += rbuf1[...]
    step = go(red.at[span(at_x + (1 - low) * eighth, eighth)], rbuf2, 2, {"seg": flip(1)})
    gs_go(2, 0)
    step.wait()
    red[span(at_one, eighth), :] += rbuf2[...]
    step = go(red.at[span(at_one + (1 - high) * last, last)], rbuf3, 3, {"seg": flip(2)})
    gs_go(3, 0)
    node_major(out_r, big, out3, out_b, ou_s, ou_r)
    step.wait()
    fin[span(at_two, last), :] = (red[span(at_two, last), :] + rbuf3[...]) * scale
    here = fin.at[span(at_two, last)]
    step = go(here, here, 4, {"seg": flip(2)})
    gs_go(2, 1)
    step.wait()
    here = fin.at[span(at_one, eighth)]
    steps = [
        go(here, here, 5, {"seg": flip(1)}),
        go(here, here, 6, across),
        go(here, here, 7, {"seg": flip(1), "tm": 1 - t})]
    gs_go(3, 1)
    gs_go(1, 0)
    gs_go(1, 1)
    for step in steps:
        step.wait()
    here = fin.at[span(at_core, half)]
    step = go(here, here, 8, core)
    node_major(gs_r, big_g, gs3, gs_b, gr_s, gr_r)
    step.wait()

    tile_z(2).wait_send()
    tile_z(1).wait_send()
    tile_on().wait_send()
    for j in (1, 2, 3):
        meta_z(j).wait_send()
        tile_x(j).wait_send()
        tile_c(j, c_me, 0).wait_send()
        tile_c(j, c_across, 1).wait_send()
    for j, m in others:
        q, tt = peer(j, m)
        field_in(stage_s, ser, se_s, se_r, j, m).wait_send()
        field_in(stage_c, cot, co_s, co_r, j, m).wait_send()
        home(out_b, out_r, ou_s, ou_r, q, tt).wait_send()
        home(gs_b, gs_r, gr_s, gr_r, q, tt).wait_send()


def finish_kernel(out_i, gs_i, fin, out_o, gs_o, o_wf, o_wg, o_bf, o_bg, o_wd, o_bd, sems):
    one = pltpu.make_async_copy(out_i, out_o, sems.at[0])
    two = pltpu.make_async_copy(gs_i, gs_o, sems.at[1])
    one.start()
    two.start()
    ch = o_wf.shape[1]
    for i in range(2):
        o_wf[i] = fin[i * ch:(i + 1) * ch, :]
        o_wg[i] = fin[(2 + i) * ch:(3 + i) * ch, :]
    for i in range(3):
        o_wd[i] = fin[(4 + i) * ch:(5 + i) * ch, :]
    o_bf[...] = fin[7 * ch:7 * ch + 1, :]
    o_bg[...] = fin[7 * ch + 1:7 * ch + 2, :]
    o_bd[...] = fin[7 * ch + 2:7 * ch + 3, :]
    one.wait()
    two.wait()


def gather_plan(mesh, series, cotangent, w_filter, w_gate, b_filter, b_gate, w_diff, b_diff,
                tile_row, tile_col, tile_val, send_nodes, send_count):
    nodes, batch, frames, ch = series.shape
    seg_n, tm_n, rep_n = mesh.shape["seg"], mesh.shape["tm"], mesh.shape["rep"]
    scale = 1.0 / math.sqrt(nodes * batch * frames * seg_n * tm_n * rep_n)
    unit = 8 * 2 * tm_n * seg_n
    total_rows = -(-(7 * ch + 8) // unit) * unit
    vmem = pl.BlockSpec(memory_space=pltpu.VMEM)
    anyw = pl.BlockSpec(memory_space=pl.ANY)
    raw = (nodes, batch * frames, ch)
    tall = (frames, nodes, ch)
    everyone = (tm_n, seg_n * nodes, ch)
    wide = tm_n * ch
    tile_rows = tile_val.shape[1] * 128
    halo = 3 * 128
    dma = pltpu.SemaphoreType.DMA
    half = total_rows // 2
    out, gs, fin = pl.pallas_call(
        functools.partial(gather_kernel, seg_n, tm_n, scale),
        out_shape=(
            jax.ShapeDtypeStruct(raw, BF),
            jax.ShapeDtypeStruct(raw, BF),
            jax.ShapeDtypeStruct((total_rows, ch), F32),
        ),
        in_specs=[vmem] * 13,
        out_specs=(vmem,) * 3,
        scratch_shapes=[
            pltpu.VMEM(raw, F32),
            pltpu.VMEM(raw, F32),
            pltpu.VMEM(tall, BF),
            pltpu.VMEM(tall, BF),
            pltpu.VMEM(everyone, BF),
            pltpu.VMEM(everyone, BF),
            pltpu.VMEM((seg_n, tile_rows, 128), BF),
            pltpu.VMEM((seg_n, 8, 128), jnp.int32),
            pltpu.VMEM((seg_n, nodes, nodes + halo), BF),
            pltpu.VMEM((seg_n, nodes, nodes + halo), BF),
            pltpu.VMEM((seg_n, halo, nodes), BF),
            pltpu.VMEM((seg_n, halo, nodes), BF),
            pltpu.VMEM((2 * ch, 2 * ch), BF),
            pltpu.VMEM((2 * ch, 2 * ch), BF),
            pltpu.VMEM((3, ch, ch), BF),
            pltpu.VMEM(everyone, F32),
            pltpu.VMEM(everyone, F32),
            pltpu.VMEM((seg_n, nodes + halo, wide), BF),
            pltpu.VMEM((seg_n, nodes + halo, wide), BF),
            pltpu.VMEM((seg_n, nodes, wide), BF),
            pltpu.VMEM((seg_n, nodes + halo, wide), BF),
            pltpu.VMEM((seg_n, nodes + halo, wide), BF),
            pltpu.VMEM((seg_n, nodes, wide), F32),
            pltpu.VMEM(everyone, BF),
            pltpu.VMEM(everyone, BF),
            pltpu.VMEM(tall, BF),
            pltpu.VMEM(tall, BF),
            pltpu.VMEM((tm_n, seg_n * nodes, 2 * ch), BF),
            pltpu.VMEM((total_rows, ch), F32),
            pltpu.VMEM((half, ch), F32),
            pltpu.VMEM((half // 2, ch), F32),
            pltpu.VMEM((half // 4, ch), F32),
            pltpu.VMEM((half // 8, ch), F32),
            dma((seg_n,)), dma((seg_n,)), dma((seg_n,)), dma((seg_n,)),
            dma((seg_n,)), dma((seg_n,)), dma((seg_n, 2)), dma((seg_n, 2)),
            dma((frames,)), dma((frames,)), dma((frames,)), dma((frames,)),
            dma((frames,)), dma((frames,)), dma((frames,)), dma((frames,)),
            dma((9,)), dma((9,)),
        ],
        compiler_params=pltpu.CompilerParams(
            collective_id=0, has_side_effects=True, vmem_limit_bytes=56 << 20),
    )(
        series.reshape(raw), cotangent.reshape(raw), w_filter, w_gate,
        b_filter.reshape(1, -1), b_gate.reshape(1, -1), w_diff, b_diff.reshape(1, -1),
        tile_row, tile_col, tile_val.reshape(tile_rows, 128), send_nodes.reshape(3, 1, 128), send_count,
    )
    vec = jax.ShapeDtypeStruct((1, ch), F32)
    out, gs, g_wf, g_wg, g_bf, g_bg, g_wd, g_bd = pl.pallas_call(
        finish_kernel,
        out_shape=(
            jax.ShapeDtypeStruct(raw, BF),
            jax.ShapeDtypeStruct(raw, BF),
            jax.ShapeDtypeStruct((2, ch, ch), F32),
            jax.ShapeDtypeStruct((2, ch, ch), F32),
            vec, vec,
            jax.ShapeDtypeStruct((3, ch, ch), F32),
            vec,
        ),
        in_specs=[anyw, anyw, vmem],
        out_specs=(vmem,) * 8,
        scratch_shapes=[dma((2,))],
    )(out, gs, fin)
    return (
        out.reshape(series.shape), gs.reshape(series.shape), g_wf, g_wg,
        g_bf.reshape(-1), g_bg.reshape(-1), g_wd, g_bd.reshape(-1))


def on_device(mesh, series, *rest):
    nodes, batch, frames, ch = series.shape
    seg_n, tm_n = mesh.shape["seg"], mesh.shape["tm"]
    fits = seg_n == 4 and tm_n == 2 and batch == 1 and frames == seg_n * tm_n and frames == DILATION_FRAMES
    plan = gather_plan if fits else halo_plan
    return plan(mesh, series, *rest)


def solution(mesh):
    field = P(("grp", "seg"), "rep", "tm", None)
    part = ("grp", "seg")
    in_specs = (
        field, field, P(), P(), P(), P(), P(), P(),
        P(part, None), P(part, None), P(part, None, None, None), P(part, None, None), P(part, None),
    )
    out_specs = (
        field, field, P("grp", None, None), P("grp", None, None), P("grp"), P("grp"),
        P("grp", None, None), P("grp"),
    )
    return jax.shard_map(
        functools.partial(on_device, mesh), mesh=mesh, in_specs=in_specs, out_specs=out_specs,
        check_vma=False)
```

```python
import functools
import math

import jax
import jax.numpy as jnp
from jax import lax
from jax.experimental import pallas as pl
from jax.experimental.pallas import tpu as pltpu
from jax.sharding import PartitionSpec as P

DILATION_FRAMES = 8
STEPS = (1, -1, 2)
MESH = pl.DeviceIdType.MESH
WIDE = 256
BF = jnp.bfloat16
F32 = jnp.float32


def mm(a, b):
    return lax.dot_general(a, b, (((1,), (0,)), ((), ())), preferred_element_type=F32)


def mm_nt(a, b):
    return lax.dot_general(a, b, (((1,), (1,)), ((), ())), preferred_element_type=F32)


def mm_tn(a, b):
    return lax.dot_general(a, b, (((0,), (0,)), ((), ())), preferred_element_type=F32)


def halo_kernel(
    seg_n, tm_n, scale,
    ser3, cot3, wf, wg, bf, bg, wd, bd, trow, tcol, tval, snodes, scount,
    out3, gs3, fin1, fin2,
    big, big_g, ser, cot, prev, ops_f, ops_b, pick, give, wblk,
    acc, act_f, act_g, hid, hop1, delayed_out, delayed_in,
    snd, rcv, wacc, dacc, bacc, cacc,
    red1, red2, rb1, rc1, sb1, rb2, rc2, sb2,
    tm_s, tm_r, ex_s, ex_r, dl_s, dl_r, ar_s, ar_r,
):
    p = lax.axis_index("seg")
    t = lax.axis_index("tm")
    rep = lax.axis_index("rep")
    chunks, nodes, _ = ser.shape
    doublings = seg_n.bit_length() - 1
    cap = 128
    ch = 128

    barrier = pltpu.get_barrier_semaphore()
    for k in range(1, seg_n):
        pl.semaphore_signal(barrier, inc=1, device_id={"seg": lax.rem(p + k, seg_n)}, device_id_type=MESH)
    crew = 2 * tm_n
    me = t * 2 + rep

    def crew_device(i):
        return {"tm": lax.div(i, 2), "rep": lax.rem(i, 2)}

    for k in range(1, crew):
        pl.semaphore_signal(barrier, inc=1, device_id=crew_device(lax.rem(me + k, crew)), device_id_type=MESH)
    pl.semaphore_wait(barrier, seg_n - 1 + crew - 1)

    def series_copy(c):
        return pltpu.make_async_remote_copy(
            src_ref=ser.at[c], dst_ref=prev.at[c], send_sem=tm_s.at[c], recv_sem=tm_r.at[c],
            device_id={"tm": lax.rem(t + 1, tm_n)}, device_id_type=MESH)

    def delayed_copy(c):
        return pltpu.make_async_remote_copy(
            src_ref=delayed_out.at[c], dst_ref=delayed_in.at[c], send_sem=dl_s.at[c], recv_sem=dl_r.at[c],
            device_id={"tm": lax.rem(t + tm_n - 1, tm_n)}, device_id_type=MESH)

    def halo_copy(e, c, j):
        step = STEPS[j] if e % 2 == 0 else -STEPS[j]
        return pltpu.make_async_remote_copy(
            src_ref=snd.at[e, c, j], dst_ref=rcv.at[e, c, j],
            send_sem=ex_s.at[e, c, j], recv_sem=ex_r.at[e, c, j],
            device_id={"seg": lax.rem(p + step + seg_n, seg_n)}, device_id_type=MESH)

    def side_by_side(src, dst):
        big[...] = src[...].astype(F32)
        for c in range(chunks):
            dst[c] = jnp.concatenate([big[:, 2 * c, :], big[:, 2 * c + 1, :]], axis=1).astype(BF)

    side_by_side(cot3, cot)

    rows_n, cols_n, tiles_n = nodes // 128, nodes // 128 + 3, tval.shape[0]
    for r in range(rows_n):
        for c in range(cols_n):
            total = jnp.zeros((128, 128), F32)
            for k in range(tiles_n):
                if k < rows_n and (r != k or c != k):
                    continue
                if rows_n <= k < cols_n and c != k:
                    continue
                hit = jnp.where(trow[0, k] == r, 1.0, 0.0) * jnp.where(tcol[0, k] == c, 1.0, 0.0)
                total = total + hit * tval[k].astype(F32)
            ops_f[r * 128:(r + 1) * 128, c * 128:(c + 1) * 128] = total.astype(BF)
            ops_b[c * 128:(c + 1) * 128, r * 128:(r + 1) * 128] = total.T.astype(BF)
    wblk[4:7] = jnp.zeros((3, WIDE, WIDE), BF)
    for i in range(2):
        lo, hi = i * ch, (i + 1) * ch
        for k in range(3):
            wblk[4 + k, lo:hi, lo:hi] = wd[k]

    def put(e, c, rows):
        for j in range(3):
            snd[e, c, j] = rows[j * cap:(j + 1) * cap]
            halo_copy(e, c, j).start()

    def back_one(c, _):
        g = cot[c]
        up = mm_nt(g, wblk[6]).astype(BF)
        put(0, c, mm(ops_b[nodes:, :], up).astype(BF))
        acc[c] = mm(ops_b[:nodes, :], up) + mm_nt(g, wblk[5])
        return 0

    lax.fori_loop(0, chunks, back_one, 0)

    side_by_side(ser3, ser)

    @pl.when(t < tm_n - 1)
    def _():
        for c in range(chunks):
            series_copy(c).start()

    @pl.when(t == 0)
    def _():
        prev[...] = jnp.zeros_like(prev)

    @pl.when(t == tm_n - 1)
    def _():
        delayed_in[...] = jnp.zeros_like(delayed_in)

    wblk[0:4] = jnp.zeros((4, WIDE, WIDE), BF)
    for i in range(2):
        lo, hi = i * ch, (i + 1) * ch
        for k in range(2):
            wblk[k, lo:hi, lo:hi] = wf[k]
            wblk[2 + k, lo:hi, lo:hi] = wg[k]

    node_ids = lax.broadcasted_iota(jnp.int32, (nodes, cap), 0)
    slot_ids = lax.broadcasted_iota(jnp.int32, (nodes, cap), 1)
    for j in range(3):
        here = jnp.where(node_ids == snodes[j:j + 1, :], 1.0, 0.0)
        live = jnp.where(slot_ids < scount[0, j], 1.0, 0.0)
        hot = here * live
        give[:, j * cap:(j + 1) * cap] = hot.astype(BF)
        pick[j * cap:(j + 1) * cap, :] = hot.T.astype(BF)
    wacc[...] = jnp.zeros_like(wacc)
    dacc[...] = jnp.zeros_like(dacc)
    bacc[...] = jnp.zeros_like(bacc)
    cacc[...] = jnp.zeros_like(cacc)
    red1[...] = jnp.zeros_like(red1)
    red2[...] = jnp.zeros_like(red2)
    ones = jnp.ones((8, nodes), BF)

    def arrived(e, c):
        for j in range(3):
            halo_copy(e, c, j).wait_recv()
        return rcv[e, c].reshape(3 * cap, WIDE)

    def back_two(c, _):
        got = arrived(0, c)
        up = (acc[c] + mm(give[...], got)).astype(BF)
        put(2, c, mm(ops_b[nodes:, :], up).astype(BF))
        acc[c] = mm(ops_b[:nodes, :], up) + mm_nt(cot[c], wblk[4])
        return 0

    lax.fori_loop(0, chunks, back_two, 0)

    bf2 = jnp.concatenate([bf[...], bf[...]], axis=1)
    bg2 = jnp.concatenate([bg[...], bg[...]], axis=1)
    bd2 = jnp.concatenate([bd[...], bd[...]], axis=1)

    def fore_one(c, _):
        @pl.when(t > 0)
        def _():
            series_copy(c).wait_recv()

        before, now = prev[c], ser[c]
        a = jnp.tanh(mm(before, wblk[0]) + mm(now, wblk[1]) + bf2)
        act_f[c] = a
        s = jax.nn.sigmoid(mm(before, wblk[2]) + mm(now, wblk[3]) + bg2)
        act_g[c] = s
        h = (a * s).astype(BF)
        hid[c] = h
        put(1, c, mm(pick[...], h).astype(BF))
        return 0

    lax.fori_loop(0, chunks, fore_one, 0)

    def back_three(c, _):
        got = arrived(2, c)
        gh = acc[c] + mm(give[...], got)
        a, s = act_f[c], act_g[c]
        gf = (gh * s * (1.0 - a * a)).astype(BF)
        gg = (gh * a * (s * (1.0 - s))).astype(BF)
        delayed_out[c] = (mm_nt(gf, wblk[0]) + mm_nt(gg, wblk[2])).astype(BF)

        @pl.when(t > 0)
        def _():
            delayed_copy(c).start()

        g = cot[c]
        acc[c] = g.astype(F32) + mm_nt(gf, wblk[1]) + mm_nt(gg, wblk[3])
        before, now, h = prev[c], ser[c], hid[c]
        for i in range(2):
            lo, hi = i * ch, (i + 1) * ch
            right = jnp.concatenate([gf[:, lo:hi], gg[:, lo:hi]], axis=1)
            left = jnp.concatenate([before[:, lo:hi], now[:, lo:hi]], axis=1)
            wacc[...] += mm_tn(left, right)
            dacc[...] += mm_tn(h[:, lo:hi], g[:, lo:hi])
            bacc[...] += mm(ones, right)
            cacc[...] += mm(ones, g[:, lo:hi])
        return 0

    lax.fori_loop(0, chunks, back_three, 0)

    red1[0:256, :] = wacc[:, 0:128]
    red1[256:512, :] = wacc[:, 128:256]
    red1[512:640, :] = dacc[...]
    rid = lax.broadcasted_iota(jnp.int32, (8, 128), 0)
    red1[640:648, :] = jnp.where(
        rid == 0, bacc[:, 0:128], jnp.where(rid == 1, bacc[:, 128:256], cacc[...]))

    def all_sum(base, direct, red, rb, rc, sb, fin):
        part = red.shape[0] // crew

        def copy(src, dst, at, device):
            made = pltpu.make_async_remote_copy(
                src_ref=src, dst_ref=dst, send_sem=ar_s.at[at], recv_sem=ar_r.at[at],
                device_id=device, device_id_type=MESH)
            made.start()
            return made

        def rows(i):
            return pl.ds(pl.multiple_of(i * part, 8), part)

        sends = []
        for k in range(1, crew):
            o = lax.rem(me + k, crew)
            sends.append(copy(red.at[rows(o)], rb.at[k - 1], base + k, crew_device(o)))
        yield
        s = red[rows(me), :]
        for k in range(1, crew):
            sends[k - 1].wait()
            s = s + rb[k - 1]
        at = base + crew
        if direct:
            sb[0] = s
            rc[p] = s
            sends = [
                copy(sb.at[0], rc.at[p], at + k, {"seg": lax.rem(p + k, seg_n)})
                for k in range(1, seg_n)]
            yield
            for one in sends:
                one.wait()
            s = rc[0]
            for k in range(1, seg_n):
                s = s + rc[k]
        else:
            bit = 1
            for k in range(doublings):
                sb[k] = s
                mate = p + (1 - 2 * lax.rem(lax.div(p, bit), 2)) * bit
                one = copy(sb.at[k], rc.at[k], at + k, {"seg": mate})
                yield
                one.wait()
                s = s + rc[k]
                bit *= 2
        fin[rows(me), :] = s * scale
        at = at + seg_n
        sends = [
            copy(fin.at[rows(me)], fin.at[rows(me)], at + k, crew_device(lax.rem(me + k, crew)))
            for k in range(1, crew)]
        yield
        for one in sends:
            one.wait()
        yield

    first = all_sum(0, False, red1, rb1, rc1, sb1, fin1)
    next(first)
    def fore_two(c, _):
        got = arrived(1, c)
        h = (mm(ops_f[:, :nodes], hid[c]) + mm(ops_f[:, nodes:], got)).astype(BF)
        hop1[c] = h
        put(3, c, mm(pick[...], h).astype(BF))
        return 0

    for c in range(chunks):
        fore_two(c, 0)
        if c in (0, 1):
            next(first)

    for c in range(chunks):
        if c >= 2:
            next(first, None)
        got = arrived(3, c)
        h, h1, g = hid[c], hop1[c], cot[c]
        h2 = (mm(ops_f[:, :nodes], h1) + mm(ops_f[:, nodes:], got)).astype(BF)
        total = mm(h, wblk[4]) + mm(h1, wblk[5]) + mm(h2, wblk[6]) + bd2
        total = ser[c].astype(F32) + total
        for i in range(2):
            lo, hi = i * ch, (i + 1) * ch
            both = jnp.concatenate([h1[:, lo:hi], h2[:, lo:hi]], axis=1)
            red2[...] += mm_tn(both, g[:, lo:hi])
            big[:, 2 * c + i, :] = total[:, lo:hi]
    second = all_sum(2 * crew + seg_n, True, red2, rb2, rc2, sb2, fin2)
    next(second)
    out3[...] = big[...].astype(BF)
    next(second)
    for c in range(chunks):
        @pl.when(t < tm_n - 1)
        def _():
            delayed_copy(c).wait_recv()

        total = acc[c] + delayed_in[c].astype(F32)
        for i in range(2):
            big_g[:, 2 * c + i, :] = total[:, i * ch:(i + 1) * ch]
    next(second)
    gs3[...] = big_g[...].astype(BF)
    for _ in first:
        pass
    for _ in second:
        pass

    def drain(c, _):
        @pl.when(t < tm_n - 1)
        def _():
            series_copy(c).wait_send()

        @pl.when(t > 0)
        def _():
            delayed_copy(c).wait_send()

        for e in range(4):
            for j in range(3):
                halo_copy(e, c, j).wait_send()
        return 0

    lax.fori_loop(0, chunks, drain, 0)


def halo_plan(mesh, series, cotangent, w_filter, w_gate, b_filter, b_gate, w_diff, b_diff,
              tile_row, tile_col, tile_val, send_nodes, send_count):
    nodes, batch, frames, channels = series.shape
    seg_n, tm_n, rep_n = mesh.shape["seg"], mesh.shape["tm"], mesh.shape["rep"]
    chunks = batch * frames * channels // WIDE
    scale = 1.0 / math.sqrt(nodes * batch * frames * seg_n * tm_n * rep_n)
    unit = 16 * tm_n
    r1 = -(-648 // unit) * unit
    r2 = -(-256 // unit) * unit

    doublings = seg_n.bit_length() - 1
    vmem = pl.BlockSpec(memory_space=pltpu.VMEM)
    smem = pl.BlockSpec(memory_space=pltpu.SMEM)
    field = (chunks, nodes, WIDE)

    def sums(r):
        crew = 2 * tm_n
        q = r // crew
        return [
            pltpu.VMEM((crew - 1, q, 128), F32),
            pltpu.VMEM((seg_n, q, 128), F32),
            pltpu.VMEM((doublings, q, 128), F32),
        ]

    n_ar = 2 * (4 * tm_n + seg_n)
    raw = (nodes, batch * frames, channels)
    halo = (4, chunks, 3, 128, WIDE)
    out, gs, fin1, fin2 = pl.pallas_call(
        functools.partial(halo_kernel, seg_n, tm_n, scale),
        out_shape=(
            jax.ShapeDtypeStruct(raw, BF),
            jax.ShapeDtypeStruct(raw, BF),
            jax.ShapeDtypeStruct((r1, 128), F32),
            jax.ShapeDtypeStruct((r2, 128), F32),
        ),
        in_specs=[vmem] * 8 + [smem, smem, vmem, vmem, smem],
        out_specs=(vmem,) * 4,
        scratch_shapes=[
            pltpu.VMEM(raw, F32),
            pltpu.VMEM(raw, F32),
            pltpu.VMEM(field, BF),
            pltpu.VMEM(field, BF),
            pltpu.VMEM(field, BF),
            pltpu.VMEM((nodes, nodes + 384), BF),
            pltpu.VMEM((nodes + 384, nodes), BF),
            pltpu.VMEM((384, nodes), BF),
            pltpu.VMEM((nodes, 384), BF),
            pltpu.VMEM((7, WIDE, WIDE), BF),
            pltpu.VMEM(field, F32),
            pltpu.VMEM(field, F32),
            pltpu.VMEM(field, F32),
            pltpu.VMEM(field, BF),
            pltpu.VMEM(field, BF),
            pltpu.VMEM(field, BF),
            pltpu.VMEM(field, BF),
            pltpu.VMEM(halo, BF),
            pltpu.VMEM(halo, BF),
            pltpu.VMEM((256, 256), F32),
            pltpu.VMEM((128, 128), F32),
            pltpu.VMEM((8, 256), F32),
            pltpu.VMEM((8, 128), F32),
            pltpu.VMEM((r1, 128), F32),
            pltpu.VMEM((r2, 128), F32),
            *sums(r1),
            *sums(r2),
            pltpu.SemaphoreType.DMA((chunks,)),
            pltpu.SemaphoreType.DMA((chunks,)),
            pltpu.SemaphoreType.DMA((4, chunks, 3)),
            pltpu.SemaphoreType.DMA((4, chunks, 3)),
            pltpu.SemaphoreType.DMA((chunks,)),
            pltpu.SemaphoreType.DMA((chunks,)),
            pltpu.SemaphoreType.DMA((n_ar,)),
            pltpu.SemaphoreType.DMA((n_ar,)),
        ],
        compiler_params=pltpu.CompilerParams(
            collective_id=0, has_side_effects=True, vmem_limit_bytes=56 << 20),
    )(
        series.reshape(raw), cotangent.reshape(raw), w_filter, w_gate,
        b_filter.reshape(1, -1), b_gate.reshape(1, -1), w_diff, b_diff.reshape(1, -1),
        tile_row, tile_col, tile_val[0], send_nodes[0], send_count,
    )
    return (
        out.reshape(series.shape),
        gs.reshape(series.shape),
        fin1[0:256].reshape(2, 128, 128),
        fin1[256:512].reshape(2, 128, 128),
        fin1[640],
        fin1[641],
        jnp.concatenate([fin1[512:640], fin2[:256]], axis=0).reshape(3, 128, 128),
        fin1[642],
    )


def gather_kernel(
    seg_n, tm_n, scale,
    ser3, cot3, wf, wg, bf, bg, wd, bd, trow, tcol, tval, snodes, scount,
    out3, gs3, fin,
    big, big_g, stage_s, stage_c, ser, cot, tiles, meta,
    opf, opb, oph, pick, wc, wct, wdt,
    act_f, act_g, src0, src1, hop2, sb0, sb1, acc,
    out_b, gs_b, out_r, gs_r, pair,
    red, rbuf0, rbuf1, rbuf2, rbuf3,
    tz_s, tz_r, mz_s, mz_r, tx_s, tx_r, tc_s, tc_r,
    se_s, se_r, co_s, co_r, ou_s, ou_r, gr_s, gr_r, ar_s, ar_r,
):
    p = lax.axis_index("seg")
    t = lax.axis_index("tm")
    rep = lax.axis_index("rep")
    nodes, frames, ch = ser3.shape
    mine = p * tm_n + t
    crew = 2 * tm_n
    quarter = tiles.shape[1] // crew

    def rc(src, dst, ss, rs, dev):
        return pltpu.make_async_remote_copy(
            src_ref=src, dst_ref=dst, send_sem=ss, recv_sem=rs, device_id=dev, device_id_type=MESH)

    low, high = lax.rem(p, 2), lax.div(p, 2)

    def flip(j):
        return lax.rem(high + j // 2, 2) * 2 + lax.rem(low + j % 2, 2)

    def peer(j, m):
        return flip(j), lax.rem(t + m, tm_n)

    others = [(2, 0), (3, 0), (2, 1), (3, 1), (1, 0), (1, 1), (0, 1)]

    def rows_of(q):
        return pl.ds(pl.multiple_of(q * nodes, 128), nodes)

    def piece(c):
        return pl.ds(pl.multiple_of(c * quarter, 16), quarter)

    core = {"rep": 1 - rep}
    across = {"tm": 1 - t}

    barrier = pltpu.get_barrier_semaphore()
    for j, m in others:
        q, tt = peer(j, m)
        pl.semaphore_signal(barrier, inc=1, device_id={"seg": q, "tm": tt}, device_id_type=MESH)
    pl.semaphore_signal(barrier, inc=1, device_id=core, device_id_type=MESH)

    meta[p] = jnp.zeros_like(meta[p])
    for j in range(3):
        meta[p, j:j + 1, :] = snodes[j]
    meta[p, 3:4, 0:trow.shape[1]] = trow[...]
    meta[p, 4:5, 0:tcol.shape[1]] = tcol[...]
    meta[p, 5:6, 0:scount.shape[1]] = scount[...]
    pl.semaphore_wait(barrier, len(others) + 1)

    c_me = t * 2 + rep
    c_across = (1 - t) * 2 + rep

    def tile_z(j):
        return rc(tval.at[piece(c_me)], tiles.at[p, piece(c_me)], tz_s.at[j], tz_r.at[j], {"seg": flip(j)})

    def tile_on():
        at = tiles.at[flip(2), piece(c_me)]
        return rc(at, at, tz_s.at[3], tz_r.at[3], {"seg": flip(1)})

    def meta_z(j):
        return rc(meta.at[p], meta.at[p], mz_s.at[j], mz_r.at[j], {"seg": flip(j)})

    def tile_x(j):
        at = tiles.at[flip(j), piece(c_me)]
        return rc(at, at, tx_s.at[j], tx_r.at[j], across)

    def tile_c(j, c, i):
        at = tiles.at[flip(j), piece(c)]
        return rc(at, at, tc_s.at[j, i], tc_r.at[j, i], core)

    def field_in(stage, whole, ss, rs, j, m):
        q, tt = peer(j, m)
        f = q * tm_n + tt
        return rc(stage.at[f], whole.at[t, rows_of(p)], ss.at[f], rs.at[mine], {"seg": q, "tm": tt})

    def field_got(stage, whole, ss, rs, j, m):
        q, tt = peer(j, m)
        f = q * tm_n + tt
        return rc(stage.at[f], whole.at[tt, rows_of(q)], ss.at[f], rs.at[f], {"seg": q, "tm": tt})

    def frame_major(source, wide, stage, whole):
        wide[...] = source[...].astype(F32)
        for f in range(frames):
            stage[f] = wide[:, f, :].astype(BF)
        whole[t, rows_of(p), :] = stage[mine]

    tile_z(2).start()
    tile_z(1).start()
    for j in (2, 3, 1):
        meta_z(j).start()
    frame_major(ser3, big, stage_s, ser)
    field_in(stage_s, ser, se_s, se_r, 2, 0).start()
    tiles[p] = tval[...]

    tile_z(2).wait_recv()
    tile_on().start()
    tile_x(2).start()
    tile_z(1).wait_recv()
    tile_x(1).start()
    field_in(stage_s, ser, se_s, se_r, 3, 0).start()
    tile_on().wait_recv()
    tile_x(3).start()
    for j, m in others[2:]:
        field_in(stage_s, ser, se_s, se_r, j, m).start()

    frame_major(cot3, big_g, stage_c, cot)
    for j, m in others:
        field_in(stage_c, cot, co_s, co_r, j, m).start()

    for j in (2, 1, 3):
        tile_x(j).wait_recv()
        tile_c(j, c_me, 0).start()
        tile_c(j, c_across, 1).start()

    for i in range(2):
        wc[i * ch:(i + 1) * ch, 0:ch] = wf[i]
        wc[i * ch:(i + 1) * ch, ch:2 * ch] = wg[i]
    wct[...] = wc[...].astype(F32).T.astype(BF)
    for i in range(3):
        wdt[i] = wd[i].astype(F32).T.astype(BF)
    bias = jnp.concatenate([bf[...], bg[...]], axis=1)
    red[...] = jnp.zeros_like(red)

    for j in (2, 1, 3):
        tile_c(j, c_me, 0).wait_recv()
        tile_c(j, c_across, 1).wait_recv()
        meta_z(j).wait_recv()

    rows_n = nodes // 128
    cols_n = rows_n + 3
    tiles_n = tiles.shape[1] // 128
    halo = 3 * 128
    lane_ids = lax.broadcasted_iota(jnp.int32, (128, nodes), 1)
    sub_ids = lax.broadcasted_iota(jnp.int32, (nodes, 128), 0)
    slot_lane = lax.broadcasted_iota(jnp.int32, (1, 128), 1)
    slot_sub = lax.broadcasted_iota(jnp.int32, (128, 1), 0)

    def build(q, _):
        info = meta[q]
        tr, tc = info[3:4, :], info[4:5, :]
        t_all = [tiles[q, k * 128:(k + 1) * 128, :].astype(F32) for k in range(tiles_n)]
        for r in range(rows_n):
            for c in range(cols_n):
                hits = jnp.where((tr == r) & (tc == c), 1.0, 0.0)
                total = jnp.zeros((128, 128), F32)
                for k in range(tiles_n):
                    if k < rows_n and (r != k or c != k):
                        continue
                    if rows_n <= k < cols_n and c != k:
                        continue
                    total = total + hits[:, k:k + 1] * t_all[k]
                flipped = total.T.astype(BF)
                opf[q, r * 128:(r + 1) * 128, c * 128:(c + 1) * 128] = total.astype(BF)
                if c < rows_n:
                    opb[q, c * 128:(c + 1) * 128, r * 128:(r + 1) * 128] = flipped
                else:
                    oph[q, (c - rows_n) * 128:(c - rows_n + 1) * 128, r * 128:(r + 1) * 128] = flipped
        col = info.astype(F32).T.astype(jnp.int32)
        for j in range(3):
            count = info[5:6, j:j + 1]
            give = jnp.where((sub_ids == info[j:j + 1, :]) & (slot_lane < count), 1.0, 0.0)
            opb[q, :, nodes + j * 128:nodes + (j + 1) * 128] = give.astype(BF)
            take = jnp.where((lane_ids == col[:, j:j + 1]) & (slot_sub < count), 1.0, 0.0)
            pick[q, j * 128:(j + 1) * 128, :] = take.astype(BF)
        return 0

    lax.fori_loop(0, seg_n, build, 0)

    for j, m in others:
        field_got(stage_s, ser, se_s, se_r, j, m).wait_recv()

    def conv(q, _):
        for tt in range(tm_n):
            now = ser[tt, rows_of(q), :]
            if tt == 0:
                pre = mm(now, wc[ch:2 * ch, :]) + bias
            else:
                pre = mm(jnp.concatenate([ser[tt - 1, rows_of(q), :], now], axis=1), wc[...]) + bias
            a = jnp.tanh(pre[:, 0:ch])
            s = jax.nn.sigmoid(pre[:, ch:2 * ch])
            act_f[tt, rows_of(q), :] = a
            act_g[tt, rows_of(q), :] = s
            src0[q, 0:nodes, tt * ch:(tt + 1) * ch] = (a * s).astype(BF)
        return 0

    def send_slots(src):
        def one(q, _):
            got = mm(pick[q], src[q, 0:nodes, :]).astype(BF)
            for j in range(3):
                reader = lax.rem(q - STEPS[j] + seg_n, seg_n)
                src[reader, nodes + j * 128:nodes + (j + 1) * 128, :] = got[j * 128:(j + 1) * 128]
            return 0
        lax.fori_loop(0, seg_n, one, 0)

    def hop(src, dst):
        def one(q, _):
            dst[q, 0:nodes, :] = mm(opf[q], src[q]).astype(BF)
            return 0
        lax.fori_loop(0, seg_n, one, 0)

    def home(buf, got, ss, rs, q, tt):
        return rc(buf.at[tt, rows_of(q)], got.at[mine], ss.at[q * tm_n + tt], rs.at[mine], {"seg": q, "tm": tt})

    def arrived(buf, got, ss, rs, f):
        return rc(buf.at[f % tm_n, pl.ds(f // tm_n * nodes, nodes)], got.at[f], ss.at[f], rs.at[f],
                  {"seg": f // tm_n, "tm": f % tm_n})

    def out_go(*pairs):
        for j, m in pairs:
            q, tt = peer(j, m)
            home(out_b, out_r, ou_s, ou_r, q, tt).start()

    def gs_go(*pairs):
        for j, m in pairs:
            q, tt = peer(j, m)
            home(gs_b, gs_r, gr_s, gr_r, q, tt).start()

    lax.fori_loop(0, seg_n, conv, 0)
    send_slots(src0)
    hop(src0, src1)
    send_slots(src1)
    hop(src1, hop2)
    bias_d = bd[...]

    def put_out(q, _):
        for tt in range(tm_n):
            lo, hi = tt * ch, (tt + 1) * ch
            two = jnp.concatenate([src0[q, 0:nodes, lo:hi], src1[q, 0:nodes, lo:hi]], axis=1)
            total = mm(two, jnp.concatenate([wd[0], wd[1]], axis=0)) + mm(hop2[q, :, lo:hi], wd[2]) + bias_d
            out_b[tt, rows_of(q), :] = (ser[tt, rows_of(q), :].astype(F32) + total).astype(BF)
        return 0

    lax.fori_loop(0, seg_n, put_out, 0)
    out_go((2, 1), (1, 1), (3, 1), (1, 0), (0, 1))

    for j, m in others:
        field_got(stage_c, cot, co_s, co_r, j, m).wait_recv()

    def back(q, _):
        for tt in range(tm_n):
            lo, hi = tt * ch, (tt + 1) * ch
            g = cot[tt, rows_of(q), :]
            u = mm(g, jnp.concatenate([wdt[2], wdt[1]], axis=1))
            sb0[q, 0:nodes, lo:hi] = u[:, 0:ch].astype(BF)
            acc[q, :, lo:hi] = u[:, ch:2 * ch]
        return 0

    def send_back(sb):
        def one(q, _):
            got = mm(oph[q], sb[q, 0:nodes, :]).astype(BF)
            for j in range(3):
                owner = lax.rem(q + STEPS[j] + seg_n, seg_n)
                sb[owner, nodes + j * 128:nodes + (j + 1) * 128, :] = got[j * 128:(j + 1) * 128]
            return 0
        lax.fori_loop(0, seg_n, one, 0)

    lax.fori_loop(0, seg_n, back, 0)
    send_back(sb0)

    def back_mid(q, _):
        sb1[q, 0:nodes, :] = (acc[q] + mm(opb[q], sb0[q])).astype(BF)
        return 0

    lax.fori_loop(0, seg_n, back_mid, 0)
    out_go((2, 0))
    send_back(sb1)

    def back_last(q, _):
        gh_all = mm(opb[q], sb1[q])
        for tt in range(tm_n):
            lo, hi = tt * ch, (tt + 1) * ch
            g = cot[tt, rows_of(q), :]
            gh = gh_all[:, lo:hi] + mm(g, wdt[0])
            a, s = act_f[tt, rows_of(q), :], act_g[tt, rows_of(q), :]
            gf = (gh * s * (1.0 - a * a)).astype(BF)
            gg = (gh * a * (s * (1.0 - s))).astype(BF)
            both = jnp.concatenate([gf, gg], axis=1)
            pair[tt, rows_of(q), :] = both
            now = ser[tt, rows_of(q), :]
            if tt == 0:
                part = mm_tn(now, both)
                red[ch:2 * ch, :] += part[:, 0:ch]
                red[3 * ch:4 * ch, :] += part[:, ch:2 * ch]
            else:
                part = mm_tn(jnp.concatenate([ser[tt - 1, rows_of(q), :], now], axis=1), both)
                red[0:2 * ch, :] += part[:, 0:ch]
                red[2 * ch:4 * ch, :] += part[:, ch:2 * ch]
            hops = jnp.concatenate(
                [src0[q, 0:nodes, lo:hi], src1[q, 0:nodes, lo:hi], hop2[q, :, lo:hi]], axis=1)
            red[4 * ch:7 * ch, :] += mm_tn(hops, g)
            base = 7 * ch
            red[base:base + 1, :] += jnp.sum(gf.astype(F32), axis=0, keepdims=True)
            red[base + 1:base + 2, :] += jnp.sum(gg.astype(F32), axis=0, keepdims=True)
            red[base + 2:base + 3, :] += jnp.sum(g.astype(F32), axis=0, keepdims=True)
        return 0

    lax.fori_loop(0, seg_n, back_last, 0)

    half = red.shape[0] // 2
    fourth, eighth, last = half // 2, half // 4, half // 8

    def span(start, size):
        return pl.ds(pl.multiple_of(start, 8), size)

    def go(src, dst, at, dev):
        made = rc(src, dst, ar_s.at[at], ar_r.at[at], dev)
        made.start()
        return made

    at_core = rep * half
    at_x = at_core + t * fourth
    at_one = at_x + low * eighth
    at_two = at_one + high * last
    step = go(red.at[span((1 - rep) * half, half)], rbuf0, 0, core)
    out_go((3, 0))

    def put_gs(q, _):
        later = None
        for tt in reversed(range(tm_n)):
            both = pair[tt, rows_of(q), :]
            if tt == 0:
                total = mm(both, wct[:, ch:2 * ch])
            else:
                r = mm(both, wct[...])
                total = r[:, ch:2 * ch]
            total = cot[tt, rows_of(q), :].astype(F32) + total
            if later is not None:
                total = total + later.astype(F32)
            if tt > 0:
                later = r[:, 0:ch].astype(BF)
            gs_b[tt, rows_of(q), :] = total.astype(BF)
        return 0

    lax.fori_loop(0, seg_n, put_gs, 0)
    step.wait()
    red[span(at_core, half), :] += rbuf0[...]
    step = go(red.at[span(at_core + (1 - t) * fourth, fourth)], rbuf1, 1, across)
    out_r[mine] = out_b[t, rows_of(p), :]
    gs_r[mine] = gs_b[t, rows_of(p), :]

    def node_major(got, wide, dest, buf, ss, rs):
        for f in range(frames):
            @pl.when(f != mine)
            def _():
                arrived(buf, got, ss, rs, f).wait_recv()

            wide[:, f, :] = got[f].astype(F32)
        dest[...] = wide[...].astype(BF)

    step.wait()
    red[span(at_x, fourth), :] += rbuf1[...]
    step = go(red.at[span(at_x + (1 - low) * eighth, eighth)], rbuf2, 2, {"seg": flip(1)})
    gs_go((2, 1), (1, 1))
    step.wait()
    red[span(at_one, eighth), :] += rbuf2[...]
    step = go(red.at[span(at_one + (1 - high) * last, last)], rbuf3, 3, {"seg": flip(2)})
    gs_go((3, 1), (0, 1))
    node_major(out_r, big, out3, out_b, ou_s, ou_r)
    step.wait()
    fin[span(at_two, last), :] = (red[span(at_two, last), :] + rbuf3[...]) * scale
    here = fin.at[span(at_two, last)]
    step = go(here, here, 4, {"seg": flip(2)})
    gs_go((2, 0), (1, 0))
    step.wait()
    here = fin.at[span(at_one, eighth)]
    steps = [
        go(here, here, 5, {"seg": flip(1)}),
        go(here, here, 6, across),
        go(here, here, 7, {"seg": flip(1), "tm": 1 - t})]
    gs_go((3, 0))
    for step in steps:
        step.wait()
    here = fin.at[span(at_core, half)]
    step = go(here, here, 8, core)
    node_major(gs_r, big_g, gs3, gs_b, gr_s, gr_r)
    step.wait()

    tile_z(2).wait_send()
    tile_z(1).wait_send()
    tile_on().wait_send()
    for j in (1, 2, 3):
        meta_z(j).wait_send()
        tile_x(j).wait_send()
        tile_c(j, c_me, 0).wait_send()
        tile_c(j, c_across, 1).wait_send()
    for j, m in others:
        q, tt = peer(j, m)
        field_in(stage_s, ser, se_s, se_r, j, m).wait_send()
        field_in(stage_c, cot, co_s, co_r, j, m).wait_send()
        home(out_b, out_r, ou_s, ou_r, q, tt).wait_send()
        home(gs_b, gs_r, gr_s, gr_r, q, tt).wait_send()


def finish_kernel(out_i, gs_i, fin, out_o, gs_o, o_wf, o_wg, o_bf, o_bg, o_wd, o_bd, sems):
    one = pltpu.make_async_copy(out_i, out_o, sems.at[0])
    two = pltpu.make_async_copy(gs_i, gs_o, sems.at[1])
    one.start()
    two.start()
    ch = o_wf.shape[1]
    for i in range(2):
        o_wf[i] = fin[i * ch:(i + 1) * ch, :]
        o_wg[i] = fin[(2 + i) * ch:(3 + i) * ch, :]
    for i in range(3):
        o_wd[i] = fin[(4 + i) * ch:(5 + i) * ch, :]
    o_bf[...] = fin[7 * ch:7 * ch + 1, :]
    o_bg[...] = fin[7 * ch + 1:7 * ch + 2, :]
    o_bd[...] = fin[7 * ch + 2:7 * ch + 3, :]
    one.wait()
    two.wait()


def gather_plan(mesh, series, cotangent, w_filter, w_gate, b_filter, b_gate, w_diff, b_diff,
                tile_row, tile_col, tile_val, send_nodes, send_count):
    nodes, batch, frames, ch = series.shape
    seg_n, tm_n, rep_n = mesh.shape["seg"], mesh.shape["tm"], mesh.shape["rep"]
    scale = 1.0 / math.sqrt(nodes * batch * frames * seg_n * tm_n * rep_n)
    unit = 8 * 2 * tm_n * seg_n
    total_rows = -(-(7 * ch + 8) // unit) * unit
    vmem = pl.BlockSpec(memory_space=pltpu.VMEM)
    anyw = pl.BlockSpec(memory_space=pl.ANY)
    raw = (nodes, batch * frames, ch)
    tall = (frames, nodes, ch)
    everyone = (tm_n, seg_n * nodes, ch)
    wide = tm_n * ch
    tile_rows = tile_val.shape[1] * 128
    halo = 3 * 128
    dma = pltpu.SemaphoreType.DMA
    half = total_rows // 2
    out, gs, fin = pl.pallas_call(
        functools.partial(gather_kernel, seg_n, tm_n, scale),
        out_shape=(
            jax.ShapeDtypeStruct(raw, BF),
            jax.ShapeDtypeStruct(raw, BF),
            jax.ShapeDtypeStruct((total_rows, ch), F32),
        ),
        in_specs=[vmem] * 13,
        out_specs=(vmem,) * 3,
        scratch_shapes=[
            pltpu.VMEM(raw, F32),
            pltpu.VMEM(raw, F32),
            pltpu.VMEM(tall, BF),
            pltpu.VMEM(tall, BF),
            pltpu.VMEM(everyone, BF),
            pltpu.VMEM(everyone, BF),
            pltpu.VMEM((seg_n, tile_rows, 128), BF),
            pltpu.VMEM((seg_n, 8, 128), jnp.int32),
            pltpu.VMEM((seg_n, nodes, nodes + halo), BF),
            pltpu.VMEM((seg_n, nodes, nodes + halo), BF),
            pltpu.VMEM((seg_n, halo, nodes), BF),
            pltpu.VMEM((seg_n, halo, nodes), BF),
            pltpu.VMEM((2 * ch, 2 * ch), BF),
            pltpu.VMEM((2 * ch, 2 * ch), BF),
            pltpu.VMEM((3, ch, ch), BF),
            pltpu.VMEM(everyone, F32),
            pltpu.VMEM(everyone, F32),
            pltpu.VMEM((seg_n, nodes + halo, wide), BF),
            pltpu.VMEM((seg_n, nodes + halo, wide), BF),
            pltpu.VMEM((seg_n, nodes, wide), BF),
            pltpu.VMEM((seg_n, nodes + halo, wide), BF),
            pltpu.VMEM((seg_n, nodes + halo, wide), BF),
            pltpu.VMEM((seg_n, nodes, wide), F32),
            pltpu.VMEM(everyone, BF),
            pltpu.VMEM(everyone, BF),
            pltpu.VMEM(tall, BF),
            pltpu.VMEM(tall, BF),
            pltpu.VMEM((tm_n, seg_n * nodes, 2 * ch), BF),
            pltpu.VMEM((total_rows, ch), F32),
            pltpu.VMEM((half, ch), F32),
            pltpu.VMEM((half // 2, ch), F32),
            pltpu.VMEM((half // 4, ch), F32),
            pltpu.VMEM((half // 8, ch), F32),
            dma((seg_n,)), dma((seg_n,)), dma((seg_n,)), dma((seg_n,)),
            dma((seg_n,)), dma((seg_n,)), dma((seg_n, 2)), dma((seg_n, 2)),
            dma((frames,)), dma((frames,)), dma((frames,)), dma((frames,)),
            dma((frames,)), dma((frames,)), dma((frames,)), dma((frames,)),
            dma((9,)), dma((9,)),
        ],
        compiler_params=pltpu.CompilerParams(
            collective_id=0, has_side_effects=True, vmem_limit_bytes=56 << 20),
    )(
        series.reshape(raw), cotangent.reshape(raw), w_filter, w_gate,
        b_filter.reshape(1, -1), b_gate.reshape(1, -1), w_diff, b_diff.reshape(1, -1),
        tile_row, tile_col, tile_val.reshape(tile_rows, 128), send_nodes.reshape(3, 1, 128), send_count,
    )
    vec = jax.ShapeDtypeStruct((1, ch), F32)
    out, gs, g_wf, g_wg, g_bf, g_bg, g_wd, g_bd = pl.pallas_call(
        finish_kernel,
        out_shape=(
            jax.ShapeDtypeStruct(raw, BF),
            jax.ShapeDtypeStruct(raw, BF),
            jax.ShapeDtypeStruct((2, ch, ch), F32),
            jax.ShapeDtypeStruct((2, ch, ch), F32),
            vec, vec,
            jax.ShapeDtypeStruct((3, ch, ch), F32),
            vec,
        ),
        in_specs=[anyw, anyw, vmem],
        out_specs=(vmem,) * 8,
        scratch_shapes=[dma((2,))],
    )(out, gs, fin)
    return (
        out.reshape(series.shape), gs.reshape(series.shape), g_wf, g_wg,
        g_bf.reshape(-1), g_bg.reshape(-1), g_wd, g_bd.reshape(-1))


def on_device(mesh, series, *rest):
    nodes, batch, frames, ch = series.shape
    seg_n, tm_n = mesh.shape["seg"], mesh.shape["tm"]
    fits = seg_n == 4 and tm_n == 2 and batch == 1 and frames == seg_n * tm_n and frames == DILATION_FRAMES
    plan = gather_plan if fits else halo_plan
    return plan(mesh, series, *rest)


def solution(mesh):
    field = P(("grp", "seg"), "rep", "tm", None)
    part = ("grp", "seg")
    in_specs = (
        field, field, P(), P(), P(), P(), P(), P(),
        P(part, None), P(part, None), P(part, None, None, None), P(part, None, None), P(part, None),
    )
    out_specs = (
        field, field, P("grp", None, None), P("grp", None, None), P("grp"), P("grp"),
        P("grp", None, None), P("grp"),
    )
    return jax.shard_map(
        functools.partial(on_device, mesh), mesh=mesh, in_specs=in_specs, out_specs=out_specs,
        check_vma=False)
```

```python
import functools
import math

import jax
import jax.numpy as jnp
from jax import lax
from jax.experimental import pallas as pl
from jax.experimental.pallas import tpu as pltpu
from jax.sharding import PartitionSpec as P

DILATION_FRAMES = 8
STEPS = (1, -1, 2)
MESH = pl.DeviceIdType.MESH
WIDE = 256
BF = jnp.bfloat16
F32 = jnp.float32


def mm(a, b):
    return lax.dot_general(a, b, (((1,), (0,)), ((), ())), preferred_element_type=F32)


def mm_nt(a, b):
    return lax.dot_general(a, b, (((1,), (1,)), ((), ())), preferred_element_type=F32)


def mm_tn(a, b):
    return lax.dot_general(a, b, (((0,), (0,)), ((), ())), preferred_element_type=F32)


def halo_kernel(
    seg_n, tm_n, scale,
    ser3, cot3, wf, wg, bf, bg, wd, bd, trow, tcol, tval, snodes, scount,
    out3, gs3, fin1, fin2,
    big, big_g, ser, cot, prev, ops_f, ops_b, pick, give, wblk,
    acc, act_f, act_g, hid, hop1, delayed_out, delayed_in,
    snd, rcv, wacc, dacc, bacc, cacc,
    red1, red2, rb1, rc1, sb1, rb2, rc2, sb2,
    tm_s, tm_r, ex_s, ex_r, dl_s, dl_r, ar_s, ar_r,
):
    p = lax.axis_index("seg")
    t = lax.axis_index("tm")
    rep = lax.axis_index("rep")
    chunks, nodes, _ = ser.shape
    doublings = seg_n.bit_length() - 1
    cap = 128
    ch = 128

    barrier = pltpu.get_barrier_semaphore()
    for k in range(1, seg_n):
        pl.semaphore_signal(barrier, inc=1, device_id={"seg": lax.rem(p + k, seg_n)}, device_id_type=MESH)
    crew = 2 * tm_n
    me = t * 2 + rep

    def crew_device(i):
        return {"tm": lax.div(i, 2), "rep": lax.rem(i, 2)}

    for k in range(1, crew):
        pl.semaphore_signal(barrier, inc=1, device_id=crew_device(lax.rem(me + k, crew)), device_id_type=MESH)
    pl.semaphore_wait(barrier, seg_n - 1 + crew - 1)

    def series_copy(c):
        return pltpu.make_async_remote_copy(
            src_ref=ser.at[c], dst_ref=prev.at[c], send_sem=tm_s.at[c], recv_sem=tm_r.at[c],
            device_id={"tm": lax.rem(t + 1, tm_n)}, device_id_type=MESH)

    def delayed_copy(c):
        return pltpu.make_async_remote_copy(
            src_ref=delayed_out.at[c], dst_ref=delayed_in.at[c], send_sem=dl_s.at[c], recv_sem=dl_r.at[c],
            device_id={"tm": lax.rem(t + tm_n - 1, tm_n)}, device_id_type=MESH)

    def halo_copy(e, c, j):
        step = STEPS[j] if e % 2 == 0 else -STEPS[j]
        return pltpu.make_async_remote_copy(
            src_ref=snd.at[e, c, j], dst_ref=rcv.at[e, c, j],
            send_sem=ex_s.at[e, c, j], recv_sem=ex_r.at[e, c, j],
            device_id={"seg": lax.rem(p + step + seg_n, seg_n)}, device_id_type=MESH)

    def side_by_side(src, dst):
        big[...] = src[...].astype(F32)
        for c in range(chunks):
            dst[c] = jnp.concatenate([big[:, 2 * c, :], big[:, 2 * c + 1, :]], axis=1).astype(BF)

    side_by_side(cot3, cot)

    rows_n, cols_n, tiles_n = nodes // 128, nodes // 128 + 3, tval.shape[0]
    for r in range(rows_n):
        for c in range(cols_n):
            total = jnp.zeros((128, 128), F32)
            for k in range(tiles_n):
                if k < rows_n and (r != k or c != k):
                    continue
                if rows_n <= k < cols_n and c != k:
                    continue
                hit = jnp.where(trow[0, k] == r, 1.0, 0.0) * jnp.where(tcol[0, k] == c, 1.0, 0.0)
                total = total + hit * tval[k].astype(F32)
            ops_f[r * 128:(r + 1) * 128, c * 128:(c + 1) * 128] = total.astype(BF)
            ops_b[c * 128:(c + 1) * 128, r * 128:(r + 1) * 128] = total.T.astype(BF)
    wblk[4:7] = jnp.zeros((3, WIDE, WIDE), BF)
    for i in range(2):
        lo, hi = i * ch, (i + 1) * ch
        for k in range(3):
            wblk[4 + k, lo:hi, lo:hi] = wd[k]

    def put(e, c, rows):
        for j in range(3):
            snd[e, c, j] = rows[j * cap:(j + 1) * cap]
            halo_copy(e, c, j).start()

    def back_one(c, _):
        g = cot[c]
        up = mm_nt(g, wblk[6]).astype(BF)
        put(0, c, mm(ops_b[nodes:, :], up).astype(BF))
        acc[c] = mm(ops_b[:nodes, :], up) + mm_nt(g, wblk[5])
        return 0

    lax.fori_loop(0, chunks, back_one, 0)

    side_by_side(ser3, ser)

    @pl.when(t < tm_n - 1)
    def _():
        for c in range(chunks):
            series_copy(c).start()

    @pl.when(t == 0)
    def _():
        prev[...] = jnp.zeros_like(prev)

    @pl.when(t == tm_n - 1)
    def _():
        delayed_in[...] = jnp.zeros_like(delayed_in)

    wblk[0:4] = jnp.zeros((4, WIDE, WIDE), BF)
    for i in range(2):
        lo, hi = i * ch, (i + 1) * ch
        for k in range(2):
            wblk[k, lo:hi, lo:hi] = wf[k]
            wblk[2 + k, lo:hi, lo:hi] = wg[k]

    node_ids = lax.broadcasted_iota(jnp.int32, (nodes, cap), 0)
    slot_ids = lax.broadcasted_iota(jnp.int32, (nodes, cap), 1)
    for j in range(3):
        here = jnp.where(node_ids == snodes[j:j + 1, :], 1.0, 0.0)
        live = jnp.where(slot_ids < scount[0, j], 1.0, 0.0)
        hot = here * live
        give[:, j * cap:(j + 1) * cap] = hot.astype(BF)
        pick[j * cap:(j + 1) * cap, :] = hot.T.astype(BF)
    wacc[...] = jnp.zeros_like(wacc)
    dacc[...] = jnp.zeros_like(dacc)
    bacc[...] = jnp.zeros_like(bacc)
    cacc[...] = jnp.zeros_like(cacc)
    red1[...] = jnp.zeros_like(red1)
    red2[...] = jnp.zeros_like(red2)
    ones = jnp.ones((8, nodes), BF)

    def arrived(e, c):
        for j in range(3):
            halo_copy(e, c, j).wait_recv()
        return rcv[e, c].reshape(3 * cap, WIDE)

    def back_two(c, _):
        got = arrived(0, c)
        up = (acc[c] + mm(give[...], got)).astype(BF)
        put(2, c, mm(ops_b[nodes:, :], up).astype(BF))
        acc[c] = mm(ops_b[:nodes, :], up) + mm_nt(cot[c], wblk[4])
        return 0

    lax.fori_loop(0, chunks, back_two, 0)

    bf2 = jnp.concatenate([bf[...], bf[...]], axis=1)
    bg2 = jnp.concatenate([bg[...], bg[...]], axis=1)
    bd2 = jnp.concatenate([bd[...], bd[...]], axis=1)

    def fore_one(c, _):
        @pl.when(t > 0)
        def _():
            series_copy(c).wait_recv()

        before, now = prev[c], ser[c]
        a = jnp.tanh(mm(before, wblk[0]) + mm(now, wblk[1]) + bf2)
        act_f[c] = a
        s = jax.nn.sigmoid(mm(before, wblk[2]) + mm(now, wblk[3]) + bg2)
        act_g[c] = s
        h = (a * s).astype(BF)
        hid[c] = h
        put(1, c, mm(pick[...], h).astype(BF))
        return 0

    lax.fori_loop(0, chunks, fore_one, 0)

    def back_three(c, _):
        got = arrived(2, c)
        gh = acc[c] + mm(give[...], got)
        a, s = act_f[c], act_g[c]
        gf = (gh * s * (1.0 - a * a)).astype(BF)
        gg = (gh * a * (s * (1.0 - s))).astype(BF)
        delayed_out[c] = (mm_nt(gf, wblk[0]) + mm_nt(gg, wblk[2])).astype(BF)

        @pl.when(t > 0)
        def _():
            delayed_copy(c).start()

        g = cot[c]
        acc[c] = g.astype(F32) + mm_nt(gf, wblk[1]) + mm_nt(gg, wblk[3])
        before, now, h = prev[c], ser[c], hid[c]
        for i in range(2):
            lo, hi = i * ch, (i + 1) * ch
            right = jnp.concatenate([gf[:, lo:hi], gg[:, lo:hi]], axis=1)
            left = jnp.concatenate([before[:, lo:hi], now[:, lo:hi]], axis=1)
            wacc[...] += mm_tn(left, right)
            dacc[...] += mm_tn(h[:, lo:hi], g[:, lo:hi])
            bacc[...] += mm(ones, right)
            cacc[...] += mm(ones, g[:, lo:hi])
        return 0

    lax.fori_loop(0, chunks, back_three, 0)

    red1[0:256, :] = wacc[:, 0:128]
    red1[256:512, :] = wacc[:, 128:256]
    red1[512:640, :] = dacc[...]
    rid = lax.broadcasted_iota(jnp.int32, (8, 128), 0)
    red1[640:648, :] = jnp.where(
        rid == 0, bacc[:, 0:128], jnp.where(rid == 1, bacc[:, 128:256], cacc[...]))

    def all_sum(base, direct, red, rb, rc, sb, fin):
        part = red.shape[0] // crew

        def copy(src, dst, at, device):
            made = pltpu.make_async_remote_copy(
                src_ref=src, dst_ref=dst, send_sem=ar_s.at[at], recv_sem=ar_r.at[at],
                device_id=device, device_id_type=MESH)
            made.start()
            return made

        def rows(i):
            return pl.ds(pl.multiple_of(i * part, 8), part)

        sends = []
        for k in range(1, crew):
            o = lax.rem(me + k, crew)
            sends.append(copy(red.at[rows(o)], rb.at[k - 1], base + k, crew_device(o)))
        yield
        s = red[rows(me), :]
        for k in range(1, crew):
            sends[k - 1].wait()
            s = s + rb[k - 1]
        at = base + crew
        if direct:
            sb[0] = s
            rc[p] = s
            sends = [
                copy(sb.at[0], rc.at[p], at + k, {"seg": lax.rem(p + k, seg_n)})
                for k in range(1, seg_n)]
            yield
            for one in sends:
                one.wait()
            s = rc[0]
            for k in range(1, seg_n):
                s = s + rc[k]
        else:
            bit = 1
            for k in range(doublings):
                sb[k] = s
                mate = p + (1 - 2 * lax.rem(lax.div(p, bit), 2)) * bit
                one = copy(sb.at[k], rc.at[k], at + k, {"seg": mate})
                yield
                one.wait()
                s = s + rc[k]
                bit *= 2
        fin[rows(me), :] = s * scale
        at = at + seg_n
        sends = [
            copy(fin.at[rows(me)], fin.at[rows(me)], at + k, crew_device(lax.rem(me + k, crew)))
            for k in range(1, crew)]
        yield
        for one in sends:
            one.wait()
        yield

    first = all_sum(0, False, red1, rb1, rc1, sb1, fin1)
    next(first)
    def fore_two(c, _):
        got = arrived(1, c)
        h = (mm(ops_f[:, :nodes], hid[c]) + mm(ops_f[:, nodes:], got)).astype(BF)
        hop1[c] = h
        put(3, c, mm(pick[...], h).astype(BF))
        return 0

    for c in range(chunks):
        fore_two(c, 0)
        if c in (0, 1):
            next(first)

    for c in range(chunks):
        if c >= 2:
            next(first, None)
        got = arrived(3, c)
        h, h1, g = hid[c], hop1[c], cot[c]
        h2 = (mm(ops_f[:, :nodes], h1) + mm(ops_f[:, nodes:], got)).astype(BF)
        total = mm(h, wblk[4]) + mm(h1, wblk[5]) + mm(h2, wblk[6]) + bd2
        total = ser[c].astype(F32) + total
        for i in range(2):
            lo, hi = i * ch, (i + 1) * ch
            both = jnp.concatenate([h1[:, lo:hi], h2[:, lo:hi]], axis=1)
            red2[...] += mm_tn(both, g[:, lo:hi])
            big[:, 2 * c + i, :] = total[:, lo:hi]
    second = all_sum(2 * crew + seg_n, True, red2, rb2, rc2, sb2, fin2)
    next(second)
    out3[...] = big[...].astype(BF)
    next(second)
    for c in range(chunks):
        @pl.when(t < tm_n - 1)
        def _():
            delayed_copy(c).wait_recv()

        total = acc[c] + delayed_in[c].astype(F32)
        for i in range(2):
            big_g[:, 2 * c + i, :] = total[:, i * ch:(i + 1) * ch]
    next(second)
    gs3[...] = big_g[...].astype(BF)
    for _ in first:
        pass
    for _ in second:
        pass

    def drain(c, _):
        @pl.when(t < tm_n - 1)
        def _():
            series_copy(c).wait_send()

        @pl.when(t > 0)
        def _():
            delayed_copy(c).wait_send()

        for e in range(4):
            for j in range(3):
                halo_copy(e, c, j).wait_send()
        return 0

    lax.fori_loop(0, chunks, drain, 0)


def halo_plan(mesh, series, cotangent, w_filter, w_gate, b_filter, b_gate, w_diff, b_diff,
              tile_row, tile_col, tile_val, send_nodes, send_count):
    nodes, batch, frames, channels = series.shape
    seg_n, tm_n, rep_n = mesh.shape["seg"], mesh.shape["tm"], mesh.shape["rep"]
    chunks = batch * frames * channels // WIDE
    scale = 1.0 / math.sqrt(nodes * batch * frames * seg_n * tm_n * rep_n)
    unit = 16 * tm_n
    r1 = -(-648 // unit) * unit
    r2 = -(-256 // unit) * unit

    doublings = seg_n.bit_length() - 1
    vmem = pl.BlockSpec(memory_space=pltpu.VMEM)
    smem = pl.BlockSpec(memory_space=pltpu.SMEM)
    field = (chunks, nodes, WIDE)

    def sums(r):
        crew = 2 * tm_n
        q = r // crew
        return [
            pltpu.VMEM((crew - 1, q, 128), F32),
            pltpu.VMEM((seg_n, q, 128), F32),
            pltpu.VMEM((doublings, q, 128), F32),
        ]

    n_ar = 2 * (4 * tm_n + seg_n)
    raw = (nodes, batch * frames, channels)
    halo = (4, chunks, 3, 128, WIDE)
    out, gs, fin1, fin2 = pl.pallas_call(
        functools.partial(halo_kernel, seg_n, tm_n, scale),
        out_shape=(
            jax.ShapeDtypeStruct(raw, BF),
            jax.ShapeDtypeStruct(raw, BF),
            jax.ShapeDtypeStruct((r1, 128), F32),
            jax.ShapeDtypeStruct((r2, 128), F32),
        ),
        in_specs=[vmem] * 8 + [smem, smem, vmem, vmem, smem],
        out_specs=(vmem,) * 4,
        scratch_shapes=[
            pltpu.VMEM(raw, F32),
            pltpu.VMEM(raw, F32),
            pltpu.VMEM(field, BF),
            pltpu.VMEM(field, BF),
            pltpu.VMEM(field, BF),
            pltpu.VMEM((nodes, nodes + 384), BF),
            pltpu.VMEM((nodes + 384, nodes), BF),
            pltpu.VMEM((384, nodes), BF),
            pltpu.VMEM((nodes, 384), BF),
            pltpu.VMEM((7, WIDE, WIDE), BF),
            pltpu.VMEM(field, F32),
            pltpu.VMEM(field, F32),
            pltpu.VMEM(field, F32),
            pltpu.VMEM(field, BF),
            pltpu.VMEM(field, BF),
            pltpu.VMEM(field, BF),
            pltpu.VMEM(field, BF),
            pltpu.VMEM(halo, BF),
            pltpu.VMEM(halo, BF),
            pltpu.VMEM((256, 256), F32),
            pltpu.VMEM((128, 128), F32),
            pltpu.VMEM((8, 256), F32),
            pltpu.VMEM((8, 128), F32),
            pltpu.VMEM((r1, 128), F32),
            pltpu.VMEM((r2, 128), F32),
            *sums(r1),
            *sums(r2),
            pltpu.SemaphoreType.DMA((chunks,)),
            pltpu.SemaphoreType.DMA((chunks,)),
            pltpu.SemaphoreType.DMA((4, chunks, 3)),
            pltpu.SemaphoreType.DMA((4, chunks, 3)),
            pltpu.SemaphoreType.DMA((chunks,)),
            pltpu.SemaphoreType.DMA((chunks,)),
            pltpu.SemaphoreType.DMA((n_ar,)),
            pltpu.SemaphoreType.DMA((n_ar,)),
        ],
        compiler_params=pltpu.CompilerParams(
            collective_id=0, has_side_effects=True, vmem_limit_bytes=56 << 20),
    )(
        series.reshape(raw), cotangent.reshape(raw), w_filter, w_gate,
        b_filter.reshape(1, -1), b_gate.reshape(1, -1), w_diff, b_diff.reshape(1, -1),
        tile_row, tile_col, tile_val[0], send_nodes[0], send_count,
    )
    return (
        out.reshape(series.shape),
        gs.reshape(series.shape),
        fin1[0:256].reshape(2, 128, 128),
        fin1[256:512].reshape(2, 128, 128),
        fin1[640],
        fin1[641],
        jnp.concatenate([fin1[512:640], fin2[:256]], axis=0).reshape(3, 128, 128),
        fin1[642],
    )


def gather_kernel(
    seg_n, tm_n, scale,
    ser_h, cot_h, wf, wg, bf, bg, wd, bd, trow, tcol, tval_h, snodes, scount,
    out3, gs3, fin,
    ser3, cot3, tval, load, big, big_g, stage_s, stage_c, ser, cot, tiles, meta,
    opf, opb, oph, pick, wc, wct, wdt,
    act_f, act_g, src0, src1, hop2, sb0, sb1, acc,
    out_b, gs_b, out_r, gs_r, pair,
    red, rbuf0, rbuf1, rbuf2,
    tz_s, tz_r, mz_s, mz_r, tx_s, tx_r, tc_s, tc_r,
    se_s, se_r, co_s, co_r, ou_s, ou_r, gr_s, gr_r, ar_s, ar_r,
):
    p = lax.axis_index("seg")
    t = lax.axis_index("tm")
    rep = lax.axis_index("rep")
    loads = [
        pltpu.make_async_copy(src, dst, load.at[i])
        for i, (src, dst) in enumerate([(tval_h, tval), (ser_h, ser3), (cot_h, cot3)])]
    nodes, frames, ch = ser3.shape
    mine = p * tm_n + t
    crew = 2 * tm_n
    quarter = tiles.shape[1] // crew

    def rc(src, dst, ss, rs, dev):
        return pltpu.make_async_remote_copy(
            src_ref=src, dst_ref=dst, send_sem=ss, recv_sem=rs, device_id=dev, device_id_type=MESH)

    low, high = lax.rem(p, 2), lax.div(p, 2)

    def flip(j):
        return lax.rem(high + j // 2, 2) * 2 + lax.rem(low + j % 2, 2)

    def peer(j, m):
        return flip(j), lax.rem(t + m, tm_n)

    others = [(2, 0), (3, 0), (2, 1), (3, 1), (1, 0), (1, 1), (0, 1)]

    def rows_of(q):
        return pl.ds(pl.multiple_of(q * nodes, 128), nodes)

    def piece(c):
        return pl.ds(pl.multiple_of(c * quarter, 16), quarter)

    core = {"rep": 1 - rep}
    across = {"tm": 1 - t}

    barrier = pltpu.get_barrier_semaphore()
    for j, m in others:
        q, tt = peer(j, m)
        pl.semaphore_signal(barrier, inc=1, device_id={"seg": q, "tm": tt}, device_id_type=MESH)
    pl.semaphore_signal(barrier, inc=1, device_id=core, device_id_type=MESH)

    for one in loads:
        one.start()
    meta[p] = jnp.zeros_like(meta[p])
    for j in range(3):
        meta[p, j:j + 1, :] = snodes[j]
    meta[p, 3:4, 0:trow.shape[1]] = trow[...]
    meta[p, 4:5, 0:tcol.shape[1]] = tcol[...]
    meta[p, 5:6, 0:scount.shape[1]] = scount[...]
    pl.semaphore_wait(barrier, len(others) + 1)
    loads[0].wait()

    c_me = t * 2 + rep
    c_across = (1 - t) * 2 + rep

    def tile_z(j):
        return rc(tval.at[piece(c_me)], tiles.at[p, piece(c_me)], tz_s.at[j], tz_r.at[j], {"seg": flip(j)})

    def tile_on():
        at = tiles.at[flip(2), piece(c_me)]
        return rc(at, at, tz_s.at[3], tz_r.at[3], {"seg": flip(1)})

    def meta_z(j):
        return rc(meta.at[p], meta.at[p], mz_s.at[j], mz_r.at[j], {"seg": flip(j)})

    def tile_x(j):
        at = tiles.at[flip(j), piece(c_me)]
        return rc(at, at, tx_s.at[j], tx_r.at[j], across)

    def tile_c(j, c, i):
        at = tiles.at[flip(j), piece(c)]
        return rc(at, at, tc_s.at[j, i], tc_r.at[j, i], core)

    def field_in(stage, whole, ss, rs, j, m):
        q, tt = peer(j, m)
        f = q * tm_n + tt
        return rc(stage.at[f], whole.at[t, rows_of(p)], ss.at[f], rs.at[mine], {"seg": q, "tm": tt})

    def field_got(stage, whole, ss, rs, j, m):
        q, tt = peer(j, m)
        f = q * tm_n + tt
        return rc(stage.at[f], whole.at[tt, rows_of(q)], ss.at[f], rs.at[f], {"seg": q, "tm": tt})

    def frame_major(source, wide, stage, whole):
        wide[...] = source[...].astype(F32)
        for f in range(frames):
            stage[f] = wide[:, f, :].astype(BF)
        whole[t, rows_of(p), :] = stage[mine]

    tile_z(2).start()
    tile_z(1).start()
    for j in (2, 3, 1):
        meta_z(j).start()
    loads[1].wait()
    frame_major(ser3, big, stage_s, ser)
    field_in(stage_s, ser, se_s, se_r, 2, 0).start()
    tiles[p] = tval[...]

    tile_z(2).wait_recv()
    tile_on().start()
    tile_x(2).start()
    tile_z(1).wait_recv()
    tile_x(1).start()
    field_in(stage_s, ser, se_s, se_r, 3, 0).start()
    tile_on().wait_recv()
    tile_x(3).start()
    for j, m in others[2:]:
        field_in(stage_s, ser, se_s, se_r, j, m).start()

    loads[2].wait()
    frame_major(cot3, big_g, stage_c, cot)
    for j, m in others:
        field_in(stage_c, cot, co_s, co_r, j, m).start()

    for j in (2, 1, 3):
        tile_x(j).wait_recv()
        tile_c(j, c_me, 0).start()
        tile_c(j, c_across, 1).start()

    for i in range(2):
        wc[i * ch:(i + 1) * ch, 0:ch] = wf[i]
        wc[i * ch:(i + 1) * ch, ch:2 * ch] = wg[i]
    wct[...] = wc[...].astype(F32).T.astype(BF)
    for i in range(3):
        wdt[i] = wd[i].astype(F32).T.astype(BF)
    bias = jnp.concatenate([bf[...], bg[...]], axis=1)
    red[...] = jnp.zeros_like(red)

    for j in (2, 1, 3):
        tile_c(j, c_me, 0).wait_recv()
        tile_c(j, c_across, 1).wait_recv()
        meta_z(j).wait_recv()

    rows_n = nodes // 128
    cols_n = rows_n + 3
    tiles_n = tiles.shape[1] // 128
    halo = 3 * 128
    lane_ids = lax.broadcasted_iota(jnp.int32, (128, nodes), 1)
    sub_ids = lax.broadcasted_iota(jnp.int32, (nodes, 128), 0)
    slot_lane = lax.broadcasted_iota(jnp.int32, (1, 128), 1)
    slot_sub = lax.broadcasted_iota(jnp.int32, (128, 1), 0)

    def build(q, _):
        info = meta[q]
        tr, tc = info[3:4, :], info[4:5, :]
        t_all = [tiles[q, k * 128:(k + 1) * 128, :].astype(F32) for k in range(tiles_n)]
        for r in range(rows_n):
            for c in range(cols_n):
                hits = jnp.where((tr == r) & (tc == c), 1.0, 0.0)
                total = jnp.zeros((128, 128), F32)
                for k in range(tiles_n):
                    if k < rows_n and (r != k or c != k):
                        continue
                    if rows_n <= k < cols_n and c != k:
                        continue
                    total = total + hits[:, k:k + 1] * t_all[k]
                flipped = total.T.astype(BF)
                opf[q, r * 128:(r + 1) * 128, c * 128:(c + 1) * 128] = total.astype(BF)
                if c < rows_n:
                    opb[q, c * 128:(c + 1) * 128, r * 128:(r + 1) * 128] = flipped
                else:
                    oph[q, (c - rows_n) * 128:(c - rows_n + 1) * 128, r * 128:(r + 1) * 128] = flipped
        col = info.astype(F32).T.astype(jnp.int32)
        for j in range(3):
            count = info[5:6, j:j + 1]
            give = jnp.where((sub_ids == info[j:j + 1, :]) & (slot_lane < count), 1.0, 0.0)
            opb[q, :, nodes + j * 128:nodes + (j + 1) * 128] = give.astype(BF)
            take = jnp.where((lane_ids == col[:, j:j + 1]) & (slot_sub < count), 1.0, 0.0)
            pick[q, j * 128:(j + 1) * 128, :] = take.astype(BF)
        return 0

    lax.fori_loop(0, seg_n, build, 0)

    for j, m in others:
        field_got(stage_s, ser, se_s, se_r, j, m).wait_recv()

    def conv(q, _):
        for tt in range(tm_n):
            now = ser[tt, rows_of(q), :]
            if tt == 0:
                pre = mm(now, wc[ch:2 * ch, :]) + bias
            else:
                pre = mm(jnp.concatenate([ser[tt - 1, rows_of(q), :], now], axis=1), wc[...]) + bias
            a = jnp.tanh(pre[:, 0:ch])
            s = jax.nn.sigmoid(pre[:, ch:2 * ch])
            act_f[tt, rows_of(q), :] = a
            act_g[tt, rows_of(q), :] = s
            src0[q, 0:nodes, tt * ch:(tt + 1) * ch] = (a * s).astype(BF)
        return 0

    def send_slots(src):
        def one(q, _):
            got = mm(pick[q], src[q, 0:nodes, :]).astype(BF)
            for j in range(3):
                reader = lax.rem(q - STEPS[j] + seg_n, seg_n)
                src[reader, nodes + j * 128:nodes + (j + 1) * 128, :] = got[j * 128:(j + 1) * 128]
            return 0
        lax.fori_loop(0, seg_n, one, 0)

    def hop(src, dst):
        def one(q, _):
            dst[q, 0:nodes, :] = mm(opf[q], src[q]).astype(BF)
            return 0
        lax.fori_loop(0, seg_n, one, 0)

    def home(buf, got, ss, rs, q, tt):
        return rc(buf.at[tt, rows_of(q)], got.at[mine], ss.at[q * tm_n + tt], rs.at[mine], {"seg": q, "tm": tt})

    def gs_arrived(f):
        for h in range(2):
            rc(gs_b.at[f % tm_n, pl.ds(f // tm_n * nodes + h * part, part)], gs_r.at[f, pl.ds(h * part, part)],
               gr_s.at[f, h], gr_r.at[f, h], {"seg": f // tm_n, "tm": f % tm_n}).wait_recv()

    def out_arrived(f):
        arrived(out_b, out_r, ou_s, ou_r, f).wait_recv()

    def arrived(buf, got, ss, rs, f):
        return rc(buf.at[f % tm_n, pl.ds(f // tm_n * nodes, nodes)], got.at[f], ss.at[f], rs.at[f],
                  {"seg": f // tm_n, "tm": f % tm_n})

    def out_go(*pairs):
        for j, m in pairs:
            q, tt = peer(j, m)
            home(out_b, out_r, ou_s, ou_r, q, tt).start()

    part = nodes // 2

    def gs_half(q, tt, h):
        start = pl.ds(pl.multiple_of(q * nodes + h * part, 16), part)
        return rc(gs_b.at[tt, start], gs_r.at[mine, pl.ds(h * part, part)],
                  gr_s.at[q * tm_n + tt, h], gr_r.at[mine, h], {"seg": q, "tm": tt})

    def gs_go(*pairs):
        for j, m, h in pairs:
            q, tt = peer(j, m)
            gs_half(q, tt, h).start()

    lax.fori_loop(0, seg_n, conv, 0)
    send_slots(src0)
    hop(src0, src1)
    send_slots(src1)
    hop(src1, hop2)
    bias_d = bd[...]

    def put_out(q, _):
        for tt in range(tm_n):
            lo, hi = tt * ch, (tt + 1) * ch
            two = jnp.concatenate([src0[q, 0:nodes, lo:hi], src1[q, 0:nodes, lo:hi]], axis=1)
            total = mm(two, jnp.concatenate([wd[0], wd[1]], axis=0)) + mm(hop2[q, :, lo:hi], wd[2]) + bias_d
            out_b[tt, rows_of(q), :] = (ser[tt, rows_of(q), :].astype(F32) + total).astype(BF)
        return 0

    lax.fori_loop(0, seg_n, put_out, 0)
    out_go((2, 1), (1, 1), (3, 1), (1, 0), (0, 1))

    for j, m in others:
        field_got(stage_c, cot, co_s, co_r, j, m).wait_recv()

    def back(q, _):
        for tt in range(tm_n):
            lo, hi = tt * ch, (tt + 1) * ch
            g = cot[tt, rows_of(q), :]
            u = mm(g, jnp.concatenate([wdt[2], wdt[1]], axis=1))
            sb0[q, 0:nodes, lo:hi] = u[:, 0:ch].astype(BF)
            acc[q, :, lo:hi] = u[:, ch:2 * ch]
        return 0

    def send_back(sb):
        def one(q, _):
            got = mm(oph[q], sb[q, 0:nodes, :]).astype(BF)
            for j in range(3):
                owner = lax.rem(q + STEPS[j] + seg_n, seg_n)
                sb[owner, nodes + j * 128:nodes + (j + 1) * 128, :] = got[j * 128:(j + 1) * 128]
            return 0
        lax.fori_loop(0, seg_n, one, 0)

    lax.fori_loop(0, seg_n, back, 0)
    send_back(sb0)

    def back_mid(q, _):
        sb1[q, 0:nodes, :] = (acc[q] + mm(opb[q], sb0[q])).astype(BF)
        return 0

    lax.fori_loop(0, seg_n, back_mid, 0)
    out_go((2, 0),)
    send_back(sb1)

    def back_last(q, _):
        gh_all = mm(opb[q], sb1[q])
        for tt in range(tm_n):
            lo, hi = tt * ch, (tt + 1) * ch
            g = cot[tt, rows_of(q), :]
            gh = gh_all[:, lo:hi] + mm(g, wdt[0])
            a, s = act_f[tt, rows_of(q), :], act_g[tt, rows_of(q), :]
            gf = (gh * s * (1.0 - a * a)).astype(BF)
            gg = (gh * a * (s * (1.0 - s))).astype(BF)
            both = jnp.concatenate([gf, gg], axis=1)
            pair[tt, rows_of(q), :] = both
            now = ser[tt, rows_of(q), :]
            if tt == 0:
                part = mm_tn(now, both)
                red[ch:2 * ch, :] += part[:, 0:ch]
                red[3 * ch:4 * ch, :] += part[:, ch:2 * ch]
            else:
                part = mm_tn(jnp.concatenate([ser[tt - 1, rows_of(q), :], now], axis=1), both)
                red[0:2 * ch, :] += part[:, 0:ch]
                red[2 * ch:4 * ch, :] += part[:, ch:2 * ch]
            hops = jnp.concatenate(
                [src0[q, 0:nodes, lo:hi], src1[q, 0:nodes, lo:hi], hop2[q, :, lo:hi]], axis=1)
            red[4 * ch:7 * ch, :] += mm_tn(hops, g)
            base = 7 * ch
            red[base:base + 1, :] += jnp.sum(gf.astype(F32), axis=0, keepdims=True)
            red[base + 1:base + 2, :] += jnp.sum(gg.astype(F32), axis=0, keepdims=True)
            red[base + 2:base + 3, :] += jnp.sum(g.astype(F32), axis=0, keepdims=True)
        return 0

    lax.fori_loop(0, seg_n, back_last, 0)

    half = red.shape[0] // 2
    eighth = half // 4

    def span(start, size):
        return pl.ds(pl.multiple_of(start, 8), size)

    def go(src, dst, at, dev):
        made = rc(src, dst, ar_s.at[at], ar_r.at[at], dev)
        made.start()
        return made

    at_core = rep * half

    def at_quad(m, k):
        return at_core + lax.rem(t + m, 2) * (2 * eighth) + lax.rem(low + k, 2) * eighth

    def quad_device(m, k):
        return {"seg": flip(k), "tm": lax.rem(t + m, 2)}

    quad = [(1, 1), (1, 0), (0, 1)]
    here = span(at_quad(0, 0), eighth)
    step = go(red.at[span((1 - rep) * half, half)], rbuf0, 0, core)
    out_go((3, 0),)

    def put_gs(q, _):
        later = None
        for tt in reversed(range(tm_n)):
            both = pair[tt, rows_of(q), :]
            if tt == 0:
                total = mm(both, wct[:, ch:2 * ch])
            else:
                r = mm(both, wct[...])
                total = r[:, ch:2 * ch]
            total = cot[tt, rows_of(q), :].astype(F32) + total
            if later is not None:
                total = total + later.astype(F32)
            if tt > 0:
                later = r[:, 0:ch].astype(BF)
            gs_b[tt, rows_of(q), :] = total.astype(BF)
        return 0

    lax.fori_loop(0, seg_n, put_gs, 0)
    step.wait()
    red[span(at_core, half), :] += rbuf0[...]
    steps = [
        go(red.at[span(at_quad(m, k), eighth)], rbuf1.at[i], 1 + i, quad_device(m, k))
        for i, (m, k) in enumerate(quad)]
    gs_go((2, 0, 0),)
    out_r[mine] = out_b[t, rows_of(p), :]
    gs_r[mine] = gs_b[t, rows_of(p), :]

    def node_major(got, wide, dest, ready):
        for f in range(frames):
            @pl.when(f != mine)
            def _():
                ready(f)

            wide[:, f, :] = got[f].astype(F32)
        dest[...] = wide[...].astype(BF)

    for step in steps:
        step.wait()
    red[here, :] += rbuf1[0] + rbuf1[1] + rbuf1[2]
    step = go(red.at[here], rbuf2, 4, {"seg": flip(2)})
    gs_go((2, 1, 0), (1, 1, 0), (2, 1, 1), (1, 1, 1), (2, 0, 1))
    node_major(out_r, big, out3, out_arrived)
    step.wait()
    fin[here, :] = (red[here, :] + rbuf2[...]) * scale
    steps = [
        go(fin.at[here], fin.at[here], 5 + i, quad_device(m, k)) for i, (m, k) in enumerate(quad)]
    gs_go((3, 1, 0), (1, 0, 0), (3, 1, 1), (1, 0, 1), (3, 0, 0), (0, 1, 0), (3, 0, 1), (0, 1, 1))
    for step in steps:
        step.wait()
    whole = fin.at[span(at_core, half)]
    step = go(whole, whole, 8, core)
    node_major(gs_r, big_g, gs3, gs_arrived)
    step.wait()

    tile_z(2).wait_send()
    tile_z(1).wait_send()
    tile_on().wait_send()
    for j in (1, 2, 3):
        meta_z(j).wait_send()
        tile_x(j).wait_send()
        tile_c(j, c_me, 0).wait_send()
        tile_c(j, c_across, 1).wait_send()
    for j, m in others:
        q, tt = peer(j, m)
        field_in(stage_s, ser, se_s, se_r, j, m).wait_send()
        field_in(stage_c, cot, co_s, co_r, j, m).wait_send()
        home(out_b, out_r, ou_s, ou_r, q, tt).wait_send()
        gs_half(q, tt, 0).wait_send()
        gs_half(q, tt, 1).wait_send()


def finish_kernel(out_i, gs_i, fin, out_o, gs_o, o_wf, o_wg, o_bf, o_bg, o_wd, o_bd, sems):
    ch = o_wf.shape[1]
    pairs = [(out_i, out_o), (gs_i, gs_o)]
    for i in range(7):
        target = o_wf.at[i] if i < 2 else o_wg.at[i - 2] if i < 4 else o_wd.at[i - 4]
        pairs.append((fin.at[pl.ds(i * ch, ch)], target))
    copies = [pltpu.make_async_copy(src, dst, sems.at[i]) for i, (src, dst) in enumerate(pairs)]
    for one in copies:
        one.start()
    o_bf[...] = fin[7 * ch:7 * ch + 1, :]
    o_bg[...] = fin[7 * ch + 1:7 * ch + 2, :]
    o_bd[...] = fin[7 * ch + 2:7 * ch + 3, :]
    for one in copies:
        one.wait()


def gather_plan(mesh, series, cotangent, w_filter, w_gate, b_filter, b_gate, w_diff, b_diff,
                tile_row, tile_col, tile_val, send_nodes, send_count):
    nodes, batch, frames, ch = series.shape
    seg_n, tm_n, rep_n = mesh.shape["seg"], mesh.shape["tm"], mesh.shape["rep"]
    scale = 1.0 / math.sqrt(nodes * batch * frames * seg_n * tm_n * rep_n)
    unit = 8 * 2 * tm_n * seg_n
    total_rows = -(-(7 * ch + 8) // unit) * unit
    vmem = pl.BlockSpec(memory_space=pltpu.VMEM)
    anyw = pl.BlockSpec(memory_space=pl.ANY)
    raw = (nodes, batch * frames, ch)
    tall = (frames, nodes, ch)
    everyone = (tm_n, seg_n * nodes, ch)
    wide = tm_n * ch
    tile_rows = tile_val.shape[1] * 128
    halo = 3 * 128
    dma = pltpu.SemaphoreType.DMA
    half = total_rows // 2
    out, gs, fin = pl.pallas_call(
        functools.partial(gather_kernel, seg_n, tm_n, scale),
        out_shape=(
            pltpu.VMEM(raw, BF),
            pltpu.VMEM(raw, BF),
            pltpu.VMEM((total_rows, ch), F32),
        ),
        in_specs=[anyw] * 2 + [vmem] * 8 + [anyw] + [vmem] * 2,
        out_specs=(vmem,) * 3,
        scratch_shapes=[
            pltpu.VMEM(raw, BF),
            pltpu.VMEM(raw, BF),
            pltpu.VMEM((tile_rows, 128), BF),
            dma((3,)),
            pltpu.VMEM(raw, F32),
            pltpu.VMEM(raw, F32),
            pltpu.VMEM(tall, BF),
            pltpu.VMEM(tall, BF),
            pltpu.VMEM(everyone, BF),
            pltpu.VMEM(everyone, BF),
            pltpu.VMEM((seg_n, tile_rows, 128), BF),
            pltpu.VMEM((seg_n, 8, 128), jnp.int32),
            pltpu.VMEM((seg_n, nodes, nodes + halo), BF),
            pltpu.VMEM((seg_n, nodes, nodes + halo), BF),
            pltpu.VMEM((seg_n, halo, nodes), BF),
            pltpu.VMEM((seg_n, halo, nodes), BF),
            pltpu.VMEM((2 * ch, 2 * ch), BF),
            pltpu.VMEM((2 * ch, 2 * ch), BF),
            pltpu.VMEM((3, ch, ch), BF),
            pltpu.VMEM(everyone, F32),
            pltpu.VMEM(everyone, F32),
            pltpu.VMEM((seg_n, nodes + halo, wide), BF),
            pltpu.VMEM((seg_n, nodes + halo, wide), BF),
            pltpu.VMEM((seg_n, nodes, wide), BF),
            pltpu.VMEM((seg_n, nodes + halo, wide), BF),
            pltpu.VMEM((seg_n, nodes + halo, wide), BF),
            pltpu.VMEM((seg_n, nodes, wide), F32),
            pltpu.VMEM(everyone, BF),
            pltpu.VMEM(everyone, BF),
            pltpu.VMEM(tall, BF),
            pltpu.VMEM(tall, BF),
            pltpu.VMEM((tm_n, seg_n * nodes, 2 * ch), BF),
            pltpu.VMEM((total_rows, ch), F32),
            pltpu.VMEM((half, ch), F32),
            pltpu.VMEM((3, half // 4, ch), F32),
            pltpu.VMEM((half // 4, ch), F32),
            dma((seg_n,)), dma((seg_n,)), dma((seg_n,)), dma((seg_n,)),
            dma((seg_n,)), dma((seg_n,)), dma((seg_n, 2)), dma((seg_n, 2)),
            dma((frames,)), dma((frames,)), dma((frames,)), dma((frames,)),
            dma((frames,)), dma((frames,)), dma((frames, 2)), dma((frames, 2)),
            dma((9,)), dma((9,)),
        ],
        compiler_params=pltpu.CompilerParams(
            collective_id=0, has_side_effects=True, vmem_limit_bytes=52 << 20),
    )(
        series.reshape(raw), cotangent.reshape(raw), w_filter, w_gate,
        b_filter.reshape(1, -1), b_gate.reshape(1, -1), w_diff, b_diff.reshape(1, -1),
        tile_row, tile_col, tile_val.reshape(tile_rows, 128), send_nodes.reshape(3, 1, 128), send_count,
    )
    vec = jax.ShapeDtypeStruct((1, ch), F32)
    out, gs, g_wf, g_wg, g_bf, g_bg, g_wd, g_bd = pl.pallas_call(
        finish_kernel,
        out_shape=(
            jax.ShapeDtypeStruct(raw, BF),
            jax.ShapeDtypeStruct(raw, BF),
            jax.ShapeDtypeStruct((2, ch, ch), F32),
            jax.ShapeDtypeStruct((2, ch, ch), F32),
            vec, vec,
            jax.ShapeDtypeStruct((3, ch, ch), F32),
            vec,
        ),
        in_specs=[anyw, anyw, vmem],
        out_specs=(anyw, anyw, anyw, anyw, vmem, vmem, anyw, vmem),
        scratch_shapes=[dma((9,))],
    )(*[pltpu.with_memory_space_constraint(x, pltpu.VMEM) for x in (out, gs, fin)])
    return (
        out.reshape(series.shape), gs.reshape(series.shape), g_wf, g_wg,
        g_bf.reshape(-1), g_bg.reshape(-1), g_wd, g_bd.reshape(-1))


def on_device(mesh, series, *rest):
    nodes, batch, frames, ch = series.shape
    seg_n, tm_n = mesh.shape["seg"], mesh.shape["tm"]
    fits = seg_n == 4 and tm_n == 2 and batch == 1 and frames == seg_n * tm_n and frames == DILATION_FRAMES
    plan = gather_plan if fits else halo_plan
    return plan(mesh, series, *rest)


def solution(mesh):
    field = P(("grp", "seg"), "rep", "tm", None)
    part = ("grp", "seg")
    in_specs = (
        field, field, P(), P(), P(), P(), P(), P(),
        P(part, None), P(part, None), P(part, None, None, None), P(part, None, None), P(part, None),
    )
    out_specs = (
        field, field, P("grp", None, None), P("grp", None, None), P("grp"), P("grp"),
        P("grp", None, None), P("grp"),
    )
    return jax.shard_map(
        functools.partial(on_device, mesh), mesh=mesh, in_specs=in_specs, out_specs=out_specs,
        check_vma=False)
```

```python
import functools
import math

import jax
import jax.numpy as jnp
from jax import lax
from jax.experimental import pallas as pl
from jax.experimental.pallas import tpu as pltpu
from jax.sharding import PartitionSpec as P

DILATION_FRAMES = 8
STEPS = (1, -1, 2)
MESH = pl.DeviceIdType.MESH
WIDE = 256
BF = jnp.bfloat16
F32 = jnp.float32


def mm(a, b):
    return lax.dot_general(a, b, (((1,), (0,)), ((), ())), preferred_element_type=F32)


def mm_nt(a, b):
    return lax.dot_general(a, b, (((1,), (1,)), ((), ())), preferred_element_type=F32)


def mm_tn(a, b):
    return lax.dot_general(a, b, (((0,), (0,)), ((), ())), preferred_element_type=F32)


def halo_kernel(
    seg_n, tm_n, scale,
    ser3, cot3, wf, wg, bf, bg, wd, bd, trow, tcol, tval, snodes, scount,
    out3, gs3, fin1, fin2,
    big, big_g, ser, cot, prev, ops_f, ops_b, pick, give, wblk,
    acc, act_f, act_g, hid, hop1, delayed_out, delayed_in,
    snd, rcv, wacc, dacc, bacc, cacc,
    red1, red2, rb1, rc1, sb1, rb2, rc2, sb2,
    tm_s, tm_r, ex_s, ex_r, dl_s, dl_r, ar_s, ar_r,
):
    p = lax.axis_index("seg")
    t = lax.axis_index("tm")
    rep = lax.axis_index("rep")
    chunks, nodes, _ = ser.shape
    doublings = seg_n.bit_length() - 1
    cap = 128
    ch = 128

    barrier = pltpu.get_barrier_semaphore()
    for k in range(1, seg_n):
        pl.semaphore_signal(barrier, inc=1, device_id={"seg": lax.rem(p + k, seg_n)}, device_id_type=MESH)
    crew = 2 * tm_n
    me = t * 2 + rep

    def crew_device(i):
        return {"tm": lax.div(i, 2), "rep": lax.rem(i, 2)}

    for k in range(1, crew):
        pl.semaphore_signal(barrier, inc=1, device_id=crew_device(lax.rem(me + k, crew)), device_id_type=MESH)
    pl.semaphore_wait(barrier, seg_n - 1 + crew - 1)

    def series_copy(c):
        return pltpu.make_async_remote_copy(
            src_ref=ser.at[c], dst_ref=prev.at[c], send_sem=tm_s.at[c], recv_sem=tm_r.at[c],
            device_id={"tm": lax.rem(t + 1, tm_n)}, device_id_type=MESH)

    def delayed_copy(c):
        return pltpu.make_async_remote_copy(
            src_ref=delayed_out.at[c], dst_ref=delayed_in.at[c], send_sem=dl_s.at[c], recv_sem=dl_r.at[c],
            device_id={"tm": lax.rem(t + tm_n - 1, tm_n)}, device_id_type=MESH)

    def halo_copy(e, c, j):
        step = STEPS[j] if e % 2 == 0 else -STEPS[j]
        return pltpu.make_async_remote_copy(
            src_ref=snd.at[e, c, j], dst_ref=rcv.at[e, c, j],
            send_sem=ex_s.at[e, c, j], recv_sem=ex_r.at[e, c, j],
            device_id={"seg": lax.rem(p + step + seg_n, seg_n)}, device_id_type=MESH)

    def side_by_side(src, dst):
        big[...] = src[...].astype(F32)
        for c in range(chunks):
            dst[c] = jnp.concatenate([big[:, 2 * c, :], big[:, 2 * c + 1, :]], axis=1).astype(BF)

    side_by_side(cot3, cot)

    rows_n, cols_n, tiles_n = nodes // 128, nodes // 128 + 3, tval.shape[0]
    for r in range(rows_n):
        for c in range(cols_n):
            total = jnp.zeros((128, 128), F32)
            for k in range(tiles_n):
                if k < rows_n and (r != k or c != k):
                    continue
                if rows_n <= k < cols_n and c != k:
                    continue
                hit = jnp.where(trow[0, k] == r, 1.0, 0.0) * jnp.where(tcol[0, k] == c, 1.0, 0.0)
                total = total + hit * tval[k].astype(F32)
            ops_f[r * 128:(r + 1) * 128, c * 128:(c + 1) * 128] = total.astype(BF)
            ops_b[c * 128:(c + 1) * 128, r * 128:(r + 1) * 128] = total.T.astype(BF)
    wblk[4:7] = jnp.zeros((3, WIDE, WIDE), BF)
    for i in range(2):
        lo, hi = i * ch, (i + 1) * ch
        for k in range(3):
            wblk[4 + k, lo:hi, lo:hi] = wd[k]

    def put(e, c, rows):
        for j in range(3):
            snd[e, c, j] = rows[j * cap:(j + 1) * cap]
            halo_copy(e, c, j).start()

    def back_one(c, _):
        g = cot[c]
        up = mm_nt(g, wblk[6]).astype(BF)
        put(0, c, mm(ops_b[nodes:, :], up).astype(BF))
        acc[c] = mm(ops_b[:nodes, :], up) + mm_nt(g, wblk[5])
        return 0

    lax.fori_loop(0, chunks, back_one, 0)

    side_by_side(ser3, ser)

    @pl.when(t < tm_n - 1)
    def _():
        for c in range(chunks):
            series_copy(c).start()

    @pl.when(t == 0)
    def _():
        prev[...] = jnp.zeros_like(prev)

    @pl.when(t == tm_n - 1)
    def _():
        delayed_in[...] = jnp.zeros_like(delayed_in)

    wblk[0:4] = jnp.zeros((4, WIDE, WIDE), BF)
    for i in range(2):
        lo, hi = i * ch, (i + 1) * ch
        for k in range(2):
            wblk[k, lo:hi, lo:hi] = wf[k]
            wblk[2 + k, lo:hi, lo:hi] = wg[k]

    node_ids = lax.broadcasted_iota(jnp.int32, (nodes, cap), 0)
    slot_ids = lax.broadcasted_iota(jnp.int32, (nodes, cap), 1)
    for j in range(3):
        here = jnp.where(node_ids == snodes[j:j + 1, :], 1.0, 0.0)
        live = jnp.where(slot_ids < scount[0, j], 1.0, 0.0)
        hot = here * live
        give[:, j * cap:(j + 1) * cap] = hot.astype(BF)
        pick[j * cap:(j + 1) * cap, :] = hot.T.astype(BF)
    wacc[...] = jnp.zeros_like(wacc)
    dacc[...] = jnp.zeros_like(dacc)
    bacc[...] = jnp.zeros_like(bacc)
    cacc[...] = jnp.zeros_like(cacc)
    red1[...] = jnp.zeros_like(red1)
    red2[...] = jnp.zeros_like(red2)
    ones = jnp.ones((8, nodes), BF)

    def arrived(e, c):
        for j in range(3):
            halo_copy(e, c, j).wait_recv()
        return rcv[e, c].reshape(3 * cap, WIDE)

    def back_two(c, _):
        got = arrived(0, c)
        up = (acc[c] + mm(give[...], got)).astype(BF)
        put(2, c, mm(ops_b[nodes:, :], up).astype(BF))
        acc[c] = mm(ops_b[:nodes, :], up) + mm_nt(cot[c], wblk[4])
        return 0

    lax.fori_loop(0, chunks, back_two, 0)

    bf2 = jnp.concatenate([bf[...], bf[...]], axis=1)
    bg2 = jnp.concatenate([bg[...], bg[...]], axis=1)
    bd2 = jnp.concatenate([bd[...], bd[...]], axis=1)

    def fore_one(c, _):
        @pl.when(t > 0)
        def _():
            series_copy(c).wait_recv()

        before, now = prev[c], ser[c]
        a = jnp.tanh(mm(before, wblk[0]) + mm(now, wblk[1]) + bf2)
        act_f[c] = a
        s = jax.nn.sigmoid(mm(before, wblk[2]) + mm(now, wblk[3]) + bg2)
        act_g[c] = s
        h = (a * s).astype(BF)
        hid[c] = h
        put(1, c, mm(pick[...], h).astype(BF))
        return 0

    lax.fori_loop(0, chunks, fore_one, 0)

    def back_three(c, _):
        got = arrived(2, c)
        gh = acc[c] + mm(give[...], got)
        a, s = act_f[c], act_g[c]
        gf = (gh * s * (1.0 - a * a)).astype(BF)
        gg = (gh * a * (s * (1.0 - s))).astype(BF)
        delayed_out[c] = (mm_nt(gf, wblk[0]) + mm_nt(gg, wblk[2])).astype(BF)

        @pl.when(t > 0)
        def _():
            delayed_copy(c).start()

        g = cot[c]
        acc[c] = g.astype(F32) + mm_nt(gf, wblk[1]) + mm_nt(gg, wblk[3])
        before, now, h = prev[c], ser[c], hid[c]
        for i in range(2):
            lo, hi = i * ch, (i + 1) * ch
            right = jnp.concatenate([gf[:, lo:hi], gg[:, lo:hi]], axis=1)
            left = jnp.concatenate([before[:, lo:hi], now[:, lo:hi]], axis=1)
            wacc[...] += mm_tn(left, right)
            dacc[...] += mm_tn(h[:, lo:hi], g[:, lo:hi])
            bacc[...] += mm(ones, right)
            cacc[...] += mm(ones, g[:, lo:hi])
        return 0

    lax.fori_loop(0, chunks, back_three, 0)

    red1[0:256, :] = wacc[:, 0:128]
    red1[256:512, :] = wacc[:, 128:256]
    red1[512:640, :] = dacc[...]
    rid = lax.broadcasted_iota(jnp.int32, (8, 128), 0)
    red1[640:648, :] = jnp.where(
        rid == 0, bacc[:, 0:128], jnp.where(rid == 1, bacc[:, 128:256], cacc[...]))

    def all_sum(base, direct, red, rb, rc, sb, fin):
        part = red.shape[0] // crew

        def copy(src, dst, at, device):
            made = pltpu.make_async_remote_copy(
                src_ref=src, dst_ref=dst, send_sem=ar_s.at[at], recv_sem=ar_r.at[at],
                device_id=device, device_id_type=MESH)
            made.start()
            return made

        def rows(i):
            return pl.ds(pl.multiple_of(i * part, 8), part)

        sends = []
        for k in range(1, crew):
            o = lax.rem(me + k, crew)
            sends.append(copy(red.at[rows(o)], rb.at[k - 1], base + k, crew_device(o)))
        yield
        s = red[rows(me), :]
        for k in range(1, crew):
            sends[k - 1].wait()
            s = s + rb[k - 1]
        at = base + crew
        if direct:
            sb[0] = s
            rc[p] = s
            sends = [
                copy(sb.at[0], rc.at[p], at + k, {"seg": lax.rem(p + k, seg_n)})
                for k in range(1, seg_n)]
            yield
            for one in sends:
                one.wait()
            s = rc[0]
            for k in range(1, seg_n):
                s = s + rc[k]
        else:
            bit = 1
            for k in range(doublings):
                sb[k] = s
                mate = p + (1 - 2 * lax.rem(lax.div(p, bit), 2)) * bit
                one = copy(sb.at[k], rc.at[k], at + k, {"seg": mate})
                yield
                one.wait()
                s = s + rc[k]
                bit *= 2
        fin[rows(me), :] = s * scale
        at = at + seg_n
        sends = [
            copy(fin.at[rows(me)], fin.at[rows(me)], at + k, crew_device(lax.rem(me + k, crew)))
            for k in range(1, crew)]
        yield
        for one in sends:
            one.wait()
        yield

    first = all_sum(0, False, red1, rb1, rc1, sb1, fin1)
    next(first)
    def fore_two(c, _):
        got = arrived(1, c)
        h = (mm(ops_f[:, :nodes], hid[c]) + mm(ops_f[:, nodes:], got)).astype(BF)
        hop1[c] = h
        put(3, c, mm(pick[...], h).astype(BF))
        return 0

    for c in range(chunks):
        fore_two(c, 0)
        if c in (0, 1):
            next(first)

    for c in range(chunks):
        if c >= 2:
            next(first, None)
        got = arrived(3, c)
        h, h1, g = hid[c], hop1[c], cot[c]
        h2 = (mm(ops_f[:, :nodes], h1) + mm(ops_f[:, nodes:], got)).astype(BF)
        total = mm(h, wblk[4]) + mm(h1, wblk[5]) + mm(h2, wblk[6]) + bd2
        total = ser[c].astype(F32) + total
        for i in range(2):
            lo, hi = i * ch, (i + 1) * ch
            both = jnp.concatenate([h1[:, lo:hi], h2[:, lo:hi]], axis=1)
            red2[...] += mm_tn(both, g[:, lo:hi])
            big[:, 2 * c + i, :] = total[:, lo:hi]
    second = all_sum(2 * crew + seg_n, True, red2, rb2, rc2, sb2, fin2)
    next(second)
    out3[...] = big[...].astype(BF)
    next(second)
    for c in range(chunks):
        @pl.when(t < tm_n - 1)
        def _():
            delayed_copy(c).wait_recv()

        total = acc[c] + delayed_in[c].astype(F32)
        for i in range(2):
            big_g[:, 2 * c + i, :] = total[:, i * ch:(i + 1) * ch]
    next(second)
    gs3[...] = big_g[...].astype(BF)
    for _ in first:
        pass
    for _ in second:
        pass

    def drain(c, _):
        @pl.when(t < tm_n - 1)
        def _():
            series_copy(c).wait_send()

        @pl.when(t > 0)
        def _():
            delayed_copy(c).wait_send()

        for e in range(4):
            for j in range(3):
                halo_copy(e, c, j).wait_send()
        return 0

    lax.fori_loop(0, chunks, drain, 0)


def halo_plan(mesh, series, cotangent, w_filter, w_gate, b_filter, b_gate, w_diff, b_diff,
              tile_row, tile_col, tile_val, send_nodes, send_count):
    nodes, batch, frames, channels = series.shape
    seg_n, tm_n, rep_n = mesh.shape["seg"], mesh.shape["tm"], mesh.shape["rep"]
    chunks = batch * frames * channels // WIDE
    scale = 1.0 / math.sqrt(nodes * batch * frames * seg_n * tm_n * rep_n)
    unit = 16 * tm_n
    r1 = -(-648 // unit) * unit
    r2 = -(-256 // unit) * unit

    doublings = seg_n.bit_length() - 1
    vmem = pl.BlockSpec(memory_space=pltpu.VMEM)
    smem = pl.BlockSpec(memory_space=pltpu.SMEM)
    field = (chunks, nodes, WIDE)

    def sums(r):
        crew = 2 * tm_n
        q = r // crew
        return [
            pltpu.VMEM((crew - 1, q, 128), F32),
            pltpu.VMEM((seg_n, q, 128), F32),
            pltpu.VMEM((doublings, q, 128), F32),
        ]

    n_ar = 2 * (4 * tm_n + seg_n)
    raw = (nodes, batch * frames, channels)
    halo = (4, chunks, 3, 128, WIDE)
    out, gs, fin1, fin2 = pl.pallas_call(
        functools.partial(halo_kernel, seg_n, tm_n, scale),
        out_shape=(
            jax.ShapeDtypeStruct(raw, BF),
            jax.ShapeDtypeStruct(raw, BF),
            jax.ShapeDtypeStruct((r1, 128), F32),
            jax.ShapeDtypeStruct((r2, 128), F32),
        ),
        in_specs=[vmem] * 8 + [smem, smem, vmem, vmem, smem],
        out_specs=(vmem,) * 4,
        scratch_shapes=[
            pltpu.VMEM(raw, F32),
            pltpu.VMEM(raw, F32),
            pltpu.VMEM(field, BF),
            pltpu.VMEM(field, BF),
            pltpu.VMEM(field, BF),
            pltpu.VMEM((nodes, nodes + 384), BF),
            pltpu.VMEM((nodes + 384, nodes), BF),
            pltpu.VMEM((384, nodes), BF),
            pltpu.VMEM((nodes, 384), BF),
            pltpu.VMEM((7, WIDE, WIDE), BF),
            pltpu.VMEM(field, F32),
            pltpu.VMEM(field, F32),
            pltpu.VMEM(field, F32),
            pltpu.VMEM(field, BF),
            pltpu.VMEM(field, BF),
            pltpu.VMEM(field, BF),
            pltpu.VMEM(field, BF),
            pltpu.VMEM(halo, BF),
            pltpu.VMEM(halo, BF),
            pltpu.VMEM((256, 256), F32),
            pltpu.VMEM((128, 128), F32),
            pltpu.VMEM((8, 256), F32),
            pltpu.VMEM((8, 128), F32),
            pltpu.VMEM((r1, 128), F32),
            pltpu.VMEM((r2, 128), F32),
            *sums(r1),
            *sums(r2),
            pltpu.SemaphoreType.DMA((chunks,)),
            pltpu.SemaphoreType.DMA((chunks,)),
            pltpu.SemaphoreType.DMA((4, chunks, 3)),
            pltpu.SemaphoreType.DMA((4, chunks, 3)),
            pltpu.SemaphoreType.DMA((chunks,)),
            pltpu.SemaphoreType.DMA((chunks,)),
            pltpu.SemaphoreType.DMA((n_ar,)),
            pltpu.SemaphoreType.DMA((n_ar,)),
        ],
        compiler_params=pltpu.CompilerParams(
            collective_id=0, has_side_effects=True, vmem_limit_bytes=56 << 20),
    )(
        series.reshape(raw), cotangent.reshape(raw), w_filter, w_gate,
        b_filter.reshape(1, -1), b_gate.reshape(1, -1), w_diff, b_diff.reshape(1, -1),
        tile_row, tile_col, tile_val[0], send_nodes[0], send_count,
    )
    return (
        out.reshape(series.shape),
        gs.reshape(series.shape),
        fin1[0:256].reshape(2, 128, 128),
        fin1[256:512].reshape(2, 128, 128),
        fin1[640],
        fin1[641],
        jnp.concatenate([fin1[512:640], fin2[:256]], axis=0).reshape(3, 128, 128),
        fin1[642],
    )


def gather_kernel(
    seg_n, tm_n, scale,
    ser_h, cot_h, wf, wg, bf, bg, wd, bd, trow, tcol, tval_h, snodes, scount,
    out3, gs3, fin,
    ser3, cot3, tval, load, big, big_g, stage_s, stage_c, ser, cot, tiles, meta,
    opf, opb, oph, pick, wc, wct, wdt,
    act_f, act_g, src0, src1, hop2, sb0, sb1, acc,
    out_b, gs_b, out_r, gs_r, pair,
    red_a, red_b, low_a, low_b, a0, a1, a2, a3, b0, b1, b2, b3,
    tz_s, tz_r, mz_s, mz_r, tx_s, tx_r, tc_s, tc_r,
    se_s, se_r, co_s, co_r, ou_s, ou_r, gr_s, gr_r, ar_s, ar_r,
):
    p = lax.axis_index("seg")
    t = lax.axis_index("tm")
    rep = lax.axis_index("rep")
    loads = [
        pltpu.make_async_copy(src, dst, load.at[i])
        for i, (src, dst) in enumerate([(tval_h, tval), (ser_h, ser3), (cot_h, cot3)])]
    nodes, frames, ch = ser3.shape
    mine = p * tm_n + t
    crew = 2 * tm_n
    quarter = tiles.shape[1] // crew

    def rc(src, dst, ss, rs, dev):
        return pltpu.make_async_remote_copy(
            src_ref=src, dst_ref=dst, send_sem=ss, recv_sem=rs, device_id=dev, device_id_type=MESH)

    low, high = lax.rem(p, 2), lax.div(p, 2)

    def flip(j):
        return lax.rem(high + j // 2, 2) * 2 + lax.rem(low + j % 2, 2)

    def peer(j, m):
        return flip(j), lax.rem(t + m, tm_n)

    others = [(2, 0), (3, 0), (2, 1), (3, 1), (1, 0), (1, 1), (0, 1)]

    def rows_of(q):
        return pl.ds(pl.multiple_of(q * nodes, 128), nodes)

    def piece(c):
        return pl.ds(pl.multiple_of(c * quarter, 16), quarter)

    core = {"rep": 1 - rep}
    across = {"tm": 1 - t}

    barrier = pltpu.get_barrier_semaphore()
    for j, m in others:
        q, tt = peer(j, m)
        pl.semaphore_signal(barrier, inc=1, device_id={"seg": q, "tm": tt}, device_id_type=MESH)
    pl.semaphore_signal(barrier, inc=1, device_id=core, device_id_type=MESH)

    for one in loads:
        one.start()
    meta[p] = jnp.zeros_like(meta[p])
    for j in range(3):
        meta[p, j:j + 1, :] = snodes[j]
    meta[p, 3:4, 0:trow.shape[1]] = trow[...]
    meta[p, 4:5, 0:tcol.shape[1]] = tcol[...]
    meta[p, 5:6, 0:scount.shape[1]] = scount[...]
    pl.semaphore_wait(barrier, len(others) + 1)
    loads[0].wait()

    c_me = t * 2 + rep
    c_across = (1 - t) * 2 + rep

    def tile_z(j):
        return rc(tval.at[piece(c_me)], tiles.at[p, piece(c_me)], tz_s.at[j], tz_r.at[j], {"seg": flip(j)})

    def tile_on():
        at = tiles.at[flip(2), piece(c_me)]
        return rc(at, at, tz_s.at[3], tz_r.at[3], {"seg": flip(1)})

    def meta_z(j):
        return rc(meta.at[p], meta.at[p], mz_s.at[j], mz_r.at[j], {"seg": flip(j)})

    def tile_x(j):
        at = tiles.at[flip(j), piece(c_me)]
        return rc(at, at, tx_s.at[j], tx_r.at[j], across)

    def tile_c(j, c, i):
        at = tiles.at[flip(j), piece(c)]
        return rc(at, at, tc_s.at[j, i], tc_r.at[j, i], core)

    def field_in(stage, whole, ss, rs, j, m):
        q, tt = peer(j, m)
        f = q * tm_n + tt
        return rc(stage.at[f], whole.at[t, rows_of(p)], ss.at[f], rs.at[mine], {"seg": q, "tm": tt})

    def field_got(stage, whole, ss, rs, j, m):
        q, tt = peer(j, m)
        f = q * tm_n + tt
        return rc(stage.at[f], whole.at[tt, rows_of(q)], ss.at[f], rs.at[f], {"seg": q, "tm": tt})

    def frame_major(source, wide, stage, whole):
        wide[...] = source[...].astype(F32)
        for f in range(frames):
            stage[f] = wide[:, f, :].astype(BF)
        whole[t, rows_of(p), :] = stage[mine]

    tile_z(2).start()
    tile_z(1).start()
    for j in (2, 3, 1):
        meta_z(j).start()
    loads[1].wait()
    frame_major(ser3, big, stage_s, ser)
    field_in(stage_s, ser, se_s, se_r, 2, 0).start()
    tiles[p] = tval[...]

    tile_z(2).wait_recv()
    tile_on().start()
    tile_x(2).start()
    tile_z(1).wait_recv()
    tile_x(1).start()
    field_in(stage_s, ser, se_s, se_r, 3, 0).start()
    tile_on().wait_recv()
    tile_x(3).start()
    for j, m in others[2:]:
        field_in(stage_s, ser, se_s, se_r, j, m).start()

    loads[2].wait()
    frame_major(cot3, big_g, stage_c, cot)
    for j, m in others:
        field_in(stage_c, cot, co_s, co_r, j, m).start()

    for j in (2, 1, 3):
        tile_x(j).wait_recv()
        tile_c(j, c_me, 0).start()
        tile_c(j, c_across, 1).start()

    for i in range(2):
        wc[i * ch:(i + 1) * ch, 0:ch] = wf[i]
        wc[i * ch:(i + 1) * ch, ch:2 * ch] = wg[i]
    wct[...] = wc[...].astype(F32).T.astype(BF)
    for i in range(3):
        wdt[i] = wd[i].astype(F32).T.astype(BF)
    bias = jnp.concatenate([bf[...], bg[...]], axis=1)
    red_a[...] = jnp.zeros_like(red_a)
    red_b[...] = jnp.zeros_like(red_b)

    for j in (2, 1, 3):
        tile_c(j, c_me, 0).wait_recv()
        tile_c(j, c_across, 1).wait_recv()
        meta_z(j).wait_recv()

    rows_n = nodes // 128
    cols_n = rows_n + 3
    tiles_n = tiles.shape[1] // 128
    halo = 3 * 128
    lane_ids = lax.broadcasted_iota(jnp.int32, (128, nodes), 1)
    sub_ids = lax.broadcasted_iota(jnp.int32, (nodes, 128), 0)
    slot_lane = lax.broadcasted_iota(jnp.int32, (1, 128), 1)
    slot_sub = lax.broadcasted_iota(jnp.int32, (128, 1), 0)

    def build(q, _):
        info = meta[q]
        tr, tc = info[3:4, :], info[4:5, :]
        t_all = [tiles[q, k * 128:(k + 1) * 128, :].astype(F32) for k in range(tiles_n)]
        for r in range(rows_n):
            for c in range(cols_n):
                hits = jnp.where((tr == r) & (tc == c), 1.0, 0.0)
                total = jnp.zeros((128, 128), F32)
                for k in range(tiles_n):
                    if k < rows_n and (r != k or c != k):
                        continue
                    if rows_n <= k < cols_n and c != k:
                        continue
                    total = total + hits[:, k:k + 1] * t_all[k]
                flipped = total.T.astype(BF)
                opf[q, r * 128:(r + 1) * 128, c * 128:(c + 1) * 128] = total.astype(BF)
                if c < rows_n:
                    opb[q, c * 128:(c + 1) * 128, r * 128:(r + 1) * 128] = flipped
                else:
                    oph[q, (c - rows_n) * 128:(c - rows_n + 1) * 128, r * 128:(r + 1) * 128] = flipped
        col = info.astype(F32).T.astype(jnp.int32)
        for j in range(3):
            count = info[5:6, j:j + 1]
            give = jnp.where((sub_ids == info[j:j + 1, :]) & (slot_lane < count), 1.0, 0.0)
            opb[q, :, nodes + j * 128:nodes + (j + 1) * 128] = give.astype(BF)
            take = jnp.where((lane_ids == col[:, j:j + 1]) & (slot_sub < count), 1.0, 0.0)
            pick[q, j * 128:(j + 1) * 128, :] = take.astype(BF)
        return 0

    lax.fori_loop(0, seg_n, build, 0)

    for j, m in others:
        field_got(stage_s, ser, se_s, se_r, j, m).wait_recv()

    def conv(q, _):
        for tt in range(tm_n):
            now = ser[tt, rows_of(q), :]
            if tt == 0:
                pre = mm(now, wc[ch:2 * ch, :]) + bias
            else:
                pre = mm(jnp.concatenate([ser[tt - 1, rows_of(q), :], now], axis=1), wc[...]) + bias
            a = jnp.tanh(pre[:, 0:ch])
            s = jax.nn.sigmoid(pre[:, ch:2 * ch])
            act_f[tt, rows_of(q), :] = a
            act_g[tt, rows_of(q), :] = s
            src0[q, 0:nodes, tt * ch:(tt + 1) * ch] = (a * s).astype(BF)
        return 0

    def send_slots(src):
        def one(q, _):
            got = mm(pick[q], src[q, 0:nodes, :]).astype(BF)
            for j in range(3):
                reader = lax.rem(q - STEPS[j] + seg_n, seg_n)
                src[reader, nodes + j * 128:nodes + (j + 1) * 128, :] = got[j * 128:(j + 1) * 128]
            return 0
        lax.fori_loop(0, seg_n, one, 0)

    def hop(src, dst):
        def one(q, _):
            dst[q, 0:nodes, :] = mm(opf[q], src[q]).astype(BF)
            return 0
        lax.fori_loop(0, seg_n, one, 0)

    def home(buf, got, ss, rs, q, tt):
        return rc(buf.at[tt, rows_of(q)], got.at[mine], ss.at[q * tm_n + tt], rs.at[mine], {"seg": q, "tm": tt})

    def gs_arrived(f):
        for h in range(2):
            rc(gs_b.at[f % tm_n, pl.ds(f // tm_n * nodes + h * part, part)], gs_r.at[f, pl.ds(h * part, part)],
               gr_s.at[f, h], gr_r.at[f, h], {"seg": f // tm_n, "tm": f % tm_n}).wait_recv()

    def out_arrived(f):
        arrived(out_b, out_r, ou_s, ou_r, f).wait_recv()

    def arrived(buf, got, ss, rs, f):
        return rc(buf.at[f % tm_n, pl.ds(f // tm_n * nodes, nodes)], got.at[f], ss.at[f], rs.at[f],
                  {"seg": f // tm_n, "tm": f % tm_n})

    def out_go(*pairs):
        for j, m in pairs:
            q, tt = peer(j, m)
            home(out_b, out_r, ou_s, ou_r, q, tt).start()

    part = nodes // 2

    def gs_half(q, tt, h):
        start = pl.ds(pl.multiple_of(q * nodes + h * part, 16), part)
        return rc(gs_b.at[tt, start], gs_r.at[mine, pl.ds(h * part, part)],
                  gr_s.at[q * tm_n + tt, h], gr_r.at[mine, h], {"seg": q, "tm": tt})

    def gs_go(*pairs):
        for j, m, h in pairs:
            q, tt = peer(j, m)
            gs_half(q, tt, h).start()

    lax.fori_loop(0, seg_n, conv, 0)
    send_slots(src0)
    hop(src0, src1)
    send_slots(src1)
    hop(src1, hop2)
    bias_d = bd[...]

    def put_out(q, _):
        for tt in range(tm_n):
            lo, hi = tt * ch, (tt + 1) * ch
            two = jnp.concatenate([src0[q, 0:nodes, lo:hi], src1[q, 0:nodes, lo:hi]], axis=1)
            total = mm(two, jnp.concatenate([wd[0], wd[1]], axis=0)) + mm(hop2[q, :, lo:hi], wd[2]) + bias_d
            out_b[tt, rows_of(q), :] = (ser[tt, rows_of(q), :].astype(F32) + total).astype(BF)
        return 0

    lax.fori_loop(0, seg_n, put_out, 0)
    out_go((2, 1), (1, 1), (3, 1), (1, 0), (0, 1))

    for j, m in others:
        field_got(stage_c, cot, co_s, co_r, j, m).wait_recv()

    base = 4 * ch

    def span(start, size):
        return pl.ds(pl.multiple_of(start, 16), size)

    def quad_device(m, k):
        return {"seg": flip(k), "tm": lax.rem(t + m, 2)}

    def summed(red, b0, b1, b2, b3, low_out, first):
        half = red.shape[0] // 2
        eighth = half // 4
        at_core = rep * half

        def at_quad(m, k):
            return span(at_core + lax.rem(t + m, 2) * (2 * eighth) + lax.rem(low + k, 2) * eighth, eighth)

        def go(src, dst, at, dev):
            made = rc(src, dst, ar_s.at[first + at], ar_r.at[first + at], dev)
            made.start()
            return made

        quad = [(1, 1), (1, 0), (0, 1)]
        here = at_quad(0, 0)
        step = go(red.at[span((1 - rep) * half, half)], b0, 0, core)
        yield
        step.wait()
        red[span(at_core, half), :] += b0[...]
        steps = [
            go(red.at[at_quad(m, k)], b1.at[i], 1 + i, quad_device(m, k))
            for i, (m, k) in enumerate(quad)]
        yield
        for step in steps:
            step.wait()
        b3[...] = (red[here, :] + b1[0] + b1[1] + b1[2]).astype(BF)
        step = go(b3, b2, 4, {"seg": flip(2)})
        yield
        step.wait()
        low_out[here, :] = ((b3[...].astype(F32) + b2[...].astype(F32)) * scale).astype(BF)
        steps = [
            go(low_out.at[here], low_out.at[here], 5 + i, quad_device(m, k))
            for i, (m, k) in enumerate(quad)]
        yield
        for step in steps:
            step.wait()
        whole = low_out.at[span(at_core, half)]
        step = go(whole, whole, 8, core)
        yield
        step.wait()
        yield

    sum_a = summed(red_a, a0, a1, a2, a3, low_a, 0)
    sum_b = summed(red_b, b0, b1, b2, b3, low_b, 9)

    def back(q, _):
        for tt in range(tm_n):
            lo, hi = tt * ch, (tt + 1) * ch
            g = cot[tt, rows_of(q), :]
            u = mm(g, jnp.concatenate([wdt[2], wdt[1]], axis=1))
            sb0[q, 0:nodes, lo:hi] = u[:, 0:ch].astype(BF)
            acc[q, :, lo:hi] = u[:, ch:2 * ch]
            hops = jnp.concatenate(
                [src0[q, 0:nodes, lo:hi], src1[q, 0:nodes, lo:hi], hop2[q, :, lo:hi]], axis=1)
            red_a[...] += mm_tn(hops, g)
            red_b[base + 2:base + 3, :] += jnp.sum(g.astype(F32), axis=0, keepdims=True)
        return 0

    def send_back(sb):
        def one(q, _):
            got = mm(oph[q], sb[q, 0:nodes, :]).astype(BF)
            for j in range(3):
                owner = lax.rem(q + STEPS[j] + seg_n, seg_n)
                sb[owner, nodes + j * 128:nodes + (j + 1) * 128, :] = got[j * 128:(j + 1) * 128]
            return 0
        lax.fori_loop(0, seg_n, one, 0)

    lax.fori_loop(0, seg_n, back, 0)
    next(sum_a)
    send_back(sb0)

    def back_mid(q, _):
        sb1[q, 0:nodes, :] = (acc[q] + mm(opb[q], sb0[q])).astype(BF)
        return 0

    next(sum_a)
    lax.fori_loop(0, seg_n, back_mid, 0)
    out_go((2, 0), (3, 0))
    send_back(sb1)

    def back_last(q, _):
        gh_all = mm(opb[q], sb1[q])
        for tt in range(tm_n):
            lo, hi = tt * ch, (tt + 1) * ch
            g = cot[tt, rows_of(q), :]
            gh = gh_all[:, lo:hi] + mm(g, wdt[0])
            a, s = act_f[tt, rows_of(q), :], act_g[tt, rows_of(q), :]
            gf = (gh * s * (1.0 - a * a)).astype(BF)
            gg = (gh * a * (s * (1.0 - s))).astype(BF)
            both = jnp.concatenate([gf, gg], axis=1)
            pair[tt, rows_of(q), :] = both
            now = ser[tt, rows_of(q), :]
            if tt == 0:
                part = mm_tn(now, both)
                red_b[ch:2 * ch, :] += part[:, 0:ch]
                red_b[3 * ch:4 * ch, :] += part[:, ch:2 * ch]
            else:
                part = mm_tn(jnp.concatenate([ser[tt - 1, rows_of(q), :], now], axis=1), both)
                red_b[0:2 * ch, :] += part[:, 0:ch]
                red_b[2 * ch:4 * ch, :] += part[:, ch:2 * ch]
            red_b[base:base + 1, :] += jnp.sum(gf.astype(F32), axis=0, keepdims=True)
            red_b[base + 1:base + 2, :] += jnp.sum(gg.astype(F32), axis=0, keepdims=True)
        return 0

    lax.fori_loop(0, seg_n, back_last, 0)

    next(sum_b)
    next(sum_a)

    def put_gs(q, _):
        later = None
        for tt in reversed(range(tm_n)):
            both = pair[tt, rows_of(q), :]
            if tt == 0:
                total = mm(both, wct[:, ch:2 * ch])
            else:
                r = mm(both, wct[...])
                total = r[:, ch:2 * ch]
            total = cot[tt, rows_of(q), :].astype(F32) + total
            if later is not None:
                total = total + later.astype(F32)
            if tt > 0:
                later = r[:, 0:ch].astype(BF)
            gs_b[tt, rows_of(q), :] = total.astype(BF)
        return 0

    lax.fori_loop(0, seg_n, put_gs, 0)
    next(sum_b)
    gs_go((2, 0, 0),)
    out_r[mine] = out_b[t, rows_of(p), :]
    gs_r[mine] = gs_b[t, rows_of(p), :]

    def node_major(got, wide, dest, ready):
        for f in range(frames):
            @pl.when(f != mine)
            def _():
                ready(f)

            wide[:, f, :] = got[f].astype(F32)
        dest[...] = wide[...].astype(BF)

    next(sum_b)
    gs_go((2, 1, 0), (1, 1, 0), (2, 1, 1), (1, 1, 1), (2, 0, 1))
    next(sum_a)
    gs_go((3, 1, 0), (1, 0, 0), (3, 1, 1), (1, 0, 1), (3, 0, 0), (0, 1, 0), (3, 0, 1), (0, 1, 1))
    node_major(out_r, big, out3, out_arrived)
    next(sum_b)
    next(sum_a)
    next(sum_b)
    next(sum_a)
    fin[base:base + 3 * ch, :] = low_a[...].astype(F32)
    node_major(gs_r, big_g, gs3, gs_arrived)
    next(sum_b)
    fin[0:base, :] = low_b[0:base, :].astype(F32)
    fin[base + 3 * ch:base + 3 * ch + 16, :] = low_b[base:base + 16, :].astype(F32)

    tile_z(2).wait_send()
    tile_z(1).wait_send()
    tile_on().wait_send()
    for j in (1, 2, 3):
        meta_z(j).wait_send()
        tile_x(j).wait_send()
        tile_c(j, c_me, 0).wait_send()
        tile_c(j, c_across, 1).wait_send()
    for j, m in others:
        q, tt = peer(j, m)
        field_in(stage_s, ser, se_s, se_r, j, m).wait_send()
        field_in(stage_c, cot, co_s, co_r, j, m).wait_send()
        home(out_b, out_r, ou_s, ou_r, q, tt).wait_send()
        gs_half(q, tt, 0).wait_send()
        gs_half(q, tt, 1).wait_send()


def finish_kernel(out_i, gs_i, fin, out_o, gs_o, o_wf, o_wg, o_bf, o_bg, o_wd, o_bd, sems):
    ch = o_wf.shape[1]
    pairs = [(out_i, out_o), (gs_i, gs_o)]
    for i in range(7):
        target = o_wf.at[i] if i < 2 else o_wg.at[i - 2] if i < 4 else o_wd.at[i - 4]
        pairs.append((fin.at[pl.ds(i * ch, ch)], target))
    copies = [pltpu.make_async_copy(src, dst, sems.at[i]) for i, (src, dst) in enumerate(pairs)]
    for one in copies:
        one.start()
    o_bf[...] = fin[7 * ch:7 * ch + 1, :]
    o_bg[...] = fin[7 * ch + 1:7 * ch + 2, :]
    o_bd[...] = fin[7 * ch + 2:7 * ch + 3, :]
    for one in copies:
        one.wait()


def gather_plan(mesh, series, cotangent, w_filter, w_gate, b_filter, b_gate, w_diff, b_diff,
                tile_row, tile_col, tile_val, send_nodes, send_count):
    nodes, batch, frames, ch = series.shape
    seg_n, tm_n, rep_n = mesh.shape["seg"], mesh.shape["tm"], mesh.shape["rep"]
    scale = 1.0 / math.sqrt(nodes * batch * frames * seg_n * tm_n * rep_n)
    unit = 16 * 8
    rows_a = 3 * ch
    rows_b = -(-(4 * ch + 8) // unit) * unit
    total_rows = 7 * ch + 16

    def steps_of(rows):
        return [
            pltpu.VMEM((rows // 2, ch), F32),
            pltpu.VMEM((3, rows // 8, ch), F32),
            pltpu.VMEM((rows // 8, ch), BF),
            pltpu.VMEM((rows // 8, ch), BF),
        ]

    vmem = pl.BlockSpec(memory_space=pltpu.VMEM)
    anyw = pl.BlockSpec(memory_space=pl.ANY)
    raw = (nodes, batch * frames, ch)
    tall = (frames, nodes, ch)
    everyone = (tm_n, seg_n * nodes, ch)
    wide = tm_n * ch
    tile_rows = tile_val.shape[1] * 128
    halo = 3 * 128
    dma = pltpu.SemaphoreType.DMA
    out, gs, fin = pl.pallas_call(
        functools.partial(gather_kernel, seg_n, tm_n, scale),
        out_shape=(
            pltpu.VMEM(raw, BF),
            pltpu.VMEM(raw, BF),
            pltpu.VMEM((total_rows, ch), F32),
        ),
        in_specs=[anyw] * 2 + [vmem] * 8 + [anyw] + [vmem] * 2,
        out_specs=(vmem,) * 3,
        scratch_shapes=[
            pltpu.VMEM(raw, BF),
            pltpu.VMEM(raw, BF),
            pltpu.VMEM((tile_rows, 128), BF),
            dma((3,)),
            pltpu.VMEM(raw, F32),
            pltpu.VMEM(raw, F32),
            pltpu.VMEM(tall, BF),
            pltpu.VMEM(tall, BF),
            pltpu.VMEM(everyone, BF),
            pltpu.VMEM(everyone, BF),
            pltpu.VMEM((seg_n, tile_rows, 128), BF),
            pltpu.VMEM((seg_n, 8, 128), jnp.int32),
            pltpu.VMEM((seg_n, nodes, nodes + halo), BF),
            pltpu.VMEM((seg_n, nodes, nodes + halo), BF),
            pltpu.VMEM((seg_n, halo, nodes), BF),
            pltpu.VMEM((seg_n, halo, nodes), BF),
            pltpu.VMEM((2 * ch, 2 * ch), BF),
            pltpu.VMEM((2 * ch, 2 * ch), BF),
            pltpu.VMEM((3, ch, ch), BF),
            pltpu.VMEM(everyone, F32),
            pltpu.VMEM(everyone, F32),
            pltpu.VMEM((seg_n, nodes + halo, wide), BF),
            pltpu.VMEM((seg_n, nodes + halo, wide), BF),
            pltpu.VMEM((seg_n, nodes, wide), BF),
            pltpu.VMEM((seg_n, nodes + halo, wide), BF),
            pltpu.VMEM((seg_n, nodes + halo, wide), BF),
            pltpu.VMEM((seg_n, nodes, wide), F32),
            pltpu.VMEM(everyone, BF),
            pltpu.VMEM(everyone, BF),
            pltpu.VMEM(tall, BF),
            pltpu.VMEM(tall, BF),
            pltpu.VMEM((tm_n, seg_n * nodes, 2 * ch), BF),
            pltpu.VMEM((rows_a, ch), F32),
            pltpu.VMEM((rows_b, ch), F32),
            pltpu.VMEM((rows_a, ch), BF),
            pltpu.VMEM((rows_b, ch), BF),
            *steps_of(rows_a),
            *steps_of(rows_b),
            dma((seg_n,)), dma((seg_n,)), dma((seg_n,)), dma((seg_n,)),
            dma((seg_n,)), dma((seg_n,)), dma((seg_n, 2)), dma((seg_n, 2)),
            dma((frames,)), dma((frames,)), dma((frames,)), dma((frames,)),
            dma((frames,)), dma((frames,)), dma((frames, 2)), dma((frames, 2)),
            dma((18,)), dma((18,)),
        ],
        compiler_params=pltpu.CompilerParams(
            collective_id=0, has_side_effects=True, vmem_limit_bytes=52 << 20),
    )(
        series.reshape(raw), cotangent.reshape(raw), w_filter, w_gate,
        b_filter.reshape(1, -1), b_gate.reshape(1, -1), w_diff, b_diff.reshape(1, -1),
        tile_row, tile_col, tile_val.reshape(tile_rows, 128), send_nodes.reshape(3, 1, 128), send_count,
    )
    vec = jax.ShapeDtypeStruct((1, ch), F32)
    out, gs, g_wf, g_wg, g_bf, g_bg, g_wd, g_bd = pl.pallas_call(
        finish_kernel,
        out_shape=(
            jax.ShapeDtypeStruct(raw, BF),
            jax.ShapeDtypeStruct(raw, BF),
            jax.ShapeDtypeStruct((2, ch, ch), F32),
            jax.ShapeDtypeStruct((2, ch, ch), F32),
            vec, vec,
            jax.ShapeDtypeStruct((3, ch, ch), F32),
            vec,
        ),
        in_specs=[anyw, anyw, vmem],
        out_specs=(anyw, anyw, anyw, anyw, vmem, vmem, anyw, vmem),
        scratch_shapes=[dma((9,))],
    )(*[pltpu.with_memory_space_constraint(x, pltpu.VMEM) for x in (out, gs, fin)])
    return (
        out.reshape(series.shape), gs.reshape(series.shape), g_wf, g_wg,
        g_bf.reshape(-1), g_bg.reshape(-1), g_wd, g_bd.reshape(-1))


def on_device(mesh, series, *rest):
    nodes, batch, frames, ch = series.shape
    seg_n, tm_n = mesh.shape["seg"], mesh.shape["tm"]
    fits = seg_n == 4 and tm_n == 2 and batch == 1 and frames == seg_n * tm_n and frames == DILATION_FRAMES
    plan = gather_plan if fits else halo_plan
    return plan(mesh, series, *rest)


def solution(mesh):
    field = P(("grp", "seg"), "rep", "tm", None)
    part = ("grp", "seg")
    in_specs = (
        field, field, P(), P(), P(), P(), P(), P(),
        P(part, None), P(part, None), P(part, None, None, None), P(part, None, None), P(part, None),
    )
    out_specs = (
        field, field, P("grp", None, None), P("grp", None, None), P("grp"), P("grp"),
        P("grp", None, None), P("grp"),
    )
    return jax.shard_map(
        functools.partial(on_device, mesh), mesh=mesh, in_specs=in_specs, out_specs=out_specs,
        check_vma=False)
```

```python
import functools
import math

import jax
import jax.numpy as jnp
from jax import lax
from jax.experimental import pallas as pl
from jax.experimental.pallas import tpu as pltpu
from jax.sharding import PartitionSpec as P

DILATION_FRAMES = 8
STEPS = (1, -1, 2)
MESH = pl.DeviceIdType.MESH
WIDE = 256
BF = jnp.bfloat16
F32 = jnp.float32


def mm(a, b):
    return lax.dot_general(a, b, (((1,), (0,)), ((), ())), preferred_element_type=F32)


def mm_nt(a, b):
    return lax.dot_general(a, b, (((1,), (1,)), ((), ())), preferred_element_type=F32)


def mm_tn(a, b):
    return lax.dot_general(a, b, (((0,), (0,)), ((), ())), preferred_element_type=F32)


def halo_kernel(
    seg_n, tm_n, scale,
    ser3, cot3, wf, wg, bf, bg, wd, bd, trow, tcol, tval, snodes, scount,
    out3, gs3, fin1, fin2,
    big, big_g, ser, cot, prev, ops_f, ops_b, pick, give, wblk,
    acc, act_f, act_g, hid, hop1, delayed_out, delayed_in,
    snd, rcv, wacc, dacc, bacc, cacc,
    red1, red2, rb1, rc1, sb1, rb2, rc2, sb2,
    tm_s, tm_r, ex_s, ex_r, dl_s, dl_r, ar_s, ar_r,
):
    p = lax.axis_index("seg")
    t = lax.axis_index("tm")
    rep = lax.axis_index("rep")
    chunks, nodes, _ = ser.shape
    doublings = seg_n.bit_length() - 1
    cap = 128
    ch = 128

    barrier = pltpu.get_barrier_semaphore()
    for k in range(1, seg_n):
        pl.semaphore_signal(barrier, inc=1, device_id={"seg": lax.rem(p + k, seg_n)}, device_id_type=MESH)
    crew = 2 * tm_n
    me = t * 2 + rep

    def crew_device(i):
        return {"tm": lax.div(i, 2), "rep": lax.rem(i, 2)}

    for k in range(1, crew):
        pl.semaphore_signal(barrier, inc=1, device_id=crew_device(lax.rem(me + k, crew)), device_id_type=MESH)
    pl.semaphore_wait(barrier, seg_n - 1 + crew - 1)

    def series_copy(c):
        return pltpu.make_async_remote_copy(
            src_ref=ser.at[c], dst_ref=prev.at[c], send_sem=tm_s.at[c], recv_sem=tm_r.at[c],
            device_id={"tm": lax.rem(t + 1, tm_n)}, device_id_type=MESH)

    def delayed_copy(c):
        return pltpu.make_async_remote_copy(
            src_ref=delayed_out.at[c], dst_ref=delayed_in.at[c], send_sem=dl_s.at[c], recv_sem=dl_r.at[c],
            device_id={"tm": lax.rem(t + tm_n - 1, tm_n)}, device_id_type=MESH)

    def halo_copy(e, c, j):
        step = STEPS[j] if e % 2 == 0 else -STEPS[j]
        return pltpu.make_async_remote_copy(
            src_ref=snd.at[e, c, j], dst_ref=rcv.at[e, c, j],
            send_sem=ex_s.at[e, c, j], recv_sem=ex_r.at[e, c, j],
            device_id={"seg": lax.rem(p + step + seg_n, seg_n)}, device_id_type=MESH)

    def side_by_side(src, dst):
        big[...] = src[...].astype(F32)
        for c in range(chunks):
            dst[c] = jnp.concatenate([big[:, 2 * c, :], big[:, 2 * c + 1, :]], axis=1).astype(BF)

    side_by_side(cot3, cot)

    rows_n, cols_n, tiles_n = nodes // 128, nodes // 128 + 3, tval.shape[0]
    for r in range(rows_n):
        for c in range(cols_n):
            total = jnp.zeros((128, 128), F32)
            for k in range(tiles_n):
                if k < rows_n and (r != k or c != k):
                    continue
                if rows_n <= k < cols_n and c != k:
                    continue
                hit = jnp.where(trow[0, k] == r, 1.0, 0.0) * jnp.where(tcol[0, k] == c, 1.0, 0.0)
                total = total + hit * tval[k].astype(F32)
            ops_f[r * 128:(r + 1) * 128, c * 128:(c + 1) * 128] = total.astype(BF)
            ops_b[c * 128:(c + 1) * 128, r * 128:(r + 1) * 128] = total.T.astype(BF)
    wblk[4:7] = jnp.zeros((3, WIDE, WIDE), BF)
    for i in range(2):
        lo, hi = i * ch, (i + 1) * ch
        for k in range(3):
            wblk[4 + k, lo:hi, lo:hi] = wd[k]

    def put(e, c, rows):
        for j in range(3):
            snd[e, c, j] = rows[j * cap:(j + 1) * cap]
            halo_copy(e, c, j).start()

    def back_one(c, _):
        g = cot[c]
        up = mm_nt(g, wblk[6]).astype(BF)
        put(0, c, mm(ops_b[nodes:, :], up).astype(BF))
        acc[c] = mm(ops_b[:nodes, :], up) + mm_nt(g, wblk[5])
        return 0

    lax.fori_loop(0, chunks, back_one, 0)

    side_by_side(ser3, ser)

    @pl.when(t < tm_n - 1)
    def _():
        for c in range(chunks):
            series_copy(c).start()

    @pl.when(t == 0)
    def _():
        prev[...] = jnp.zeros_like(prev)

    @pl.when(t == tm_n - 1)
    def _():
        delayed_in[...] = jnp.zeros_like(delayed_in)

    wblk[0:4] = jnp.zeros((4, WIDE, WIDE), BF)
    for i in range(2):
        lo, hi = i * ch, (i + 1) * ch
        for k in range(2):
            wblk[k, lo:hi, lo:hi] = wf[k]
            wblk[2 + k, lo:hi, lo:hi] = wg[k]

    node_ids = lax.broadcasted_iota(jnp.int32, (nodes, cap), 0)
    slot_ids = lax.broadcasted_iota(jnp.int32, (nodes, cap), 1)
    for j in range(3):
        here = jnp.where(node_ids == snodes[j:j + 1, :], 1.0, 0.0)
        live = jnp.where(slot_ids < scount[0, j], 1.0, 0.0)
        hot = here * live
        give[:, j * cap:(j + 1) * cap] = hot.astype(BF)
        pick[j * cap:(j + 1) * cap, :] = hot.T.astype(BF)
    wacc[...] = jnp.zeros_like(wacc)
    dacc[...] = jnp.zeros_like(dacc)
    bacc[...] = jnp.zeros_like(bacc)
    cacc[...] = jnp.zeros_like(cacc)
    red1[...] = jnp.zeros_like(red1)
    red2[...] = jnp.zeros_like(red2)
    ones = jnp.ones((8, nodes), BF)

    def arrived(e, c):
        for j in range(3):
            halo_copy(e, c, j).wait_recv()
        return rcv[e, c].reshape(3 * cap, WIDE)

    def back_two(c, _):
        got = arrived(0, c)
        up = (acc[c] + mm(give[...], got)).astype(BF)
        put(2, c, mm(ops_b[nodes:, :], up).astype(BF))
        acc[c] = mm(ops_b[:nodes, :], up) + mm_nt(cot[c], wblk[4])
        return 0

    lax.fori_loop(0, chunks, back_two, 0)

    bf2 = jnp.concatenate([bf[...], bf[...]], axis=1)
    bg2 = jnp.concatenate([bg[...], bg[...]], axis=1)
    bd2 = jnp.concatenate([bd[...], bd[...]], axis=1)

    def fore_one(c, _):
        @pl.when(t > 0)
        def _():
            series_copy(c).wait_recv()

        before, now = prev[c], ser[c]
        a = jnp.tanh(mm(before, wblk[0]) + mm(now, wblk[1]) + bf2)
        act_f[c] = a
        s = jax.nn.sigmoid(mm(before, wblk[2]) + mm(now, wblk[3]) + bg2)
        act_g[c] = s
        h = (a * s).astype(BF)
        hid[c] = h
        put(1, c, mm(pick[...], h).astype(BF))
        return 0

    lax.fori_loop(0, chunks, fore_one, 0)

    def back_three(c, _):
        got = arrived(2, c)
        gh = acc[c] + mm(give[...], got)
        a, s = act_f[c], act_g[c]
        gf = (gh * s * (1.0 - a * a)).astype(BF)
        gg = (gh * a * (s * (1.0 - s))).astype(BF)
        delayed_out[c] = (mm_nt(gf, wblk[0]) + mm_nt(gg, wblk[2])).astype(BF)

        @pl.when(t > 0)
        def _():
            delayed_copy(c).start()

        g = cot[c]
        acc[c] = g.astype(F32) + mm_nt(gf, wblk[1]) + mm_nt(gg, wblk[3])
        before, now, h = prev[c], ser[c], hid[c]
        for i in range(2):
            lo, hi = i * ch, (i + 1) * ch
            right = jnp.concatenate([gf[:, lo:hi], gg[:, lo:hi]], axis=1)
            left = jnp.concatenate([before[:, lo:hi], now[:, lo:hi]], axis=1)
            wacc[...] += mm_tn(left, right)
            dacc[...] += mm_tn(h[:, lo:hi], g[:, lo:hi])
            bacc[...] += mm(ones, right)
            cacc[...] += mm(ones, g[:, lo:hi])
        return 0

    lax.fori_loop(0, chunks, back_three, 0)

    red1[0:256, :] = wacc[:, 0:128]
    red1[256:512, :] = wacc[:, 128:256]
    red1[512:640, :] = dacc[...]
    rid = lax.broadcasted_iota(jnp.int32, (8, 128), 0)
    red1[640:648, :] = jnp.where(
        rid == 0, bacc[:, 0:128], jnp.where(rid == 1, bacc[:, 128:256], cacc[...]))

    def all_sum(base, direct, red, rb, rc, sb, fin):
        part = red.shape[0] // crew

        def copy(src, dst, at, device):
            made = pltpu.make_async_remote_copy(
                src_ref=src, dst_ref=dst, send_sem=ar_s.at[at], recv_sem=ar_r.at[at],
                device_id=device, device_id_type=MESH)
            made.start()
            return made

        def rows(i):
            return pl.ds(pl.multiple_of(i * part, 8), part)

        sends = []
        for k in range(1, crew):
            o = lax.rem(me + k, crew)
            sends.append(copy(red.at[rows(o)], rb.at[k - 1], base + k, crew_device(o)))
        yield
        s = red[rows(me), :]
        for k in range(1, crew):
            sends[k - 1].wait()
            s = s + rb[k - 1]
        at = base + crew
        if direct:
            sb[0] = s
            rc[p] = s
            sends = [
                copy(sb.at[0], rc.at[p], at + k, {"seg": lax.rem(p + k, seg_n)})
                for k in range(1, seg_n)]
            yield
            for one in sends:
                one.wait()
            s = rc[0]
            for k in range(1, seg_n):
                s = s + rc[k]
        else:
            bit = 1
            for k in range(doublings):
                sb[k] = s
                mate = p + (1 - 2 * lax.rem(lax.div(p, bit), 2)) * bit
                one = copy(sb.at[k], rc.at[k], at + k, {"seg": mate})
                yield
                one.wait()
                s = s + rc[k]
                bit *= 2
        fin[rows(me), :] = s * scale
        at = at + seg_n
        sends = [
            copy(fin.at[rows(me)], fin.at[rows(me)], at + k, crew_device(lax.rem(me + k, crew)))
            for k in range(1, crew)]
        yield
        for one in sends:
            one.wait()
        yield

    first = all_sum(0, False, red1, rb1, rc1, sb1, fin1)
    next(first)
    def fore_two(c, _):
        got = arrived(1, c)
        h = (mm(ops_f[:, :nodes], hid[c]) + mm(ops_f[:, nodes:], got)).astype(BF)
        hop1[c] = h
        put(3, c, mm(pick[...], h).astype(BF))
        return 0

    for c in range(chunks):
        fore_two(c, 0)
        if c in (0, 1):
            next(first)

    for c in range(chunks):
        if c >= 2:
            next(first, None)
        got = arrived(3, c)
        h, h1, g = hid[c], hop1[c], cot[c]
        h2 = (mm(ops_f[:, :nodes], h1) + mm(ops_f[:, nodes:], got)).astype(BF)
        total = mm(h, wblk[4]) + mm(h1, wblk[5]) + mm(h2, wblk[6]) + bd2
        total = ser[c].astype(F32) + total
        for i in range(2):
            lo, hi = i * ch, (i + 1) * ch
            both = jnp.concatenate([h1[:, lo:hi], h2[:, lo:hi]], axis=1)
            red2[...] += mm_tn(both, g[:, lo:hi])
            big[:, 2 * c + i, :] = total[:, lo:hi]
    second = all_sum(2 * crew + seg_n, True, red2, rb2, rc2, sb2, fin2)
    next(second)
    out3[...] = big[...].astype(BF)
    next(second)
    for c in range(chunks):
        @pl.when(t < tm_n - 1)
        def _():
            delayed_copy(c).wait_recv()

        total = acc[c] + delayed_in[c].astype(F32)
        for i in range(2):
            big_g[:, 2 * c + i, :] = total[:, i * ch:(i + 1) * ch]
    next(second)
    gs3[...] = big_g[...].astype(BF)
    for _ in first:
        pass
    for _ in second:
        pass

    def drain(c, _):
        @pl.when(t < tm_n - 1)
        def _():
            series_copy(c).wait_send()

        @pl.when(t > 0)
        def _():
            delayed_copy(c).wait_send()

        for e in range(4):
            for j in range(3):
                halo_copy(e, c, j).wait_send()
        return 0

    lax.fori_loop(0, chunks, drain, 0)


def halo_plan(mesh, series, cotangent, w_filter, w_gate, b_filter, b_gate, w_diff, b_diff,
              tile_row, tile_col, tile_val, send_nodes, send_count):
    nodes, batch, frames, channels = series.shape
    seg_n, tm_n, rep_n = mesh.shape["seg"], mesh.shape["tm"], mesh.shape["rep"]
    chunks = batch * frames * channels // WIDE
    scale = 1.0 / math.sqrt(nodes * batch * frames * seg_n * tm_n * rep_n)
    unit = 16 * tm_n
    r1 = -(-648 // unit) * unit
    r2 = -(-256 // unit) * unit

    doublings = seg_n.bit_length() - 1
    vmem = pl.BlockSpec(memory_space=pltpu.VMEM)
    smem = pl.BlockSpec(memory_space=pltpu.SMEM)
    field = (chunks, nodes, WIDE)

    def sums(r):
        crew = 2 * tm_n
        q = r // crew
        return [
            pltpu.VMEM((crew - 1, q, 128), F32),
            pltpu.VMEM((seg_n, q, 128), F32),
            pltpu.VMEM((doublings, q, 128), F32),
        ]

    n_ar = 2 * (4 * tm_n + seg_n)
    raw = (nodes, batch * frames, channels)
    halo = (4, chunks, 3, 128, WIDE)
    out, gs, fin1, fin2 = pl.pallas_call(
        functools.partial(halo_kernel, seg_n, tm_n, scale),
        out_shape=(
            jax.ShapeDtypeStruct(raw, BF),
            jax.ShapeDtypeStruct(raw, BF),
            jax.ShapeDtypeStruct((r1, 128), F32),
            jax.ShapeDtypeStruct((r2, 128), F32),
        ),
        in_specs=[vmem] * 8 + [smem, smem, vmem, vmem, smem],
        out_specs=(vmem,) * 4,
        scratch_shapes=[
            pltpu.VMEM(raw, F32),
            pltpu.VMEM(raw, F32),
            pltpu.VMEM(field, BF),
            pltpu.VMEM(field, BF),
            pltpu.VMEM(field, BF),
            pltpu.VMEM((nodes, nodes + 384), BF),
            pltpu.VMEM((nodes + 384, nodes), BF),
            pltpu.VMEM((384, nodes), BF),
            pltpu.VMEM((nodes, 384), BF),
            pltpu.VMEM((7, WIDE, WIDE), BF),
            pltpu.VMEM(field, F32),
            pltpu.VMEM(field, F32),
            pltpu.VMEM(field, F32),
            pltpu.VMEM(field, BF),
            pltpu.VMEM(field, BF),
            pltpu.VMEM(field, BF),
            pltpu.VMEM(field, BF),
            pltpu.VMEM(halo, BF),
            pltpu.VMEM(halo, BF),
            pltpu.VMEM((256, 256), F32),
            pltpu.VMEM((128, 128), F32),
            pltpu.VMEM((8, 256), F32),
            pltpu.VMEM((8, 128), F32),
            pltpu.VMEM((r1, 128), F32),
            pltpu.VMEM((r2, 128), F32),
            *sums(r1),
            *sums(r2),
            pltpu.SemaphoreType.DMA((chunks,)),
            pltpu.SemaphoreType.DMA((chunks,)),
            pltpu.SemaphoreType.DMA((4, chunks, 3)),
            pltpu.SemaphoreType.DMA((4, chunks, 3)),
            pltpu.SemaphoreType.DMA((chunks,)),
            pltpu.SemaphoreType.DMA((chunks,)),
            pltpu.SemaphoreType.DMA((n_ar,)),
            pltpu.SemaphoreType.DMA((n_ar,)),
        ],
        compiler_params=pltpu.CompilerParams(
            collective_id=0, has_side_effects=True, vmem_limit_bytes=56 << 20),
    )(
        series.reshape(raw), cotangent.reshape(raw), w_filter, w_gate,
        b_filter.reshape(1, -1), b_gate.reshape(1, -1), w_diff, b_diff.reshape(1, -1),
        tile_row, tile_col, tile_val[0], send_nodes[0], send_count,
    )
    return (
        out.reshape(series.shape),
        gs.reshape(series.shape),
        fin1[0:256].reshape(2, 128, 128),
        fin1[256:512].reshape(2, 128, 128),
        fin1[640],
        fin1[641],
        jnp.concatenate([fin1[512:640], fin2[:256]], axis=0).reshape(3, 128, 128),
        fin1[642],
    )


def gather_kernel(
    seg_n, tm_n, scale,
    ser_h, cot_h, wf_h, wg_h, bf_h, bg_h, wd_h, bd_h, trow_h, tcol_h, tval_h, snodes_h, scount_h,
    out3, gs3, fin,
    ser3, cot3, wf, wg, bf, bg, wd, bd, trow, tcol, tval, snodes, scount, load, big, big_g, stage_s, stage_c, ser, cot, tiles, meta,
    opf, opb, oph, pick, wc, wct, wdt,
    act_f, act_g, src0, src1, hop2, sb0, sb1, acc,
    out_b, gs_b, out_r, gs_r, pair,
    red_a, red_b, low_a, low_b, a0, a1, a2, a3, b0, b1, b2, b3,
    tz_s, tz_r, mz_s, mz_r, tx_s, tx_r, tc_s, tc_r,
    se_s, se_r, co_s, co_r, ou_s, ou_r, gr_s, gr_r, ar_s, ar_r,
):
    p = lax.axis_index("seg")
    t = lax.axis_index("tm")
    rep = lax.axis_index("rep")
    loads = [
        pltpu.make_async_copy(src, dst, load.at[i])
        for i, (src, dst) in enumerate([
            (tval_h, tval), (snodes_h, snodes), (trow_h, trow), (tcol_h, tcol), (scount_h, scount),
            (ser_h, ser3), (cot_h, cot3), (wf_h, wf), (wg_h, wg), (bf_h, bf), (bg_h, bg), (wd_h, wd), (bd_h, bd)])]
    nodes, frames, ch = ser3.shape
    mine = p * tm_n + t
    crew = 2 * tm_n
    quarter = tiles.shape[1] // crew

    def rc(src, dst, ss, rs, dev):
        return pltpu.make_async_remote_copy(
            src_ref=src, dst_ref=dst, send_sem=ss, recv_sem=rs, device_id=dev, device_id_type=MESH)

    low, high = lax.rem(p, 2), lax.div(p, 2)

    def flip(j):
        return lax.rem(high + j // 2, 2) * 2 + lax.rem(low + j % 2, 2)

    def peer(j, m):
        return flip(j), lax.rem(t + m, tm_n)

    others = [(2, 0), (3, 0), (2, 1), (3, 1), (1, 0), (1, 1), (0, 1)]

    def rows_of(q):
        return pl.ds(pl.multiple_of(q * nodes, 128), nodes)

    def piece(c):
        return pl.ds(pl.multiple_of(c * quarter, 16), quarter)

    core = {"rep": 1 - rep}
    across = {"tm": 1 - t}

    barrier = pltpu.get_barrier_semaphore()
    for j, m in others:
        q, tt = peer(j, m)
        pl.semaphore_signal(barrier, inc=1, device_id={"seg": q, "tm": tt}, device_id_type=MESH)
    pl.semaphore_signal(barrier, inc=1, device_id=core, device_id_type=MESH)

    for one in loads:
        one.start()
    pl.semaphore_wait(barrier, len(others) + 1)
    loads[0].wait()

    c_me = t * 2 + rep
    c_across = (1 - t) * 2 + rep

    def tile_z(j):
        return rc(tval.at[piece(c_me)], tiles.at[p, piece(c_me)], tz_s.at[j], tz_r.at[j], {"seg": flip(j)})

    def tile_on():
        at = tiles.at[flip(2), piece(c_me)]
        return rc(at, at, tz_s.at[3], tz_r.at[3], {"seg": flip(1)})

    def meta_z(j):
        return rc(meta.at[p], meta.at[p], mz_s.at[j], mz_r.at[j], {"seg": flip(j)})

    def tile_x(j):
        at = tiles.at[flip(j), piece(c_me)]
        return rc(at, at, tx_s.at[j], tx_r.at[j], across)

    def tile_c(j, c, i):
        at = tiles.at[flip(j), piece(c)]
        return rc(at, at, tc_s.at[j, i], tc_r.at[j, i], core)

    def field_in(stage, whole, ss, rs, j, m):
        q, tt = peer(j, m)
        f = q * tm_n + tt
        return rc(stage.at[f], whole.at[t, rows_of(p)], ss.at[f], rs.at[mine], {"seg": q, "tm": tt})

    def field_got(stage, whole, ss, rs, j, m):
        q, tt = peer(j, m)
        f = q * tm_n + tt
        return rc(stage.at[f], whole.at[tt, rows_of(q)], ss.at[f], rs.at[f], {"seg": q, "tm": tt})

    def frame_major(source, wide, stage, whole):
        wide[...] = source[...].astype(F32)
        for f in range(frames):
            stage[f] = wide[:, f, :].astype(BF)
        whole[t, rows_of(p), :] = stage[mine]

    tile_z(2).start()
    tile_z(1).start()
    for one in loads[1:5]:
        one.wait()
    meta[p] = jnp.zeros_like(meta[p])
    for j in range(3):
        meta[p, j:j + 1, :] = snodes[j]
    meta[p, 3:4, 0:trow.shape[1]] = trow[...]
    meta[p, 4:5, 0:tcol.shape[1]] = tcol[...]
    meta[p, 5:6, 0:scount.shape[1]] = scount[...]
    for j in (2, 3, 1):
        meta_z(j).start()
    loads[5].wait()
    frame_major(ser3, big, stage_s, ser)
    field_in(stage_s, ser, se_s, se_r, 2, 0).start()
    tiles[p] = tval[...]

    tile_z(2).wait_recv()
    tile_on().start()
    tile_x(2).start()
    tile_z(1).wait_recv()
    tile_x(1).start()
    field_in(stage_s, ser, se_s, se_r, 3, 0).start()
    tile_on().wait_recv()
    tile_x(3).start()
    for j, m in others[2:]:
        field_in(stage_s, ser, se_s, se_r, j, m).start()

    for one in loads[6:]:
        one.wait()
    frame_major(cot3, big_g, stage_c, cot)
    for j, m in others:
        field_in(stage_c, cot, co_s, co_r, j, m).start()

    for j in (2, 1, 3):
        tile_x(j).wait_recv()
        tile_c(j, c_me, 0).start()
        tile_c(j, c_across, 1).start()

    for i in range(2):
        wc[i * ch:(i + 1) * ch, 0:ch] = wf[i]
        wc[i * ch:(i + 1) * ch, ch:2 * ch] = wg[i]
    wct[...] = wc[...].astype(F32).T.astype(BF)
    for i in range(3):
        wdt[i] = wd[i].astype(F32).T.astype(BF)
    bias = jnp.concatenate([bf[...], bg[...]], axis=1)
    red_a[...] = jnp.zeros_like(red_a)
    red_b[...] = jnp.zeros_like(red_b)

    for j in (2, 1, 3):
        tile_c(j, c_me, 0).wait_recv()
        tile_c(j, c_across, 1).wait_recv()
        meta_z(j).wait_recv()

    rows_n = nodes // 128
    cols_n = rows_n + 3
    tiles_n = tiles.shape[1] // 128
    halo = 3 * 128
    lane_ids = lax.broadcasted_iota(jnp.int32, (128, nodes), 1)
    sub_ids = lax.broadcasted_iota(jnp.int32, (nodes, 128), 0)
    slot_lane = lax.broadcasted_iota(jnp.int32, (1, 128), 1)
    slot_sub = lax.broadcasted_iota(jnp.int32, (128, 1), 0)

    def build(q, _):
        info = meta[q]
        tr, tc = info[3:4, :], info[4:5, :]
        t_all = [tiles[q, k * 128:(k + 1) * 128, :].astype(F32) for k in range(tiles_n)]
        for r in range(rows_n):
            for c in range(cols_n):
                hits = jnp.where((tr == r) & (tc == c), 1.0, 0.0)
                total = jnp.zeros((128, 128), F32)
                for k in range(tiles_n):
                    if k < rows_n and (r != k or c != k):
                        continue
                    if rows_n <= k < cols_n and c != k:
                        continue
                    total = total + hits[:, k:k + 1] * t_all[k]
                flipped = total.T.astype(BF)
                opf[q, r * 128:(r + 1) * 128, c * 128:(c + 1) * 128] = total.astype(BF)
                if c < rows_n:
                    opb[q, c * 128:(c + 1) * 128, r * 128:(r + 1) * 128] = flipped
                else:
                    oph[q, (c - rows_n) * 128:(c - rows_n + 1) * 128, r * 128:(r + 1) * 128] = flipped
        col = info.astype(F32).T.astype(jnp.int32)
        for j in range(3):
            count = info[5:6, j:j + 1]
            give = jnp.where((sub_ids == info[j:j + 1, :]) & (slot_lane < count), 1.0, 0.0)
            opb[q, :, nodes + j * 128:nodes + (j + 1) * 128] = give.astype(BF)
            take = jnp.where((lane_ids == col[:, j:j + 1]) & (slot_sub < count), 1.0, 0.0)
            pick[q, j * 128:(j + 1) * 128, :] = take.astype(BF)
        return 0

    lax.fori_loop(0, seg_n, build, 0)

    for j, m in others:
        field_got(stage_s, ser, se_s, se_r, j, m).wait_recv()

    def conv(q, _):
        for tt in range(tm_n):
            now = ser[tt, rows_of(q), :]
            if tt == 0:
                pre = mm(now, wc[ch:2 * ch, :]) + bias
            else:
                pre = mm(jnp.concatenate([ser[tt - 1, rows_of(q), :], now], axis=1), wc[...]) + bias
            a = jnp.tanh(pre[:, 0:ch])
            s = jax.nn.sigmoid(pre[:, ch:2 * ch])
            act_f[tt, rows_of(q), :] = a
            act_g[tt, rows_of(q), :] = s
            src0[q, 0:nodes, tt * ch:(tt + 1) * ch] = (a * s).astype(BF)
        return 0

    def send_slots(src):
        def one(q, _):
            got = mm(pick[q], src[q, 0:nodes, :]).astype(BF)
            for j in range(3):
                reader = lax.rem(q - STEPS[j] + seg_n, seg_n)
                src[reader, nodes + j * 128:nodes + (j + 1) * 128, :] = got[j * 128:(j + 1) * 128]
            return 0
        lax.fori_loop(0, seg_n, one, 0)

    def hop(src, dst):
        def one(q, _):
            dst[q, 0:nodes, :] = mm(opf[q], src[q]).astype(BF)
            return 0
        lax.fori_loop(0, seg_n, one, 0)

    def home(buf, got, ss, rs, q, tt):
        return rc(buf.at[tt, rows_of(q)], got.at[mine], ss.at[q * tm_n + tt], rs.at[mine], {"seg": q, "tm": tt})

    def gs_arrived(f):
        for h in range(2):
            rc(gs_b.at[f % tm_n, pl.ds(f // tm_n * nodes + h * part, part)], gs_r.at[f, pl.ds(h * part, part)],
               gr_s.at[f, h], gr_r.at[f, h], {"seg": f // tm_n, "tm": f % tm_n}).wait_recv()

    def out_arrived(f):
        arrived(out_b, out_r, ou_s, ou_r, f).wait_recv()

    def arrived(buf, got, ss, rs, f):
        return rc(buf.at[f % tm_n, pl.ds(f // tm_n * nodes, nodes)], got.at[f], ss.at[f], rs.at[f],
                  {"seg": f // tm_n, "tm": f % tm_n})

    def out_go(*pairs):
        for j, m in pairs:
            q, tt = peer(j, m)
            home(out_b, out_r, ou_s, ou_r, q, tt).start()

    part = nodes // 2

    def gs_half(q, tt, h):
        start = pl.ds(pl.multiple_of(q * nodes + h * part, 16), part)
        return rc(gs_b.at[tt, start], gs_r.at[mine, pl.ds(h * part, part)],
                  gr_s.at[q * tm_n + tt, h], gr_r.at[mine, h], {"seg": q, "tm": tt})

    def gs_go(*pairs):
        for j, m, h in pairs:
            q, tt = peer(j, m)
            gs_half(q, tt, h).start()

    lax.fori_loop(0, seg_n, conv, 0)
    send_slots(src0)
    hop(src0, src1)
    send_slots(src1)
    hop(src1, hop2)
    bias_d = bd[...]

    def put_out(q, _):
        for tt in range(tm_n):
            lo, hi = tt * ch, (tt + 1) * ch
            two = jnp.concatenate([src0[q, 0:nodes, lo:hi], src1[q, 0:nodes, lo:hi]], axis=1)
            total = mm(two, jnp.concatenate([wd[0], wd[1]], axis=0)) + mm(hop2[q, :, lo:hi], wd[2]) + bias_d
            out_b[tt, rows_of(q), :] = (ser[tt, rows_of(q), :].astype(F32) + total).astype(BF)
        return 0

    lax.fori_loop(0, seg_n, put_out, 0)
    out_go((2, 1), (1, 1), (3, 1), (1, 0), (0, 1))

    for j, m in others:
        field_got(stage_c, cot, co_s, co_r, j, m).wait_recv()

    base = 4 * ch

    def span(start, size):
        return pl.ds(pl.multiple_of(start, 16), size)

    def quad_device(m, k):
        return {"seg": flip(k), "tm": lax.rem(t + m, 2)}

    def summed(red, b0, b1, b2, b3, low_out, first):
        half = red.shape[0] // 2
        eighth = half // 4
        at_core = rep * half

        def at_quad(m, k):
            return span(at_core + lax.rem(t + m, 2) * (2 * eighth) + lax.rem(low + k, 2) * eighth, eighth)

        def go(src, dst, at, dev):
            made = rc(src, dst, ar_s.at[first + at], ar_r.at[first + at], dev)
            made.start()
            return made

        quad = [(1, 1), (1, 0), (0, 1)]
        here = at_quad(0, 0)
        step = go(red.at[span((1 - rep) * half, half)], b0, 0, core)
        yield
        step.wait()
        red[span(at_core, half), :] += b0[...]
        steps = [
            go(red.at[at_quad(m, k)], b1.at[i], 1 + i, quad_device(m, k))
            for i, (m, k) in enumerate(quad)]
        yield
        for step in steps:
            step.wait()
        b3[...] = (red[here, :] + b1[0] + b1[1] + b1[2]).astype(BF)
        step = go(b3, b2, 4, {"seg": flip(2)})
        yield
        step.wait()
        low_out[here, :] = ((b3[...].astype(F32) + b2[...].astype(F32)) * scale).astype(BF)
        steps = [
            go(low_out.at[here], low_out.at[here], 5 + i, quad_device(m, k))
            for i, (m, k) in enumerate(quad)]
        yield
        for step in steps:
            step.wait()
        whole = low_out.at[span(at_core, half)]
        step = go(whole, whole, 8, core)
        yield
        step.wait()
        yield

    sum_a = summed(red_a, a0, a1, a2, a3, low_a, 0)
    sum_b = summed(red_b, b0, b1, b2, b3, low_b, 9)

    def back(q, _):
        for tt in range(tm_n):
            lo, hi = tt * ch, (tt + 1) * ch
            g = cot[tt, rows_of(q), :]
            u = mm(g, jnp.concatenate([wdt[2], wdt[1]], axis=1))
            sb0[q, 0:nodes, lo:hi] = u[:, 0:ch].astype(BF)
            acc[q, :, lo:hi] = u[:, ch:2 * ch]
            hops = jnp.concatenate(
                [src0[q, 0:nodes, lo:hi], src1[q, 0:nodes, lo:hi], hop2[q, :, lo:hi]], axis=1)
            red_a[...] += mm_tn(hops, g)
            red_b[base + 2:base + 3, :] += jnp.sum(g.astype(F32), axis=0, keepdims=True)
        return 0

    def send_back(sb):
        def one(q, _):
            got = mm(oph[q], sb[q, 0:nodes, :]).astype(BF)
            for j in range(3):
                owner = lax.rem(q + STEPS[j] + seg_n, seg_n)
                sb[owner, nodes + j * 128:nodes + (j + 1) * 128, :] = got[j * 128:(j + 1) * 128]
            return 0
        lax.fori_loop(0, seg_n, one, 0)

    lax.fori_loop(0, seg_n, back, 0)
    next(sum_a)
    send_back(sb0)

    def back_mid(q, _):
        sb1[q, 0:nodes, :] = (acc[q] + mm(opb[q], sb0[q])).astype(BF)
        return 0

    next(sum_a)
    lax.fori_loop(0, seg_n, back_mid, 0)
    out_go((2, 0), (3, 0))
    send_back(sb1)

    def back_last(q, _):
        gh_all = mm(opb[q], sb1[q])
        for tt in range(tm_n):
            lo, hi = tt * ch, (tt + 1) * ch
            g = cot[tt, rows_of(q), :]
            gh = gh_all[:, lo:hi] + mm(g, wdt[0])
            a, s = act_f[tt, rows_of(q), :], act_g[tt, rows_of(q), :]
            gf = (gh * s * (1.0 - a * a)).astype(BF)
            gg = (gh * a * (s * (1.0 - s))).astype(BF)
            both = jnp.concatenate([gf, gg], axis=1)
            pair[tt, rows_of(q), :] = both
            now = ser[tt, rows_of(q), :]
            if tt == 0:
                part = mm_tn(now, both)
                red_b[ch:2 * ch, :] += part[:, 0:ch]
                red_b[3 * ch:4 * ch, :] += part[:, ch:2 * ch]
            else:
                part = mm_tn(jnp.concatenate([ser[tt - 1, rows_of(q), :], now], axis=1), both)
                red_b[0:2 * ch, :] += part[:, 0:ch]
                red_b[2 * ch:4 * ch, :] += part[:, ch:2 * ch]
            red_b[base:base + 1, :] += jnp.sum(gf.astype(F32), axis=0, keepdims=True)
            red_b[base + 1:base + 2, :] += jnp.sum(gg.astype(F32), axis=0, keepdims=True)
        return 0

    lax.fori_loop(0, seg_n, back_last, 0)

    next(sum_b)
    next(sum_a)

    def put_gs(q, _):
        later = None
        for tt in reversed(range(tm_n)):
            both = pair[tt, rows_of(q), :]
            if tt == 0:
                total = mm(both, wct[:, ch:2 * ch])
            else:
                r = mm(both, wct[...])
                total = r[:, ch:2 * ch]
            total = cot[tt, rows_of(q), :].astype(F32) + total
            if later is not None:
                total = total + later.astype(F32)
            if tt > 0:
                later = r[:, 0:ch].astype(BF)
            gs_b[tt, rows_of(q), :] = total.astype(BF)
        return 0

    lax.fori_loop(0, seg_n, put_gs, 0)
    next(sum_b)
    gs_go((2, 0, 0),)
    out_r[mine] = out_b[t, rows_of(p), :]
    gs_r[mine] = gs_b[t, rows_of(p), :]

    def node_major(got, wide, dest, ready):
        for f in range(frames):
            @pl.when(f != mine)
            def _():
                ready(f)

            wide[:, f, :] = got[f].astype(F32)
        dest[...] = wide[...].astype(BF)

    next(sum_b)
    gs_go((2, 1, 0), (1, 1, 0), (2, 1, 1), (1, 1, 1), (2, 0, 1))
    next(sum_a)
    gs_go((3, 1, 0), (1, 0, 0), (3, 1, 1), (1, 0, 1), (3, 0, 0), (0, 1, 0), (3, 0, 1), (0, 1, 1))
    node_major(out_r, big, out3, out_arrived)
    next(sum_b)
    next(sum_a)
    next(sum_b)
    next(sum_a)
    fin[base:base + 3 * ch, :] = low_a[...].astype(F32)
    node_major(gs_r, big_g, gs3, gs_arrived)
    next(sum_b)
    fin[0:base, :] = low_b[0:base, :].astype(F32)
    fin[base + 3 * ch:base + 3 * ch + 16, :] = low_b[base:base + 16, :].astype(F32)

    tile_z(2).wait_send()
    tile_z(1).wait_send()
    tile_on().wait_send()
    for j in (1, 2, 3):
        meta_z(j).wait_send()
        tile_x(j).wait_send()
        tile_c(j, c_me, 0).wait_send()
        tile_c(j, c_across, 1).wait_send()
    for j, m in others:
        q, tt = peer(j, m)
        field_in(stage_s, ser, se_s, se_r, j, m).wait_send()
        field_in(stage_c, cot, co_s, co_r, j, m).wait_send()
        home(out_b, out_r, ou_s, ou_r, q, tt).wait_send()
        gs_half(q, tt, 0).wait_send()
        gs_half(q, tt, 1).wait_send()


def finish_kernel(out_i, gs_i, fin, out_o, gs_o, o_wf, o_wg, o_bf, o_bg, o_wd, o_bd, sems):
    ch = o_wf.shape[1]
    pairs = [(out_i, out_o), (gs_i, gs_o)]
    for i in range(7):
        target = o_wf.at[i] if i < 2 else o_wg.at[i - 2] if i < 4 else o_wd.at[i - 4]
        pairs.append((fin.at[pl.ds(i * ch, ch)], target))
    copies = [pltpu.make_async_copy(src, dst, sems.at[i]) for i, (src, dst) in enumerate(pairs)]
    for one in copies:
        one.start()
    o_bf[...] = fin[7 * ch:7 * ch + 1, :]
    o_bg[...] = fin[7 * ch + 1:7 * ch + 2, :]
    o_bd[...] = fin[7 * ch + 2:7 * ch + 3, :]
    for one in copies:
        one.wait()


def gather_plan(mesh, series, cotangent, w_filter, w_gate, b_filter, b_gate, w_diff, b_diff,
                tile_row, tile_col, tile_val, send_nodes, send_count):
    nodes, batch, frames, ch = series.shape
    seg_n, tm_n, rep_n = mesh.shape["seg"], mesh.shape["tm"], mesh.shape["rep"]
    scale = 1.0 / math.sqrt(nodes * batch * frames * seg_n * tm_n * rep_n)
    unit = 16 * 8
    rows_a = 3 * ch
    rows_b = -(-(4 * ch + 8) // unit) * unit
    total_rows = 7 * ch + 16

    def steps_of(rows):
        return [
            pltpu.VMEM((rows // 2, ch), F32),
            pltpu.VMEM((3, rows // 8, ch), F32),
            pltpu.VMEM((rows // 8, ch), BF),
            pltpu.VMEM((rows // 8, ch), BF),
        ]

    vmem = pl.BlockSpec(memory_space=pltpu.VMEM)
    anyw = pl.BlockSpec(memory_space=pl.ANY)
    raw = (nodes, batch * frames, ch)
    tall = (frames, nodes, ch)
    everyone = (tm_n, seg_n * nodes, ch)
    wide = tm_n * ch
    tile_rows = tile_val.shape[1] * 128
    halo = 3 * 128
    dma = pltpu.SemaphoreType.DMA
    out, gs, fin = pl.pallas_call(
        functools.partial(gather_kernel, seg_n, tm_n, scale),
        out_shape=(
            pltpu.VMEM(raw, BF),
            pltpu.VMEM(raw, BF),
            pltpu.VMEM((total_rows, ch), F32),
        ),
        in_specs=[anyw] * 13,
        out_specs=(vmem,) * 3,
        scratch_shapes=[
            pltpu.VMEM(raw, BF),
            pltpu.VMEM(raw, BF),
            pltpu.VMEM(w_filter.shape, BF),
            pltpu.VMEM(w_gate.shape, BF),
            pltpu.VMEM((1, ch), F32),
            pltpu.VMEM((1, ch), F32),
            pltpu.VMEM(w_diff.shape, BF),
            pltpu.VMEM((1, ch), F32),
            pltpu.VMEM(tile_row.shape, jnp.int32),
            pltpu.VMEM(tile_col.shape, jnp.int32),
            pltpu.VMEM((tile_rows, 128), BF),
            pltpu.VMEM((3, 1, 128), jnp.int32),
            pltpu.VMEM(send_count.shape, jnp.int32),
            dma((13,)),
            pltpu.VMEM(raw, F32),
            pltpu.VMEM(raw, F32),
            pltpu.VMEM(tall, BF),
            pltpu.VMEM(tall, BF),
            pltpu.VMEM(everyone, BF),
            pltpu.VMEM(everyone, BF),
            pltpu.VMEM((seg_n, tile_rows, 128), BF),
            pltpu.VMEM((seg_n, 8, 128), jnp.int32),
            pltpu.VMEM((seg_n, nodes, nodes + halo), BF),
            pltpu.VMEM((seg_n, nodes, nodes + halo), BF),
            pltpu.VMEM((seg_n, halo, nodes), BF),
            pltpu.VMEM((seg_n, halo, nodes), BF),
            pltpu.VMEM((2 * ch, 2 * ch), BF),
            pltpu.VMEM((2 * ch, 2 * ch), BF),
            pltpu.VMEM((3, ch, ch), BF),
            pltpu.VMEM(everyone, F32),
            pltpu.VMEM(everyone, F32),
            pltpu.VMEM((seg_n, nodes + halo, wide), BF),
            pltpu.VMEM((seg_n, nodes + halo, wide), BF),
            pltpu.VMEM((seg_n, nodes, wide), BF),
            pltpu.VMEM((seg_n, nodes + halo, wide), BF),
            pltpu.VMEM((seg_n, nodes + halo, wide), BF),
            pltpu.VMEM((seg_n, nodes, wide), F32),
            pltpu.VMEM(everyone, BF),
            pltpu.VMEM(everyone, BF),
            pltpu.VMEM(tall, BF),
            pltpu.VMEM(tall, BF),
            pltpu.VMEM((tm_n, seg_n * nodes, 2 * ch), BF),
            pltpu.VMEM((rows_a, ch), F32),
            pltpu.VMEM((rows_b, ch), F32),
            pltpu.VMEM((rows_a, ch), BF),
            pltpu.VMEM((rows_b, ch), BF),
            *steps_of(rows_a),
            *steps_of(rows_b),
            dma((seg_n,)), dma((seg_n,)), dma((seg_n,)), dma((seg_n,)),
            dma((seg_n,)), dma((seg_n,)), dma((seg_n, 2)), dma((seg_n, 2)),
            dma((frames,)), dma((frames,)), dma((frames,)), dma((frames,)),
            dma((frames,)), dma((frames,)), dma((frames, 2)), dma((frames, 2)),
            dma((18,)), dma((18,)),
        ],
        compiler_params=pltpu.CompilerParams(
            collective_id=0, has_side_effects=True, vmem_limit_bytes=52 << 20),
    )(
        series.reshape(raw), cotangent.reshape(raw), w_filter, w_gate,
        b_filter.reshape(1, -1), b_gate.reshape(1, -1), w_diff, b_diff.reshape(1, -1),
        tile_row, tile_col, tile_val.reshape(tile_rows, 128), send_nodes.reshape(3, 1, 128), send_count,
    )
    vec = jax.ShapeDtypeStruct((1, ch), F32)
    out, gs, g_wf, g_wg, g_bf, g_bg, g_wd, g_bd = pl.pallas_call(
        finish_kernel,
        out_shape=(
            jax.ShapeDtypeStruct(raw, BF),
            jax.ShapeDtypeStruct(raw, BF),
            jax.ShapeDtypeStruct((2, ch, ch), F32),
            jax.ShapeDtypeStruct((2, ch, ch), F32),
            vec, vec,
            jax.ShapeDtypeStruct((3, ch, ch), F32),
            vec,
        ),
        in_specs=[anyw, anyw, vmem],
        out_specs=(anyw, anyw, anyw, anyw, vmem, vmem, anyw, vmem),
        scratch_shapes=[dma((9,))],
    )(*[pltpu.with_memory_space_constraint(x, pltpu.VMEM) for x in (out, gs, fin)])
    return (
        out.reshape(series.shape), gs.reshape(series.shape), g_wf, g_wg,
        g_bf.reshape(-1), g_bg.reshape(-1), g_wd, g_bd.reshape(-1))


def on_device(mesh, series, *rest):
    nodes, batch, frames, ch = series.shape
    seg_n, tm_n = mesh.shape["seg"], mesh.shape["tm"]
    fits = seg_n == 4 and tm_n == 2 and batch == 1 and frames == seg_n * tm_n and frames == DILATION_FRAMES
    plan = gather_plan if fits else halo_plan
    return plan(mesh, series, *rest)


def solution(mesh):
    field = P(("grp", "seg"), "rep", "tm", None)
    part = ("grp", "seg")
    in_specs = (
        field, field, P(), P(), P(), P(), P(), P(),
        P(part, None), P(part, None), P(part, None, None, None), P(part, None, None), P(part, None),
    )
    out_specs = (
        field, field, P("grp", None, None), P("grp", None, None), P("grp"), P("grp"),
        P("grp", None, None), P("grp"),
    )
    return jax.shard_map(
        functools.partial(on_device, mesh), mesh=mesh, in_specs=in_specs, out_specs=out_specs,
        check_vma=False)
```

```python
import functools
import math

import jax
import jax.numpy as jnp
from jax import lax
from jax.experimental import pallas as pl
from jax.experimental.pallas import tpu as pltpu
from jax.sharding import PartitionSpec as P

DILATION_FRAMES = 8
STEPS = (1, -1, 2)
MESH = pl.DeviceIdType.MESH
WIDE = 256
BF = jnp.bfloat16
F32 = jnp.float32


def mm(a, b):
    return lax.dot_general(a, b, (((1,), (0,)), ((), ())), preferred_element_type=F32)


def mm_nt(a, b):
    return lax.dot_general(a, b, (((1,), (1,)), ((), ())), preferred_element_type=F32)


def mm_tn(a, b):
    return lax.dot_general(a, b, (((0,), (0,)), ((), ())), preferred_element_type=F32)


def halo_kernel(
    seg_n, tm_n, scale,
    ser3, cot3, wf, wg, bf, bg, wd, bd, trow, tcol, tval, snodes, scount,
    out3, gs3, fin1, fin2,
    big, big_g, ser, cot, prev, ops_f, ops_b, pick, give, wblk,
    acc, act_f, act_g, hid, hop1, delayed_out, delayed_in,
    snd, rcv, wacc, dacc, bacc, cacc,
    red1, red2, rb1, rc1, sb1, rb2, rc2, sb2,
    tm_s, tm_r, ex_s, ex_r, dl_s, dl_r, ar_s, ar_r,
):
    p = lax.axis_index("seg")
    t = lax.axis_index("tm")
    rep = lax.axis_index("rep")
    chunks, nodes, _ = ser.shape
    doublings = seg_n.bit_length() - 1
    cap = 128
    ch = 128

    barrier = pltpu.get_barrier_semaphore()
    for k in range(1, seg_n):
        pl.semaphore_signal(barrier, inc=1, device_id={"seg": lax.rem(p + k, seg_n)}, device_id_type=MESH)
    crew = 2 * tm_n
    me = t * 2 + rep

    def crew_device(i):
        return {"tm": lax.div(i, 2), "rep": lax.rem(i, 2)}

    for k in range(1, crew):
        pl.semaphore_signal(barrier, inc=1, device_id=crew_device(lax.rem(me + k, crew)), device_id_type=MESH)
    pl.semaphore_wait(barrier, seg_n - 1 + crew - 1)

    def series_copy(c):
        return pltpu.make_async_remote_copy(
            src_ref=ser.at[c], dst_ref=prev.at[c], send_sem=tm_s.at[c], recv_sem=tm_r.at[c],
            device_id={"tm": lax.rem(t + 1, tm_n)}, device_id_type=MESH)

    def delayed_copy(c):
        return pltpu.make_async_remote_copy(
            src_ref=delayed_out.at[c], dst_ref=delayed_in.at[c], send_sem=dl_s.at[c], recv_sem=dl_r.at[c],
            device_id={"tm": lax.rem(t + tm_n - 1, tm_n)}, device_id_type=MESH)

    def halo_copy(e, c, j):
        step = STEPS[j] if e % 2 == 0 else -STEPS[j]
        return pltpu.make_async_remote_copy(
            src_ref=snd.at[e, c, j], dst_ref=rcv.at[e, c, j],
            send_sem=ex_s.at[e, c, j], recv_sem=ex_r.at[e, c, j],
            device_id={"seg": lax.rem(p + step + seg_n, seg_n)}, device_id_type=MESH)

    def side_by_side(src, dst):
        big[...] = src[...].astype(F32)
        for c in range(chunks):
            dst[c] = jnp.concatenate([big[:, 2 * c, :], big[:, 2 * c + 1, :]], axis=1).astype(BF)

    side_by_side(cot3, cot)

    rows_n, cols_n, tiles_n = nodes // 128, nodes // 128 + 3, tval.shape[0]
    for r in range(rows_n):
        for c in range(cols_n):
            total = jnp.zeros((128, 128), F32)
            for k in range(tiles_n):
                if k < rows_n and (r != k or c != k):
                    continue
                if rows_n <= k < cols_n and c != k:
                    continue
                hit = jnp.where(trow[0, k] == r, 1.0, 0.0) * jnp.where(tcol[0, k] == c, 1.0, 0.0)
                total = total + hit * tval[k].astype(F32)
            ops_f[r * 128:(r + 1) * 128, c * 128:(c + 1) * 128] = total.astype(BF)
            ops_b[c * 128:(c + 1) * 128, r * 128:(r + 1) * 128] = total.T.astype(BF)
    wblk[4:7] = jnp.zeros((3, WIDE, WIDE), BF)
    for i in range(2):
        lo, hi = i * ch, (i + 1) * ch
        for k in range(3):
            wblk[4 + k, lo:hi, lo:hi] = wd[k]

    def put(e, c, rows):
        for j in range(3):
            snd[e, c, j] = rows[j * cap:(j + 1) * cap]
            halo_copy(e, c, j).start()

    def back_one(c, _):
        g = cot[c]
        up = mm_nt(g, wblk[6]).astype(BF)
        put(0, c, mm(ops_b[nodes:, :], up).astype(BF))
        acc[c] = mm(ops_b[:nodes, :], up) + mm_nt(g, wblk[5])
        return 0

    lax.fori_loop(0, chunks, back_one, 0)

    side_by_side(ser3, ser)

    @pl.when(t < tm_n - 1)
    def _():
        for c in range(chunks):
            series_copy(c).start()

    @pl.when(t == 0)
    def _():
        prev[...] = jnp.zeros_like(prev)

    @pl.when(t == tm_n - 1)
    def _():
        delayed_in[...] = jnp.zeros_like(delayed_in)

    wblk[0:4] = jnp.zeros((4, WIDE, WIDE), BF)
    for i in range(2):
        lo, hi = i * ch, (i + 1) * ch
        for k in range(2):
            wblk[k, lo:hi, lo:hi] = wf[k]
            wblk[2 + k, lo:hi, lo:hi] = wg[k]

    node_ids = lax.broadcasted_iota(jnp.int32, (nodes, cap), 0)
    slot_ids = lax.broadcasted_iota(jnp.int32, (nodes, cap), 1)
    for j in range(3):
        here = jnp.where(node_ids == snodes[j:j + 1, :], 1.0, 0.0)
        live = jnp.where(slot_ids < scount[0, j], 1.0, 0.0)
        hot = here * live
        give[:, j * cap:(j + 1) * cap] = hot.astype(BF)
        pick[j * cap:(j + 1) * cap, :] = hot.T.astype(BF)
    wacc[...] = jnp.zeros_like(wacc)
    dacc[...] = jnp.zeros_like(dacc)
    bacc[...] = jnp.zeros_like(bacc)
    cacc[...] = jnp.zeros_like(cacc)
    red1[...] = jnp.zeros_like(red1)
    red2[...] = jnp.zeros_like(red2)
    ones = jnp.ones((8, nodes), BF)

    def arrived(e, c):
        for j in range(3):
            halo_copy(e, c, j).wait_recv()
        return rcv[e, c].reshape(3 * cap, WIDE)

    def back_two(c, _):
        got = arrived(0, c)
        up = (acc[c] + mm(give[...], got)).astype(BF)
        put(2, c, mm(ops_b[nodes:, :], up).astype(BF))
        acc[c] = mm(ops_b[:nodes, :], up) + mm_nt(cot[c], wblk[4])
        return 0

    lax.fori_loop(0, chunks, back_two, 0)

    bf2 = jnp.concatenate([bf[...], bf[...]], axis=1)
    bg2 = jnp.concatenate([bg[...], bg[...]], axis=1)
    bd2 = jnp.concatenate([bd[...], bd[...]], axis=1)

    def fore_one(c, _):
        @pl.when(t > 0)
        def _():
            series_copy(c).wait_recv()

        before, now = prev[c], ser[c]
        a = jnp.tanh(mm(before, wblk[0]) + mm(now, wblk[1]) + bf2)
        act_f[c] = a
        s = jax.nn.sigmoid(mm(before, wblk[2]) + mm(now, wblk[3]) + bg2)
        act_g[c] = s
        h = (a * s).astype(BF)
        hid[c] = h
        put(1, c, mm(pick[...], h).astype(BF))
        return 0

    lax.fori_loop(0, chunks, fore_one, 0)

    def back_three(c, _):
        got = arrived(2, c)
        gh = acc[c] + mm(give[...], got)
        a, s = act_f[c], act_g[c]
        gf = (gh * s * (1.0 - a * a)).astype(BF)
        gg = (gh * a * (s * (1.0 - s))).astype(BF)
        delayed_out[c] = (mm_nt(gf, wblk[0]) + mm_nt(gg, wblk[2])).astype(BF)

        @pl.when(t > 0)
        def _():
            delayed_copy(c).start()

        g = cot[c]
        acc[c] = g.astype(F32) + mm_nt(gf, wblk[1]) + mm_nt(gg, wblk[3])
        before, now, h = prev[c], ser[c], hid[c]
        for i in range(2):
            lo, hi = i * ch, (i + 1) * ch
            right = jnp.concatenate([gf[:, lo:hi], gg[:, lo:hi]], axis=1)
            left = jnp.concatenate([before[:, lo:hi], now[:, lo:hi]], axis=1)
            wacc[...] += mm_tn(left, right)
            dacc[...] += mm_tn(h[:, lo:hi], g[:, lo:hi])
            bacc[...] += mm(ones, right)
            cacc[...] += mm(ones, g[:, lo:hi])
        return 0

    lax.fori_loop(0, chunks, back_three, 0)

    red1[0:256, :] = wacc[:, 0:128]
    red1[256:512, :] = wacc[:, 128:256]
    red1[512:640, :] = dacc[...]
    rid = lax.broadcasted_iota(jnp.int32, (8, 128), 0)
    red1[640:648, :] = jnp.where(
        rid == 0, bacc[:, 0:128], jnp.where(rid == 1, bacc[:, 128:256], cacc[...]))

    def all_sum(base, direct, red, rb, rc, sb, fin):
        part = red.shape[0] // crew

        def copy(src, dst, at, device):
            made = pltpu.make_async_remote_copy(
                src_ref=src, dst_ref=dst, send_sem=ar_s.at[at], recv_sem=ar_r.at[at],
                device_id=device, device_id_type=MESH)
            made.start()
            return made

        def rows(i):
            return pl.ds(pl.multiple_of(i * part, 8), part)

        sends = []
        for k in range(1, crew):
            o = lax.rem(me + k, crew)
            sends.append(copy(red.at[rows(o)], rb.at[k - 1], base + k, crew_device(o)))
        yield
        s = red[rows(me), :]
        for k in range(1, crew):
            sends[k - 1].wait()
            s = s + rb[k - 1]
        at = base + crew
        if direct:
            sb[0] = s
            rc[p] = s
            sends = [
                copy(sb.at[0], rc.at[p], at + k, {"seg": lax.rem(p + k, seg_n)})
                for k in range(1, seg_n)]
            yield
            for one in sends:
                one.wait()
            s = rc[0]
            for k in range(1, seg_n):
                s = s + rc[k]
        else:
            bit = 1
            for k in range(doublings):
                sb[k] = s
                mate = p + (1 - 2 * lax.rem(lax.div(p, bit), 2)) * bit
                one = copy(sb.at[k], rc.at[k], at + k, {"seg": mate})
                yield
                one.wait()
                s = s + rc[k]
                bit *= 2
        fin[rows(me), :] = s * scale
        at = at + seg_n
        sends = [
            copy(fin.at[rows(me)], fin.at[rows(me)], at + k, crew_device(lax.rem(me + k, crew)))
            for k in range(1, crew)]
        yield
        for one in sends:
            one.wait()
        yield

    first = all_sum(0, False, red1, rb1, rc1, sb1, fin1)
    next(first)
    def fore_two(c, _):
        got = arrived(1, c)
        h = (mm(ops_f[:, :nodes], hid[c]) + mm(ops_f[:, nodes:], got)).astype(BF)
        hop1[c] = h
        put(3, c, mm(pick[...], h).astype(BF))
        return 0

    for c in range(chunks):
        fore_two(c, 0)
        if c in (0, 1):
            next(first)

    for c in range(chunks):
        if c >= 2:
            next(first, None)
        got = arrived(3, c)
        h, h1, g = hid[c], hop1[c], cot[c]
        h2 = (mm(ops_f[:, :nodes], h1) + mm(ops_f[:, nodes:], got)).astype(BF)
        total = mm(h, wblk[4]) + mm(h1, wblk[5]) + mm(h2, wblk[6]) + bd2
        total = ser[c].astype(F32) + total
        for i in range(2):
            lo, hi = i * ch, (i + 1) * ch
            both = jnp.concatenate([h1[:, lo:hi], h2[:, lo:hi]], axis=1)
            red2[...] += mm_tn(both, g[:, lo:hi])
            big[:, 2 * c + i, :] = total[:, lo:hi]
    second = all_sum(2 * crew + seg_n, True, red2, rb2, rc2, sb2, fin2)
    next(second)
    out3[...] = big[...].astype(BF)
    next(second)
    for c in range(chunks):
        @pl.when(t < tm_n - 1)
        def _():
            delayed_copy(c).wait_recv()

        total = acc[c] + delayed_in[c].astype(F32)
        for i in range(2):
            big_g[:, 2 * c + i, :] = total[:, i * ch:(i + 1) * ch]
    next(second)
    gs3[...] = big_g[...].astype(BF)
    for _ in first:
        pass
    for _ in second:
        pass

    def drain(c, _):
        @pl.when(t < tm_n - 1)
        def _():
            series_copy(c).wait_send()

        @pl.when(t > 0)
        def _():
            delayed_copy(c).wait_send()

        for e in range(4):
            for j in range(3):
                halo_copy(e, c, j).wait_send()
        return 0

    lax.fori_loop(0, chunks, drain, 0)


def halo_plan(mesh, series, cotangent, w_filter, w_gate, b_filter, b_gate, w_diff, b_diff,
              tile_row, tile_col, tile_val, send_nodes, send_count):
    nodes, batch, frames, channels = series.shape
    seg_n, tm_n, rep_n = mesh.shape["seg"], mesh.shape["tm"], mesh.shape["rep"]
    chunks = batch * frames * channels // WIDE
    scale = 1.0 / math.sqrt(nodes * batch * frames * seg_n * tm_n * rep_n)
    unit = 16 * tm_n
    r1 = -(-648 // unit) * unit
    r2 = -(-256 // unit) * unit

    doublings = seg_n.bit_length() - 1
    vmem = pl.BlockSpec(memory_space=pltpu.VMEM)
    smem = pl.BlockSpec(memory_space=pltpu.SMEM)
    field = (chunks, nodes, WIDE)

    def sums(r):
        crew = 2 * tm_n
        q = r // crew
        return [
            pltpu.VMEM((crew - 1, q, 128), F32),
            pltpu.VMEM((seg_n, q, 128), F32),
            pltpu.VMEM((doublings, q, 128), F32),
        ]

    n_ar = 2 * (4 * tm_n + seg_n)
    raw = (nodes, batch * frames, channels)
    halo = (4, chunks, 3, 128, WIDE)
    out, gs, fin1, fin2 = pl.pallas_call(
        functools.partial(halo_kernel, seg_n, tm_n, scale),
        out_shape=(
            jax.ShapeDtypeStruct(raw, BF),
            jax.ShapeDtypeStruct(raw, BF),
            jax.ShapeDtypeStruct((r1, 128), F32),
            jax.ShapeDtypeStruct((r2, 128), F32),
        ),
        in_specs=[vmem] * 8 + [smem, smem, vmem, vmem, smem],
        out_specs=(vmem,) * 4,
        scratch_shapes=[
            pltpu.VMEM(raw, F32),
            pltpu.VMEM(raw, F32),
            pltpu.VMEM(field, BF),
            pltpu.VMEM(field, BF),
            pltpu.VMEM(field, BF),
            pltpu.VMEM((nodes, nodes + 384), BF),
            pltpu.VMEM((nodes + 384, nodes), BF),
            pltpu.VMEM((384, nodes), BF),
            pltpu.VMEM((nodes, 384), BF),
            pltpu.VMEM((7, WIDE, WIDE), BF),
            pltpu.VMEM(field, F32),
            pltpu.VMEM(field, F32),
            pltpu.VMEM(field, F32),
            pltpu.VMEM(field, BF),
            pltpu.VMEM(field, BF),
            pltpu.VMEM(field, BF),
            pltpu.VMEM(field, BF),
            pltpu.VMEM(halo, BF),
            pltpu.VMEM(halo, BF),
            pltpu.VMEM((256, 256), F32),
            pltpu.VMEM((128, 128), F32),
            pltpu.VMEM((8, 256), F32),
            pltpu.VMEM((8, 128), F32),
            pltpu.VMEM((r1, 128), F32),
            pltpu.VMEM((r2, 128), F32),
            *sums(r1),
            *sums(r2),
            pltpu.SemaphoreType.DMA((chunks,)),
            pltpu.SemaphoreType.DMA((chunks,)),
            pltpu.SemaphoreType.DMA((4, chunks, 3)),
            pltpu.SemaphoreType.DMA((4, chunks, 3)),
            pltpu.SemaphoreType.DMA((chunks,)),
            pltpu.SemaphoreType.DMA((chunks,)),
            pltpu.SemaphoreType.DMA((n_ar,)),
            pltpu.SemaphoreType.DMA((n_ar,)),
        ],
        compiler_params=pltpu.CompilerParams(
            collective_id=0, has_side_effects=True, vmem_limit_bytes=56 << 20),
    )(
        series.reshape(raw), cotangent.reshape(raw), w_filter, w_gate,
        b_filter.reshape(1, -1), b_gate.reshape(1, -1), w_diff, b_diff.reshape(1, -1),
        tile_row, tile_col, tile_val[0], send_nodes[0], send_count,
    )
    return (
        out.reshape(series.shape),
        gs.reshape(series.shape),
        fin1[0:256].reshape(2, 128, 128),
        fin1[256:512].reshape(2, 128, 128),
        fin1[640],
        fin1[641],
        jnp.concatenate([fin1[512:640], fin2[:256]], axis=0).reshape(3, 128, 128),
        fin1[642],
    )


def gather_kernel(
    seg_n, tm_n, scale,
    ser_h, cot_h, wf_h, wg_h, bf_h, bg_h, wd_h, bd_h, trow_h, tcol_h, tval_h, snodes_h, scount_h,
    out3, gs3, fin,
    ser3, cot3, wf, wg, bf, bg, wd, bd, trow, tcol, tval, snodes, scount, load, big, big_g, stage_s, stage_c, ser, cot, tiles, meta,
    opf, opb, oph, pick, wc, wct, wdt,
    act_f, act_g, src0, src1, hop2, sb0, sb1, acc,
    out_b, gs_b, out_r, gs_r, pair,
    red_a, red_b, low_a, low_b, a0, a1, a2, a3, b0, b1, b2, b3,
    tz_s, tz_r, mz_s, mz_r, tx_s, tx_r, tc_s, tc_r,
    se_s, se_r, co_s, co_r, ou_s, ou_r, gr_s, gr_r, ar_s, ar_r,
):
    p = lax.axis_index("seg")
    t = lax.axis_index("tm")
    rep = lax.axis_index("rep")
    loads = [
        pltpu.make_async_copy(src, dst, load.at[i])
        for i, (src, dst) in enumerate([
            (tval_h, tval), (snodes_h, snodes), (trow_h, trow), (tcol_h, tcol), (scount_h, scount),
            (ser_h, ser3), (cot_h, cot3), (wf_h, wf), (wg_h, wg), (bf_h, bf), (bg_h, bg), (wd_h, wd), (bd_h, bd)])]
    nodes, frames, ch = ser3.shape
    mine = p * tm_n + t
    crew = 2 * tm_n
    quarter = tiles.shape[1] // crew

    def rc(src, dst, ss, rs, dev):
        return pltpu.make_async_remote_copy(
            src_ref=src, dst_ref=dst, send_sem=ss, recv_sem=rs, device_id=dev, device_id_type=MESH)

    low, high = lax.rem(p, 2), lax.div(p, 2)

    def flip(j):
        return lax.rem(high + j // 2, 2) * 2 + lax.rem(low + j % 2, 2)

    def peer(j, m):
        return flip(j), lax.rem(t + m, tm_n)

    others = [(2, 0), (3, 0), (2, 1), (3, 1), (1, 0), (1, 1), (0, 1)]

    def rows_of(q):
        return pl.ds(pl.multiple_of(q * nodes, 128), nodes)

    def piece(c):
        return pl.ds(pl.multiple_of(c * quarter, 16), quarter)

    core = {"rep": 1 - rep}
    across = {"tm": 1 - t}

    barrier = pltpu.get_barrier_semaphore()
    for j, m in others:
        q, tt = peer(j, m)
        pl.semaphore_signal(barrier, inc=1, device_id={"seg": q, "tm": tt}, device_id_type=MESH)
    pl.semaphore_signal(barrier, inc=1, device_id=core, device_id_type=MESH)

    for one in loads:
        one.start()
    pl.semaphore_wait(barrier, len(others) + 1)
    loads[0].wait()

    c_me = t * 2 + rep
    c_across = (1 - t) * 2 + rep

    def tile_z(j):
        return rc(tval.at[piece(c_me)], tiles.at[p, piece(c_me)], tz_s.at[j], tz_r.at[j], {"seg": flip(j)})

    def tile_on():
        at = tiles.at[flip(2), piece(c_me)]
        return rc(at, at, tz_s.at[3], tz_r.at[3], {"seg": flip(1)})

    def meta_z(j):
        return rc(meta.at[p], meta.at[p], mz_s.at[j], mz_r.at[j], {"seg": flip(j)})

    def tile_x(j):
        at = tiles.at[flip(j), piece(c_me)]
        return rc(at, at, tx_s.at[j], tx_r.at[j], across)

    def tile_c(j, c, i):
        at = tiles.at[flip(j), piece(c)]
        return rc(at, at, tc_s.at[j, i], tc_r.at[j, i], core)

    def field_in(stage, whole, ss, rs, j, m):
        q, tt = peer(j, m)
        f = q * tm_n + tt
        return rc(stage.at[f], whole.at[t, rows_of(p)], ss.at[f], rs.at[mine], {"seg": q, "tm": tt})

    def field_got(stage, whole, ss, rs, j, m):
        q, tt = peer(j, m)
        f = q * tm_n + tt
        return rc(stage.at[f], whole.at[tt, rows_of(q)], ss.at[f], rs.at[f], {"seg": q, "tm": tt})

    def frame_major(source, wide, stage, whole):
        wide[...] = source[...].astype(F32)
        for f in range(frames):
            stage[f] = wide[:, f, :].astype(BF)
        whole[t, rows_of(p), :] = stage[mine]

    tile_z(2).start()
    tile_z(1).start()
    for one in loads[1:5]:
        one.wait()
    meta[p] = jnp.zeros_like(meta[p])
    for j in range(3):
        meta[p, j:j + 1, :] = snodes[j]
    meta[p, 3:4, 0:trow.shape[1]] = trow[...]
    meta[p, 4:5, 0:tcol.shape[1]] = tcol[...]
    meta[p, 5:6, 0:scount.shape[1]] = scount[...]
    for j in (2, 3, 1):
        meta_z(j).start()
    loads[5].wait()
    frame_major(ser3, big, stage_s, ser)
    field_in(stage_s, ser, se_s, se_r, 2, 0).start()
    tiles[p] = tval[...]

    tile_z(2).wait_recv()
    tile_on().start()
    tile_x(2).start()
    tile_z(1).wait_recv()
    tile_x(1).start()
    field_in(stage_s, ser, se_s, se_r, 3, 0).start()
    tile_on().wait_recv()
    tile_x(3).start()
    for j, m in [(2, 1), (1, 1), (3, 1), (1, 0), (0, 1)]:
        field_in(stage_s, ser, se_s, se_r, j, m).start()

    for one in loads[6:]:
        one.wait()
    frame_major(cot3, big_g, stage_c, cot)
    for j, m in others:
        field_in(stage_c, cot, co_s, co_r, j, m).start()

    for j in (2, 1, 3):
        tile_x(j).wait_recv()
        tile_c(j, c_me, 0).start()
        tile_c(j, c_across, 1).start()

    for i in range(2):
        wc[i * ch:(i + 1) * ch, 0:ch] = wf[i]
        wc[i * ch:(i + 1) * ch, ch:2 * ch] = wg[i]
    wct[...] = wc[...].astype(F32).T.astype(BF)
    for i in range(3):
        wdt[i] = wd[i].astype(F32).T.astype(BF)
    bias = jnp.concatenate([bf[...], bg[...]], axis=1)
    red_a[...] = jnp.zeros_like(red_a)
    red_b[...] = jnp.zeros_like(red_b)

    for j in (2, 1, 3):
        tile_c(j, c_me, 0).wait_recv()
        tile_c(j, c_across, 1).wait_recv()
        meta_z(j).wait_recv()

    rows_n = nodes // 128
    cols_n = rows_n + 3
    tiles_n = tiles.shape[1] // 128
    halo = 3 * 128
    lane_ids = lax.broadcasted_iota(jnp.int32, (128, nodes), 1)
    sub_ids = lax.broadcasted_iota(jnp.int32, (nodes, 128), 0)
    slot_lane = lax.broadcasted_iota(jnp.int32, (1, 128), 1)
    slot_sub = lax.broadcasted_iota(jnp.int32, (128, 1), 0)

    def build(q, _):
        info = meta[q]
        tr, tc = info[3:4, :], info[4:5, :]
        t_all = [tiles[q, k * 128:(k + 1) * 128, :].astype(F32) for k in range(tiles_n)]
        for r in range(rows_n):
            for c in range(cols_n):
                hits = jnp.where((tr == r) & (tc == c), 1.0, 0.0)
                total = jnp.zeros((128, 128), F32)
                for k in range(tiles_n):
                    if k < rows_n and (r != k or c != k):
                        continue
                    if rows_n <= k < cols_n and c != k:
                        continue
                    total = total + hits[:, k:k + 1] * t_all[k]
                flipped = total.T.astype(BF)
                opf[q, r * 128:(r + 1) * 128, c * 128:(c + 1) * 128] = total.astype(BF)
                if c < rows_n:
                    opb[q, c * 128:(c + 1) * 128, r * 128:(r + 1) * 128] = flipped
                else:
                    oph[q, (c - rows_n) * 128:(c - rows_n + 1) * 128, r * 128:(r + 1) * 128] = flipped
        col = info.astype(F32).T.astype(jnp.int32)
        for j in range(3):
            count = info[5:6, j:j + 1]
            give = jnp.where((sub_ids == info[j:j + 1, :]) & (slot_lane < count), 1.0, 0.0)
            opb[q, :, nodes + j * 128:nodes + (j + 1) * 128] = give.astype(BF)
            take = jnp.where((lane_ids == col[:, j:j + 1]) & (slot_sub < count), 1.0, 0.0)
            pick[q, j * 128:(j + 1) * 128, :] = take.astype(BF)
        return 0

    lax.fori_loop(0, seg_n, build, 0)

    for j, m in others:
        field_got(stage_s, ser, se_s, se_r, j, m).wait_recv()

    def conv(q, _):
        for tt in range(tm_n):
            now = ser[tt, rows_of(q), :]
            if tt == 0:
                pre = mm(now, wc[ch:2 * ch, :]) + bias
            else:
                pre = mm(jnp.concatenate([ser[tt - 1, rows_of(q), :], now], axis=1), wc[...]) + bias
            a = jnp.tanh(pre[:, 0:ch])
            s = jax.nn.sigmoid(pre[:, ch:2 * ch])
            act_f[tt, rows_of(q), :] = a
            act_g[tt, rows_of(q), :] = s
            src0[q, 0:nodes, tt * ch:(tt + 1) * ch] = (a * s).astype(BF)
        return 0

    def send_slots(src):
        def one(q, _):
            got = mm(pick[q], src[q, 0:nodes, :]).astype(BF)
            for j in range(3):
                reader = lax.rem(q - STEPS[j] + seg_n, seg_n)
                src[reader, nodes + j * 128:nodes + (j + 1) * 128, :] = got[j * 128:(j + 1) * 128]
            return 0
        lax.fori_loop(0, seg_n, one, 0)

    def hop(src, dst):
        def one(q, _):
            dst[q, 0:nodes, :] = mm(opf[q], src[q]).astype(BF)
            return 0
        lax.fori_loop(0, seg_n, one, 0)

    def home(buf, got, ss, rs, q, tt):
        return rc(buf.at[tt, rows_of(q)], got.at[mine], ss.at[q * tm_n + tt], rs.at[mine], {"seg": q, "tm": tt})

    def gs_arrived(f):
        for h in range(2):
            rc(gs_b.at[f % tm_n, pl.ds(f // tm_n * nodes + h * part, part)], gs_r.at[f, pl.ds(h * part, part)],
               gr_s.at[f, h], gr_r.at[f, h], {"seg": f // tm_n, "tm": f % tm_n}).wait_recv()

    def out_arrived(f):
        arrived(out_b, out_r, ou_s, ou_r, f).wait_recv()

    def arrived(buf, got, ss, rs, f):
        return rc(buf.at[f % tm_n, pl.ds(f // tm_n * nodes, nodes)], got.at[f], ss.at[f], rs.at[f],
                  {"seg": f // tm_n, "tm": f % tm_n})

    def out_go(*pairs):
        for j, m in pairs:
            q, tt = peer(j, m)
            home(out_b, out_r, ou_s, ou_r, q, tt).start()

    part = nodes // 2

    def gs_half(q, tt, h):
        start = pl.ds(pl.multiple_of(q * nodes + h * part, 16), part)
        return rc(gs_b.at[tt, start], gs_r.at[mine, pl.ds(h * part, part)],
                  gr_s.at[q * tm_n + tt, h], gr_r.at[mine, h], {"seg": q, "tm": tt})

    def gs_go(*pairs):
        for j, m, h in pairs:
            q, tt = peer(j, m)
            gs_half(q, tt, h).start()

    lax.fori_loop(0, seg_n, conv, 0)
    send_slots(src0)
    hop(src0, src1)
    send_slots(src1)
    hop(src1, hop2)
    bias_d = bd[...]

    def put_out(q, _):
        for tt in range(tm_n):
            lo, hi = tt * ch, (tt + 1) * ch
            two = jnp.concatenate([src0[q, 0:nodes, lo:hi], src1[q, 0:nodes, lo:hi]], axis=1)
            total = mm(two, jnp.concatenate([wd[0], wd[1]], axis=0)) + mm(hop2[q, :, lo:hi], wd[2]) + bias_d
            out_b[tt, rows_of(q), :] = (ser[tt, rows_of(q), :].astype(F32) + total).astype(BF)
        return 0

    lax.fori_loop(0, seg_n, put_out, 0)
    out_go((2, 1), (1, 1), (3, 1), (1, 0), (0, 1))

    for j, m in others:
        field_got(stage_c, cot, co_s, co_r, j, m).wait_recv()

    base = 4 * ch

    def span(start, size):
        return pl.ds(pl.multiple_of(start, 16), size)

    def quad_device(m, k):
        return {"seg": flip(k), "tm": lax.rem(t + m, 2)}

    def summed(red, b0, b1, b2, b3, low_out, first):
        half = red.shape[0] // 2
        eighth = half // 4
        at_core = rep * half

        def at_quad(m, k):
            return span(at_core + lax.rem(t + m, 2) * (2 * eighth) + lax.rem(low + k, 2) * eighth, eighth)

        def go(src, dst, at, dev):
            made = rc(src, dst, ar_s.at[first + at], ar_r.at[first + at], dev)
            made.start()
            return made

        quad = [(1, 1), (1, 0), (0, 1)]
        here = at_quad(0, 0)
        step = go(red.at[span((1 - rep) * half, half)], b0, 0, core)
        yield
        step.wait()
        red[span(at_core, half), :] += b0[...]
        steps = [
            go(red.at[at_quad(m, k)], b1.at[i], 1 + i, quad_device(m, k))
            for i, (m, k) in enumerate(quad)]
        yield
        for step in steps:
            step.wait()
        b3[...] = (red[here, :] + b1[0] + b1[1] + b1[2]).astype(BF)
        step = go(b3, b2, 4, {"seg": flip(2)})
        yield
        step.wait()
        low_out[here, :] = ((b3[...].astype(F32) + b2[...].astype(F32)) * scale).astype(BF)
        steps = [
            go(low_out.at[here], low_out.at[here], 5 + i, quad_device(m, k))
            for i, (m, k) in enumerate(quad)]
        yield
        for step in steps:
            step.wait()
        whole = low_out.at[span(at_core, half)]
        step = go(whole, whole, 8, core)
        yield
        step.wait()
        yield

    sum_a = summed(red_a, a0, a1, a2, a3, low_a, 0)
    sum_b = summed(red_b, b0, b1, b2, b3, low_b, 9)

    def back(q, _):
        for tt in range(tm_n):
            lo, hi = tt * ch, (tt + 1) * ch
            g = cot[tt, rows_of(q), :]
            u = mm(g, jnp.concatenate([wdt[2], wdt[1]], axis=1))
            sb0[q, 0:nodes, lo:hi] = u[:, 0:ch].astype(BF)
            acc[q, :, lo:hi] = u[:, ch:2 * ch]
            hops = jnp.concatenate(
                [src0[q, 0:nodes, lo:hi], src1[q, 0:nodes, lo:hi], hop2[q, :, lo:hi]], axis=1)
            red_a[...] += mm_tn(hops, g)
            red_b[base + 2:base + 3, :] += jnp.sum(g.astype(F32), axis=0, keepdims=True)
        return 0

    def send_back(sb):
        def one(q, _):
            got = mm(oph[q], sb[q, 0:nodes, :]).astype(BF)
            for j in range(3):
                owner = lax.rem(q + STEPS[j] + seg_n, seg_n)
                sb[owner, nodes + j * 128:nodes + (j + 1) * 128, :] = got[j * 128:(j + 1) * 128]
            return 0
        lax.fori_loop(0, seg_n, one, 0)

    lax.fori_loop(0, seg_n, back, 0)
    next(sum_a)
    send_back(sb0)

    def back_mid(q, _):
        sb1[q, 0:nodes, :] = (acc[q] + mm(opb[q], sb0[q])).astype(BF)
        return 0

    next(sum_a)
    lax.fori_loop(0, seg_n, back_mid, 0)
    out_go((2, 0), (3, 0))
    send_back(sb1)

    def back_last(q, _):
        gh_all = mm(opb[q], sb1[q])
        for tt in range(tm_n):
            lo, hi = tt * ch, (tt + 1) * ch
            g = cot[tt, rows_of(q), :]
            gh = gh_all[:, lo:hi] + mm(g, wdt[0])
            a, s = act_f[tt, rows_of(q), :], act_g[tt, rows_of(q), :]
            gf = (gh * s * (1.0 - a * a)).astype(BF)
            gg = (gh * a * (s * (1.0 - s))).astype(BF)
            both = jnp.concatenate([gf, gg], axis=1)
            pair[tt, rows_of(q), :] = both
            now = ser[tt, rows_of(q), :]
            if tt == 0:
                part = mm_tn(now, both)
                red_b[ch:2 * ch, :] += part[:, 0:ch]
                red_b[3 * ch:4 * ch, :] += part[:, ch:2 * ch]
            else:
                part = mm_tn(jnp.concatenate([ser[tt - 1, rows_of(q), :], now], axis=1), both)
                red_b[0:2 * ch, :] += part[:, 0:ch]
                red_b[2 * ch:4 * ch, :] += part[:, ch:2 * ch]
            red_b[base:base + 1, :] += jnp.sum(gf.astype(F32), axis=0, keepdims=True)
            red_b[base + 1:base + 2, :] += jnp.sum(gg.astype(F32), axis=0, keepdims=True)
        return 0

    lax.fori_loop(0, seg_n, back_last, 0)

    next(sum_b)
    next(sum_a)

    def put_gs(q, _):
        later = None
        for tt in reversed(range(tm_n)):
            both = pair[tt, rows_of(q), :]
            if tt == 0:
                total = mm(both, wct[:, ch:2 * ch])
            else:
                r = mm(both, wct[...])
                total = r[:, ch:2 * ch]
            total = cot[tt, rows_of(q), :].astype(F32) + total
            if later is not None:
                total = total + later.astype(F32)
            if tt > 0:
                later = r[:, 0:ch].astype(BF)
            gs_b[tt, rows_of(q), :] = total.astype(BF)
        return 0

    lax.fori_loop(0, seg_n, put_gs, 0)
    next(sum_b)
    gs_go((2, 0, 0),)
    out_r[mine] = out_b[t, rows_of(p), :]
    gs_r[mine] = gs_b[t, rows_of(p), :]

    def node_major(got, wide, dest, ready):
        for f in range(frames):
            @pl.when(f != mine)
            def _():
                ready(f)

            wide[:, f, :] = got[f].astype(F32)
        dest[...] = wide[...].astype(BF)

    next(sum_b)
    gs_go((2, 1, 0), (1, 1, 0), (2, 1, 1), (1, 1, 1), (2, 0, 1))
    next(sum_a)
    gs_go((3, 1, 0), (1, 0, 0), (3, 1, 1), (1, 0, 1), (3, 0, 0), (0, 1, 0), (3, 0, 1), (0, 1, 1))
    next(sum_b)
    node_major(out_r, big, out3, out_arrived)
    next(sum_a)
    next(sum_b)
    next(sum_a)
    fin[base:base + 3 * ch, :] = low_a[...].astype(F32)
    node_major(gs_r, big_g, gs3, gs_arrived)
    next(sum_b)
    fin[0:base, :] = low_b[0:base, :].astype(F32)
    fin[base + 3 * ch:base + 3 * ch + 16, :] = low_b[base:base + 16, :].astype(F32)

    tile_z(2).wait_send()
    tile_z(1).wait_send()
    tile_on().wait_send()
    for j in (1, 2, 3):
        meta_z(j).wait_send()
        tile_x(j).wait_send()
        tile_c(j, c_me, 0).wait_send()
        tile_c(j, c_across, 1).wait_send()
    for j, m in others:
        q, tt = peer(j, m)
        field_in(stage_s, ser, se_s, se_r, j, m).wait_send()
        field_in(stage_c, cot, co_s, co_r, j, m).wait_send()
        home(out_b, out_r, ou_s, ou_r, q, tt).wait_send()
        gs_half(q, tt, 0).wait_send()
        gs_half(q, tt, 1).wait_send()


def finish_kernel(out_i, gs_i, fin, out_o, gs_o, o_wf, o_wg, o_bf, o_bg, o_wd, o_bd, sems):
    ch = o_wf.shape[1]
    pairs = [(out_i, out_o), (gs_i, gs_o)]
    for i in range(7):
        target = o_wf.at[i] if i < 2 else o_wg.at[i - 2] if i < 4 else o_wd.at[i - 4]
        pairs.append((fin.at[pl.ds(i * ch, ch)], target))
    for i, target in enumerate((o_bf, o_bg, o_bd)):
        pairs.append((fin.at[pl.ds(7 * ch + i, 1)], target))
    copies = [pltpu.make_async_copy(src, dst, sems.at[i]) for i, (src, dst) in enumerate(pairs)]
    for one in copies:
        one.start()
    for one in copies:
        one.wait()


def gather_plan(mesh, series, cotangent, w_filter, w_gate, b_filter, b_gate, w_diff, b_diff,
                tile_row, tile_col, tile_val, send_nodes, send_count):
    nodes, batch, frames, ch = series.shape
    seg_n, tm_n, rep_n = mesh.shape["seg"], mesh.shape["tm"], mesh.shape["rep"]
    scale = 1.0 / math.sqrt(nodes * batch * frames * seg_n * tm_n * rep_n)
    unit = 16 * 8
    rows_a = 3 * ch
    rows_b = -(-(4 * ch + 8) // unit) * unit
    total_rows = 7 * ch + 16

    def steps_of(rows):
        return [
            pltpu.VMEM((rows // 2, ch), F32),
            pltpu.VMEM((3, rows // 8, ch), F32),
            pltpu.VMEM((rows // 8, ch), BF),
            pltpu.VMEM((rows // 8, ch), BF),
        ]

    vmem = pl.BlockSpec(memory_space=pltpu.VMEM)
    anyw = pl.BlockSpec(memory_space=pl.ANY)
    raw = (nodes, batch * frames, ch)
    tall = (frames, nodes, ch)
    everyone = (tm_n, seg_n * nodes, ch)
    wide = tm_n * ch
    tile_rows = tile_val.shape[1] * 128
    halo = 3 * 128
    dma = pltpu.SemaphoreType.DMA
    out, gs, fin = pl.pallas_call(
        functools.partial(gather_kernel, seg_n, tm_n, scale),
        out_shape=(
            pltpu.VMEM(raw, BF),
            pltpu.VMEM(raw, BF),
            pltpu.VMEM((total_rows, ch), F32),
        ),
        in_specs=[anyw] * 13,
        out_specs=(vmem,) * 3,
        scratch_shapes=[
            pltpu.VMEM(raw, BF),
            pltpu.VMEM(raw, BF),
            pltpu.VMEM(w_filter.shape, BF),
            pltpu.VMEM(w_gate.shape, BF),
            pltpu.VMEM((1, ch), F32),
            pltpu.VMEM((1, ch), F32),
            pltpu.VMEM(w_diff.shape, BF),
            pltpu.VMEM((1, ch), F32),
            pltpu.VMEM(tile_row.shape, jnp.int32),
            pltpu.VMEM(tile_col.shape, jnp.int32),
            pltpu.VMEM((tile_rows, 128), BF),
            pltpu.VMEM((3, 1, 128), jnp.int32),
            pltpu.VMEM(send_count.shape, jnp.int32),
            dma((13,)),
            pltpu.VMEM(raw, F32),
            pltpu.VMEM(raw, F32),
            pltpu.VMEM(tall, BF),
            pltpu.VMEM(tall, BF),
            pltpu.VMEM(everyone, BF),
            pltpu.VMEM(everyone, BF),
            pltpu.VMEM((seg_n, tile_rows, 128), BF),
            pltpu.VMEM((seg_n, 8, 128), jnp.int32),
            pltpu.VMEM((seg_n, nodes, nodes + halo), BF),
            pltpu.VMEM((seg_n, nodes, nodes + halo), BF),
            pltpu.VMEM((seg_n, halo, nodes), BF),
            pltpu.VMEM((seg_n, halo, nodes), BF),
            pltpu.VMEM((2 * ch, 2 * ch), BF),
            pltpu.VMEM((2 * ch, 2 * ch), BF),
            pltpu.VMEM((3, ch, ch), BF),
            pltpu.VMEM(everyone, F32),
            pltpu.VMEM(everyone, F32),
            pltpu.VMEM((seg_n, nodes + halo, wide), BF),
            pltpu.VMEM((seg_n, nodes + halo, wide), BF),
            pltpu.VMEM((seg_n, nodes, wide), BF),
            pltpu.VMEM((seg_n, nodes + halo, wide), BF),
            pltpu.VMEM((seg_n, nodes + halo, wide), BF),
            pltpu.VMEM((seg_n, nodes, wide), F32),
            pltpu.VMEM(everyone, BF),
            pltpu.VMEM(everyone, BF),
            pltpu.VMEM(tall, BF),
            pltpu.VMEM(tall, BF),
            pltpu.VMEM((tm_n, seg_n * nodes, 2 * ch), BF),
            pltpu.VMEM((rows_a, ch), F32),
            pltpu.VMEM((rows_b, ch), F32),
            pltpu.VMEM((rows_a, ch), BF),
            pltpu.VMEM((rows_b, ch), BF),
            *steps_of(rows_a),
            *steps_of(rows_b),
            dma((seg_n,)), dma((seg_n,)), dma((seg_n,)), dma((seg_n,)),
            dma((seg_n,)), dma((seg_n,)), dma((seg_n, 2)), dma((seg_n, 2)),
            dma((frames,)), dma((frames,)), dma((frames,)), dma((frames,)),
            dma((frames,)), dma((frames,)), dma((frames, 2)), dma((frames, 2)),
            dma((18,)), dma((18,)),
        ],
        compiler_params=pltpu.CompilerParams(
            collective_id=0, has_side_effects=True, vmem_limit_bytes=52 << 20),
    )(
        series.reshape(raw), cotangent.reshape(raw), w_filter, w_gate,
        b_filter.reshape(1, -1), b_gate.reshape(1, -1), w_diff, b_diff.reshape(1, -1),
        tile_row, tile_col, tile_val.reshape(tile_rows, 128), send_nodes.reshape(3, 1, 128), send_count,
    )
    vec = jax.ShapeDtypeStruct((1, ch), F32)
    out, gs, g_wf, g_wg, g_bf, g_bg, g_wd, g_bd = pl.pallas_call(
        finish_kernel,
        out_shape=(
            jax.ShapeDtypeStruct(raw, BF),
            jax.ShapeDtypeStruct(raw, BF),
            jax.ShapeDtypeStruct((2, ch, ch), F32),
            jax.ShapeDtypeStruct((2, ch, ch), F32),
            vec, vec,
            jax.ShapeDtypeStruct((3, ch, ch), F32),
            vec,
        ),
        in_specs=[anyw, anyw, vmem],
        out_specs=(anyw,) * 8,
        scratch_shapes=[dma((12,))],
    )(*[pltpu.with_memory_space_constraint(x, pltpu.VMEM) for x in (out, gs, fin)])
    return (
        out.reshape(series.shape), gs.reshape(series.shape), g_wf, g_wg,
        g_bf.reshape(-1), g_bg.reshape(-1), g_wd, g_bd.reshape(-1))


def on_device(mesh, series, *rest):
    nodes, batch, frames, ch = series.shape
    seg_n, tm_n = mesh.shape["seg"], mesh.shape["tm"]
    fits = seg_n == 4 and tm_n == 2 and batch == 1 and frames == seg_n * tm_n and frames == DILATION_FRAMES
    plan = gather_plan if fits else halo_plan
    return plan(mesh, series, *rest)


def solution(mesh):
    field = P(("grp", "seg"), "rep", "tm", None)
    part = ("grp", "seg")
    in_specs = (
        field, field, P(), P(), P(), P(), P(), P(),
        P(part, None), P(part, None), P(part, None, None, None), P(part, None, None), P(part, None),
    )
    out_specs = (
        field, field, P("grp", None, None), P("grp", None, None), P("grp"), P("grp"),
        P("grp", None, None), P("grp"),
    )
    return jax.shard_map(
        functools.partial(on_device, mesh), mesh=mesh, in_specs=in_specs, out_specs=out_specs,
        check_vma=False)
```

```python
import functools
import math

import jax
import jax.numpy as jnp
from jax import lax
from jax.experimental import pallas as pl
from jax.experimental.pallas import tpu as pltpu
from jax.sharding import PartitionSpec as P

DILATION_FRAMES = 8
STEPS = (1, -1, 2)
MESH = pl.DeviceIdType.MESH
WIDE = 256
BF = jnp.bfloat16
F32 = jnp.float32


def mm(a, b):
    return lax.dot_general(a, b, (((1,), (0,)), ((), ())), preferred_element_type=F32)


def mm_nt(a, b):
    return lax.dot_general(a, b, (((1,), (1,)), ((), ())), preferred_element_type=F32)


def mm_tn(a, b):
    return lax.dot_general(a, b, (((0,), (0,)), ((), ())), preferred_element_type=F32)


def halo_kernel(
    seg_n, tm_n, scale,
    ser3, cot3, wf, wg, bf, bg, wd, bd, trow, tcol, tval, snodes, scount,
    out3, gs3, fin1, fin2,
    big, big_g, ser, cot, prev, ops_f, ops_b, pick, give, wblk,
    acc, act_f, act_g, hid, hop1, delayed_out, delayed_in,
    snd, rcv, wacc, dacc, bacc, cacc,
    red1, red2, rb1, rc1, sb1, rb2, rc2, sb2,
    tm_s, tm_r, ex_s, ex_r, dl_s, dl_r, ar_s, ar_r,
):
    p = lax.axis_index("seg")
    t = lax.axis_index("tm")
    rep = lax.axis_index("rep")
    chunks, nodes, _ = ser.shape
    doublings = seg_n.bit_length() - 1
    cap = 128
    ch = 128

    barrier = pltpu.get_barrier_semaphore()
    for k in range(1, seg_n):
        pl.semaphore_signal(barrier, inc=1, device_id={"seg": lax.rem(p + k, seg_n)}, device_id_type=MESH)
    crew = 2 * tm_n
    me = t * 2 + rep

    def crew_device(i):
        return {"tm": lax.div(i, 2), "rep": lax.rem(i, 2)}

    for k in range(1, crew):
        pl.semaphore_signal(barrier, inc=1, device_id=crew_device(lax.rem(me + k, crew)), device_id_type=MESH)
    pl.semaphore_wait(barrier, seg_n - 1 + crew - 1)

    def series_copy(c):
        return pltpu.make_async_remote_copy(
            src_ref=ser.at[c], dst_ref=prev.at[c], send_sem=tm_s.at[c], recv_sem=tm_r.at[c],
            device_id={"tm": lax.rem(t + 1, tm_n)}, device_id_type=MESH)

    def delayed_copy(c):
        return pltpu.make_async_remote_copy(
            src_ref=delayed_out.at[c], dst_ref=delayed_in.at[c], send_sem=dl_s.at[c], recv_sem=dl_r.at[c],
            device_id={"tm": lax.rem(t + tm_n - 1, tm_n)}, device_id_type=MESH)

    def halo_copy(e, c, j):
        step = STEPS[j] if e % 2 == 0 else -STEPS[j]
        return pltpu.make_async_remote_copy(
            src_ref=snd.at[e, c, j], dst_ref=rcv.at[e, c, j],
            send_sem=ex_s.at[e, c, j], recv_sem=ex_r.at[e, c, j],
            device_id={"seg": lax.rem(p + step + seg_n, seg_n)}, device_id_type=MESH)

    def side_by_side(src, dst):
        big[...] = src[...].astype(F32)
        for c in range(chunks):
            dst[c] = jnp.concatenate([big[:, 2 * c, :], big[:, 2 * c + 1, :]], axis=1).astype(BF)

    side_by_side(cot3, cot)

    rows_n, cols_n, tiles_n = nodes // 128, nodes // 128 + 3, tval.shape[0]
    for r in range(rows_n):
        for c in range(cols_n):
            total = jnp.zeros((128, 128), F32)
            for k in range(tiles_n):
                if k < rows_n and (r != k or c != k):
                    continue
                if rows_n <= k < cols_n and c != k:
                    continue
                hit = jnp.where(trow[0, k] == r, 1.0, 0.0) * jnp.where(tcol[0, k] == c, 1.0, 0.0)
                total = total + hit * tval[k].astype(F32)
            ops_f[r * 128:(r + 1) * 128, c * 128:(c + 1) * 128] = total.astype(BF)
            ops_b[c * 128:(c + 1) * 128, r * 128:(r + 1) * 128] = total.T.astype(BF)
    wblk[4:7] = jnp.zeros((3, WIDE, WIDE), BF)
    for i in range(2):
        lo, hi = i * ch, (i + 1) * ch
        for k in range(3):
            wblk[4 + k, lo:hi, lo:hi] = wd[k]

    def put(e, c, rows):
        for j in range(3):
            snd[e, c, j] = rows[j * cap:(j + 1) * cap]
            halo_copy(e, c, j).start()

    def back_one(c, _):
        g = cot[c]
        up = mm_nt(g, wblk[6]).astype(BF)
        put(0, c, mm(ops_b[nodes:, :], up).astype(BF))
        acc[c] = mm(ops_b[:nodes, :], up) + mm_nt(g, wblk[5])
        return 0

    lax.fori_loop(0, chunks, back_one, 0)

    side_by_side(ser3, ser)

    @pl.when(t < tm_n - 1)
    def _():
        for c in range(chunks):
            series_copy(c).start()

    @pl.when(t == 0)
    def _():
        prev[...] = jnp.zeros_like(prev)

    @pl.when(t == tm_n - 1)
    def _():
        delayed_in[...] = jnp.zeros_like(delayed_in)

    wblk[0:4] = jnp.zeros((4, WIDE, WIDE), BF)
    for i in range(2):
        lo, hi = i * ch, (i + 1) * ch
        for k in range(2):
            wblk[k, lo:hi, lo:hi] = wf[k]
            wblk[2 + k, lo:hi, lo:hi] = wg[k]

    node_ids = lax.broadcasted_iota(jnp.int32, (nodes, cap), 0)
    slot_ids = lax.broadcasted_iota(jnp.int32, (nodes, cap), 1)
    for j in range(3):
        here = jnp.where(node_ids == snodes[j:j + 1, :], 1.0, 0.0)
        live = jnp.where(slot_ids < scount[0, j], 1.0, 0.0)
        hot = here * live
        give[:, j * cap:(j + 1) * cap] = hot.astype(BF)
        pick[j * cap:(j + 1) * cap, :] = hot.T.astype(BF)
    wacc[...] = jnp.zeros_like(wacc)
    dacc[...] = jnp.zeros_like(dacc)
    bacc[...] = jnp.zeros_like(bacc)
    cacc[...] = jnp.zeros_like(cacc)
    red1[...] = jnp.zeros_like(red1)
    red2[...] = jnp.zeros_like(red2)
    ones = jnp.ones((8, nodes), BF)

    def arrived(e, c):
        for j in range(3):
            halo_copy(e, c, j).wait_recv()
        return rcv[e, c].reshape(3 * cap, WIDE)

    def back_two(c, _):
        got = arrived(0, c)
        up = (acc[c] + mm(give[...], got)).astype(BF)
        put(2, c, mm(ops_b[nodes:, :], up).astype(BF))
        acc[c] = mm(ops_b[:nodes, :], up) + mm_nt(cot[c], wblk[4])
        return 0

    lax.fori_loop(0, chunks, back_two, 0)

    bf2 = jnp.concatenate([bf[...], bf[...]], axis=1)
    bg2 = jnp.concatenate([bg[...], bg[...]], axis=1)
    bd2 = jnp.concatenate([bd[...], bd[...]], axis=1)

    def fore_one(c, _):
        @pl.when(t > 0)
        def _():
            series_copy(c).wait_recv()

        before, now = prev[c], ser[c]
        a = jnp.tanh(mm(before, wblk[0]) + mm(now, wblk[1]) + bf2)
        act_f[c] = a
        s = jax.nn.sigmoid(mm(before, wblk[2]) + mm(now, wblk[3]) + bg2)
        act_g[c] = s
        h = (a * s).astype(BF)
        hid[c] = h
        put(1, c, mm(pick[...], h).astype(BF))
        return 0

    lax.fori_loop(0, chunks, fore_one, 0)

    def back_three(c, _):
        got = arrived(2, c)
        gh = acc[c] + mm(give[...], got)
        a, s = act_f[c], act_g[c]
        gf = (gh * s * (1.0 - a * a)).astype(BF)
        gg = (gh * a * (s * (1.0 - s))).astype(BF)
        delayed_out[c] = (mm_nt(gf, wblk[0]) + mm_nt(gg, wblk[2])).astype(BF)

        @pl.when(t > 0)
        def _():
            delayed_copy(c).start()

        g = cot[c]
        acc[c] = g.astype(F32) + mm_nt(gf, wblk[1]) + mm_nt(gg, wblk[3])
        before, now, h = prev[c], ser[c], hid[c]
        for i in range(2):
            lo, hi = i * ch, (i + 1) * ch
            right = jnp.concatenate([gf[:, lo:hi], gg[:, lo:hi]], axis=1)
            left = jnp.concatenate([before[:, lo:hi], now[:, lo:hi]], axis=1)
            wacc[...] += mm_tn(left, right)
            dacc[...] += mm_tn(h[:, lo:hi], g[:, lo:hi])
            bacc[...] += mm(ones, right)
            cacc[...] += mm(ones, g[:, lo:hi])
        return 0

    lax.fori_loop(0, chunks, back_three, 0)

    red1[0:256, :] = wacc[:, 0:128]
    red1[256:512, :] = wacc[:, 128:256]
    red1[512:640, :] = dacc[...]
    rid = lax.broadcasted_iota(jnp.int32, (8, 128), 0)
    red1[640:648, :] = jnp.where(
        rid == 0, bacc[:, 0:128], jnp.where(rid == 1, bacc[:, 128:256], cacc[...]))

    def all_sum(base, direct, red, rb, rc, sb, fin):
        part = red.shape[0] // crew

        def copy(src, dst, at, device):
            made = pltpu.make_async_remote_copy(
                src_ref=src, dst_ref=dst, send_sem=ar_s.at[at], recv_sem=ar_r.at[at],
                device_id=device, device_id_type=MESH)
            made.start()
            return made

        def rows(i):
            return pl.ds(pl.multiple_of(i * part, 8), part)

        sends = []
        for k in range(1, crew):
            o = lax.rem(me + k, crew)
            sends.append(copy(red.at[rows(o)], rb.at[k - 1], base + k, crew_device(o)))
        yield
        s = red[rows(me), :]
        for k in range(1, crew):
            sends[k - 1].wait()
            s = s + rb[k - 1]
        at = base + crew
        if direct:
            sb[0] = s
            rc[p] = s
            sends = [
                copy(sb.at[0], rc.at[p], at + k, {"seg": lax.rem(p + k, seg_n)})
                for k in range(1, seg_n)]
            yield
            for one in sends:
                one.wait()
            s = rc[0]
            for k in range(1, seg_n):
                s = s + rc[k]
        else:
            bit = 1
            for k in range(doublings):
                sb[k] = s
                mate = p + (1 - 2 * lax.rem(lax.div(p, bit), 2)) * bit
                one = copy(sb.at[k], rc.at[k], at + k, {"seg": mate})
                yield
                one.wait()
                s = s + rc[k]
                bit *= 2
        fin[rows(me), :] = s * scale
        at = at + seg_n
        sends = [
            copy(fin.at[rows(me)], fin.at[rows(me)], at + k, crew_device(lax.rem(me + k, crew)))
            for k in range(1, crew)]
        yield
        for one in sends:
            one.wait()
        yield

    first = all_sum(0, False, red1, rb1, rc1, sb1, fin1)
    next(first)
    def fore_two(c, _):
        got = arrived(1, c)
        h = (mm(ops_f[:, :nodes], hid[c]) + mm(ops_f[:, nodes:], got)).astype(BF)
        hop1[c] = h
        put(3, c, mm(pick[...], h).astype(BF))
        return 0

    for c in range(chunks):
        fore_two(c, 0)
        if c in (0, 1):
            next(first)

    for c in range(chunks):
        if c >= 2:
            next(first, None)
        got = arrived(3, c)
        h, h1, g = hid[c], hop1[c], cot[c]
        h2 = (mm(ops_f[:, :nodes], h1) + mm(ops_f[:, nodes:], got)).astype(BF)
        total = mm(h, wblk[4]) + mm(h1, wblk[5]) + mm(h2, wblk[6]) + bd2
        total = ser[c].astype(F32) + total
        for i in range(2):
            lo, hi = i * ch, (i + 1) * ch
            both = jnp.concatenate([h1[:, lo:hi], h2[:, lo:hi]], axis=1)
            red2[...] += mm_tn(both, g[:, lo:hi])
            big[:, 2 * c + i, :] = total[:, lo:hi]
    second = all_sum(2 * crew + seg_n, True, red2, rb2, rc2, sb2, fin2)
    next(second)
    out3[...] = big[...].astype(BF)
    next(second)
    for c in range(chunks):
        @pl.when(t < tm_n - 1)
        def _():
            delayed_copy(c).wait_recv()

        total = acc[c] + delayed_in[c].astype(F32)
        for i in range(2):
            big_g[:, 2 * c + i, :] = total[:, i * ch:(i + 1) * ch]
    next(second)
    gs3[...] = big_g[...].astype(BF)
    for _ in first:
        pass
    for _ in second:
        pass

    def drain(c, _):
        @pl.when(t < tm_n - 1)
        def _():
            series_copy(c).wait_send()

        @pl.when(t > 0)
        def _():
            delayed_copy(c).wait_send()

        for e in range(4):
            for j in range(3):
                halo_copy(e, c, j).wait_send()
        return 0

    lax.fori_loop(0, chunks, drain, 0)


def halo_plan(mesh, series, cotangent, w_filter, w_gate, b_filter, b_gate, w_diff, b_diff,
              tile_row, tile_col, tile_val, send_nodes, send_count):
    nodes, batch, frames, channels = series.shape
    seg_n, tm_n, rep_n = mesh.shape["seg"], mesh.shape["tm"], mesh.shape["rep"]
    chunks = batch * frames * channels // WIDE
    scale = 1.0 / math.sqrt(nodes * batch * frames * seg_n * tm_n * rep_n)
    unit = 16 * tm_n
    r1 = -(-648 // unit) * unit
    r2 = -(-256 // unit) * unit

    doublings = seg_n.bit_length() - 1
    vmem = pl.BlockSpec(memory_space=pltpu.VMEM)
    smem = pl.BlockSpec(memory_space=pltpu.SMEM)
    field = (chunks, nodes, WIDE)

    def sums(r):
        crew = 2 * tm_n
        q = r // crew
        return [
            pltpu.VMEM((crew - 1, q, 128), F32),
            pltpu.VMEM((seg_n, q, 128), F32),
            pltpu.VMEM((doublings, q, 128), F32),
        ]

    n_ar = 2 * (4 * tm_n + seg_n)
    raw = (nodes, batch * frames, channels)
    halo = (4, chunks, 3, 128, WIDE)
    out, gs, fin1, fin2 = pl.pallas_call(
        functools.partial(halo_kernel, seg_n, tm_n, scale),
        out_shape=(
            jax.ShapeDtypeStruct(raw, BF),
            jax.ShapeDtypeStruct(raw, BF),
            jax.ShapeDtypeStruct((r1, 128), F32),
            jax.ShapeDtypeStruct((r2, 128), F32),
        ),
        in_specs=[vmem] * 8 + [smem, smem, vmem, vmem, smem],
        out_specs=(vmem,) * 4,
        scratch_shapes=[
            pltpu.VMEM(raw, F32),
            pltpu.VMEM(raw, F32),
            pltpu.VMEM(field, BF),
            pltpu.VMEM(field, BF),
            pltpu.VMEM(field, BF),
            pltpu.VMEM((nodes, nodes + 384), BF),
            pltpu.VMEM((nodes + 384, nodes), BF),
            pltpu.VMEM((384, nodes), BF),
            pltpu.VMEM((nodes, 384), BF),
            pltpu.VMEM((7, WIDE, WIDE), BF),
            pltpu.VMEM(field, F32),
            pltpu.VMEM(field, F32),
            pltpu.VMEM(field, F32),
            pltpu.VMEM(field, BF),
            pltpu.VMEM(field, BF),
            pltpu.VMEM(field, BF),
            pltpu.VMEM(field, BF),
            pltpu.VMEM(halo, BF),
            pltpu.VMEM(halo, BF),
            pltpu.VMEM((256, 256), F32),
            pltpu.VMEM((128, 128), F32),
            pltpu.VMEM((8, 256), F32),
            pltpu.VMEM((8, 128), F32),
            pltpu.VMEM((r1, 128), F32),
            pltpu.VMEM((r2, 128), F32),
            *sums(r1),
            *sums(r2),
            pltpu.SemaphoreType.DMA((chunks,)),
            pltpu.SemaphoreType.DMA((chunks,)),
            pltpu.SemaphoreType.DMA((4, chunks, 3)),
            pltpu.SemaphoreType.DMA((4, chunks, 3)),
            pltpu.SemaphoreType.DMA((chunks,)),
            pltpu.SemaphoreType.DMA((chunks,)),
            pltpu.SemaphoreType.DMA((n_ar,)),
            pltpu.SemaphoreType.DMA((n_ar,)),
        ],
        compiler_params=pltpu.CompilerParams(
            collective_id=0, has_side_effects=True, vmem_limit_bytes=56 << 20),
    )(
        series.reshape(raw), cotangent.reshape(raw), w_filter, w_gate,
        b_filter.reshape(1, -1), b_gate.reshape(1, -1), w_diff, b_diff.reshape(1, -1),
        tile_row, tile_col, tile_val[0], send_nodes[0], send_count,
    )
    return (
        out.reshape(series.shape),
        gs.reshape(series.shape),
        fin1[0:256].reshape(2, 128, 128),
        fin1[256:512].reshape(2, 128, 128),
        fin1[640],
        fin1[641],
        jnp.concatenate([fin1[512:640], fin2[:256]], axis=0).reshape(3, 128, 128),
        fin1[642],
    )


def gather_kernel(
    seg_n, tm_n, scale,
    ser_h, cot_h, wf_h, wg_h, bf_h, bg_h, wd_h, bd_h, trow_h, tcol_h, tval_h, snodes_h, scount_h,
    out3, gs3, fin,
    ser3, cot3, wf, wg, bf, bg, wd, bd, trow, tcol, tval, snodes, scount, load, big, big_g, stage_s, stage_c, ser, cot, tiles, meta,
    opf, opb, oph, pick, wc, wct, wdt,
    act_f, act_g, src0, src1, hop2, sb0, sb1, acc,
    out_b, gs_b, out_r, gs_r, pair,
    red_a, red_b, low_a, low_b, a0, a1, a2, a3, b0, b1, b2, b3,
    tz_s, tz_r, mz_s, mz_r, tx_s, tx_r, tc_s, tc_r,
    se_s, se_r, co_s, co_r, ou_s, ou_r, gr_s, gr_r, ar_s, ar_r,
):
    p = lax.axis_index("seg")
    t = lax.axis_index("tm")
    rep = lax.axis_index("rep")
    loads = [
        pltpu.make_async_copy(src, dst, load.at[i])
        for i, (src, dst) in enumerate([
            (tval_h, tval), (snodes_h, snodes), (trow_h, trow), (tcol_h, tcol), (scount_h, scount),
            (ser_h, ser3), (cot_h, cot3), (wf_h, wf), (wg_h, wg), (bf_h, bf), (bg_h, bg), (wd_h, wd), (bd_h, bd)])]
    nodes, frames, ch = ser3.shape
    mine = p * tm_n + t
    crew = 2 * tm_n
    quarter = tiles.shape[1] // crew

    def rc(src, dst, ss, rs, dev):
        return pltpu.make_async_remote_copy(
            src_ref=src, dst_ref=dst, send_sem=ss, recv_sem=rs, device_id=dev, device_id_type=MESH)

    low, high = lax.rem(p, 2), lax.div(p, 2)

    def flip(j):
        return lax.rem(high + j // 2, 2) * 2 + lax.rem(low + j % 2, 2)

    def peer(j, m):
        return flip(j), lax.rem(t + m, tm_n)

    others = [(2, 0), (3, 0), (2, 1), (3, 1), (1, 0), (1, 1), (0, 1)]

    def rows_of(q):
        return pl.ds(pl.multiple_of(q * nodes, 128), nodes)

    def piece(c):
        return pl.ds(pl.multiple_of(c * quarter, 16), quarter)

    core = {"rep": 1 - rep}
    across = {"tm": 1 - t}

    barrier = pltpu.get_barrier_semaphore()
    for j, m in others:
        q, tt = peer(j, m)
        pl.semaphore_signal(barrier, inc=1, device_id={"seg": q, "tm": tt}, device_id_type=MESH)
    pl.semaphore_signal(barrier, inc=1, device_id=core, device_id_type=MESH)

    for one in loads:
        one.start()
    pl.semaphore_wait(barrier, len(others) + 1)
    loads[0].wait()

    c_me = t * 2 + rep
    c_across = (1 - t) * 2 + rep

    def tile_z(j):
        return rc(tval.at[piece(c_me)], tiles.at[p, piece(c_me)], tz_s.at[j], tz_r.at[j], {"seg": flip(j)})

    def tile_on():
        at = tiles.at[flip(2), piece(c_me)]
        return rc(at, at, tz_s.at[3], tz_r.at[3], {"seg": flip(1)})

    def meta_z(j):
        return rc(meta.at[p], meta.at[p], mz_s.at[j], mz_r.at[j], {"seg": flip(j)})

    def tile_x(j):
        at = tiles.at[flip(j), piece(c_me)]
        return rc(at, at, tx_s.at[j], tx_r.at[j], across)

    def tile_c(j, c, i):
        at = tiles.at[flip(j), piece(c)]
        return rc(at, at, tc_s.at[j, i], tc_r.at[j, i], core)

    def field_in(stage, whole, ss, rs, j, m):
        q, tt = peer(j, m)
        f = q * tm_n + tt
        return rc(stage.at[f], whole.at[t, rows_of(p)], ss.at[f], rs.at[mine], {"seg": q, "tm": tt})

    def field_got(stage, whole, ss, rs, j, m):
        q, tt = peer(j, m)
        f = q * tm_n + tt
        return rc(stage.at[f], whole.at[tt, rows_of(q)], ss.at[f], rs.at[f], {"seg": q, "tm": tt})

    def frame_major(source, wide, stage, whole):
        wide[...] = source[...].astype(F32)
        for f in range(frames):
            stage[f] = wide[:, f, :].astype(BF)
        whole[t, rows_of(p), :] = stage[mine]

    tile_z(2).start()
    tile_z(1).start()
    for one in loads[1:5]:
        one.wait()
    meta[p] = jnp.zeros_like(meta[p])
    for j in range(3):
        meta[p, j:j + 1, :] = snodes[j]
    meta[p, 3:4, 0:trow.shape[1]] = trow[...]
    meta[p, 4:5, 0:tcol.shape[1]] = tcol[...]
    meta[p, 5:6, 0:scount.shape[1]] = scount[...]
    for j in (2, 3, 1):
        meta_z(j).start()
    loads[5].wait()
    frame_major(ser3, big, stage_s, ser)
    field_in(stage_s, ser, se_s, se_r, 2, 0).start()
    tiles[p] = tval[...]

    tile_z(2).wait_recv()
    tile_on().start()
    tile_x(2).start()
    tile_z(1).wait_recv()
    tile_x(1).start()
    field_in(stage_s, ser, se_s, se_r, 3, 0).start()
    tile_on().wait_recv()
    tile_x(3).start()
    for j, m in [(2, 1), (1, 1), (3, 1), (1, 0), (0, 1)]:
        field_in(stage_s, ser, se_s, se_r, j, m).start()

    for one in loads[6:]:
        one.wait()
    frame_major(cot3, big_g, stage_c, cot)
    for j, m in others:
        field_in(stage_c, cot, co_s, co_r, j, m).start()

    for j in (2, 1, 3):
        tile_x(j).wait_recv()
        tile_c(j, c_me, 0).start()
        tile_c(j, c_across, 1).start()

    for i in range(2):
        wc[i * ch:(i + 1) * ch, 0:ch] = wf[i]
        wc[i * ch:(i + 1) * ch, ch:2 * ch] = wg[i]
    wct[...] = wc[...].astype(F32).T.astype(BF)
    for i in range(3):
        wdt[i] = wd[i].astype(F32).T.astype(BF)
    bias = jnp.concatenate([bf[...], bg[...]], axis=1)
    red_a[...] = jnp.zeros_like(red_a)
    red_b[...] = jnp.zeros_like(red_b)

    for j in (2, 1, 3):
        tile_c(j, c_me, 0).wait_recv()
        tile_c(j, c_across, 1).wait_recv()
        meta_z(j).wait_recv()

    rows_n = nodes // 128
    cols_n = rows_n + 3
    tiles_n = tiles.shape[1] // 128
    halo = 3 * 128
    lane_ids = lax.broadcasted_iota(jnp.int32, (128, nodes), 1)
    sub_ids = lax.broadcasted_iota(jnp.int32, (nodes, 128), 0)
    slot_lane = lax.broadcasted_iota(jnp.int32, (1, 128), 1)
    slot_sub = lax.broadcasted_iota(jnp.int32, (128, 1), 0)

    def build(q, _):
        info = meta[q]
        tr, tc = info[3:4, :], info[4:5, :]
        t_all = [tiles[q, k * 128:(k + 1) * 128, :].astype(F32) for k in range(tiles_n)]
        for r in range(rows_n):
            for c in range(cols_n):
                hits = jnp.where((tr == r) & (tc == c), 1.0, 0.0)
                total = jnp.zeros((128, 128), F32)
                for k in range(tiles_n):
                    if k < rows_n and (r != k or c != k):
                        continue
                    if rows_n <= k < cols_n and c != k:
                        continue
                    total = total + hits[:, k:k + 1] * t_all[k]
                flipped = total.T.astype(BF)
                opf[q, r * 128:(r + 1) * 128, c * 128:(c + 1) * 128] = total.astype(BF)
                if c < rows_n:
                    opb[q, c * 128:(c + 1) * 128, r * 128:(r + 1) * 128] = flipped
                else:
                    oph[q, (c - rows_n) * 128:(c - rows_n + 1) * 128, r * 128:(r + 1) * 128] = flipped
        col = info.astype(F32).T.astype(jnp.int32)
        for j in range(3):
            count = info[5:6, j:j + 1]
            give = jnp.where((sub_ids == info[j:j + 1, :]) & (slot_lane < count), 1.0, 0.0)
            opb[q, :, nodes + j * 128:nodes + (j + 1) * 128] = give.astype(BF)
            take = jnp.where((lane_ids == col[:, j:j + 1]) & (slot_sub < count), 1.0, 0.0)
            pick[q, j * 128:(j + 1) * 128, :] = take.astype(BF)
        return 0

    lax.fori_loop(0, seg_n, build, 0)

    for j, m in others:
        field_got(stage_s, ser, se_s, se_r, j, m).wait_recv()

    def conv(q, _):
        for tt in range(tm_n):
            now = ser[tt, rows_of(q), :]
            if tt == 0:
                pre = mm(now, wc[ch:2 * ch, :]) + bias
            else:
                pre = mm(jnp.concatenate([ser[tt - 1, rows_of(q), :], now], axis=1), wc[...]) + bias
            a = jnp.tanh(pre[:, 0:ch])
            s = jax.nn.sigmoid(pre[:, ch:2 * ch])
            act_f[tt, rows_of(q), :] = a
            act_g[tt, rows_of(q), :] = s
            src0[q, 0:nodes, tt * ch:(tt + 1) * ch] = (a * s).astype(BF)
        return 0

    def send_slots(src):
        def one(q, _):
            got = mm(pick[q], src[q, 0:nodes, :]).astype(BF)
            for j in range(3):
                reader = lax.rem(q - STEPS[j] + seg_n, seg_n)
                src[reader, nodes + j * 128:nodes + (j + 1) * 128, :] = got[j * 128:(j + 1) * 128]
            return 0
        lax.fori_loop(0, seg_n, one, 0)

    def hop(src, dst):
        def one(q, _):
            dst[q, 0:nodes, :] = mm(opf[q], src[q]).astype(BF)
            return 0
        lax.fori_loop(0, seg_n, one, 0)

    def home(buf, got, ss, rs, q, tt):
        return rc(buf.at[tt, rows_of(q)], got.at[mine], ss.at[q * tm_n + tt], rs.at[mine], {"seg": q, "tm": tt})

    def gs_arrived(f):
        for h in range(2):
            rc(gs_b.at[f % tm_n, pl.ds(f // tm_n * nodes + h * part, part)], gs_r.at[f, pl.ds(h * part, part)],
               gr_s.at[f, h], gr_r.at[f, h], {"seg": f // tm_n, "tm": f % tm_n}).wait_recv()

    def out_arrived(f):
        arrived(out_b, out_r, ou_s, ou_r, f).wait_recv()

    def arrived(buf, got, ss, rs, f):
        return rc(buf.at[f % tm_n, pl.ds(f // tm_n * nodes, nodes)], got.at[f], ss.at[f], rs.at[f],
                  {"seg": f // tm_n, "tm": f % tm_n})

    def out_go(*pairs):
        for j, m in pairs:
            q, tt = peer(j, m)
            home(out_b, out_r, ou_s, ou_r, q, tt).start()

    part = nodes // 2

    def gs_half(q, tt, h):
        start = pl.ds(pl.multiple_of(q * nodes + h * part, 16), part)
        return rc(gs_b.at[tt, start], gs_r.at[mine, pl.ds(h * part, part)],
                  gr_s.at[q * tm_n + tt, h], gr_r.at[mine, h], {"seg": q, "tm": tt})

    def gs_go(*pairs):
        for j, m, h in pairs:
            q, tt = peer(j, m)
            gs_half(q, tt, h).start()

    lax.fori_loop(0, seg_n, conv, 0)
    send_slots(src0)
    hop(src0, src1)
    send_slots(src1)
    hop(src1, hop2)
    bias_d = bd[...]

    def put_out(q, _):
        for tt in range(tm_n):
            lo, hi = tt * ch, (tt + 1) * ch
            two = jnp.concatenate([src0[q, 0:nodes, lo:hi], src1[q, 0:nodes, lo:hi]], axis=1)
            total = mm(two, jnp.concatenate([wd[0], wd[1]], axis=0)) + mm(hop2[q, :, lo:hi], wd[2]) + bias_d
            out_b[tt, rows_of(q), :] = (ser[tt, rows_of(q), :].astype(F32) + total).astype(BF)
        return 0

    lax.fori_loop(0, seg_n, put_out, 0)
    out_go((2, 1), (1, 1), (3, 1), (1, 0), (0, 1))

    for j, m in others:
        field_got(stage_c, cot, co_s, co_r, j, m).wait_recv()

    base = 4 * ch

    def span(start, size):
        return pl.ds(pl.multiple_of(start, 16), size)

    def quad_device(m, k):
        return {"seg": flip(k), "tm": lax.rem(t + m, 2)}

    def summed(red, b0, b1, b2, b3, low_out, first):
        half = red.shape[0] // 2
        eighth = half // 4
        at_core = rep * half

        def at_quad(m, k):
            return span(at_core + lax.rem(t + m, 2) * (2 * eighth) + lax.rem(low + k, 2) * eighth, eighth)

        def go(src, dst, at, dev):
            made = rc(src, dst, ar_s.at[first + at], ar_r.at[first + at], dev)
            made.start()
            return made

        quad = [(1, 1), (1, 0), (0, 1)]
        here = at_quad(0, 0)
        step = go(red.at[span((1 - rep) * half, half)], b0, 0, core)
        yield
        step.wait()
        red[span(at_core, half), :] += b0[...]
        steps = [
            go(red.at[at_quad(m, k)], b1.at[i], 1 + i, quad_device(m, k))
            for i, (m, k) in enumerate(quad)]
        yield
        for step in steps:
            step.wait()
        b3[...] = (red[here, :] + b1[0] + b1[1] + b1[2]).astype(BF)
        step = go(b3, b2, 4, {"seg": flip(2)})
        yield
        step.wait()
        low_out[here, :] = ((b3[...].astype(F32) + b2[...].astype(F32)) * scale).astype(BF)
        steps = [
            go(low_out.at[here], low_out.at[here], 5 + i, quad_device(m, k))
            for i, (m, k) in enumerate(quad)]
        yield
        for step in steps:
            step.wait()
        whole = low_out.at[span(at_core, half)]
        step = go(whole, whole, 8, core)
        yield
        step.wait()
        yield

    sum_a = summed(red_a, a0, a1, a2, a3, low_a, 0)
    sum_b = summed(red_b, b0, b1, b2, b3, low_b, 9)

    def back(q, _):
        for tt in range(tm_n):
            lo, hi = tt * ch, (tt + 1) * ch
            g = cot[tt, rows_of(q), :]
            u = mm(g, jnp.concatenate([wdt[2], wdt[1]], axis=1))
            sb0[q, 0:nodes, lo:hi] = u[:, 0:ch].astype(BF)
            acc[q, :, lo:hi] = u[:, ch:2 * ch]
            hops = jnp.concatenate(
                [src0[q, 0:nodes, lo:hi], src1[q, 0:nodes, lo:hi], hop2[q, :, lo:hi]], axis=1)
            red_a[...] += mm_tn(hops, g)
            red_b[base + 2:base + 3, :] += jnp.sum(g.astype(F32), axis=0, keepdims=True)
        return 0

    def send_back(sb):
        def one(q, _):
            got = mm(oph[q], sb[q, 0:nodes, :]).astype(BF)
            for j in range(3):
                owner = lax.rem(q + STEPS[j] + seg_n, seg_n)
                sb[owner, nodes + j * 128:nodes + (j + 1) * 128, :] = got[j * 128:(j + 1) * 128]
            return 0
        lax.fori_loop(0, seg_n, one, 0)

    lax.fori_loop(0, seg_n, back, 0)
    next(sum_a)
    send_back(sb0)

    def back_mid(q, _):
        sb1[q, 0:nodes, :] = (acc[q] + mm(opb[q], sb0[q])).astype(BF)
        return 0

    next(sum_a)
    lax.fori_loop(0, seg_n, back_mid, 0)
    out_go((2, 0), (3, 0))
    send_back(sb1)

    def back_last(q, _):
        gh_all = mm(opb[q], sb1[q])
        for tt in range(tm_n):
            lo, hi = tt * ch, (tt + 1) * ch
            g = cot[tt, rows_of(q), :]
            gh = gh_all[:, lo:hi] + mm(g, wdt[0])
            a, s = act_f[tt, rows_of(q), :], act_g[tt, rows_of(q), :]
            gf = (gh * s * (1.0 - a * a)).astype(BF)
            gg = (gh * a * (s * (1.0 - s))).astype(BF)
            both = jnp.concatenate([gf, gg], axis=1)
            pair[tt, rows_of(q), :] = both
            now = ser[tt, rows_of(q), :]
            if tt == 0:
                part = mm_tn(now, both)
                red_b[ch:2 * ch, :] += part[:, 0:ch]
                red_b[3 * ch:4 * ch, :] += part[:, ch:2 * ch]
            else:
                part = mm_tn(jnp.concatenate([ser[tt - 1, rows_of(q), :], now], axis=1), both)
                red_b[0:2 * ch, :] += part[:, 0:ch]
                red_b[2 * ch:4 * ch, :] += part[:, ch:2 * ch]
            red_b[base:base + 1, :] += jnp.sum(gf.astype(F32), axis=0, keepdims=True)
            red_b[base + 1:base + 2, :] += jnp.sum(gg.astype(F32), axis=0, keepdims=True)
        return 0

    lax.fori_loop(0, seg_n, back_last, 0)

    next(sum_b)
    next(sum_a)

    def put_gs(q, _):
        later = None
        for tt in reversed(range(tm_n)):
            both = pair[tt, rows_of(q), :]
            if tt == 0:
                total = mm(both, wct[:, ch:2 * ch])
            else:
                r = mm(both, wct[...])
                total = r[:, ch:2 * ch]
            total = cot[tt, rows_of(q), :].astype(F32) + total
            if later is not None:
                total = total + later.astype(F32)
            if tt > 0:
                later = r[:, 0:ch].astype(BF)
            gs_b[tt, rows_of(q), :] = total.astype(BF)
        return 0

    lax.fori_loop(0, seg_n, put_gs, 0)
    next(sum_b)
    gs_go((2, 0, 0),)
    out_r[mine] = out_b[t, rows_of(p), :]
    gs_r[mine] = gs_b[t, rows_of(p), :]

    def node_major(got, wide, dest, ready):
        def take(order):
            for f in order:
                @pl.when(f != mine)
                def _():
                    ready(f)

                wide[:, f, :] = got[f].astype(F32)

        early, late = list(range(frames // 2)), list(range(frames // 2, frames))

        @pl.when(high == 0)
        def _():
            take(early + late)

        @pl.when(high == 1)
        def _():
            take(late + early)

        dest[...] = wide[...].astype(BF)

    next(sum_b)
    gs_go((2, 1, 0), (1, 1, 0), (2, 1, 1), (1, 1, 1), (2, 0, 1))
    next(sum_a)
    gs_go((3, 1, 0), (1, 0, 0), (3, 1, 1), (1, 0, 1), (3, 0, 0), (0, 1, 0), (3, 0, 1), (0, 1, 1))
    next(sum_b)
    node_major(out_r, big, out3, out_arrived)
    next(sum_a)
    next(sum_b)
    next(sum_a)
    fin[base:base + 3 * ch, :] = low_a[...].astype(F32)
    node_major(gs_r, big_g, gs3, gs_arrived)
    next(sum_b)
    fin[0:base, :] = low_b[0:base, :].astype(F32)
    fin[base + 3 * ch:base + 3 * ch + 16, :] = low_b[base:base + 16, :].astype(F32)

    tile_z(2).wait_send()
    tile_z(1).wait_send()
    tile_on().wait_send()
    for j in (1, 2, 3):
        meta_z(j).wait_send()
        tile_x(j).wait_send()
        tile_c(j, c_me, 0).wait_send()
        tile_c(j, c_across, 1).wait_send()
    for j, m in others:
        q, tt = peer(j, m)
        field_in(stage_s, ser, se_s, se_r, j, m).wait_send()
        field_in(stage_c, cot, co_s, co_r, j, m).wait_send()
        home(out_b, out_r, ou_s, ou_r, q, tt).wait_send()
        gs_half(q, tt, 0).wait_send()
        gs_half(q, tt, 1).wait_send()


def finish_kernel(out_i, gs_i, fin, out_o, gs_o, o_wf, o_wg, o_bf, o_bg, o_wd, o_bd, sems):
    ch = o_wf.shape[1]
    pairs = [(out_i, out_o), (gs_i, gs_o)]
    for i in range(7):
        target = o_wf.at[i] if i < 2 else o_wg.at[i - 2] if i < 4 else o_wd.at[i - 4]
        pairs.append((fin.at[pl.ds(i * ch, ch)], target))
    for i, target in enumerate((o_bf, o_bg, o_bd)):
        pairs.append((fin.at[pl.ds(7 * ch + i, 1)], target))
    copies = [pltpu.make_async_copy(src, dst, sems.at[i]) for i, (src, dst) in enumerate(pairs)]
    for one in copies:
        one.start()
    for one in copies:
        one.wait()


def gather_plan(mesh, series, cotangent, w_filter, w_gate, b_filter, b_gate, w_diff, b_diff,
                tile_row, tile_col, tile_val, send_nodes, send_count):
    nodes, batch, frames, ch = series.shape
    seg_n, tm_n, rep_n = mesh.shape["seg"], mesh.shape["tm"], mesh.shape["rep"]
    scale = 1.0 / math.sqrt(nodes * batch * frames * seg_n * tm_n * rep_n)
    unit = 16 * 8
    rows_a = 3 * ch
    rows_b = -(-(4 * ch + 8) // unit) * unit
    total_rows = 7 * ch + 16

    def steps_of(rows):
        return [
            pltpu.VMEM((rows // 2, ch), F32),
            pltpu.VMEM((3, rows // 8, ch), F32),
            pltpu.VMEM((rows // 8, ch), BF),
            pltpu.VMEM((rows // 8, ch), BF),
        ]

    vmem = pl.BlockSpec(memory_space=pltpu.VMEM)
    anyw = pl.BlockSpec(memory_space=pl.ANY)
    raw = (nodes, batch * frames, ch)
    tall = (frames, nodes, ch)
    everyone = (tm_n, seg_n * nodes, ch)
    wide = tm_n * ch
    tile_rows = tile_val.shape[1] * 128
    halo = 3 * 128
    dma = pltpu.SemaphoreType.DMA
    out, gs, fin = pl.pallas_call(
        functools.partial(gather_kernel, seg_n, tm_n, scale),
        out_shape=(
            pltpu.VMEM(raw, BF),
            pltpu.VMEM(raw, BF),
            pltpu.VMEM((total_rows, ch), F32),
        ),
        in_specs=[anyw] * 13,
        out_specs=(vmem,) * 3,
        scratch_shapes=[
            pltpu.VMEM(raw, BF),
            pltpu.VMEM(raw, BF),
            pltpu.VMEM(w_filter.shape, BF),
            pltpu.VMEM(w_gate.shape, BF),
            pltpu.VMEM((1, ch), F32),
            pltpu.VMEM((1, ch), F32),
            pltpu.VMEM(w_diff.shape, BF),
            pltpu.VMEM((1, ch), F32),
            pltpu.VMEM(tile_row.shape, jnp.int32),
            pltpu.VMEM(tile_col.shape, jnp.int32),
            pltpu.VMEM((tile_rows, 128), BF),
            pltpu.VMEM((3, 1, 128), jnp.int32),
            pltpu.VMEM(send_count.shape, jnp.int32),
            dma((13,)),
            pltpu.VMEM(raw, F32),
            pltpu.VMEM(raw, F32),
            pltpu.VMEM(tall, BF),
            pltpu.VMEM(tall, BF),
            pltpu.VMEM(everyone, BF),
            pltpu.VMEM(everyone, BF),
            pltpu.VMEM((seg_n, tile_rows, 128), BF),
            pltpu.VMEM((seg_n, 8, 128), jnp.int32),
            pltpu.VMEM((seg_n, nodes, nodes + halo), BF),
            pltpu.VMEM((seg_n, nodes, nodes + halo), BF),
            pltpu.VMEM((seg_n, halo, nodes), BF),
            pltpu.VMEM((seg_n, halo, nodes), BF),
            pltpu.VMEM((2 * ch, 2 * ch), BF),
            pltpu.VMEM((2 * ch, 2 * ch), BF),
            pltpu.VMEM((3, ch, ch), BF),
            pltpu.VMEM(everyone, F32),
            pltpu.VMEM(everyone, F32),
            pltpu.VMEM((seg_n, nodes + halo, wide), BF),
            pltpu.VMEM((seg_n, nodes + halo, wide), BF),
            pltpu.VMEM((seg_n, nodes, wide), BF),
            pltpu.VMEM((seg_n, nodes + halo, wide), BF),
            pltpu.VMEM((seg_n, nodes + halo, wide), BF),
            pltpu.VMEM((seg_n, nodes, wide), F32),
            pltpu.VMEM(everyone, BF),
            pltpu.VMEM(everyone, BF),
            pltpu.VMEM(tall, BF),
            pltpu.VMEM(tall, BF),
            pltpu.VMEM((tm_n, seg_n * nodes, 2 * ch), BF),
            pltpu.VMEM((rows_a, ch), F32),
            pltpu.VMEM((rows_b, ch), F32),
            pltpu.VMEM((rows_a, ch), BF),
            pltpu.VMEM((rows_b, ch), BF),
            *steps_of(rows_a),
            *steps_of(rows_b),
            dma((seg_n,)), dma((seg_n,)), dma((seg_n,)), dma((seg_n,)),
            dma((seg_n,)), dma((seg_n,)), dma((seg_n, 2)), dma((seg_n, 2)),
            dma((frames,)), dma((frames,)), dma((frames,)), dma((frames,)),
            dma((frames,)), dma((frames,)), dma((frames, 2)), dma((frames, 2)),
            dma((18,)), dma((18,)),
        ],
        compiler_params=pltpu.CompilerParams(
            collective_id=0, has_side_effects=True, vmem_limit_bytes=52 << 20),
    )(
        series.reshape(raw), cotangent.reshape(raw), w_filter, w_gate,
        b_filter.reshape(1, -1), b_gate.reshape(1, -1), w_diff, b_diff.reshape(1, -1),
        tile_row, tile_col, tile_val.reshape(tile_rows, 128), send_nodes.reshape(3, 1, 128), send_count,
    )
    vec = jax.ShapeDtypeStruct((1, ch), F32)
    out, gs, g_wf, g_wg, g_bf, g_bg, g_wd, g_bd = pl.pallas_call(
        finish_kernel,
        out_shape=(
            jax.ShapeDtypeStruct(raw, BF),
            jax.ShapeDtypeStruct(raw, BF),
            jax.ShapeDtypeStruct((2, ch, ch), F32),
            jax.ShapeDtypeStruct((2, ch, ch), F32),
            vec, vec,
            jax.ShapeDtypeStruct((3, ch, ch), F32),
            vec,
        ),
        in_specs=[anyw, anyw, vmem],
        out_specs=(anyw,) * 8,
        scratch_shapes=[dma((12,))],
    )(*[pltpu.with_memory_space_constraint(x, pltpu.VMEM) for x in (out, gs, fin)])
    return (
        out.reshape(series.shape), gs.reshape(series.shape), g_wf, g_wg,
        g_bf.reshape(-1), g_bg.reshape(-1), g_wd, g_bd.reshape(-1))


def on_device(mesh, series, *rest):
    nodes, batch, frames, ch = series.shape
    seg_n, tm_n = mesh.shape["seg"], mesh.shape["tm"]
    fits = seg_n == 4 and tm_n == 2 and batch == 1 and frames == seg_n * tm_n and frames == DILATION_FRAMES
    plan = gather_plan if fits else halo_plan
    return plan(mesh, series, *rest)


def solution(mesh):
    field = P(("grp", "seg"), "rep", "tm", None)
    part = ("grp", "seg")
    in_specs = (
        field, field, P(), P(), P(), P(), P(), P(),
        P(part, None), P(part, None), P(part, None, None, None), P(part, None, None), P(part, None),
    )
    out_specs = (
        field, field, P("grp", None, None), P("grp", None, None), P("grp"), P("grp"),
        P("grp", None, None), P("grp"),
    )
    return jax.shard_map(
        functools.partial(on_device, mesh), mesh=mesh, in_specs=in_specs, out_specs=out_specs,
        check_vma=False)
```

```python
import functools
import math

import jax
import jax.numpy as jnp
from jax import lax
from jax.experimental import pallas as pl
from jax.experimental.pallas import tpu as pltpu
from jax.sharding import PartitionSpec as P

DILATION_FRAMES = 8
STEPS = (1, -1, 2)
MESH = pl.DeviceIdType.MESH
WIDE = 256
BF = jnp.bfloat16
F32 = jnp.float32


def mm(a, b):
    return lax.dot_general(a, b, (((1,), (0,)), ((), ())), preferred_element_type=F32)


def mm_nt(a, b):
    return lax.dot_general(a, b, (((1,), (1,)), ((), ())), preferred_element_type=F32)


def mm_tn(a, b):
    return lax.dot_general(a, b, (((0,), (0,)), ((), ())), preferred_element_type=F32)


def halo_kernel(
    seg_n, tm_n, scale,
    ser3, cot3, wf, wg, bf, bg, wd, bd, trow, tcol, tval, snodes, scount,
    out3, gs3, fin1, fin2,
    big, big_g, ser, cot, prev, ops_f, ops_b, pick, give, wblk,
    acc, act_f, act_g, hid, hop1, delayed_out, delayed_in,
    snd, rcv, wacc, dacc, bacc, cacc,
    red1, red2, rb1, rc1, sb1, rb2, rc2, sb2,
    tm_s, tm_r, ex_s, ex_r, dl_s, dl_r, ar_s, ar_r,
):
    p = lax.axis_index("seg")
    t = lax.axis_index("tm")
    rep = lax.axis_index("rep")
    chunks, nodes, _ = ser.shape
    doublings = seg_n.bit_length() - 1
    cap = 128
    ch = 128

    barrier = pltpu.get_barrier_semaphore()
    for k in range(1, seg_n):
        pl.semaphore_signal(barrier, inc=1, device_id={"seg": lax.rem(p + k, seg_n)}, device_id_type=MESH)
    crew = 2 * tm_n
    me = t * 2 + rep

    def crew_device(i):
        return {"tm": lax.div(i, 2), "rep": lax.rem(i, 2)}

    for k in range(1, crew):
        pl.semaphore_signal(barrier, inc=1, device_id=crew_device(lax.rem(me + k, crew)), device_id_type=MESH)
    pl.semaphore_wait(barrier, seg_n - 1 + crew - 1)

    def series_copy(c):
        return pltpu.make_async_remote_copy(
            src_ref=ser.at[c], dst_ref=prev.at[c], send_sem=tm_s.at[c], recv_sem=tm_r.at[c],
            device_id={"tm": lax.rem(t + 1, tm_n)}, device_id_type=MESH)

    def delayed_copy(c):
        return pltpu.make_async_remote_copy(
            src_ref=delayed_out.at[c], dst_ref=delayed_in.at[c], send_sem=dl_s.at[c], recv_sem=dl_r.at[c],
            device_id={"tm": lax.rem(t + tm_n - 1, tm_n)}, device_id_type=MESH)

    def halo_copy(e, c, j):
        step = STEPS[j] if e % 2 == 0 else -STEPS[j]
        return pltpu.make_async_remote_copy(
            src_ref=snd.at[e, c, j], dst_ref=rcv.at[e, c, j],
            send_sem=ex_s.at[e, c, j], recv_sem=ex_r.at[e, c, j],
            device_id={"seg": lax.rem(p + step + seg_n, seg_n)}, device_id_type=MESH)

    def side_by_side(src, dst):
        big[...] = src[...].astype(F32)
        for c in range(chunks):
            dst[c] = jnp.concatenate([big[:, 2 * c, :], big[:, 2 * c + 1, :]], axis=1).astype(BF)

    side_by_side(cot3, cot)

    rows_n, cols_n, tiles_n = nodes // 128, nodes // 128 + 3, tval.shape[0]
    for r in range(rows_n):
        for c in range(cols_n):
            total = jnp.zeros((128, 128), F32)
            for k in range(tiles_n):
                if k < rows_n and (r != k or c != k):
                    continue
                if rows_n <= k < cols_n and c != k:
                    continue
                hit = jnp.where(trow[0, k] == r, 1.0, 0.0) * jnp.where(tcol[0, k] == c, 1.0, 0.0)
                total = total + hit * tval[k].astype(F32)
            ops_f[r * 128:(r + 1) * 128, c * 128:(c + 1) * 128] = total.astype(BF)
            ops_b[c * 128:(c + 1) * 128, r * 128:(r + 1) * 128] = total.T.astype(BF)
    wblk[4:7] = jnp.zeros((3, WIDE, WIDE), BF)
    for i in range(2):
        lo, hi = i * ch, (i + 1) * ch
        for k in range(3):
            wblk[4 + k, lo:hi, lo:hi] = wd[k]

    def put(e, c, rows):
        for j in range(3):
            snd[e, c, j] = rows[j * cap:(j + 1) * cap]
            halo_copy(e, c, j).start()

    def back_one(c, _):
        g = cot[c]
        up = mm_nt(g, wblk[6]).astype(BF)
        put(0, c, mm(ops_b[nodes:, :], up).astype(BF))
        acc[c] = mm(ops_b[:nodes, :], up) + mm_nt(g, wblk[5])
        return 0

    lax.fori_loop(0, chunks, back_one, 0)

    side_by_side(ser3, ser)

    @pl.when(t < tm_n - 1)
    def _():
        for c in range(chunks):
            series_copy(c).start()

    @pl.when(t == 0)
    def _():
        prev[...] = jnp.zeros_like(prev)

    @pl.when(t == tm_n - 1)
    def _():
        delayed_in[...] = jnp.zeros_like(delayed_in)

    wblk[0:4] = jnp.zeros((4, WIDE, WIDE), BF)
    for i in range(2):
        lo, hi = i * ch, (i + 1) * ch
        for k in range(2):
            wblk[k, lo:hi, lo:hi] = wf[k]
            wblk[2 + k, lo:hi, lo:hi] = wg[k]

    node_ids = lax.broadcasted_iota(jnp.int32, (nodes, cap), 0)
    slot_ids = lax.broadcasted_iota(jnp.int32, (nodes, cap), 1)
    for j in range(3):
        here = jnp.where(node_ids == snodes[j:j + 1, :], 1.0, 0.0)
        live = jnp.where(slot_ids < scount[0, j], 1.0, 0.0)
        hot = here * live
        give[:, j * cap:(j + 1) * cap] = hot.astype(BF)
        pick[j * cap:(j + 1) * cap, :] = hot.T.astype(BF)
    wacc[...] = jnp.zeros_like(wacc)
    dacc[...] = jnp.zeros_like(dacc)
    bacc[...] = jnp.zeros_like(bacc)
    cacc[...] = jnp.zeros_like(cacc)
    red1[...] = jnp.zeros_like(red1)
    red2[...] = jnp.zeros_like(red2)
    ones = jnp.ones((8, nodes), BF)

    def arrived(e, c):
        for j in range(3):
            halo_copy(e, c, j).wait_recv()
        return rcv[e, c].reshape(3 * cap, WIDE)

    def back_two(c, _):
        got = arrived(0, c)
        up = (acc[c] + mm(give[...], got)).astype(BF)
        put(2, c, mm(ops_b[nodes:, :], up).astype(BF))
        acc[c] = mm(ops_b[:nodes, :], up) + mm_nt(cot[c], wblk[4])
        return 0

    lax.fori_loop(0, chunks, back_two, 0)

    bf2 = jnp.concatenate([bf[...], bf[...]], axis=1)
    bg2 = jnp.concatenate([bg[...], bg[...]], axis=1)
    bd2 = jnp.concatenate([bd[...], bd[...]], axis=1)

    def fore_one(c, _):
        @pl.when(t > 0)
        def _():
            series_copy(c).wait_recv()

        before, now = prev[c], ser[c]
        a = jnp.tanh(mm(before, wblk[0]) + mm(now, wblk[1]) + bf2)
        act_f[c] = a
        s = jax.nn.sigmoid(mm(before, wblk[2]) + mm(now, wblk[3]) + bg2)
        act_g[c] = s
        h = (a * s).astype(BF)
        hid[c] = h
        put(1, c, mm(pick[...], h).astype(BF))
        return 0

    lax.fori_loop(0, chunks, fore_one, 0)

    def back_three(c, _):
        got = arrived(2, c)
        gh = acc[c] + mm(give[...], got)
        a, s = act_f[c], act_g[c]
        gf = (gh * s * (1.0 - a * a)).astype(BF)
        gg = (gh * a * (s * (1.0 - s))).astype(BF)
        delayed_out[c] = (mm_nt(gf, wblk[0]) + mm_nt(gg, wblk[2])).astype(BF)

        @pl.when(t > 0)
        def _():
            delayed_copy(c).start()

        g = cot[c]
        acc[c] = g.astype(F32) + mm_nt(gf, wblk[1]) + mm_nt(gg, wblk[3])
        before, now, h = prev[c], ser[c], hid[c]
        for i in range(2):
            lo, hi = i * ch, (i + 1) * ch
            right = jnp.concatenate([gf[:, lo:hi], gg[:, lo:hi]], axis=1)
            left = jnp.concatenate([before[:, lo:hi], now[:, lo:hi]], axis=1)
            wacc[...] += mm_tn(left, right)
            dacc[...] += mm_tn(h[:, lo:hi], g[:, lo:hi])
            bacc[...] += mm(ones, right)
            cacc[...] += mm(ones, g[:, lo:hi])
        return 0

    lax.fori_loop(0, chunks, back_three, 0)

    red1[0:256, :] = wacc[:, 0:128]
    red1[256:512, :] = wacc[:, 128:256]
    red1[512:640, :] = dacc[...]
    rid = lax.broadcasted_iota(jnp.int32, (8, 128), 0)
    red1[640:648, :] = jnp.where(
        rid == 0, bacc[:, 0:128], jnp.where(rid == 1, bacc[:, 128:256], cacc[...]))

    def all_sum(base, direct, red, rb, rc, sb, fin):
        part = red.shape[0] // crew

        def copy(src, dst, at, device):
            made = pltpu.make_async_remote_copy(
                src_ref=src, dst_ref=dst, send_sem=ar_s.at[at], recv_sem=ar_r.at[at],
                device_id=device, device_id_type=MESH)
            made.start()
            return made

        def rows(i):
            return pl.ds(pl.multiple_of(i * part, 8), part)

        sends = []
        for k in range(1, crew):
            o = lax.rem(me + k, crew)
            sends.append(copy(red.at[rows(o)], rb.at[k - 1], base + k, crew_device(o)))
        yield
        s = red[rows(me), :]
        for k in range(1, crew):
            sends[k - 1].wait()
            s = s + rb[k - 1]
        at = base + crew
        if direct:
            sb[0] = s
            rc[p] = s
            sends = [
                copy(sb.at[0], rc.at[p], at + k, {"seg": lax.rem(p + k, seg_n)})
                for k in range(1, seg_n)]
            yield
            for one in sends:
                one.wait()
            s = rc[0]
            for k in range(1, seg_n):
                s = s + rc[k]
        else:
            bit = 1
            for k in range(doublings):
                sb[k] = s
                mate = p + (1 - 2 * lax.rem(lax.div(p, bit), 2)) * bit
                one = copy(sb.at[k], rc.at[k], at + k, {"seg": mate})
                yield
                one.wait()
                s = s + rc[k]
                bit *= 2
        fin[rows(me), :] = s * scale
        at = at + seg_n
        sends = [
            copy(fin.at[rows(me)], fin.at[rows(me)], at + k, crew_device(lax.rem(me + k, crew)))
            for k in range(1, crew)]
        yield
        for one in sends:
            one.wait()
        yield

    first = all_sum(0, False, red1, rb1, rc1, sb1, fin1)
    next(first)
    def fore_two(c, _):
        got = arrived(1, c)
        h = (mm(ops_f[:, :nodes], hid[c]) + mm(ops_f[:, nodes:], got)).astype(BF)
        hop1[c] = h
        put(3, c, mm(pick[...], h).astype(BF))
        return 0

    for c in range(chunks):
        fore_two(c, 0)
        if c in (0, 1):
            next(first)

    for c in range(chunks):
        if c >= 2:
            next(first, None)
        got = arrived(3, c)
        h, h1, g = hid[c], hop1[c], cot[c]
        h2 = (mm(ops_f[:, :nodes], h1) + mm(ops_f[:, nodes:], got)).astype(BF)
        total = mm(h, wblk[4]) + mm(h1, wblk[5]) + mm(h2, wblk[6]) + bd2
        total = ser[c].astype(F32) + total
        for i in range(2):
            lo, hi = i * ch, (i + 1) * ch
            both = jnp.concatenate([h1[:, lo:hi], h2[:, lo:hi]], axis=1)
            red2[...] += mm_tn(both, g[:, lo:hi])
            big[:, 2 * c + i, :] = total[:, lo:hi]
    second = all_sum(2 * crew + seg_n, True, red2, rb2, rc2, sb2, fin2)
    next(second)
    out3[...] = big[...].astype(BF)
    next(second)
    for c in range(chunks):
        @pl.when(t < tm_n - 1)
        def _():
            delayed_copy(c).wait_recv()

        total = acc[c] + delayed_in[c].astype(F32)
        for i in range(2):
            big_g[:, 2 * c + i, :] = total[:, i * ch:(i + 1) * ch]
    next(second)
    gs3[...] = big_g[...].astype(BF)
    for _ in first:
        pass
    for _ in second:
        pass

    def drain(c, _):
        @pl.when(t < tm_n - 1)
        def _():
            series_copy(c).wait_send()

        @pl.when(t > 0)
        def _():
            delayed_copy(c).wait_send()

        for e in range(4):
            for j in range(3):
                halo_copy(e, c, j).wait_send()
        return 0

    lax.fori_loop(0, chunks, drain, 0)


def halo_plan(mesh, series, cotangent, w_filter, w_gate, b_filter, b_gate, w_diff, b_diff,
              tile_row, tile_col, tile_val, send_nodes, send_count):
    nodes, batch, frames, channels = series.shape
    seg_n, tm_n, rep_n = mesh.shape["seg"], mesh.shape["tm"], mesh.shape["rep"]
    chunks = batch * frames * channels // WIDE
    scale = 1.0 / math.sqrt(nodes * batch * frames * seg_n * tm_n * rep_n)
    unit = 16 * tm_n
    r1 = -(-648 // unit) * unit
    r2 = -(-256 // unit) * unit

    doublings = seg_n.bit_length() - 1
    vmem = pl.BlockSpec(memory_space=pltpu.VMEM)
    smem = pl.BlockSpec(memory_space=pltpu.SMEM)
    field = (chunks, nodes, WIDE)

    def sums(r):
        crew = 2 * tm_n
        q = r // crew
        return [
            pltpu.VMEM((crew - 1, q, 128), F32),
            pltpu.VMEM((seg_n, q, 128), F32),
            pltpu.VMEM((doublings, q, 128), F32),
        ]

    n_ar = 2 * (4 * tm_n + seg_n)
    raw = (nodes, batch * frames, channels)
    halo = (4, chunks, 3, 128, WIDE)
    out, gs, fin1, fin2 = pl.pallas_call(
        functools.partial(halo_kernel, seg_n, tm_n, scale),
        out_shape=(
            jax.ShapeDtypeStruct(raw, BF),
            jax.ShapeDtypeStruct(raw, BF),
            jax.ShapeDtypeStruct((r1, 128), F32),
            jax.ShapeDtypeStruct((r2, 128), F32),
        ),
        in_specs=[vmem] * 8 + [smem, smem, vmem, vmem, smem],
        out_specs=(vmem,) * 4,
        scratch_shapes=[
            pltpu.VMEM(raw, F32),
            pltpu.VMEM(raw, F32),
            pltpu.VMEM(field, BF),
            pltpu.VMEM(field, BF),
            pltpu.VMEM(field, BF),
            pltpu.VMEM((nodes, nodes + 384), BF),
            pltpu.VMEM((nodes + 384, nodes), BF),
            pltpu.VMEM((384, nodes), BF),
            pltpu.VMEM((nodes, 384), BF),
            pltpu.VMEM((7, WIDE, WIDE), BF),
            pltpu.VMEM(field, F32),
            pltpu.VMEM(field, F32),
            pltpu.VMEM(field, F32),
            pltpu.VMEM(field, BF),
            pltpu.VMEM(field, BF),
            pltpu.VMEM(field, BF),
            pltpu.VMEM(field, BF),
            pltpu.VMEM(halo, BF),
            pltpu.VMEM(halo, BF),
            pltpu.VMEM((256, 256), F32),
            pltpu.VMEM((128, 128), F32),
            pltpu.VMEM((8, 256), F32),
            pltpu.VMEM((8, 128), F32),
            pltpu.VMEM((r1, 128), F32),
            pltpu.VMEM((r2, 128), F32),
            *sums(r1),
            *sums(r2),
            pltpu.SemaphoreType.DMA((chunks,)),
            pltpu.SemaphoreType.DMA((chunks,)),
            pltpu.SemaphoreType.DMA((4, chunks, 3)),
            pltpu.SemaphoreType.DMA((4, chunks, 3)),
            pltpu.SemaphoreType.DMA((chunks,)),
            pltpu.SemaphoreType.DMA((chunks,)),
            pltpu.SemaphoreType.DMA((n_ar,)),
            pltpu.SemaphoreType.DMA((n_ar,)),
        ],
        compiler_params=pltpu.CompilerParams(
            collective_id=0, has_side_effects=True, vmem_limit_bytes=56 << 20),
    )(
        series.reshape(raw), cotangent.reshape(raw), w_filter, w_gate,
        b_filter.reshape(1, -1), b_gate.reshape(1, -1), w_diff, b_diff.reshape(1, -1),
        tile_row, tile_col, tile_val[0], send_nodes[0], send_count,
    )
    return (
        out.reshape(series.shape),
        gs.reshape(series.shape),
        fin1[0:256].reshape(2, 128, 128),
        fin1[256:512].reshape(2, 128, 128),
        fin1[640],
        fin1[641],
        jnp.concatenate([fin1[512:640], fin2[:256]], axis=0).reshape(3, 128, 128),
        fin1[642],
    )


def gather_kernel(
    seg_n, tm_n, scale,
    ser_h, cot_h, wf_h, wg_h, bf_h, bg_h, wd_h, bd_h, trow_h, tcol_h, tval_h, snodes_h, scount_h,
    out3, gs3, fin,
    ser3, cot3, wf, wg, bf, bg, wd, bd, trow, tcol, tval, snodes, scount, load, big, big_g, stage_s, stage_c, ser, cot, tiles, meta,
    opf, opb, oph, pick, wc, wct, wdt,
    act_f, act_g, src0, src1, hop2, sb0, sb1, acc,
    out_b, gs_b, out_r, gs_r, pair,
    red_a, red_b, low_a, low_b, a0, a1, a2, a3, b0, b1, b2, b3,
    tz_s, tz_r, mz_s, mz_r, tx_s, tx_r, tc_s, tc_r,
    se_s, se_r, co_s, co_r, ou_s, ou_r, gr_s, gr_r, ar_s, ar_r,
):
    p = lax.axis_index("seg")
    t = lax.axis_index("tm")
    rep = lax.axis_index("rep")
    loads = [
        pltpu.make_async_copy(src, dst, load.at[i])
        for i, (src, dst) in enumerate([
            (tval_h, tval), (snodes_h, snodes), (trow_h, trow), (tcol_h, tcol), (scount_h, scount),
            (ser_h, ser3), (cot_h, cot3), (wf_h, wf), (wg_h, wg), (bf_h, bf), (bg_h, bg), (wd_h, wd), (bd_h, bd)])]
    nodes, frames, ch = ser3.shape
    mine = p * tm_n + t
    crew = 2 * tm_n
    quarter = tiles.shape[1] // crew

    def rc(src, dst, ss, rs, dev):
        return pltpu.make_async_remote_copy(
            src_ref=src, dst_ref=dst, send_sem=ss, recv_sem=rs, device_id=dev, device_id_type=MESH)

    low, high = lax.rem(p, 2), lax.div(p, 2)

    def flip(j):
        return lax.rem(high + j // 2, 2) * 2 + lax.rem(low + j % 2, 2)

    def peer(j, m):
        return flip(j), lax.rem(t + m, tm_n)

    others = [(2, 0), (3, 0), (2, 1), (3, 1), (1, 0), (1, 1), (0, 1)]

    def rows_of(q):
        return pl.ds(pl.multiple_of(q * nodes, 128), nodes)

    def piece(c):
        return pl.ds(pl.multiple_of(c * quarter, 16), quarter)

    core = {"rep": 1 - rep}
    across = {"tm": 1 - t}

    barrier = pltpu.get_barrier_semaphore()
    for j, m in others:
        q, tt = peer(j, m)
        pl.semaphore_signal(barrier, inc=1, device_id={"seg": q, "tm": tt}, device_id_type=MESH)
    pl.semaphore_signal(barrier, inc=1, device_id=core, device_id_type=MESH)

    for one in loads:
        one.start()
    pl.semaphore_wait(barrier, len(others) + 1)

    c_me = t * 2 + rep
    c_across = (1 - t) * 2 + rep

    def tile_z(j):
        return rc(tval_h.at[piece(c_me)], tiles.at[p, piece(c_me)], tz_s.at[j], tz_r.at[j], {"seg": flip(j)})

    def tile_on():
        at = tiles.at[flip(2), piece(c_me)]
        return rc(at, at, tz_s.at[3], tz_r.at[3], {"seg": flip(1)})

    def meta_z(j):
        return rc(meta.at[p], meta.at[p], mz_s.at[j], mz_r.at[j], {"seg": flip(j)})

    def tile_x(j):
        at = tiles.at[flip(j), piece(c_me)]
        return rc(at, at, tx_s.at[j], tx_r.at[j], across)

    def tile_c(j, c, i):
        at = tiles.at[flip(j), piece(c)]
        return rc(at, at, tc_s.at[j, i], tc_r.at[j, i], core)

    def field_in(stage, whole, ss, rs, j, m):
        q, tt = peer(j, m)
        f = q * tm_n + tt
        return rc(stage.at[f], whole.at[t, rows_of(p)], ss.at[f], rs.at[mine], {"seg": q, "tm": tt})

    def field_got(stage, whole, ss, rs, j, m):
        q, tt = peer(j, m)
        f = q * tm_n + tt
        return rc(stage.at[f], whole.at[tt, rows_of(q)], ss.at[f], rs.at[f], {"seg": q, "tm": tt})

    def frame_major(source, wide, stage, whole):
        wide[...] = source[...].astype(F32)
        for f in range(frames):
            stage[f] = wide[:, f, :].astype(BF)
        whole[t, rows_of(p), :] = stage[mine]

    tile_z(2).start()
    tile_z(1).start()
    for one in loads[1:5]:
        one.wait()
    meta[p] = jnp.zeros_like(meta[p])
    for j in range(3):
        meta[p, j:j + 1, :] = snodes[j]
    meta[p, 3:4, 0:trow.shape[1]] = trow[...]
    meta[p, 4:5, 0:tcol.shape[1]] = tcol[...]
    meta[p, 5:6, 0:scount.shape[1]] = scount[...]
    for j in (2, 3, 1):
        meta_z(j).start()
    loads[5].wait()
    frame_major(ser3, big, stage_s, ser)
    field_in(stage_s, ser, se_s, se_r, 2, 0).start()
    loads[0].wait()
    tiles[p] = tval[...]

    tile_z(2).wait_recv()
    tile_on().start()
    tile_x(2).start()
    tile_z(1).wait_recv()
    tile_x(1).start()
    field_in(stage_s, ser, se_s, se_r, 3, 0).start()
    tile_on().wait_recv()
    tile_x(3).start()
    for j, m in [(2, 1), (1, 1), (3, 1), (1, 0), (0, 1)]:
        field_in(stage_s, ser, se_s, se_r, j, m).start()

    for one in loads[6:]:
        one.wait()
    frame_major(cot3, big_g, stage_c, cot)
    for j, m in others:
        field_in(stage_c, cot, co_s, co_r, j, m).start()

    for j in (2, 1, 3):
        tile_x(j).wait_recv()
        tile_c(j, c_me, 0).start()
        tile_c(j, c_across, 1).start()

    for i in range(2):
        wc[i * ch:(i + 1) * ch, 0:ch] = wf[i]
        wc[i * ch:(i + 1) * ch, ch:2 * ch] = wg[i]
    wct[...] = wc[...].astype(F32).T.astype(BF)
    for i in range(3):
        wdt[i] = wd[i].astype(F32).T.astype(BF)
    bias = jnp.concatenate([bf[...], bg[...]], axis=1)
    red_a[...] = jnp.zeros_like(red_a)
    red_b[...] = jnp.zeros_like(red_b)

    for j in (2, 1, 3):
        tile_c(j, c_me, 0).wait_recv()
        tile_c(j, c_across, 1).wait_recv()
        meta_z(j).wait_recv()

    rows_n = nodes // 128
    cols_n = rows_n + 3
    tiles_n = tiles.shape[1] // 128
    halo = 3 * 128
    lane_ids = lax.broadcasted_iota(jnp.int32, (128, nodes), 1)
    sub_ids = lax.broadcasted_iota(jnp.int32, (nodes, 128), 0)
    slot_lane = lax.broadcasted_iota(jnp.int32, (1, 128), 1)
    slot_sub = lax.broadcasted_iota(jnp.int32, (128, 1), 0)

    def build(q, _):
        info = meta[q]
        tr, tc = info[3:4, :], info[4:5, :]
        t_all = [tiles[q, k * 128:(k + 1) * 128, :].astype(F32) for k in range(tiles_n)]
        for r in range(rows_n):
            for c in range(cols_n):
                hits = jnp.where((tr == r) & (tc == c), 1.0, 0.0)
                total = jnp.zeros((128, 128), F32)
                for k in range(tiles_n):
                    if k < rows_n and (r != k or c != k):
                        continue
                    if rows_n <= k < cols_n and c != k:
                        continue
                    total = total + hits[:, k:k + 1] * t_all[k]
                flipped = total.T.astype(BF)
                opf[q, r * 128:(r + 1) * 128, c * 128:(c + 1) * 128] = total.astype(BF)
                if c < rows_n:
                    opb[q, c * 128:(c + 1) * 128, r * 128:(r + 1) * 128] = flipped
                else:
                    oph[q, (c - rows_n) * 128:(c - rows_n + 1) * 128, r * 128:(r + 1) * 128] = flipped
        col = info.astype(F32).T.astype(jnp.int32)
        for j in range(3):
            count = info[5:6, j:j + 1]
            give = jnp.where((sub_ids == info[j:j + 1, :]) & (slot_lane < count), 1.0, 0.0)
            opb[q, :, nodes + j * 128:nodes + (j + 1) * 128] = give.astype(BF)
            take = jnp.where((lane_ids == col[:, j:j + 1]) & (slot_sub < count), 1.0, 0.0)
            pick[q, j * 128:(j + 1) * 128, :] = take.astype(BF)
        return 0

    lax.fori_loop(0, seg_n, build, 0)

    for j, m in others:
        field_got(stage_s, ser, se_s, se_r, j, m).wait_recv()

    def conv(q, _):
        for tt in range(tm_n):
            now = ser[tt, rows_of(q), :]
            if tt == 0:
                pre = mm(now, wc[ch:2 * ch, :]) + bias
            else:
                pre = mm(jnp.concatenate([ser[tt - 1, rows_of(q), :], now], axis=1), wc[...]) + bias
            a = jnp.tanh(pre[:, 0:ch])
            s = jax.nn.sigmoid(pre[:, ch:2 * ch])
            act_f[tt, rows_of(q), :] = a
            act_g[tt, rows_of(q), :] = s
            src0[q, 0:nodes, tt * ch:(tt + 1) * ch] = (a * s).astype(BF)
        return 0

    def send_slots(src):
        def one(q, _):
            got = mm(pick[q], src[q, 0:nodes, :]).astype(BF)
            for j in range(3):
                reader = lax.rem(q - STEPS[j] + seg_n, seg_n)
                src[reader, nodes + j * 128:nodes + (j + 1) * 128, :] = got[j * 128:(j + 1) * 128]
            return 0
        lax.fori_loop(0, seg_n, one, 0)

    def hop(src, dst):
        def one(q, _):
            dst[q, 0:nodes, :] = mm(opf[q], src[q]).astype(BF)
            return 0
        lax.fori_loop(0, seg_n, one, 0)

    def home(buf, got, ss, rs, q, tt):
        return rc(buf.at[tt, rows_of(q)], got.at[mine], ss.at[q * tm_n + tt], rs.at[mine], {"seg": q, "tm": tt})

    def gs_arrived(f):
        for h in range(2):
            rc(gs_b.at[f % tm_n, pl.ds(f // tm_n * nodes + h * part, part)], gs_r.at[f, pl.ds(h * part, part)],
               gr_s.at[f, h], gr_r.at[f, h], {"seg": f // tm_n, "tm": f % tm_n}).wait_recv()

    def out_arrived(f):
        arrived(out_b, out_r, ou_s, ou_r, f).wait_recv()

    def arrived(buf, got, ss, rs, f):
        return rc(buf.at[f % tm_n, pl.ds(f // tm_n * nodes, nodes)], got.at[f], ss.at[f], rs.at[f],
                  {"seg": f // tm_n, "tm": f % tm_n})

    def out_go(*pairs):
        for j, m in pairs:
            q, tt = peer(j, m)
            home(out_b, out_r, ou_s, ou_r, q, tt).start()

    part = nodes // 2

    def gs_half(q, tt, h):
        start = pl.ds(pl.multiple_of(q * nodes + h * part, 16), part)
        return rc(gs_b.at[tt, start], gs_r.at[mine, pl.ds(h * part, part)],
                  gr_s.at[q * tm_n + tt, h], gr_r.at[mine, h], {"seg": q, "tm": tt})

    def gs_go(*pairs):
        for j, m, h in pairs:
            q, tt = peer(j, m)
            gs_half(q, tt, h).start()

    lax.fori_loop(0, seg_n, conv, 0)
    send_slots(src0)
    hop(src0, src1)
    send_slots(src1)
    hop(src1, hop2)
    bias_d = bd[...]

    def put_out(q, _):
        for tt in range(tm_n):
            lo, hi = tt * ch, (tt + 1) * ch
            two = jnp.concatenate([src0[q, 0:nodes, lo:hi], src1[q, 0:nodes, lo:hi]], axis=1)
            total = mm(two, jnp.concatenate([wd[0], wd[1]], axis=0)) + mm(hop2[q, :, lo:hi], wd[2]) + bias_d
            out_b[tt, rows_of(q), :] = (ser[tt, rows_of(q), :].astype(F32) + total).astype(BF)
        return 0

    lax.fori_loop(0, seg_n, put_out, 0)
    out_go((2, 1), (1, 1), (3, 1), (1, 0), (0, 1))

    for j, m in others:
        field_got(stage_c, cot, co_s, co_r, j, m).wait_recv()

    base = 4 * ch

    def span(start, size):
        return pl.ds(pl.multiple_of(start, 16), size)

    def quad_device(m, k):
        return {"seg": flip(k), "tm": lax.rem(t + m, 2)}

    def summed(red, b0, b1, b2, b3, low_out, first):
        half = red.shape[0] // 2
        eighth = half // 4
        at_core = rep * half

        def at_quad(m, k):
            return span(at_core + lax.rem(t + m, 2) * (2 * eighth) + lax.rem(low + k, 2) * eighth, eighth)

        def go(src, dst, at, dev):
            made = rc(src, dst, ar_s.at[first + at], ar_r.at[first + at], dev)
            made.start()
            return made

        quad = [(1, 1), (1, 0), (0, 1)]
        here = at_quad(0, 0)
        step = go(red.at[span((1 - rep) * half, half)], b0, 0, core)
        yield
        step.wait()
        red[span(at_core, half), :] += b0[...]
        steps = [
            go(red.at[at_quad(m, k)], b1.at[i], 1 + i, quad_device(m, k))
            for i, (m, k) in enumerate(quad)]
        yield
        for step in steps:
            step.wait()
        b3[...] = (red[here, :] + b1[0] + b1[1] + b1[2]).astype(BF)
        step = go(b3, b2, 4, {"seg": flip(2)})
        yield
        step.wait()
        low_out[here, :] = ((b3[...].astype(F32) + b2[...].astype(F32)) * scale).astype(BF)
        steps = [
            go(low_out.at[here], low_out.at[here], 5 + i, quad_device(m, k))
            for i, (m, k) in enumerate(quad)]
        yield
        for step in steps:
            step.wait()
        whole = low_out.at[span(at_core, half)]
        step = go(whole, whole, 8, core)
        yield
        step.wait()
        yield

    sum_a = summed(red_a, a0, a1, a2, a3, low_a, 0)
    sum_b = summed(red_b, b0, b1, b2, b3, low_b, 9)

    def back(q, _):
        for tt in range(tm_n):
            lo, hi = tt * ch, (tt + 1) * ch
            g = cot[tt, rows_of(q), :]
            u = mm(g, jnp.concatenate([wdt[2], wdt[1]], axis=1))
            sb0[q, 0:nodes, lo:hi] = u[:, 0:ch].astype(BF)
            acc[q, :, lo:hi] = u[:, ch:2 * ch]
            hops = jnp.concatenate(
                [src0[q, 0:nodes, lo:hi], src1[q, 0:nodes, lo:hi], hop2[q, :, lo:hi]], axis=1)
            red_a[...] += mm_tn(hops, g)
            red_b[base + 2:base + 3, :] += jnp.sum(g.astype(F32), axis=0, keepdims=True)
        return 0

    def send_back(sb):
        def one(q, _):
            got = mm(oph[q], sb[q, 0:nodes, :]).astype(BF)
            for j in range(3):
                owner = lax.rem(q + STEPS[j] + seg_n, seg_n)
                sb[owner, nodes + j * 128:nodes + (j + 1) * 128, :] = got[j * 128:(j + 1) * 128]
            return 0
        lax.fori_loop(0, seg_n, one, 0)

    lax.fori_loop(0, seg_n, back, 0)
    next(sum_a)
    send_back(sb0)

    def back_mid(q, _):
        sb1[q, 0:nodes, :] = (acc[q] + mm(opb[q], sb0[q])).astype(BF)
        return 0

    next(sum_a)
    lax.fori_loop(0, seg_n, back_mid, 0)
    out_go((2, 0), (3, 0))
    send_back(sb1)

    def back_last(q, _):
        gh_all = mm(opb[q], sb1[q])
        for tt in range(tm_n):
            lo, hi = tt * ch, (tt + 1) * ch
            g = cot[tt, rows_of(q), :]
            gh = gh_all[:, lo:hi] + mm(g, wdt[0])
            a, s = act_f[tt, rows_of(q), :], act_g[tt, rows_of(q), :]
            gf = (gh * s * (1.0 - a * a)).astype(BF)
            gg = (gh * a * (s * (1.0 - s))).astype(BF)
            both = jnp.concatenate([gf, gg], axis=1)
            pair[tt, rows_of(q), :] = both
            now = ser[tt, rows_of(q), :]
            if tt == 0:
                part = mm_tn(now, both)
                red_b[ch:2 * ch, :] += part[:, 0:ch]
                red_b[3 * ch:4 * ch, :] += part[:, ch:2 * ch]
            else:
                part = mm_tn(jnp.concatenate([ser[tt - 1, rows_of(q), :], now], axis=1), both)
                red_b[0:2 * ch, :] += part[:, 0:ch]
                red_b[2 * ch:4 * ch, :] += part[:, ch:2 * ch]
            red_b[base:base + 1, :] += jnp.sum(gf.astype(F32), axis=0, keepdims=True)
            red_b[base + 1:base + 2, :] += jnp.sum(gg.astype(F32), axis=0, keepdims=True)
        return 0

    lax.fori_loop(0, seg_n, back_last, 0)

    next(sum_b)
    next(sum_a)

    def put_gs(q, _):
        later = None
        for tt in reversed(range(tm_n)):
            both = pair[tt, rows_of(q), :]
            if tt == 0:
                total = mm(both, wct[:, ch:2 * ch])
            else:
                r = mm(both, wct[...])
                total = r[:, ch:2 * ch]
            total = cot[tt, rows_of(q), :].astype(F32) + total
            if later is not None:
                total = total + later.astype(F32)
            if tt > 0:
                later = r[:, 0:ch].astype(BF)
            gs_b[tt, rows_of(q), :] = total.astype(BF)
        return 0

    lax.fori_loop(0, seg_n, put_gs, 0)
    next(sum_b)
    gs_go((2, 0, 0),)
    out_r[mine] = out_b[t, rows_of(p), :]
    gs_r[mine] = gs_b[t, rows_of(p), :]

    def node_major(got, wide, dest, ready):
        for f in range(frames):
            @pl.when(f != mine)
            def _():
                ready(f)

            wide[:, f, :] = got[f].astype(F32)
        dest[...] = wide[...].astype(BF)

    next(sum_b)
    gs_go((2, 1, 0), (1, 1, 0), (2, 1, 1), (1, 1, 1), (2, 0, 1))
    next(sum_a)
    gs_go((3, 1, 0), (1, 0, 0), (3, 1, 1), (1, 0, 1), (3, 0, 0), (0, 1, 0), (3, 0, 1), (0, 1, 1))
    next(sum_b)
    node_major(out_r, big, out3, out_arrived)
    next(sum_a)
    next(sum_b)
    next(sum_a)
    fin[base:base + 3 * ch, :] = low_a[...].astype(F32)
    node_major(gs_r, big_g, gs3, gs_arrived)
    next(sum_b)
    fin[0:base, :] = low_b[0:base, :].astype(F32)
    fin[base + 3 * ch:base + 3 * ch + 16, :] = low_b[base:base + 16, :].astype(F32)

    tile_z(2).wait_send()
    tile_z(1).wait_send()
    tile_on().wait_send()
    for j in (1, 2, 3):
        meta_z(j).wait_send()
        tile_x(j).wait_send()
        tile_c(j, c_me, 0).wait_send()
        tile_c(j, c_across, 1).wait_send()
    for j, m in others:
        q, tt = peer(j, m)
        field_in(stage_s, ser, se_s, se_r, j, m).wait_send()
        field_in(stage_c, cot, co_s, co_r, j, m).wait_send()
        home(out_b, out_r, ou_s, ou_r, q, tt).wait_send()
        gs_half(q, tt, 0).wait_send()
        gs_half(q, tt, 1).wait_send()


def finish_kernel(out_i, gs_i, fin, out_o, gs_o, o_wf, o_wg, o_bf, o_bg, o_wd, o_bd, sems):
    ch = o_wf.shape[1]
    pairs = [(out_i, out_o), (gs_i, gs_o)]
    for i in range(7):
        target = o_wf.at[i] if i < 2 else o_wg.at[i - 2] if i < 4 else o_wd.at[i - 4]
        pairs.append((fin.at[pl.ds(i * ch, ch)], target))
    for i, target in enumerate((o_bf, o_bg, o_bd)):
        pairs.append((fin.at[pl.ds(7 * ch + i, 1)], target))
    copies = [pltpu.make_async_copy(src, dst, sems.at[i]) for i, (src, dst) in enumerate(pairs)]
    for one in copies:
        one.start()
    for one in copies:
        one.wait()


def gather_plan(mesh, series, cotangent, w_filter, w_gate, b_filter, b_gate, w_diff, b_diff,
                tile_row, tile_col, tile_val, send_nodes, send_count):
    nodes, batch, frames, ch = series.shape
    seg_n, tm_n, rep_n = mesh.shape["seg"], mesh.shape["tm"], mesh.shape["rep"]
    scale = 1.0 / math.sqrt(nodes * batch * frames * seg_n * tm_n * rep_n)
    unit = 16 * 8
    rows_a = 3 * ch
    rows_b = -(-(4 * ch + 8) // unit) * unit
    total_rows = 7 * ch + 16

    def steps_of(rows):
        return [
            pltpu.VMEM((rows // 2, ch), F32),
            pltpu.VMEM((3, rows // 8, ch), F32),
            pltpu.VMEM((rows // 8, ch), BF),
            pltpu.VMEM((rows // 8, ch), BF),
        ]

    vmem = pl.BlockSpec(memory_space=pltpu.VMEM)
    anyw = pl.BlockSpec(memory_space=pl.ANY)
    raw = (nodes, batch * frames, ch)
    tall = (frames, nodes, ch)
    everyone = (tm_n, seg_n * nodes, ch)
    wide = tm_n * ch
    tile_rows = tile_val.shape[1] * 128
    halo = 3 * 128
    dma = pltpu.SemaphoreType.DMA
    out, gs, fin = pl.pallas_call(
        functools.partial(gather_kernel, seg_n, tm_n, scale),
        out_shape=(
            pltpu.VMEM(raw, BF),
            pltpu.VMEM(raw, BF),
            pltpu.VMEM((total_rows, ch), F32),
        ),
        in_specs=[anyw] * 13,
        out_specs=(vmem,) * 3,
        scratch_shapes=[
            pltpu.VMEM(raw, BF),
            pltpu.VMEM(raw, BF),
            pltpu.VMEM(w_filter.shape, BF),
            pltpu.VMEM(w_gate.shape, BF),
            pltpu.VMEM((1, ch), F32),
            pltpu.VMEM((1, ch), F32),
            pltpu.VMEM(w_diff.shape, BF),
            pltpu.VMEM((1, ch), F32),
            pltpu.VMEM(tile_row.shape, jnp.int32),
            pltpu.VMEM(tile_col.shape, jnp.int32),
            pltpu.VMEM((tile_rows, 128), BF),
            pltpu.VMEM((3, 1, 128), jnp.int32),
            pltpu.VMEM(send_count.shape, jnp.int32),
            dma((13,)),
            pltpu.VMEM(raw, F32),
            pltpu.VMEM(raw, F32),
            pltpu.VMEM(tall, BF),
            pltpu.VMEM(tall, BF),
            pltpu.VMEM(everyone, BF),
            pltpu.VMEM(everyone, BF),
            pltpu.VMEM((seg_n, tile_rows, 128), BF),
            pltpu.VMEM((seg_n, 8, 128), jnp.int32),
            pltpu.VMEM((seg_n, nodes, nodes + halo), BF),
            pltpu.VMEM((seg_n, nodes, nodes + halo), BF),
            pltpu.VMEM((seg_n, halo, nodes), BF),
            pltpu.VMEM((seg_n, halo, nodes), BF),
            pltpu.VMEM((2 * ch, 2 * ch), BF),
            pltpu.VMEM((2 * ch, 2 * ch), BF),
            pltpu.VMEM((3, ch, ch), BF),
            pltpu.VMEM(everyone, F32),
            pltpu.VMEM(everyone, F32),
            pltpu.VMEM((seg_n, nodes + halo, wide), BF),
            pltpu.VMEM((seg_n, nodes + halo, wide), BF),
            pltpu.VMEM((seg_n, nodes, wide), BF),
            pltpu.VMEM((seg_n, nodes + halo, wide), BF),
            pltpu.VMEM((seg_n, nodes + halo, wide), BF),
            pltpu.VMEM((seg_n, nodes, wide), F32),
            pltpu.VMEM(everyone, BF),
            pltpu.VMEM(everyone, BF),
            pltpu.VMEM(tall, BF),
            pltpu.VMEM(tall, BF),
            pltpu.VMEM((tm_n, seg_n * nodes, 2 * ch), BF),
            pltpu.VMEM((rows_a, ch), F32),
            pltpu.VMEM((rows_b, ch), F32),
            pltpu.VMEM((rows_a, ch), BF),
            pltpu.VMEM((rows_b, ch), BF),
            *steps_of(rows_a),
            *steps_of(rows_b),
            dma((seg_n,)), dma((seg_n,)), dma((seg_n,)), dma((seg_n,)),
            dma((seg_n,)), dma((seg_n,)), dma((seg_n, 2)), dma((seg_n, 2)),
            dma((frames,)), dma((frames,)), dma((frames,)), dma((frames,)),
            dma((frames,)), dma((frames,)), dma((frames, 2)), dma((frames, 2)),
            dma((18,)), dma((18,)),
        ],
        compiler_params=pltpu.CompilerParams(
            collective_id=0, has_side_effects=True, vmem_limit_bytes=52 << 20),
    )(
        series.reshape(raw), cotangent.reshape(raw), w_filter, w_gate,
        b_filter.reshape(1, -1), b_gate.reshape(1, -1), w_diff, b_diff.reshape(1, -1),
        tile_row, tile_col, tile_val.reshape(tile_rows, 128), send_nodes.reshape(3, 1, 128), send_count,
    )
    vec = jax.ShapeDtypeStruct((1, ch), F32)
    out, gs, g_wf, g_wg, g_bf, g_bg, g_wd, g_bd = pl.pallas_call(
        finish_kernel,
        out_shape=(
            jax.ShapeDtypeStruct(raw, BF),
            jax.ShapeDtypeStruct(raw, BF),
            jax.ShapeDtypeStruct((2, ch, ch), F32),
            jax.ShapeDtypeStruct((2, ch, ch), F32),
            vec, vec,
            jax.ShapeDtypeStruct((3, ch, ch), F32),
            vec,
        ),
        in_specs=[anyw, anyw, vmem],
        out_specs=(anyw,) * 8,
        scratch_shapes=[dma((12,))],
    )(*[pltpu.with_memory_space_constraint(x, pltpu.VMEM) for x in (out, gs, fin)])
    return (
        out.reshape(series.shape), gs.reshape(series.shape), g_wf, g_wg,
        g_bf.reshape(-1), g_bg.reshape(-1), g_wd, g_bd.reshape(-1))


def on_device(mesh, series, *rest):
    nodes, batch, frames, ch = series.shape
    seg_n, tm_n = mesh.shape["seg"], mesh.shape["tm"]
    fits = seg_n == 4 and tm_n == 2 and batch == 1 and frames == seg_n * tm_n and frames == DILATION_FRAMES
    plan = gather_plan if fits else halo_plan
    return plan(mesh, series, *rest)


def solution(mesh):
    field = P(("grp", "seg"), "rep", "tm", None)
    part = ("grp", "seg")
    in_specs = (
        field, field, P(), P(), P(), P(), P(), P(),
        P(part, None), P(part, None), P(part, None, None, None), P(part, None, None), P(part, None),
    )
    out_specs = (
        field, field, P("grp", None, None), P("grp", None, None), P("grp"), P("grp"),
        P("grp", None, None), P("grp"),
    )
    return jax.shard_map(
        functools.partial(on_device, mesh), mesh=mesh, in_specs=in_specs, out_specs=out_specs,
        check_vma=False)
```
